32 devices in a mesh: seq: 32 (over z, y, x, core).
Axes of the slice: x: 2, y: 2, z: 4, core: 2. Of those that a mesh axis runs over, the one named last changes fastest.
Arguments:
- block_input: bfloat16 [4096, 1536], P('seq'), may hold values from -6 to 6
- documents: int32 [4096], replicated, may hold values from 0 to 3, never falling along the last dimension, each value on 1 to 2048 neighbouring positions
- first_gain: bfloat16 [1536], P('seq'), may hold values from 0.5 to 1.5
- inner_weight: bfloat16 [1536, 6144], P(None, 'seq'), may hold values from -0.15625 to 0.15625
- conv_weight: bfloat16 [4, 3072], P(None, 'seq'), may hold values from -3 to 3
- conv_bias: bfloat16 [3072], P('seq'), may hold values from -3 to 3
- select_weight: bfloat16 [3072, 128], P('seq'), may hold values from -0.109375 to 0.109375
- select_gain: bfloat16 [128], P('seq'), may hold values from 0.5 to 1.5
- step_weight: bfloat16 [96, 3072], P(None, 'seq'), may hold values from -0.625 to 0.625
- step_bias: bfloat16 [3072], P('seq'), may hold values from -9 to -2
- decay_log: bfloat16 [16, 3072], P(None, 'seq'), may hold values from 0 to 2.765625
- skip_gain: bfloat16 [3072], P('seq'), may hold values from 0.099609375 to 1.8984375
- mixer_weight: bfloat16 [3072, 1536], P('seq'), may hold values from -0.109375 to 0.109375
- second_gain: bfloat16 [1536], P('seq'), may hold values from 0.5 to 1.5
- gate_weight: bfloat16 [1536, 4096], P(None, 'seq'), may hold values from -0.15625 to 0.15625
- up_weight: bfloat16 [1536, 4096], P(None, 'seq'), may hold values from -0.15625 to 0.15625
- down_weight: bfloat16 [4096, 1536], P('seq'), may hold values from -0.09375 to 0.09375
- cotangent: bfloat16 [4096, 1536], P('seq'), may hold values from -6 to 6
Outputs:
- block_output: bfloat16 [4096, 1536], P('seq')
- input_grad: float32 [4096, 1536], P('seq')
- first_gain_grad: float32 [1536], P('seq')
- inner_weight_grad: float32 [1536, 6144], P(None, 'seq')
- conv_weight_grad: float32 [4, 3072], P(None, 'seq')
- conv_bias_grad: float32 [3072], P('seq')
- select_weight_grad: float32 [3072, 128], P('seq')
- select_gain_grad: float32 [128], P('seq')
- step_weight_grad: float32 [96, 3072], P(None, 'seq')
- step_bias_grad: float32 [3072], P('seq')
- decay_log_grad: float32 [16, 3072], P(None, 'seq')
- skip_gain_grad: float32 [3072], P('seq')
- mixer_weight_grad: float32 [3072, 1536], P('seq')
- second_gain_grad: float32 [1536], P('seq')
- gate_weight_grad: float32 [1536, 4096], P(None, 'seq')
- up_weight_grad: float32 [1536, 4096], P(None, 'seq')
- down_weight_grad: float32 [4096, 1536], P('seq')
The draws below stay inside these ranges and needn't reach their ends.
Inputs may be any that keep to these rules, and one draw needn't show every extreme that they name: documents never falls along the stream; 4 documents, each of 1 to 2048 tokens, one of exactly 2048.
All inputs are finite; a program needn't handle non-finite values.
Results may differ from the reference program's by a relative error of at most 0.015.
Values may be sent and summed in bfloat16 or wider, within the bound.
A program may use at most 384 MiB of HBM per device.

```python
import math
import jax
import jax.numpy as jnp
import numpy as np
from jax import lax

D = 1536
INNER = 3072
STATE = 16
CONV = 4
RANK = 96
FF = 4096
BLOCK = 16
TOKENS = 4096
DOCS = 4
DOC_MOST = 2048
REF_BLOCK = 4096


def raised(array, key, source, target, blocks, factor):
    def block_of(dim):
        return (jnp.arange(array.shape[dim]) // (array.shape[dim] // blocks)).reshape((-1,) + (1,) * (array.ndim - 1 - dim))

    one_side = jax.random.permutation(key, blocks)[block_of(target)]
    far = (block_of(target) + blocks // 2) % blocks
    return jnp.where((block_of(source) == one_side) | (block_of(source) == far), factor * array, array)


def block_levels(own_key, shape, split, least, high):
    def one(dim, shards_of):
        draws = jax.random.uniform(jax.random.fold_in(jax.random.fold_in(own_key, 6), dim), (shards_of,), jnp.float32, least / len(split), high / len(split))
        return jnp.repeat(jnp.exp(draws), shape[dim] // shards_of).reshape((-1,) + (1,) * (len(shape) - dim - 1))

    factor_of = one(*split[0])
    for cut in split[1:]:
        factor_of = factor_of * one(*cut)
    return factor_of


def profile(count, total, limit, lean):
    portions = [(1 << 20) // math.isqrt(standing ** lean) + 1 for standing in range(2, count + 1)]
    surplus, given = total - limit - (count - 1), [1] * (count - 1)
    while surplus > 0:
        movable = [i for i in range(count - 1) if given[i] < limit]
        whole, budget = sum([portions[i] for i in movable]), surplus
        for i in movable:
            addition = min(limit - given[i], max(1, budget * portions[i] // whole), surplus)
            given[i] = given[i] + addition
            surplus = surplus - addition
    return np.array([limit] + given)


def uneven(key, amount, total, reach, slope):
    if amount == 2:
        one = jax.random.randint(key, (), max(1, total - reach), min(reach, total - 1) + 1)
        return jnp.stack([one, total - one])
    lengths = jnp.asarray(profile(amount, total, reach, slope), jnp.int32)
    pairs = (amount - 1) // 2
    donor, taker = lengths[1:1 + 2 * pairs:2], lengths[2:2 + 2 * pairs:2]
    slack = jnp.minimum(donor - 1, reach - taker)
    shifted = jax.random.randint(jax.random.fold_in(key, 1), (pairs,), 0, 1 << 20) % (slack + 1)
    lengths = lengths.at[1:1 + 2 * pairs:2].set(donor - shifted).at[2:2 + 2 * pairs:2].set(taker + shifted)
    return lengths[jax.random.permutation(jax.random.fold_in(key, 2), amount)]


def normal_values(stream_key, dims, width, limit, shards=(), kind=jnp.bfloat16):
    entries = width * jax.random.normal(stream_key, dims, jnp.float32)
    if shards:
        entries = entries * block_levels(stream_key, dims, shards, -0.22, 0.18)
    return jnp.clip(entries, -limit, limit).astype(kind)


def noise_with(key, shape, scale, most, split, heavy, kind=jnp.bfloat16):
    values = scale * jax.random.normal(key, shape, jnp.float32)
    if split:
        values = values * block_levels(key, shape, split, -0.22, 0.18)
    return jnp.clip(raised(values, jax.random.fold_in(key, 3), *heavy), -most, most).astype(kind)


def setup_inputs(seed: int = 0) -> dict:
    seeds = jax.random.split(jax.random.key(seed), 19)
    block_input = normal_values(seeds[0], (TOKENS, D), 1.0, 6.0, ((0, 32),))
    documents = jnp.searchsorted(jnp.cumsum(uneven(seeds[1], DOCS, TOKENS, DOC_MOST, 1)), jnp.arange(TOKENS), side="right").astype(jnp.int32)
    first_gain = jnp.clip(1.0 + 0.1 * jax.random.normal(seeds[2], (D,), jnp.float32), 0.5, 1.5).astype(jnp.bfloat16)
    inner_weight = normal_values(seeds[3], (D, 2 * INNER), D ** -0.5, 0.15625, ((1, 32),))
    conv_weight = normal_values(seeds[4], (CONV, INNER), CONV ** -0.5, 3.0, ((1, 32),))
    conv_bias = normal_values(seeds[5], (INNER,), 0.5, 3.0, ((0, 32),))
    select_weight = normal_values(seeds[6], (INNER, RANK + 2 * STATE), INNER ** -0.5, 0.109375, ((0, 32),))
    select_gain = jnp.clip(1.0 + 0.1 * jax.random.normal(seeds[7], (RANK + 2 * STATE,), jnp.float32), 0.5, 1.5).astype(jnp.bfloat16)
    step_weight = normal_values(seeds[8], (RANK, INNER), RANK ** -0.5, 0.625, ((1, 32),))
    step_bias = jnp.clip(-9.0 + 7.0 * jax.random.uniform(seeds[9], (INNER,), jnp.float32) ** block_levels(seeds[9], (INNER,), ((0, 32),), -0.2, 0.2), -9.0, -2.0).astype(jnp.bfloat16)
    decay_log = jnp.clip(2.765625 * jax.random.uniform(seeds[10], (STATE, INNER), jnp.float32) ** block_levels(seeds[10], (STATE, INNER), ((1, 32),), -0.2, 0.2), 0.0, 2.765625).astype(jnp.bfloat16)
    skip_gain = jnp.clip(1.0 + 0.18 * jax.random.normal(seeds[11], (INNER,), jnp.float32), 0.099609375, 1.8984375).astype(jnp.bfloat16)
    mixer_weight = normal_values(seeds[12], (INNER, D), INNER ** -0.5, 0.109375, ((0, 32),))
    second_gain = jnp.clip(1.0 + 0.1 * jax.random.normal(seeds[13], (D,), jnp.float32), 0.5, 1.5).astype(jnp.bfloat16)
    gate_weight = normal_values(seeds[14], (D, FF), D ** -0.5, 0.15625, ((1, 32),))
    up_weight = normal_values(seeds[15], (D, FF), D ** -0.5, 0.15625, ((1, 32),))
    down_weight = normal_values(seeds[16], (FF, D), FF ** -0.5, 0.09375, ((0, 32),))
    cotangent = noise_with(seeds[17], (TOKENS, D), 1.0, 6.0, ((0, 32),), (0, 1, 32, 2.75))
    return dict(block_input=block_input, documents=documents, first_gain=first_gain, inner_weight=inner_weight, conv_weight=conv_weight, conv_bias=conv_bias, select_weight=select_weight, select_gain=select_gain, step_weight=step_weight, step_bias=step_bias, decay_log=decay_log, skip_gain=skip_gain, mixer_weight=mixer_weight, second_gain=second_gain, gate_weight=gate_weight, up_weight=up_weight, down_weight=down_weight, cotangent=cotangent)


EPSILON = 1e-06

@jax.custom_vjp
def low(v):
    return lax.optimization_barrier(v.astype(jnp.bfloat16)).astype(jnp.float32)

@jax.custom_vjp
def low_back(v):
    return v

def low_keep(v):
    return (low(v), None)

def low_pass(kept, grad):
    return (grad,)

def back_keep(v):
    return (v, None)

def back_low(kept, grad):
    return (low(grad),)
low.defvjp(low_keep, low_pass)
low_back.defvjp(back_keep, back_low)

def exact_dot(left, right):
    return jnp.dot(left, right, precision=lax.Precision.HIGHEST, preferred_element_type=jnp.float32)

def rms_scale(values, scale_gain):
    return values * lax.rsqrt(lax.optimization_barrier(jnp.mean(values * values, axis=-1, keepdims=True)) + EPSILON) * scale_gain

def make_block(neg_rate):

    def run_block(carried, pieces):
        step_size, mixed_in, input_map, output_map, keep_mask = pieces
        results = []
        for position in range(step_size.shape[0]):
            decay_now = jnp.exp(step_size[position][None, :] * neg_rate) * keep_mask[position]
            carried = decay_now * carried + (step_size[position] * mixed_in[position])[None, :] * input_map[position][:, None]
            results.append(lax.optimization_barrier(jnp.sum(carried * output_map[position][:, None], axis=0)))
        return (carried, jnp.stack(results))
    return jax.checkpoint(run_block)

def reference(block_input, documents, first_gain, inner_weight, conv_weight, conv_bias, select_weight, select_gain, step_weight, step_bias, decay_log, skip_gain, mixer_weight, second_gain, gate_weight, up_weight, down_weight, cotangent):
    params = tuple((argument.astype(jnp.float32) for argument in (first_gain, inner_weight, conv_weight, conv_bias, select_weight, select_gain, step_weight, step_bias, decay_log, skip_gain, mixer_weight, second_gain, gate_weight, up_weight, down_weight)))
    padded_docs = jnp.concatenate([jnp.full((3,), -1, jnp.int32), documents.astype(jnp.int32)])
    count = REF_BLOCK // BLOCK

    def forward(resid_all, weights):
        first_f, inner_f, conv_w, conv_b, select_f, sel_gain, step_f, bias_f, decay_f, skip_f, mixer_f, second_f, gate_f, up_f, down_f = weights
        neg_rate = -jnp.exp(decay_f)
        run_block = make_block(neg_rate)

        def segment(carried_pair, index):
            carried, tail = carried_pair
            offset = (index * REF_BLOCK).astype(jnp.int32)
            resid_in = lax.dynamic_slice_in_dim(resid_all, offset, REF_BLOCK, 0)
            doc_ids = lax.dynamic_slice_in_dim(padded_docs, offset, REF_BLOCK + 3, 0)
            current = doc_ids[3:]
            keep_mask = (current == doc_ids[2:REF_BLOCK + 2]).astype(jnp.float32)
            normed_one = low(rms_scale(resid_in, first_f))
            inner_both = low_back(exact_dot(normed_one, inner_f))
            conv_input = low(inner_both[:, :INNER])
            gate_inner = inner_both[:, INNER:]
            extended = jnp.concatenate([tail, conv_input], 0)
            total = conv_b + conv_w[3] * conv_input
            for delay in range(3):
                same_doc = (doc_ids[delay:delay + REF_BLOCK] == current).astype(jnp.float32)[:, None]
                total = total + conv_w[delay] * extended[delay:delay + REF_BLOCK] * same_doc
            mixed_in = low(jax.nn.silu(total))
            proj_small = low_back(exact_dot(mixed_in, select_f))
            step_low = low(rms_scale(proj_small[:, :RANK], sel_gain[:RANK]))
            input_map = rms_scale(proj_small[:, RANK:RANK + STATE], sel_gain[RANK:RANK + STATE])
            output_map = rms_scale(proj_small[:, RANK + STATE:], sel_gain[RANK + STATE:])
            step_size = jax.nn.softplus(low_back(exact_dot(step_low, step_f)) + bias_f)
            carried, results = lax.scan(run_block, carried, (step_size.reshape(count, BLOCK, INNER), mixed_in.reshape(count, BLOCK, INNER), input_map.reshape(count, BLOCK, STATE), output_map.reshape(count, BLOCK, STATE), keep_mask.reshape(count, BLOCK)))
            mixed = results.reshape(REF_BLOCK, INNER) + skip_f * mixed_in
            gated = low(mixed * jax.nn.silu(gate_inner))
            resid_mid = resid_in + low_back(exact_dot(gated, mixer_f))
            normed_two = low(rms_scale(resid_mid, second_f))
            ffn_gate = low_back(exact_dot(normed_two, gate_f))
            ffn_up = low_back(exact_dot(normed_two, up_f))
            ffn_hidden = low(jax.nn.silu(ffn_gate) * ffn_up)
            result_rows = resid_mid + low_back(exact_dot(ffn_hidden, down_f))
            return ((carried, conv_input[REF_BLOCK - 3:]), result_rows)
        initial = (jnp.zeros((STATE, INNER), jnp.float32), jnp.zeros((3, INNER), jnp.float32))
        _, blocks_out = lax.scan(jax.checkpoint(segment), initial, jnp.arange(TOKENS // REF_BLOCK, dtype=jnp.int32))
        return blocks_out.reshape(TOKENS, D)
    output, pullback = jax.vjp(forward, block_input.astype(jnp.float32), params)
    input_grad, grads = pullback(cotangent.astype(jnp.float32))
    return (output.astype(jnp.bfloat16), input_grad, grads[0], grads[1], grads[2], grads[3], grads[4], grads[5], grads[6], grads[7], grads[8], grads[9], grads[10], grads[11], grads[12], grads[13], grads[14])
```

```python
import jax
import jax.numpy as jnp
from jax import lax
from jax.experimental import pallas as pl
from jax.experimental.pallas import tpu as pltpu
from jax.sharding import Mesh
from jax.sharding import PartitionSpec as P

STATE = 16
RANK = 96
PLANE = 8
HALO = 16
GROUP = 8
CUT = 1e4
EPSILON = 1e-06
F32 = jnp.float32
BF16 = jnp.bfloat16
MESH_ID = pl.DeviceIdType.MESH
ANY = pl.BlockSpec(memory_space=pl.ANY)
VMEM = pl.BlockSpec(memory_space=pltpu.VMEM)


def xor(p, k):
    out = p
    for bit in (1, 2, 4):
        if k & bit:
            out = out + bit - 2 * bit * lax.rem(lax.div(out, bit), 2)
    return out


def remote(src, dst, send_sem, recv_sem, z, p):
    return pltpu.make_async_remote_copy(
        src_ref=src,
        dst_ref=dst,
        send_sem=send_sem,
        recv_sem=recv_sem,
        device_id={"z": z, "p": p},
        device_id_type=MESH_ID,
    )


def greet(z, p):
    pl.semaphore_signal(
        pltpu.get_barrier_semaphore(), inc=1, device_id={"z": z, "p": p}, device_id_type=MESH_ID
    )


def comm_params(number, vmem=None):
    return pltpu.CompilerParams(
        collective_id=number, has_side_effects=True, vmem_limit_bytes=vmem
    )


def dma(*shape):
    return pltpu.SemaphoreType.DMA(shape)


def block_route(z, p):
    half = lax.div(PLANE * z + p, 2)
    return lax.rem(half, PLANE), 2 * lax.div(half, PLANE) + lax.rem(p, 2)


def block_source(s, p):
    k = 2 * (PLANE * (s // 2) + p) + s % 2
    return lax.div(k, PLANE), lax.rem(k, PLANE)


NEAR = (6, 2, 4)


def plane_greet(z, p):
    for k in (1, 2, 4, 6):
        greet(z, xor(p, k))
    return 4


def plane_reduce(z, p, part, sbuf, obuf, rbuf, s1, r1, s2, r2, finish, rows):
    sib = xor(p, 1)
    count = part.shape[1] // rows
    first, second = [], []
    for i, k in enumerate(NEAR + (0,)):
        c = remote(part.at[xor(sib, k)], sbuf.at[i], s1.at[i], r1.at[i], z, sib)
        c.start()
        first.append(c)
    for i, k in enumerate(NEAR):
        first[i].wait_recv()
        q = xor(p, k)

        def add(n, _, i=i, q=q):
            at = pl.ds(pl.multiple_of(n * rows, rows), rows)
            obuf[i, at] = (part[q, at].astype(F32) + sbuf[i, at].astype(F32)).astype(obuf.dtype)
            return 0

        lax.fori_loop(0, count, add, 0)
        c = remote(obuf.at[i], rbuf.at[i], s2.at[i], r2.at[i], z, q)
        c.start()
        second.append(c)
    first[3].wait_recv()
    for c in second:
        c.wait_recv()

    def last(n, _):
        at = pl.ds(pl.multiple_of(n * rows, rows), rows)
        total = part[p, at].astype(F32) + sbuf[3, at].astype(F32)
        for i in range(3):
            total = total + rbuf[i, at].astype(F32)
        finish(at, total)
        return 0

    lax.fori_loop(0, count, last, 0)
    for c in first + second:
        c.wait_send()


def plane_gather(z, p, own, place, ss, rs, fs, fr, ls):
    sib = xor(p, 1)
    sent, passed = [], []
    for i, k in enumerate(NEAR + (1,)):
        c = remote(own, place(p), ss.at[i], rs.at[i], z, xor(p, k))
        c.start()
        sent.append(c)
    local = pltpu.make_async_copy(own, place(p), ls)
    local.start()
    for i, k in ((1, 2), (2, 4), (0, 6)):
        sent[i].wait_recv()
        q = xor(p, k)
        c = remote(place(q), place(q), fs.at[i], fr.at[i], z, sib)
        c.start()
        passed.append(c)
    sent[3].wait_recv()
    for c in passed:
        c.wait_recv()
    for c in sent + passed:
        c.wait_send()
    local.wait()


GATHER_SEMS = (4, 4, 3, 3)
REDUCE_SEMS = (4, 4, 3, 3)


def opening(planes, x, slab, gains, inner, mixer):
    tok, width = x.shape

    def kernel(
        x_ref,
        slab_ref,
        gain_ref,
        inner_ref,
        mixer_ref,
        xg_ref,
        slabs_ref,
        gains_ref,
        inners_ref,
        mixers_ref,
        xs,
        xr,
        xfs,
        xfr,
        xl,
        hs,
        hr,
        gs,
        gr,
        gl,
        gs2,
        gr2,
        ins,
        inr,
        inl,
        bs,
        br,
        ms,
        mr,
    ):
        z, p = lax.axis_index("z"), lax.axis_index("p")
        column, slot = block_route(z, p)
        alone = (column == p).astype(jnp.int32)
        after = lax.rem(z + 1, planes)
        for k in range(1, PLANE):
            greet(z, xor(p, k))
        for r in range(1, planes):
            greet(lax.rem(z + r, planes), p)
        for s in range(planes):
            zs, ps = block_source(s, p)

            @pl.when(jnp.logical_or(zs != z, ps != p))
            def _(zs=zs, ps=ps):
                greet(zs, ps)

        greet(lax.rem(z + planes - 1, planes), PLANE - 1)
        last = (p == PLANE - 1).astype(jnp.int32)
        pl.semaphore_wait(
            pltpu.get_barrier_semaphore(),
            PLANE - 1 + planes - 1 + planes - alone + PLANE * last,
        )

        gain_out = []
        for r in range(1, planes):
            c = remote(
                gain_ref, gains_ref.at[p, z], gs.at[r], gr.at[r], lax.rem(z + r, planes), p
            )
            c.start()
            gain_out.append(c)
        gain_own = pltpu.make_async_copy(gain_ref, gains_ref.at[p, z], gl)
        gain_own.start()

        def block_send(src, dst, send, recv):
            for r in range(planes):
                to = lax.rem(z + r, planes)
                if r:
                    remote(src, dst.at[slot], send.at[r], recv.at[slot], to, column).start()
                else:

                    @pl.when(column == p)
                    def _():
                        pltpu.make_async_copy(src, dst.at[slot], recv.at[slot]).start()

                    @pl.when(column != p)
                    def _():
                        remote(src, dst.at[slot], send.at[r], recv.at[slot], to, column).start()

        def block_wait(src, dst, send, recv):
            for s in range(planes):
                pltpu.make_async_copy(src, dst.at[s], recv.at[s]).wait()
            for r in range(planes):
                to = lax.rem(z + r, planes)
                done = remote(src, dst.at[slot], send.at[r], recv.at[slot], to, column)
                if r:
                    done.wait_send()
                else:

                    @pl.when(column != p)
                    def _():
                        done.wait_send()

        block_send(slab_ref, slabs_ref, bs, br)

        edge = x_ref.at[pl.ds(tok - HALO, HALO)]
        front = xg_ref.at[pl.ds(0, HALO)]

        @pl.when(p == PLANE - 1)
        def _():
            for q in range(PLANE):
                remote(edge, front, hs.at[q], hr, after, q).start()

        inner_out = []
        for r in range(1, planes):
            c = remote(
                inner_ref, inners_ref.at[z], ins.at[r], inr.at[r], lax.rem(z + r, planes), p
            )
            c.start()
            inner_out.append(c)
        inner_own = pltpu.make_async_copy(inner_ref, inners_ref.at[z], inl)
        inner_own.start()
        block_send(mixer_ref, mixers_ref, ms, mr)

        for c in gain_out:
            c.wait_recv()
        gain_own.wait()
        gain_on = []
        for k in range(1, PLANE):
            c = remote(gains_ref.at[p], gains_ref.at[p], gs2.at[k], gr2.at[k], z, xor(p, k))
            c.start()
            gain_on.append(c)

        def place(q):
            return xg_ref.at[pl.ds(pl.multiple_of(HALO + q * tok, HALO), tok)]

        plane_gather(z, p, x_ref, place, xs, xr, xfs, xfr, xl)
        pltpu.make_async_copy(edge, front, hr).wait()

        @pl.when(p == PLANE - 1)
        def _():
            for q in range(PLANE):
                remote(edge, front, hs.at[q], hr, after, q).wait_send()

        for c in gain_out:
            c.wait_send()
        for c in gain_on:
            c.wait()
        block_wait(slab_ref, slabs_ref, bs, br)
        for c in inner_out:
            c.wait()
        inner_own.wait()
        block_wait(mixer_ref, mixers_ref, ms, mr)

    def shape(*dims, kind=BF16):
        return jax.ShapeDtypeStruct(dims, kind)

    return pl.pallas_call(
        kernel,
        out_shape=(
            shape(HALO + PLANE * tok, width),
            shape(planes, *slab.shape),
            shape(PLANE, planes, *gains.shape, kind=F32),
            shape(planes, *inner.shape),
            shape(planes, *mixer.shape),
        ),
        in_specs=[ANY] * 5,
        out_specs=(ANY,) * 5,
        scratch_shapes=[
            dma(4),
            dma(4),
            dma(3),
            dma(3),
            pltpu.SemaphoreType.DMA,
            dma(PLANE),
            pltpu.SemaphoreType.DMA,
            dma(planes),
            dma(planes),
            pltpu.SemaphoreType.DMA,
            dma(PLANE),
            dma(PLANE),
            dma(planes),
            dma(planes),
            pltpu.SemaphoreType.DMA,
            dma(planes),
            dma(planes),
            dma(planes),
            dma(planes),
        ],
        compiler_params=comm_params(0),
        name="opening",
    )(x, slab, gains, inner, mixer)


def plane_sum(part, number):
    _, tok, columns = part.shape

    def kernel(part_ref, out_ref, own, sbuf, obuf, rbuf, s1, r1, s2, r2, ss, rs, fs, fr, ls):
        z, p = lax.axis_index("z"), lax.axis_index("p")
        pl.semaphore_wait(pltpu.get_barrier_semaphore(), plane_greet(z, p))

        def finish(at, total):
            own[at] = total

        plane_reduce(z, p, part_ref, sbuf, obuf, rbuf, s1, r1, s2, r2, finish, tok)
        plane_gather(z, p, own, lambda q: out_ref.at[q], ss, rs, fs, fr, ls)

    return pl.pallas_call(
        kernel,
        out_shape=jax.ShapeDtypeStruct(part.shape, F32),
        in_specs=[VMEM],
        out_specs=VMEM,
        scratch_shapes=[
            pltpu.VMEM((tok, columns), F32),
            pltpu.VMEM((4, tok, columns), F32),
            pltpu.VMEM((3, tok, columns), F32),
            pltpu.VMEM((3, tok, columns), F32),
            *[dma(n) for n in REDUCE_SEMS],
            *[dma(n) for n in GATHER_SEMS],
            pltpu.SemaphoreType.DMA,
        ],
        compiler_params=comm_params(number),
        name="plane_sum",
    )(part)


def reduce_scratch(tok, width):
    return [
        pltpu.VMEM((4, tok, width), BF16),
        pltpu.VMEM((3, tok, width), BF16),
        pltpu.VMEM((3, tok, width), BF16),
        *[dma(n) for n in REDUCE_SEMS],
    ]


def mixer_join(part, x, gain):
    _, tok, width = part.shape

    def kernel(
        part_ref, x_ref, gain_ref, resid_ref, out_ref, own, sbuf, obuf, rbuf, s1, r1, s2, r2, *g
    ):
        z, p = lax.axis_index("z"), lax.axis_index("p")
        pl.semaphore_wait(pltpu.get_barrier_semaphore(), plane_greet(z, p))

        def finish(at, total):
            v = total + x_ref[at].astype(F32)
            resid_ref[at] = v
            r = lax.rsqrt(jnp.mean(v * v, axis=-1, keepdims=True) + EPSILON)
            own[at] = (v * r * gain_ref[...]).astype(BF16)

        plane_reduce(z, p, part_ref, sbuf, obuf, rbuf, s1, r1, s2, r2, finish, 16)
        plane_gather(z, p, own, lambda q: out_ref.at[q], *g)

    return pl.pallas_call(
        kernel,
        out_shape=(
            jax.ShapeDtypeStruct((tok, width), F32),
            jax.ShapeDtypeStruct(part.shape, BF16),
        ),
        in_specs=[VMEM] * 3,
        out_specs=(VMEM, VMEM),
        scratch_shapes=[
            pltpu.VMEM((tok, width), BF16),
            *reduce_scratch(tok, width),
            *[dma(n) for n in GATHER_SEMS],
            pltpu.SemaphoreType.DMA,
        ],
        compiler_params=comm_params(2, 32 << 20),
        name="mixer_join",
    )(part, x, gain)


def ffn_join(part, resid, gain, cot):
    _, tok, width = part.shape

    def kernel(
        part_ref,
        v_ref,
        gain_ref,
        cot_ref,
        grad_ref,
        out_ref,
        gg_ref,
        own,
        sbuf,
        obuf,
        rbuf,
        s1,
        r1,
        s2,
        r2,
        *g,
    ):
        z, p = lax.axis_index("z"), lax.axis_index("p")
        pl.semaphore_wait(pltpu.get_barrier_semaphore(), plane_greet(z, p))
        gg_ref[...] = jnp.zeros_like(gg_ref)

        def finish(at, u):
            v = v_ref[at]
            r = lax.rsqrt(jnp.mean(v * v, axis=-1, keepdims=True) + EPSILON)
            ug = u * gain_ref[...]
            mid = r * ug - v * (r * r * r) * jnp.mean(ug * v, axis=-1, keepdims=True)
            gg_ref[...] += jnp.sum(u * v * r, axis=0, keepdims=True)
            total = cot_ref[at].astype(F32) + mid
            grad_ref[at] = total
            own[at] = total.astype(BF16)

        plane_reduce(z, p, part_ref, sbuf, obuf, rbuf, s1, r1, s2, r2, finish, 16)
        plane_gather(z, p, own, lambda q: out_ref.at[q], *g)

    return pl.pallas_call(
        kernel,
        out_shape=(
            jax.ShapeDtypeStruct((tok, width), F32),
            jax.ShapeDtypeStruct(part.shape, BF16),
            jax.ShapeDtypeStruct((1, width), F32),
        ),
        in_specs=[VMEM] * 4,
        out_specs=(VMEM,) * 3,
        scratch_shapes=[
            pltpu.VMEM((tok, width), BF16),
            *reduce_scratch(tok, width),
            *[dma(n) for n in GATHER_SEMS],
            pltpu.SemaphoreType.DMA,
        ],
        compiler_params=comm_params(3, 32 << 20),
        name="ffn_join",
    )(part, resid, gain, cot)


def state_chain(planes, through, local, number, forward):
    def kernel(t_ref, l_ref, out_ref, got, s0, r0, s1, r1):
        z, p = lax.axis_index("z"), lax.axis_index("p")
        for r in range(1, planes):
            greet(lax.rem(z + r, planes), p)
        pl.semaphore_wait(pltpu.get_barrier_semaphore(), planes - 1)
        sent = []
        for r in range(1, planes):
            to = lax.rem(z + r, planes)
            c = remote(t_ref, got.at[z, 0], s0.at[r], r0.at[r], to, p)
            d = remote(l_ref, got.at[z, 1], s1.at[r], r1.at[r], to, p)
            c.start()
            d.start()
            sent += [c, d]
        got[z, 0] = t_ref[...]
        got[z, 1] = l_ref[...]
        for c in sent:
            c.wait()
        state = jnp.zeros_like(l_ref)
        for k in range(planes) if forward else reversed(range(planes)):
            new = got[k, 0] * state + got[k, 1]
            state = jnp.where((k < z) if forward else (k > z), new, state)
        out_ref[...] = state

    return pl.pallas_call(
        kernel,
        out_shape=jax.ShapeDtypeStruct(local.shape, F32),
        in_specs=[VMEM] * 2,
        out_specs=VMEM,
        scratch_shapes=[
            pltpu.VMEM((planes, 2) + local.shape, F32),
            dma(planes),
            dma(planes),
            dma(planes),
            dma(planes),
        ],
        compiler_params=comm_params(number),
        name="state_chain",
    )(through, local)


def closing(planes, part, halo, x, gain, resid_grad, inner_g, mixer_g, slab_g, gain_g):
    _, tok, width = part.shape

    def kernel(
        part_ref,
        halo_ref,
        x_ref,
        gain_ref,
        rg_ref,
        ig_ref,
        mg_ref,
        sg_ref,
        gg_ref,
        out_ref,
        io_ref,
        mo_ref,
        so_ref,
        go_ref,
        sbuf,
        obuf,
        rbuf,
        s1,
        r1,
        s2,
        r2,
        hbuf,
        hs,
        hr,
        ibuf,
        is_,
        ir,
        mbuf,
        ms,
        mr,
        bbuf,
        bs,
        br,
        gbuf,
        gs,
        gr,
        gown,
        gbuf2,
        gs2,
        gr2,
    ):
        z, p = lax.axis_index("z"), lax.axis_index("p")
        column, slot = block_route(z, p)
        alone = (column == p).astype(jnp.int32)
        last = (p == PLANE - 1).astype(jnp.int32)
        before = lax.rem(z + planes - 1, planes)
        after = lax.rem(z + 1, planes)
        for k in range(1, PLANE):
            greet(z, xor(p, k))
        for r in range(1, planes):
            greet(lax.rem(z + r, planes), p)
        for r in range(planes):
            to = lax.rem(z + r, planes)
            if r:
                greet(to, column)
            else:

                @pl.when(column != p)
                def _():
                    greet(to, column)

        @pl.when(p == PLANE - 1)
        def _():
            for q in range(PLANE):
                greet(after, q)

        pl.semaphore_wait(
            pltpu.get_barrier_semaphore(), PLANE - 1 + planes - 1 + planes - alone + 1
        )

        z_sent = []
        for r in range(1, planes):
            to = lax.rem(z + r, planes)
            c = remote(gg_ref.at[to], gbuf.at[z], gs.at[r], gr.at[r], to, p)
            c.start()
            z_sent.append(c)
        halo_send = remote(halo_ref, hbuf.at[p], hs, hr.at[p], before, PLANE - 1)
        halo_send.start()

        def block_send(src, buf, send, recv):
            for s in range(planes):
                zs, ps = block_source(s, p)

                @pl.when(jnp.logical_or(zs != z, ps != p))
                def _(s=s, zs=zs, ps=ps):
                    remote(src.at[s], buf.at[z], send.at[s], recv.at[z], zs, ps).start()

        def block_wait(src, buf, send, recv):
            for r in range(planes):
                at = lax.rem(z + r, planes)
                got = pltpu.make_async_copy(src.at[0], buf.at[at], recv.at[at])
                if r:
                    got.wait()
                else:

                    @pl.when(column != p)
                    def _():
                        got.wait()

                    @pl.when(column == p)
                    def _():
                        buf[z] = src[slot]

            for s in range(planes):
                zs, ps = block_source(s, p)

                @pl.when(jnp.logical_or(zs != z, ps != p))
                def _(s=s, zs=zs, ps=ps):
                    remote(src.at[s], buf.at[z], send.at[s], recv.at[z], zs, ps).wait_send()

        block_send(sg_ref, bbuf, bs, br)
        inner_sent = []
        for r in range(1, planes):
            to = lax.rem(z + r, planes)
            c = remote(ig_ref.at[to], ibuf.at[z], is_.at[r], ir.at[r], to, p)
            c.start()
            inner_sent.append(c)
        block_send(mg_ref, mbuf, ms, mr)

        for c in z_sent:
            c.wait()
        total = gg_ref[z]
        for r in range(1, planes):
            total = total + gbuf[lax.rem(z + r, planes)]
        gown[...] = total
        p_sent = []
        for k in range(1, PLANE):
            c = remote(gown, gbuf2.at[k], gs2.at[k], gr2.at[k], z, xor(p, k))
            c.start()
            p_sent.append(c)

        def finish(at, u):
            out_ref[at] = u

        plane_reduce(z, p, part_ref, sbuf, obuf, rbuf, s1, r1, s2, r2, finish, 16)

        @pl.when(p == PLANE - 1)
        def _():
            for q in range(PLANE):
                pltpu.make_async_copy(halo_ref, hbuf.at[q], hr.at[q]).wait()

            @pl.when(z < planes - 1)
            def _():
                add = hbuf[0].astype(F32)
                for q in range(1, PLANE):
                    add = add + hbuf[q].astype(F32)
                out_ref[pl.ds(tok - HALO, HALO)] += add

        halo_send.wait_send()

        def norm(n, _):
            at = pl.ds(pl.multiple_of(n * 16, 16), 16)
            u = out_ref[at]
            v = x_ref[at].astype(F32)
            r = lax.rsqrt(jnp.mean(v * v, axis=-1, keepdims=True) + EPSILON)
            ug = u * gain_ref[...]
            grad = r * ug - v * (r * r * r) * jnp.mean(ug * v, axis=-1, keepdims=True)
            out_ref[at] = rg_ref[at] + grad
            return 0

        lax.fori_loop(0, tok // 16, norm, 0)

        for c in p_sent:
            c.wait()
        total = gown[...]
        for k in range(1, PLANE):
            total = total + gbuf2[k]
        go_ref[...] = total

        block_wait(sg_ref, bbuf, bs, br)
        so_ref[...] = sum(bbuf[k] for k in range(1, planes)) + bbuf[0]
        for c in inner_sent:
            c.wait()
        acc = ig_ref[z].astype(F32)
        for r in range(1, planes):
            acc = acc + ibuf[lax.rem(z + r, planes)].astype(F32)
        io_ref[...] = acc
        block_wait(mg_ref, mbuf, ms, mr)
        acc = mbuf[0].astype(F32)
        for k in range(1, planes):
            acc = acc + mbuf[k].astype(F32)
        mo_ref[...] = acc

    def z_bufs(array):
        return [pltpu.VMEM(array.shape, array.dtype), dma(planes), dma(planes)]

    return pl.pallas_call(
        kernel,
        out_shape=(
            jax.ShapeDtypeStruct((tok, width), F32),
            jax.ShapeDtypeStruct(inner_g.shape[1:], F32),
            jax.ShapeDtypeStruct(mixer_g.shape[1:], F32),
            jax.ShapeDtypeStruct(slab_g.shape[1:], F32),
            jax.ShapeDtypeStruct(gain_g.shape[1:], F32),
        ),
        in_specs=[VMEM] * 9,
        out_specs=(VMEM,) * 5,
        scratch_shapes=[
            *reduce_scratch(tok, width),
            pltpu.VMEM((PLANE, HALO, width), BF16),
            pltpu.SemaphoreType.DMA,
            dma(PLANE),
            *z_bufs(inner_g),
            *z_bufs(mixer_g),
            *z_bufs(slab_g),
            *z_bufs(gain_g),
            pltpu.VMEM(gain_g.shape[1:], F32),
            pltpu.VMEM((PLANE,) + gain_g.shape[1:], F32),
            dma(PLANE),
            dma(PLANE),
        ],
        compiler_params=comm_params(6, 48 << 20),
        name="closing",
    )(part, halo, x, gain, resid_grad, inner_g, mixer_g, slab_g, gain_g)


def scan_specs(chunk, channels, count, backward):
    def at(i):
        return count - 1 - i if backward else i

    return (
        pl.BlockSpec((chunk, channels), lambda i: (at(i), 0)),
        pl.BlockSpec((chunk // GROUP, 2 * STATE, GROUP), lambda i: (at(i), 0, 0)),
        pl.BlockSpec((chunk, STATE, channels), lambda i: (at(i), 0, 0)),
        pl.BlockSpec((STATE, channels), lambda i: (0, 0)),
    )


def rows_of(g):
    return pl.ds(pl.multiple_of(g * GROUP, GROUP), GROUP)


CHUNK = 128


def forward_final(step, drive, maps, rate):
    tokens, channels = step.shape
    count = tokens // CHUNK
    rows, cols, _, const = scan_specs(CHUNK, channels, count, False)

    def kernel(step_ref, drive_ref, maps_ref, rate_ref, state_ref, through_ref):
        @pl.when(pl.program_id(0) == 0)
        def _():
            state_ref[...] = jnp.zeros_like(state_ref)
            through_ref[...] = jnp.zeros_like(through_ref)

        rate_v = rate_ref[...]

        def body(g, carry):
            h, total = carry
            d8, w8, b8 = step_ref[rows_of(g), :], drive_ref[rows_of(g), :], maps_ref[g]
            for k in range(GROUP):
                decay = jnp.exp(d8[k : k + 1, :] * rate_v)
                h = decay * h + w8[k : k + 1, :] * b8[:STATE, k : k + 1]
            return h, total + d8

        h, total = lax.fori_loop(
            0,
            CHUNK // GROUP,
            body,
            (state_ref[...], jnp.zeros((GROUP, channels), F32)),
        )
        state_ref[...] = h
        through_ref[...] += jnp.sum(total, axis=0, keepdims=True)

        @pl.when(pl.program_id(0) == count - 1)
        def _():
            through_ref[...] = jnp.exp(through_ref[...] * rate_v)

    shape = jax.ShapeDtypeStruct(rate.shape, F32)
    return pl.pallas_call(
        kernel,
        grid=(count,),
        out_shape=(shape, shape),
        in_specs=[rows, rows, cols, const],
        out_specs=(const, const),
        name="forward_final",
    )(step, drive, maps, rate)


def forward_all(step, drive, maps, rate, start):
    tokens, channels = step.shape
    count = tokens // CHUNK
    rows, cols, states, const = scan_specs(CHUNK, channels, count, False)

    def kernel(step_ref, drive_ref, maps_ref, rate_ref, start_ref, y_ref, hs_ref, h_sc):
        @pl.when(pl.program_id(0) == 0)
        def _():
            h_sc[...] = start_ref[...]

        rate_v = rate_ref[...]

        def body(g, h):
            d8, w8, b8 = step_ref[rows_of(g), :], drive_ref[rows_of(g), :], maps_ref[g]
            out = []
            for k in range(GROUP):
                hs_ref[g * GROUP + k] = h
                decay = jnp.exp(d8[k : k + 1, :] * rate_v)
                h = decay * h + w8[k : k + 1, :] * b8[:STATE, k : k + 1]
                out.append(jnp.sum(h * b8[STATE:, k : k + 1], axis=0, keepdims=True))
            y_ref[rows_of(g), :] = jnp.concatenate(out, axis=0)
            return h

        h_sc[...] = lax.fori_loop(0, CHUNK // GROUP, body, h_sc[...])

    return pl.pallas_call(
        kernel,
        grid=(count,),
        out_shape=(
            jax.ShapeDtypeStruct((tokens, channels), F32),
            jax.ShapeDtypeStruct((tokens, STATE, channels), F32),
        ),
        in_specs=[rows, rows, cols, const, const],
        out_specs=(rows, states),
        scratch_shapes=[pltpu.VMEM((STATE, channels), F32)],
        name="forward_all",
    )(step, drive, maps, rate, start)


def backward_first(step, mix_grad, maps, rate):
    tokens, channels = step.shape
    count = tokens // CHUNK
    rows, cols, _, const = scan_specs(CHUNK, channels, count, True)

    def kernel(step_ref, mix_ref, maps_ref, rate_ref, out_ref):
        @pl.when(pl.program_id(0) == 0)
        def _():
            out_ref[...] = jnp.zeros_like(out_ref)

        rate_v = rate_ref[...]

        def body(n, q):
            g = CHUNK // GROUP - 1 - n
            d8, m8, b8 = step_ref[rows_of(g), :], mix_ref[rows_of(g), :], maps_ref[g]
            for k in reversed(range(GROUP)):
                decay = jnp.exp(d8[k : k + 1, :] * rate_v)
                q = decay * (q + m8[k : k + 1, :] * b8[STATE:, k : k + 1])
            return q

        out_ref[...] = lax.fori_loop(0, CHUNK // GROUP, body, out_ref[...])

    return pl.pallas_call(
        kernel,
        grid=(count,),
        out_shape=jax.ShapeDtypeStruct(rate.shape, F32),
        in_specs=[rows, rows, cols, const],
        out_specs=const,
        name="backward_first",
    )(step, mix_grad, maps, rate)


def backward_all(step, drive, mix_grad, maps, rate, states_in, start):
    tokens, channels = step.shape
    count = tokens // CHUNK
    rows, cols, states, const = scan_specs(CHUNK, channels, count, True)

    def kernel(
        step_ref,
        drive_ref,
        mix_ref,
        maps_ref,
        rate_ref,
        hs_ref,
        start_ref,
        sb_ref,
        sr_ref,
        map_ref,
        dd_ref,
        q_sc,
    ):
        @pl.when(pl.program_id(0) == 0)
        def _():
            q_sc[...] = start_ref[...]
            dd_ref[...] = jnp.zeros_like(dd_ref)

        rate_v = rate_ref[...]
        lane = lax.broadcasted_iota(jnp.int32, (2 * STATE, GROUP), 1)

        def body(n, carry):
            q, dd = carry
            g = CHUNK // GROUP - 1 - n
            at = rows_of(g)
            d8, w8, m8, b8 = step_ref[at, :], drive_ref[at, :], mix_ref[at, :], maps_ref[g]
            sb, sr = [], []
            grads = jnp.zeros((2 * STATE, GROUP), F32)
            for k in reversed(range(GROUP)):
                d, w, m = d8[k : k + 1, :], w8[k : k + 1, :], m8[k : k + 1, :]
                b, c = b8[:STATE, k : k + 1], b8[STATE:, k : k + 1]
                decay = jnp.exp(d * rate_v)
                kept = decay * hs_ref[g * GROUP + k]
                h = kept + w * b
                hbar = q + m * c
                flow = hbar * kept
                q = decay * hbar
                dd = dd + flow * d
                sb.append(jnp.sum(hbar * b, axis=0, keepdims=True))
                sr.append(jnp.sum(flow * rate_v, axis=0, keepdims=True))
                col = jnp.concatenate(
                    [
                        jnp.sum(hbar * w, axis=1, keepdims=True),
                        jnp.sum(h * m, axis=1, keepdims=True),
                    ],
                    axis=0,
                )
                grads = jnp.where(lane == k, col, grads)
            sb_ref[at, :] = jnp.concatenate(sb[::-1], axis=0)
            sr_ref[at, :] = jnp.concatenate(sr[::-1], axis=0)
            map_ref[g] = grads
            return q, dd

        q, dd = lax.fori_loop(0, CHUNK // GROUP, body, (q_sc[...], dd_ref[...]))
        q_sc[...] = q
        dd_ref[...] = dd

    wide = jax.ShapeDtypeStruct((tokens, channels), F32)
    return pl.pallas_call(
        kernel,
        grid=(count,),
        out_shape=(
            wide,
            wide,
            jax.ShapeDtypeStruct(maps.shape, F32),
            jax.ShapeDtypeStruct(rate.shape, F32),
        ),
        in_specs=[rows, rows, rows, cols, const, states, const],
        out_specs=(rows, rows, cols, const),
        scratch_shapes=[pltpu.VMEM((STATE, channels), F32)],
        name="backward_all",
    )(step, drive, mix_grad, maps, rate, states_in, start)


def contract(left, right, left_dim, right_dim, kind=F32):
    return lax.dot_general(
        left, right, (((left_dim,), (right_dim,)), ((), ())), preferred_element_type=F32
    ).astype(kind)


def silu_slope(v):
    s = jax.nn.sigmoid(v)
    return s * (1.0 + v * (1.0 - s))


def group_mean(values, lane):
    def mean(low, high):
        inside = jnp.logical_and(lane >= low, lane < high)
        return jnp.sum(jnp.where(inside, values, 0.0), axis=-1, keepdims=True) / (high - low)

    return jnp.where(
        lane < RANK,
        mean(0, RANK),
        jnp.where(lane < RANK + STATE, mean(RANK, RANK + STATE), mean(RANK + STATE, RANK + 2 * STATE)),
    )


def on_device(
    planes,
    block_input,
    documents,
    first_gain,
    inner_weight,
    conv_weight,
    conv_bias,
    select_weight,
    select_gain,
    step_weight,
    step_bias,
    decay_log,
    skip_gain,
    mixer_weight,
    second_gain,
    gate_weight,
    up_weight,
    down_weight,
    cotangent,
):
    tok, width = block_input.shape
    devices = planes * PLANE
    rows = PLANE * tok
    z = lax.axis_index("z")
    own_block = mixer_weight.shape[0]
    inner_block = inner_weight.shape[1]
    channels = planes * own_block
    columns = RANK + 2 * STATE
    taps = conv_weight.shape[0]

    parts = [
        select_weight,
        step_weight.T,
        conv_weight.T,
        conv_bias[:, None],
        step_bias[:, None],
        decay_log.T,
        skip_gain[:, None],
    ]
    used = sum(a.shape[1] for a in parts)
    slab_width = -(-used // 128) * 128
    slab = jnp.pad(jnp.concatenate(parts, axis=1), ((0, 0), (0, slab_width - used)))
    widths = [first_gain.shape[0], second_gain.shape[0], select_gain.shape[0]]
    gains = jnp.concatenate([first_gain, second_gain, select_gain]).astype(F32)
    gains = jnp.pad(gains[None, :], ((0, 7), (0, 128 - sum(widths))))

    x_ext, slabs, gains_all, inners, mixers = opening(
        planes, block_input, slab, gains, inner_weight.T, mixer_weight
    )
    gate_t, up_t, down_t, cot_t, _ = lax.optimization_barrier(
        (gate_weight.T, up_weight.T, down_weight, cotangent, slabs)
    )
    gate_w = lax.all_gather(gate_t, "z", axis=0, tiled=True)
    up_w = lax.all_gather(up_t, "z", axis=0, tiled=True)
    down_w = lax.all_gather(down_t, "z", axis=0, tiled=True)
    cot_all = lax.all_gather(cot_t, "p", axis=0, tiled=True)

    gains_all = jnp.transpose(gains_all[:, :, 0, :], (1, 0, 2)).reshape(devices, 128)
    first_f = gains_all[:, : widths[0]].reshape(1, width)
    second_f = gains_all[:, widths[0] : widths[0] + widths[1]].reshape(1, width)
    select_f = gains_all[:, widths[0] + widths[1] : sum(widths)].reshape(1, columns)
    slab_all = slabs.reshape(channels, slab_width)
    select_w = slab_all[:, :columns]
    step_w = jnp.pad(slab_all[:, columns : columns + RANK], ((0, 0), (0, columns - RANK)))
    rest = slab_all[:, columns + RANK :].astype(F32).T
    conv_w = [rest[k][None, :] for k in range(taps)]
    conv_b = rest[taps][None, :]
    step_b = rest[taps + 1][None, :]
    rate = -jnp.exp(rest[taps + 2 : taps + 2 + STATE])
    skip = rest[taps + 2 + STATE][None, :]
    inner_w = inners.reshape(2 * channels, width)
    mixer_w = mixers.reshape(channels, width)

    padded = jnp.concatenate([jnp.full((taps - 1,), -1, jnp.int32), documents])
    ids = lax.dynamic_slice_in_dim(padded, z * rows, rows + taps - 1, 0)
    here = ids[taps - 1 :]
    same = [(ids[k : k + rows] == here)[:, None] for k in range(taps)]
    keep = same[taps - 2]

    x_f = x_ext.astype(F32)
    r_one = lax.rsqrt(jnp.mean(x_f * x_f, axis=-1, keepdims=True) + EPSILON)
    normed_one = (x_f * r_one * first_f).astype(BF16)
    conv_input = contract(normed_one, inner_w[:channels], 1, 1, BF16)
    gate_inner = contract(normed_one[HALO:], inner_w[channels:], 1, 1)
    shift = HALO - taps + 1
    total = conv_b
    for k in range(taps):
        tap = conv_input[shift + k : shift + k + rows].astype(F32)
        total = total + conv_w[k] * jnp.where(same[k], tap, 0.0)
    mixed_in = jax.nn.silu(total).astype(BF16)
    proj_part = contract(mixed_in, select_w, 1, 0)
    proj = plane_sum(proj_part.reshape(PLANE, tok, columns), 1).reshape(rows, columns)
    lane = lax.broadcasted_iota(jnp.int32, (1, columns), 1)
    r_sel = lax.rsqrt(group_mean(proj * proj, lane) + EPSILON)
    select_out = proj * r_sel * select_f
    step_low = select_out.astype(BF16)
    step_raw = contract(step_low, step_w, 1, 1) + step_b
    step = jax.nn.softplus(step_raw)
    mixed_f = mixed_in.astype(F32)
    drive = step * mixed_f
    step_cut = jnp.where(keep, step, CUT)
    maps = jnp.transpose(
        select_out[:, RANK:].reshape(rows // GROUP, GROUP, 2 * STATE), (0, 2, 1)
    )
    local_final, through = forward_final(step_cut, drive, maps, rate)
    state_in = state_chain(planes, through, local_final, 4, True)
    sums, states = forward_all(step_cut, drive, maps, rate, state_in)
    mix = sums + skip * mixed_f
    gate_silu = jax.nn.silu(gate_inner)
    gated = (mix * gate_silu).astype(BF16)
    mixer_part = contract(gated, mixer_w, 1, 0, BF16)
    resid_mid, normed_two = mixer_join(
        mixer_part.reshape(PLANE, tok, width), block_input, second_f
    )
    normed_two = normed_two.reshape(rows, width)

    ffn_gate = contract(normed_two, gate_w, 1, 1)
    ffn_up = contract(normed_two, up_w, 1, 1)
    ffn_silu = jax.nn.silu(ffn_gate)
    ffn_hidden = (ffn_silu * ffn_up).astype(BF16)
    hidden_grad = contract(cot_all, down_w, 1, 1)
    gate_back = (hidden_grad * ffn_up * silu_slope(ffn_gate)).astype(BF16)
    up_back = (hidden_grad * ffn_silu).astype(BF16)
    two_part = (contract(gate_back, gate_w, 1, 0) + contract(up_back, up_w, 1, 0)).astype(BF16)
    resid_grad, mixer_back, second_grad = ffn_join(
        two_part.reshape(PLANE, tok, width), resid_mid, second_f, cotangent
    )
    mixer_back = mixer_back.reshape(rows, width)
    out_part = contract(ffn_hidden, down_w, 1, 0, BF16)
    out_sum = lax.psum_scatter(out_part, "p", scatter_dimension=0, tiled=True)
    block_output = (resid_mid + out_sum.astype(F32)).astype(BF16)
    ffn_grads = [
        lax.psum_scatter(contract(a, b, 0, 0, BF16), "z", scatter_dimension=0, tiled=True)
        for a, b in ((gate_back, normed_two), (up_back, normed_two), (ffn_hidden, cot_all))
    ]

    gated_grad = contract(mixer_back, mixer_w, 1, 1)
    mixer_grad = contract(gated, mixer_back, 0, 0, BF16)
    mix_grad = gated_grad * gate_silu
    gate_inner_grad = gated_grad * mix * silu_slope(gate_inner)
    local_back = backward_first(step_cut, mix_grad, maps, rate)
    state_back = state_chain(planes, through, local_back, 5, False)
    map_sum, rate_sum, map_grads, decay_sum = backward_all(
        step_cut, drive, mix_grad, maps, rate, states, state_back
    )
    step_raw_grad = (mixed_f * map_sum + rate_sum) * jax.nn.sigmoid(step_raw)
    step_back = step_raw_grad.astype(BF16)
    map_grads = jnp.transpose(map_grads, (0, 2, 1)).reshape(rows, 2 * STATE)
    select_part = contract(step_back, step_w, 1, 0) + jnp.pad(map_grads, ((0, 0), (RANK, 0)))
    select_grad = plane_sum(select_part.reshape(PLANE, tok, columns), 7).reshape(rows, columns)
    scaled = select_grad * select_f
    proj_grad = r_sel * scaled - proj * r_sel * r_sel * r_sel * group_mean(scaled * proj, lane)
    select_gain_grad = jnp.sum(select_grad * proj * r_sel, axis=0) * (1.0 / PLANE)
    proj_back = proj_grad.astype(BF16)
    mixed_grad = step * map_sum + skip * mix_grad + contract(proj_back, select_w, 1, 1)
    pre_grad = mixed_grad * silu_slope(total)
    conv_grads, ext_grad = [], None
    for k in range(taps):
        tap = conv_input[shift + k : shift + k + rows].astype(F32)
        masked = jnp.where(same[k], pre_grad, 0.0)
        conv_grads.append(jnp.sum(masked * tap, axis=0))
        part = jnp.pad(masked * conv_w[k], ((shift + k, taps - 1 - k), (0, 0)))
        ext_grad = part if ext_grad is None else ext_grad + part
    inner_back = jnp.concatenate(
        [ext_grad, jnp.pad(gate_inner_grad, ((HALO, 0), (0, 0)))], axis=1
    ).astype(BF16)
    inner_grad = contract(inner_back, normed_one, 0, 0, BF16)
    one_part = contract(inner_back, inner_w, 1, 0, BF16)
    first_grad = jnp.sum(one_part.astype(F32) * x_f * r_one, axis=0)

    slab_grad = jnp.concatenate(
        [
            contract(mixed_in, proj_back, 0, 0),
            contract(step_back, step_low, 0, 0)[:, :RANK],
            jnp.concatenate(
                [
                    jnp.stack(conv_grads + [jnp.sum(pre_grad, axis=0), jnp.sum(step_raw_grad, axis=0)]),
                    decay_sum * rate,
                    jnp.sum(mix_grad * mixed_f, axis=0)[None, :],
                ]
            ).T,
        ],
        axis=1,
    )
    slab_grad = jnp.pad(slab_grad, ((0, 0), (0, slab_width - used)))
    gain_grad = jnp.concatenate(
        [
            first_grad.reshape(devices, widths[0]),
            second_grad.reshape(devices, widths[1]),
            select_gain_grad.reshape(devices, widths[2]),
        ],
        axis=1,
    )
    gain_grad = jnp.pad(gain_grad, ((0, 0), (0, 128 - sum(widths))))

    input_grad, inner_out, mixer_out, slab_out, gain_out = closing(
        planes,
        one_part[HALO:].reshape(PLANE, tok, width),
        one_part[:HALO],
        block_input,
        first_f,
        resid_grad,
        inner_grad.reshape(planes, inner_block, width),
        mixer_grad.reshape(planes, own_block, width),
        slab_grad.reshape(planes, own_block, slab_width),
        gain_grad.reshape(planes, PLANE, 128),
    )
    mine = lax.dynamic_index_in_dim(gain_out, lax.axis_index("p"), 0, False)
    small = slab_out[:, columns + RANK :].T
    return (
        block_output,
        input_grad,
        mine[: widths[0]],
        inner_out.T,
        small[:taps],
        small[taps],
        slab_out[:, :columns],
        mine[widths[0] + widths[1] : sum(widths)],
        slab_out[:, columns : columns + RANK].T,
        small[taps + 1],
        small[taps + 2 : taps + 2 + STATE],
        small[taps + 2 + STATE],
        mixer_out,
        mine[widths[0] : widths[0] + widths[1]],
        ffn_grads[0].astype(F32).T,
        ffn_grads[1].astype(F32).T,
        ffn_grads[2].astype(F32),
    )


def solution(mesh):
    planes = mesh.devices.size // PLANE
    grid = Mesh(mesh.devices.reshape(planes, PLANE), ("z", "p"))
    seq = ("z", "p")
    by_row, by_column, flat = P(seq, None), P(None, seq), P(seq)

    def program(*args):
        return on_device(planes, *args)

    return jax.shard_map(
        program,
        mesh=grid,
        in_specs=(
            by_row,
            P(),
            flat,
            by_column,
            by_column,
            flat,
            by_row,
            flat,
            by_column,
            flat,
            by_column,
            flat,
            by_row,
            flat,
            by_column,
            by_column,
            by_row,
            by_row,
        ),
        out_specs=(
            by_row,
            by_row,
            flat,
            by_column,
            by_column,
            flat,
            by_row,
            flat,
            by_column,
            flat,
            by_column,
            flat,
            by_row,
            flat,
            by_column,
            by_column,
            by_row,
        ),
        check_vma=False,
    )
```

```python
import jax
import jax.numpy as jnp
from jax import lax
from jax.experimental import pallas as pl
from jax.experimental.pallas import tpu as pltpu
from jax.sharding import Mesh
from jax.sharding import PartitionSpec as P

STATE = 16
RANK = 96
PLANE = 8
HALO = 16
GROUP = 8
CUT = 1e4
EPSILON = 1e-06
F32 = jnp.float32
BF16 = jnp.bfloat16
MESH_ID = pl.DeviceIdType.MESH
ANY = pl.BlockSpec(memory_space=pl.ANY)
VMEM = pl.BlockSpec(memory_space=pltpu.VMEM)


def xor(p, k):
    out = p
    for bit in (1, 2, 4):
        if k & bit:
            out = out + bit - 2 * bit * lax.rem(lax.div(out, bit), 2)
    return out


def remote(src, dst, send_sem, recv_sem, z, p):
    return pltpu.make_async_remote_copy(
        src_ref=src,
        dst_ref=dst,
        send_sem=send_sem,
        recv_sem=recv_sem,
        device_id={"z": z, "p": p},
        device_id_type=MESH_ID,
    )


def greet(z, p):
    pl.semaphore_signal(
        pltpu.get_barrier_semaphore(), inc=1, device_id={"z": z, "p": p}, device_id_type=MESH_ID
    )


def comm_params(number, vmem=None):
    return pltpu.CompilerParams(
        collective_id=number, has_side_effects=True, vmem_limit_bytes=vmem
    )


def dma(*shape):
    return pltpu.SemaphoreType.DMA(shape)


def block_route(z, p):
    half = lax.div(PLANE * z + p, 2)
    return lax.rem(half, PLANE), 2 * lax.div(half, PLANE) + lax.rem(p, 2)


def block_source_of(z, p):
    k = 2 * (PLANE * lax.div(z, 2) + p) + lax.rem(z, 2)
    return lax.div(k, PLANE), lax.rem(k, PLANE)


def moves_in(z, p):
    zs, ps = block_source_of(z, p)
    return jnp.logical_or(zs != z, ps != p)


def plane_greet(z, p):
    for k in (1, 2, 4):
        greet(z, xor(p, k))
    return 3


def plane_reduce(z, p, part, sbuf, obuf, dbuf, rbuf, s1, r1, s2, r2, finish, rows, during=None):
    sib, near, side = xor(p, 1), xor(p, 2), xor(p, 4)
    half = part.shape[1] // 2
    top, low = pl.ds(0, half), pl.ds(half, half)
    wide = (part.dtype == F32) and (obuf.dtype == F32)

    def chunks(first, length, body):
        def step(n, _):
            body(pl.ds(pl.multiple_of(first + n * rows, rows), rows))
            return 0

        lax.fori_loop(0, length // rows, step, 0)

    def put(n, value):
        return value if wide else value.astype(obuf.dtype)

    first = []
    for i, k in enumerate((6, 2, 4, 0)):
        c = remote(part.at[xor(sib, k)], sbuf.at[i], s1.at[i], r1.at[i], z, sib)
        c.start()
        first.append(c)
    second = []

    def send(i, src, dst, to):
        c = remote(src, dst, s2.at[i], r2.at[i], z, to)
        c.start()
        second.append(c)
        return c

    for i, k in enumerate((6, 2, 4)):
        first[i].wait_recv()
        q = xor(p, k)

        def add(at, i=i, q=q):
            obuf[i, at] = put(i, part[q, at].astype(F32) + sbuf[i, at].astype(F32))

        chunks(0, 2 * half, add)
        if k == 6:
            far_top = send(0, obuf.at[0, top], dbuf.at[0], near)
            far_low = send(1, obuf.at[0, low], dbuf.at[1], side)
        elif k == 2:
            send(2, obuf.at[1, top], rbuf.at[0, top], near)
        else:
            send(3, obuf.at[2, low], rbuf.at[1, low], side)
    if during is not None:
        during(0)
    far_top.wait_recv()

    def join_top(at):
        obuf[2, at] = put(2, obuf[2, at].astype(F32) + dbuf[0, at].astype(F32))

    chunks(0, half, join_top)
    send(4, obuf.at[2, top], rbuf.at[1, top], side)
    far_low.wait_recv()

    def join_low(at):
        down = pl.ds(pl.multiple_of(at.start + half, rows), rows)
        obuf[1, down] = put(1, obuf[1, down].astype(F32) + dbuf[1, at].astype(F32))

    chunks(0, half, join_low)
    send(5, obuf.at[1, low], rbuf.at[0, low], near)
    if during is not None:
        during(1)
    first[3].wait_recv()
    for c in second[2:]:
        c.wait_recv()

    def last(at):
        total = part[p, at].astype(F32) + sbuf[3, at].astype(F32)
        finish(at, total + rbuf[0, at].astype(F32) + rbuf[1, at].astype(F32))

    chunks(0, 2 * half, last)
    for c in first + second:
        c.wait_send()


def plane_gather(z, p, own, place, ss, rs, fs, fr, ls, during=None):
    sib, near, side = xor(p, 1), xor(p, 2), xor(p, 4)
    far = xor(p, 6)
    half = own.shape[0] // 2
    top, low = pl.ds(0, half), pl.ds(half, half)
    sent = []

    def send(i, src, dst, to):
        c = remote(src, dst, ss.at[i], rs.at[i], z, to)
        c.start()
        sent.append(c)
        return c

    near_top = send(0, own.at[top], place(p).at[top], near)
    side_low = send(1, own.at[low], place(p).at[low], side)
    near_low = send(2, own.at[low], place(p).at[low], near)
    side_top = send(3, own.at[top], place(p).at[top], side)
    mate = send(4, own, place(p), sib)
    local = pltpu.make_async_copy(own, place(p), ls)
    local.start()
    if during is not None:
        during(2)
    passed = []

    def pass_on(i, q):
        c = remote(place(q), place(q), fs.at[i], fr.at[i], z, sib)
        c.start()
        passed.append(c)

    near_top.wait_recv()
    far_top = send(5, place(near).at[top], place(near).at[top], side)
    side_low.wait_recv()
    far_low = send(6, place(side).at[low], place(side).at[low], near)
    near_low.wait_recv()
    pass_on(0, near)
    side_top.wait_recv()
    pass_on(1, side)
    far_top.wait_recv()
    far_low.wait_recv()
    pass_on(2, far)
    mate.wait_recv()
    for c in passed:
        c.wait_recv()
    for c in sent + passed:
        c.wait_send()
    local.wait()


GATHER_SEMS = (7, 7, 3, 3)
REDUCE_SEMS = (4, 4, 6, 6)


def ring_gather(planes, z, p, own, out, ss, rs, ls):
    local = pltpu.make_async_copy(own, out.at[z], ls)
    local.start()
    sent = []

    def send(i, src, dst, r):
        c = remote(src, dst, ss.at[i], rs.at[i], lax.rem(z + r, planes), p)
        c.start()
        sent.append(c)
        return c

    if planes != 4:
        for r in range(1, planes):
            send(r, own, out.at[z], r)
        return local, sent, lambda: None
    half = own.shape[0] // 2
    top, low = pl.ds(0, half), pl.ds(half, half)
    up = send(0, own.at[top], out.at[z, top], 1)
    down = send(1, own.at[low], out.at[z, low], 3)
    send(2, own.at[low], out.at[z, low], 1)
    send(3, own.at[top], out.at[z, top], 3)

    def relay():
        before, after = lax.rem(z + 3, 4), lax.rem(z + 1, 4)
        up.wait_recv()
        send(4, out.at[before, top], out.at[before, top], 1)
        down.wait_recv()
        send(5, out.at[after, low], out.at[after, low], 3)

    return local, sent, relay


def ring_finish(local, sent, relayed):
    for i, c in enumerate(sent):
        if not (relayed and i < 2):
            c.wait_recv()
        c.wait_send()
    local.wait()


def ring_reduce(planes, z, p, src, ibuf, fbuf, mbuf, ss, rs):
    half = src.shape[1] // 2
    top, low = pl.ds(0, half), pl.ds(half, half)
    before, after = lax.rem(z + planes - 1, planes), lax.rem(z + 1, planes)
    sent = []

    def send(i, part, dst, r):
        c = remote(part, dst, ss.at[i], rs.at[i], lax.rem(z + r, planes), p)
        c.start()
        sent.append(c)

    if planes == 4:
        far = lax.rem(z + 2, 4)
        send(0, src.at[far, top], fbuf.at[0], 1)
        send(1, src.at[far, low], fbuf.at[1], 3)
        send(2, src.at[after, low], ibuf.at[0, low], 1)
        send(3, src.at[before, top], ibuf.at[1, top], 3)
    else:
        for r in range(1, planes):
            send(r, src.at[lax.rem(z + r, planes)], ibuf.at[r], r)

    def relay():
        if planes == 4:
            sent[0].wait_recv()
            mbuf[0] = (src[after, top].astype(F32) + fbuf[0].astype(F32)).astype(mbuf.dtype)
            send(4, mbuf.at[0], ibuf.at[0, top], 1)
            sent[1].wait_recv()
            mbuf[1] = (src[before, low].astype(F32) + fbuf[1].astype(F32)).astype(mbuf.dtype)
            send(5, mbuf.at[1], ibuf.at[1, low], 3)

    def finish():
        for i, c in enumerate(sent):
            if not (planes == 4 and i < 2):
                c.wait_recv()
            c.wait_send()
        total = src[z].astype(F32)
        for k in range(2) if planes == 4 else range(1, planes):
            total = total + ibuf[k].astype(F32)
        return total

    return relay, finish


def ring_reduce_scratch(planes, block, width, kind=BF16):
    return [
        pltpu.VMEM((2 if planes == 4 else planes, block, width), kind),
        pltpu.VMEM((2, block // 2, width), kind),
        pltpu.VMEM((2, block // 2, width), kind),
        dma(ring_sems(planes)),
        dma(ring_sems(planes)),
    ]


def ring_greet(planes, z, p):
    for r in range(1, planes):
        greet(lax.rem(z + r, planes), p)
    return planes - 1


def ring_sems(planes):
    return max(6, planes)


def opening(planes, x, cot, slab, gains, inner):
    tok, width = x.shape
    relayed = planes == 4

    def kernel(
        x_ref,
        cot_ref,
        slab_ref,
        gain_ref,
        inner_ref,
        xg_ref,
        cots_ref,
        slabs_ref,
        gains_ref,
        inners_ref,
        landed,
        xs,
        xr,
        xfs,
        xfr,
        xl,
        cs,
        cr,
        cfs,
        cfr,
        cl,
        hs,
        hr,
        gs,
        gr,
        gl,
        gs2,
        gr2,
        ins,
        inr,
        inl,
        ps,
        pr,
        bs,
        br,
        bl,
    ):
        z, p = lax.axis_index("z"), lax.axis_index("p")
        column, slot = block_route(z, p)
        from_z, from_p = block_source_of(z, p)
        moves = jnp.logical_or(column != p, slot != z)
        after = lax.rem(z + 1, planes)
        for k in range(1, PLANE):
            greet(z, xor(p, k))
        for r in range(1, planes):
            greet(lax.rem(z + r, planes), p)

        @pl.when(moves_in(z, p))
        def _():
            greet(from_z, from_p)

        greet(lax.rem(z + planes - 1, planes), PLANE - 1)
        last = (p == PLANE - 1).astype(jnp.int32)
        pl.semaphore_wait(
            pltpu.get_barrier_semaphore(),
            PLANE - 1 + planes - 1 + moves.astype(jnp.int32) + PLANE * last,
        )

        home = remote(slab_ref, landed, ps, pr, slot, column)

        @pl.when(moves)
        def _():
            home.start()

        @pl.when(jnp.logical_not(moves))
        def _():
            pltpu.make_async_copy(slab_ref, landed, pr).start()

        gain_out = []
        for r in range(1, planes):
            c = remote(
                gain_ref, gains_ref.at[p, z], gs.at[r], gr.at[r], lax.rem(z + r, planes), p
            )
            c.start()
            gain_out.append(c)
        gain_own = pltpu.make_async_copy(gain_ref, gains_ref.at[p, z], gl)
        gain_own.start()

        edge = x_ref.at[pl.ds(tok - HALO, HALO)]
        front = xg_ref.at[pl.ds(0, HALO)]

        @pl.when(p == PLANE - 1)
        def _():
            for q in range(PLANE):
                remote(edge, front, hs.at[q], hr, after, q).start()

        def place(q):
            return xg_ref.at[pl.ds(pl.multiple_of(HALO + q * tok, HALO), tok)]

        local, sent, relay = ring_gather(planes, z, p, inner_ref, inners_ref, ins, inr, inl)
        slab_sent = []
        gain_on = []

        def during(_):
            pltpu.make_async_copy(slab_ref, landed, pr).wait()
            for r in range(1, planes):
                c = remote(
                    landed, slabs_ref.at[z], bs.at[r], br.at[r], lax.rem(z + r, planes), p
                )
                c.start()
                slab_sent.append(c)
            c = pltpu.make_async_copy(landed, slabs_ref.at[z], bl)
            c.start()
            slab_sent.append(c)
            for c in gain_out:
                c.wait_recv()
            gain_own.wait()
            for k in range(1, PLANE):
                c = remote(gains_ref.at[p], gains_ref.at[p], gs2.at[k], gr2.at[k], z, xor(p, k))
                c.start()
                gain_on.append(c)
            relay()

        plane_gather(z, p, x_ref, place, xs, xr, xfs, xfr, xl, during)
        plane_gather(z, p, cot_ref, lambda q: cots_ref.at[q], cs, cr, cfs, cfr, cl)
        pltpu.make_async_copy(edge, front, hr).wait()

        @pl.when(p == PLANE - 1)
        def _():
            for q in range(PLANE):
                remote(edge, front, hs.at[q], hr, after, q).wait_send()

        @pl.when(moves)
        def _():
            home.wait_send()

        for c in gain_out:
            c.wait_send()
        for c in gain_on + slab_sent:
            c.wait()
        ring_finish(local, sent, relayed)

    def shape(*dims, kind=BF16):
        return jax.ShapeDtypeStruct(dims, kind)

    one = pltpu.SemaphoreType.DMA
    return pl.pallas_call(
        kernel,
        out_shape=(
            shape(HALO + PLANE * tok, width),
            shape(PLANE, tok, width),
            shape(planes, *slab.shape),
            shape(PLANE, planes, *gains.shape, kind=F32),
            shape(planes, *inner.shape),
        ),
        in_specs=[ANY] * 5,
        out_specs=(ANY,) * 5,
        scratch_shapes=[
            pltpu.VMEM(slab.shape, slab.dtype),
            *[dma(n) for n in GATHER_SEMS],
            one,
            *[dma(n) for n in GATHER_SEMS],
            one,
            dma(PLANE),
            one,
            dma(planes),
            dma(planes),
            one,
            dma(PLANE),
            dma(PLANE),
            dma(ring_sems(planes)),
            dma(ring_sems(planes)),
            one,
            one,
            one,
            dma(planes),
            dma(planes),
            one,
        ],
        compiler_params=comm_params(0),
        name="opening",
    )(x, cot, slab, gains, inner)


def plane_sum(part, number, planes, grads=None):
    _, tok, columns = part.shape
    beside = [] if grads is None else [grads]

    def kernel(part_ref, *refs):
        grads_ref, refs = refs[: len(beside)], refs[len(beside) :]
        out_ref, refs = refs[0], refs[1:]
        done_ref, refs = refs[: len(beside)], refs[len(beside) :]
        (own, sbuf, obuf, dbuf, rbuf, s1, r1, s2, r2), refs = refs[:9], refs[9:]
        g, ring = refs[:5], refs[5:]
        z, p = lax.axis_index("z"), lax.axis_index("p")
        guests = plane_greet(z, p)
        if beside:
            guests += ring_greet(planes, z, p)
        pl.semaphore_wait(pltpu.get_barrier_semaphore(), guests)
        if beside:
            relay, total = ring_reduce(planes, z, p, grads_ref[0], *ring)

        def finish(at, value):
            own[at] = value

        def during(step):
            if step == 2 and beside:
                relay()

        plane_reduce(
            z, p, part_ref, sbuf, obuf, dbuf, rbuf, s1, r1, s2, r2, finish, tok // 2, during
        )
        plane_gather(z, p, own, lambda q: out_ref.at[q], *g, during)
        if beside:
            done_ref[0][...] = total()

    done, ring = (), []
    if beside:
        done = (jax.ShapeDtypeStruct(grads.shape[1:], F32),)
        ring = ring_reduce_scratch(planes, *grads.shape[1:])
    out = pl.pallas_call(
        kernel,
        out_shape=(jax.ShapeDtypeStruct(part.shape, F32),) + done,
        in_specs=[VMEM] * (1 + len(beside)),
        out_specs=(VMEM,) * (1 + len(beside)),
        scratch_shapes=[
            pltpu.VMEM((tok, columns), F32),
            *reduce_scratch(tok, columns, F32),
            *[dma(n) for n in GATHER_SEMS],
            pltpu.SemaphoreType.DMA,
            *ring,
        ],
        compiler_params=comm_params(number, 32 << 20),
        name="plane_sum",
    )(part, *beside)
    return out if beside else out[0]


def reduce_scratch(tok, width, kind=BF16):
    return [
        pltpu.VMEM((4, tok, width), kind),
        pltpu.VMEM((3, tok, width), kind),
        pltpu.VMEM((2, tok // 2, width), kind),
        pltpu.VMEM((2, tok, width), kind),
        *[dma(n) for n in REDUCE_SEMS],
    ]


def mixer_join(part, x, gain):
    _, tok, width = part.shape

    def kernel(
        part_ref,
        x_ref,
        gain_ref,
        resid_ref,
        out_ref,
        own,
        sbuf,
        obuf,
        dbuf,
        rbuf,
        s1,
        r1,
        s2,
        r2,
        *g,
    ):
        z, p = lax.axis_index("z"), lax.axis_index("p")
        pl.semaphore_wait(pltpu.get_barrier_semaphore(), plane_greet(z, p))

        def finish(at, total):
            v = total + x_ref[at].astype(F32)
            resid_ref[at] = v
            r = lax.rsqrt(jnp.mean(v * v, axis=-1, keepdims=True) + EPSILON)
            own[at] = (v * r * gain_ref[...]).astype(BF16)

        plane_reduce(z, p, part_ref, sbuf, obuf, dbuf, rbuf, s1, r1, s2, r2, finish, 16)
        plane_gather(z, p, own, lambda q: out_ref.at[q], *g)

    return pl.pallas_call(
        kernel,
        out_shape=(
            jax.ShapeDtypeStruct((tok, width), F32),
            jax.ShapeDtypeStruct(part.shape, BF16),
        ),
        in_specs=[VMEM] * 3,
        out_specs=(VMEM, VMEM),
        scratch_shapes=[
            pltpu.VMEM((tok, width), BF16),
            *reduce_scratch(tok, width),
            *[dma(n) for n in GATHER_SEMS],
            pltpu.SemaphoreType.DMA,
        ],
        compiler_params=comm_params(2, 32 << 20),
        name="mixer_join",
    )(part, x, gain)


def feed_forward(normed, cot, weights):
    rows, width = normed.shape
    planes, triple, _ = weights.shape
    units = triple // 3
    hidden = planes * units
    block = 256

    def kernel(n_ref, c_ref, w_ref, two_ref, out_ref, h_ref, gb_ref, ub_ref, gw, uw, dw, sem):
        @pl.when(pl.program_id(0) == 0)
        def _():
            copies = []
            for i, dst in enumerate((gw, uw, dw)):
                for k in range(planes):
                    copies.append(
                        pltpu.make_async_copy(
                            w_ref.at[k, pl.ds(i * units, units)],
                            dst.at[pl.ds(k * units, units)],
                            sem.at[i, k],
                        )
                    )
            for c in copies:
                c.start()
            for c in copies:
                c.wait()

        n, c = n_ref[...], c_ref[...]
        gate = contract(n, gw[...], 1, 1)
        up = contract(n, uw[...], 1, 1)
        back = contract(c, dw[...], 1, 1)
        s = jax.nn.sigmoid(gate)
        silu = gate * s
        h = (silu * up).astype(BF16)
        gb = (back * up * (s * (1.0 + gate * (1.0 - s)))).astype(BF16)
        ub = (back * silu).astype(BF16)
        h_ref[...] = h
        gb_ref[...] = gb
        ub_ref[...] = ub
        two_ref[...] = (contract(gb, gw[...], 1, 0) + contract(ub, uw[...], 1, 0)).astype(BF16)
        out_ref[...] = contract(h, dw[...], 1, 0, BF16)

    wide = pl.BlockSpec((block, width), lambda i: (i, 0))
    thin = pl.BlockSpec((block, hidden), lambda i: (i, 0))
    return pl.pallas_call(
        kernel,
        grid=(rows // block,),
        out_shape=(jax.ShapeDtypeStruct((rows, width), BF16),) * 2
        + (jax.ShapeDtypeStruct((rows, hidden), BF16),) * 3,
        in_specs=[wide, wide, ANY],
        out_specs=(wide, wide, thin, thin, thin),
        scratch_shapes=[pltpu.VMEM((hidden, width), BF16)] * 3
        + [pltpu.SemaphoreType.DMA((3, planes))],
        compiler_params=pltpu.CompilerParams(vmem_limit_bytes=48 << 20),
        name="feed_forward",
    )(normed, cot, weights)


def ffn_join(planes, part, resid, gain, cot, normed, cot_all, h, gb, ub):
    _, tok, width = part.shape
    hidden = h.shape[1]
    units = hidden // planes
    step_units = 128

    def kernel(
        part_ref,
        v_ref,
        gain_ref,
        cot_ref,
        n_ref,
        c_ref,
        h_ref,
        gb_ref,
        ub_ref,
        grad_ref,
        out_ref,
        gg_ref,
        w_ref,
        own,
        sbuf,
        obuf,
        dbuf,
        rbuf,
        s1,
        r1,
        s2,
        r2,
        *g,
    ):
        g, (gw, uw, dw, wsem) = g[:5], g[5:]
        z, p = lax.axis_index("z"), lax.axis_index("p")
        pl.semaphore_wait(pltpu.get_barrier_semaphore(), plane_greet(z, p))
        gg_ref[...] = jnp.zeros_like(gg_ref)
        copies = []

        def weight_grad(i, dst, left, right):
            for n in range(hidden // step_units):
                at = pl.ds(n * step_units, step_units)
                dst[at, :] = contract(left[:, at], right[...], 0, 0, BF16)
            for k in range(planes):
                c = pltpu.make_async_copy(
                    dst.at[pl.ds(k * units, units)],
                    w_ref.at[k, pl.ds(i * units, units)],
                    wsem.at[i, k],
                )
                c.start()
                copies.append(c)

        def during(step):
            if step == 0:
                weight_grad(0, gw, gb_ref, n_ref)
            if step == 1:
                weight_grad(1, uw, ub_ref, n_ref)
            if step == 2:
                weight_grad(2, dw, h_ref, c_ref)

        def finish(at, u):
            v = v_ref[at]
            r = lax.rsqrt(jnp.mean(v * v, axis=-1, keepdims=True) + EPSILON)
            ug = u * gain_ref[...]
            mid = r * ug - v * (r * r * r) * jnp.mean(ug * v, axis=-1, keepdims=True)
            gg_ref[...] += jnp.sum(u * v * r, axis=0, keepdims=True)
            total = cot_ref[at].astype(F32) + mid
            grad_ref[at] = total
            own[at] = total.astype(BF16)

        plane_reduce(
            z, p, part_ref, sbuf, obuf, dbuf, rbuf, s1, r1, s2, r2, finish, 16, during
        )
        plane_gather(z, p, own, lambda q: out_ref.at[q], *g, during)
        for c in copies:
            c.wait()

    return pl.pallas_call(
        kernel,
        out_shape=(
            jax.ShapeDtypeStruct((tok, width), F32),
            jax.ShapeDtypeStruct(part.shape, BF16),
            jax.ShapeDtypeStruct((1, width), F32),
            jax.ShapeDtypeStruct((planes, 3 * units, width), BF16),
        ),
        in_specs=[VMEM] * 9,
        out_specs=(VMEM, VMEM, VMEM, ANY),
        scratch_shapes=[
            pltpu.VMEM((tok, width), BF16),
            *reduce_scratch(tok, width),
            *[dma(n) for n in GATHER_SEMS],
            pltpu.SemaphoreType.DMA,
            *[pltpu.VMEM((hidden, width), BF16)] * 3,
            pltpu.SemaphoreType.DMA((3, planes)),
        ],
        compiler_params=comm_params(3, 48 << 20),
        name="ffn_join",
    )(part, resid, gain, cot, normed, cot_all, h, gb, ub)


def state_chain(planes, through, local, number, forward):
    def kernel(t_ref, l_ref, out_ref, got, s0, r0, s1, r1):
        z, p = lax.axis_index("z"), lax.axis_index("p")
        for r in range(1, planes):
            greet(lax.rem(z + r, planes), p)
        pl.semaphore_wait(pltpu.get_barrier_semaphore(), planes - 1)
        sent = []
        for r in range(1, planes):
            to = lax.rem(z + r, planes)
            c = remote(t_ref, got.at[z, 0], s0.at[r], r0.at[r], to, p)
            d = remote(l_ref, got.at[z, 1], s1.at[r], r1.at[r], to, p)
            c.start()
            d.start()
            sent += [c, d]
        got[z, 0] = t_ref[...]
        got[z, 1] = l_ref[...]
        for c in sent:
            c.wait()
        state = jnp.zeros_like(l_ref)
        for k in range(planes) if forward else reversed(range(planes)):
            new = got[k, 0] * state + got[k, 1]
            state = jnp.where((k < z) if forward else (k > z), new, state)
        out_ref[...] = state

    return pl.pallas_call(
        kernel,
        out_shape=jax.ShapeDtypeStruct(local.shape, F32),
        in_specs=[VMEM] * 2,
        out_specs=VMEM,
        scratch_shapes=[
            pltpu.VMEM((planes, 2) + local.shape, F32),
            dma(planes),
            dma(planes),
            dma(planes),
            dma(planes),
        ],
        compiler_params=comm_params(number),
        name="state_chain",
    )(through, local)


def closing(
    planes, part, halo, x, gain, resid_grad, inner_g, slab_g, gain_g, out_part, resid
):
    _, tok, width = part.shape
    block = inner_g.shape[1]

    def kernel(
        part_ref,
        halo_ref,
        x_ref,
        gain_ref,
        rg_ref,
        ig_ref,
        sg_ref,
        gg_ref,
        fp_ref,
        rm_ref,
        out_ref,
        io_ref,
        so_ref,
        go_ref,
        bo_ref,
        sbuf,
        obuf,
        dbuf,
        rbuf,
        s1,
        r1,
        s2,
        r2,
        sbuf2,
        obuf2,
        dbuf2,
        rbuf2,
        s3,
        r3,
        s4,
        r4,
        hbuf,
        hs,
        hr,
        ibuf,
        fbuf,
        mbuf,
        is_,
        ir,
        bbuf,
        bown,
        bs,
        br,
        os_,
        or_,
        gbuf,
        gs,
        gr,
        gown,
        gbuf2,
        gs2,
        gr2,
    ):
        z, p = lax.axis_index("z"), lax.axis_index("p")
        column, slot = block_route(z, p)
        to_z, to_p = block_source_of(z, p)
        moves = moves_in(z, p)
        gets = jnp.logical_or(column != p, slot != z)
        before = lax.rem(z + planes - 1, planes)
        after = lax.rem(z + 1, planes)
        for k in range(1, PLANE):
            greet(z, xor(p, k))
        for r in range(1, planes):
            greet(lax.rem(z + r, planes), p)

        @pl.when(gets)
        def _():
            greet(slot, column)

        @pl.when(p == PLANE - 1)
        def _():
            for q in range(PLANE):
                greet(after, q)

        pl.semaphore_wait(
            pltpu.get_barrier_semaphore(),
            PLANE - 1 + planes - 1 + moves.astype(jnp.int32) + 1,
        )

        relay, inner_total = ring_reduce(planes, z, p, ig_ref, ibuf, fbuf, mbuf, is_, ir)
        slab_sent, z_sent = [], []
        for r in range(1, planes):
            to = lax.rem(z + r, planes)
            c = remote(gg_ref.at[to], gbuf.at[z], gs.at[r], gr.at[r], to, p)
            c.start()
            z_sent.append(c)
            c = remote(sg_ref.at[to], bbuf.at[z], bs.at[r], br.at[r], to, p)
            c.start()
            slab_sent.append(c)
        halo_send = remote(halo_ref, hbuf.at[p], hs, hr.at[p], before, PLANE - 1)
        halo_send.start()
        home = remote(bown, so_ref, os_, or_, to_z, to_p)
        p_sent = []

        def during(step):
            if step == 0:
                for c in z_sent:
                    c.wait()
                total = gg_ref[z]
                for r in range(1, planes):
                    total = total + gbuf[lax.rem(z + r, planes)]
                gown[...] = total
                for k in range(1, PLANE):
                    c = remote(gown, gbuf2.at[k], gs2.at[k], gr2.at[k], z, xor(p, k))
                    c.start()
                    p_sent.append(c)
                return
            relay()
            for c in slab_sent:
                c.wait()
            total = sg_ref[z]
            for r in range(1, planes):
                total = total + bbuf[lax.rem(z + r, planes)]
            bown[...] = total

            @pl.when(moves)
            def _():
                home.start()

            @pl.when(jnp.logical_not(moves))
            def _():
                pltpu.make_async_copy(bown, so_ref, or_).start()

        def finish(at, u):
            out_ref[at] = u

        plane_reduce(
            z, p, part_ref, sbuf, obuf, dbuf, rbuf, s1, r1, s2, r2, finish, 16, during
        )

        @pl.when(p == PLANE - 1)
        def _():
            for q in range(PLANE):
                pltpu.make_async_copy(halo_ref, hbuf.at[q], hr.at[q]).wait()

            @pl.when(z < planes - 1)
            def _():
                add = hbuf[0].astype(F32)
                for q in range(1, PLANE):
                    add = add + hbuf[q].astype(F32)
                out_ref[pl.ds(tok - HALO, HALO)] += add

        halo_send.wait_send()

        def output(at, u):
            bo_ref[at] = (rm_ref[at] + u).astype(BF16)

        plane_reduce(z, p, fp_ref, sbuf2, obuf2, dbuf2, rbuf2, s3, r3, s4, r4, output, 16)

        def norm(n, _):
            at = pl.ds(pl.multiple_of(n * 16, 16), 16)
            u = out_ref[at]
            v = x_ref[at].astype(F32)
            r = lax.rsqrt(jnp.mean(v * v, axis=-1, keepdims=True) + EPSILON)
            ug = u * gain_ref[...]
            grad = r * ug - v * (r * r * r) * jnp.mean(ug * v, axis=-1, keepdims=True)
            out_ref[at] = rg_ref[at] + grad
            return 0

        lax.fori_loop(0, tok // 16, norm, 0)

        for c in p_sent:
            c.wait()
        total = gown[...]
        for k in range(1, PLANE):
            total = total + gbuf2[k]
        go_ref[...] = total

        pltpu.make_async_copy(bown, so_ref, or_).wait()

        @pl.when(moves)
        def _():
            home.wait_send()

        io_ref[...] = inner_total()

    one = pltpu.SemaphoreType.DMA
    return pl.pallas_call(
        kernel,
        out_shape=(
            jax.ShapeDtypeStruct((tok, width), F32),
            jax.ShapeDtypeStruct(inner_g.shape[1:], F32),
            jax.ShapeDtypeStruct(slab_g.shape[1:], F32),
            jax.ShapeDtypeStruct(gain_g.shape[1:], F32),
            jax.ShapeDtypeStruct((tok, width), BF16),
        ),
        in_specs=[VMEM] * 10,
        out_specs=(VMEM,) * 5,
        scratch_shapes=[
            *reduce_scratch(tok, width),
            *reduce_scratch(tok, width),
            pltpu.VMEM((PLANE, HALO, width), BF16),
            one,
            dma(PLANE),
            *ring_reduce_scratch(planes, block, width),
            pltpu.VMEM(slab_g.shape, F32),
            pltpu.VMEM(slab_g.shape[1:], F32),
            dma(planes),
            dma(planes),
            one,
            one,
            pltpu.VMEM(gain_g.shape, F32),
            dma(planes),
            dma(planes),
            pltpu.VMEM(gain_g.shape[1:], F32),
            pltpu.VMEM((PLANE,) + gain_g.shape[1:], F32),
            dma(PLANE),
            dma(PLANE),
        ],
        compiler_params=comm_params(6, 48 << 20),
        name="closing",
    )(part, halo, x, gain, resid_grad, inner_g, slab_g, gain_g, out_part, resid)


CHUNK = 256


def scan_specs(channels, count, backward):
    def at(i):
        return count - 1 - i if backward else i

    return (
        pl.BlockSpec((CHUNK, channels), lambda i: (at(i), 0)),
        lambda part, size: pl.BlockSpec((CHUNK, size * STATE, 128), lambda i: (at(i), part, 0)),
        pl.BlockSpec((CHUNK, STATE, channels), lambda i: (at(i), 0, 0)),
        pl.BlockSpec((STATE, channels), lambda i: (0, 0)),
    )


def rows_of(g, size=GROUP):
    return pl.ds(pl.multiple_of(g * size, size), size)


def across(maps, channels):
    return jnp.concatenate([maps.astype(F32)] * (channels // 128), axis=1)


SCAN_PARAMS = pltpu.CompilerParams(vmem_limit_bytes=48 << 20)


def prepare(proj, gain, step_w, step_b, mixed, keep):
    tokens, columns = proj.shape
    channels = mixed.shape[1]
    edges = (0, RANK, RANK + STATE, RANK + 2 * STATE)

    def kernel(
        proj_ref, gain_ref, w_ref, b_ref, mixed_ref, keep_ref, step_ref, cut_ref, drive_ref,
        low_ref, maps_ref,
    ):
        row = lax.broadcasted_iota(jnp.int32, (columns, columns), 0)
        col = lax.broadcasted_iota(jnp.int32, (columns, columns), 1)
        mean = jnp.zeros((columns, columns), F32)
        for low, high in zip(edges, edges[1:]):
            inside = (row >= low) & (row < high) & (col >= low) & (col < high)
            mean = mean + jnp.where(inside, 1.0, 0.0)
        mean = mean.astype(BF16)
        lane = lax.broadcasted_iota(jnp.int32, (1, columns), 1)
        share = jnp.where(lane < RANK, 1.0 / RANK, 1.0 / STATE)
        v = proj_ref[...]
        square = v * v
        high = square.astype(BF16)
        rest = (square - high.astype(F32)).astype(BF16)
        total = jnp.dot(high, mean, preferred_element_type=F32) + jnp.dot(
            rest, mean, preferred_element_type=F32
        )
        out = v * lax.rsqrt(total * share + EPSILON) * gain_ref[...]
        low = out.astype(BF16)
        low_ref[...] = low
        raw = contract(low, w_ref[...], 1, 1) + b_ref[...]
        step = jnp.maximum(raw, 0.0) + jnp.log1p(jnp.exp(-jnp.abs(raw)))
        step_ref[...] = step
        drive_ref[...] = step * mixed_ref[...].astype(F32)
        cut_ref[...] = jnp.where(keep_ref[...] > 0.0, step, CUT)

        wide = (2 * STATE, columns)
        pick = lax.broadcasted_iota(jnp.int32, wide, 1) == (
            lax.broadcasted_iota(jnp.int32, wide, 0) + columns - 2 * STATE
        )
        pick = jnp.where(pick, 1.0, 0.0).astype(BF16)
        first = lax.broadcasted_iota(jnp.int32, (2 * columns, 256), 0) < columns
        left = lax.broadcasted_iota(jnp.int32, (2 * columns, 256), 1) < 128
        ones = jnp.where(first == left, 1.0, 0.0).astype(BF16)
        many = 32

        def spread(g, _):
            at = rows_of(g, many)
            rows = low_ref[at, :]
            pairs = []
            for k in range(many // 2):
                pairs.append(
                    jnp.concatenate(
                        [
                            jnp.broadcast_to(rows[k : k + 1], wide) * pick,
                            jnp.broadcast_to(rows[k + many // 2 : k + many // 2 + 1], wide) * pick,
                        ],
                        axis=1,
                    )
                )
            result = jnp.dot(
                jnp.concatenate(pairs, axis=0), ones, preferred_element_type=F32
            ).astype(BF16)
            maps_ref[rows_of(2 * g, many // 2)] = result[:, :128].reshape(many // 2, 2 * STATE, 128)
            maps_ref[rows_of(2 * g + 1, many // 2)] = result[:, 128:].reshape(
                many // 2, 2 * STATE, 128
            )
            return 0

        lax.fori_loop(0, CHUNK // many, spread, 0)

    def tile(size):
        return pl.BlockSpec((CHUNK, size), lambda i: (i, 0))

    def whole(array):
        return pl.BlockSpec(array.shape, lambda i: (0, 0))

    shape = jax.ShapeDtypeStruct((tokens, channels), F32)
    return pl.pallas_call(
        kernel,
        grid=(tokens // CHUNK,),
        out_shape=(
            shape,
            shape,
            shape,
            jax.ShapeDtypeStruct((tokens, columns), BF16),
            jax.ShapeDtypeStruct((tokens, 2 * STATE, 128), BF16),
        ),
        in_specs=[
            tile(columns),
            whole(gain),
            whole(step_w),
            whole(step_b),
            tile(channels),
            tile(1),
        ],
        out_specs=(
            tile(channels),
            tile(channels),
            tile(channels),
            tile(columns),
            pl.BlockSpec((CHUNK, 2 * STATE, 128), lambda i: (i, 0, 0)),
        ),
        compiler_params=SCAN_PARAMS,
        name="prepare",
    )(proj, gain, step_w, step_b, mixed, keep)


def forward_final(step, drive, maps, rate):
    tokens, channels = step.shape
    count = tokens // CHUNK
    rows, cols, _, const = scan_specs(channels, count, False)

    def kernel(step_ref, drive_ref, in_ref, rate_ref, state_ref, through_ref):
        @pl.when(pl.program_id(0) == 0)
        def _():
            state_ref[...] = jnp.zeros_like(state_ref)
            through_ref[...] = jnp.zeros_like(through_ref)

        rate_v = rate_ref[...]

        def body(g, carry):
            h, total = carry
            d8, w8 = step_ref[rows_of(g), :], drive_ref[rows_of(g), :]
            for k in range(GROUP):
                decay = jnp.exp(d8[k : k + 1, :] * rate_v)
                h = decay * h + w8[k : k + 1, :] * across(in_ref[g * GROUP + k], channels)
            return h, total + d8

        h, total = lax.fori_loop(
            0,
            CHUNK // GROUP,
            body,
            (state_ref[...], jnp.zeros((GROUP, channels), F32)),
        )
        state_ref[...] = h
        through_ref[...] += jnp.sum(total, axis=0, keepdims=True)

        @pl.when(pl.program_id(0) == count - 1)
        def _():
            through_ref[...] = jnp.exp(through_ref[...] * rate_v)

    shape = jax.ShapeDtypeStruct(rate.shape, F32)
    return pl.pallas_call(
        kernel,
        grid=(count,),
        out_shape=(shape, shape),
        in_specs=[rows, rows, cols(0, 1), const],
        out_specs=(const, const),
        compiler_params=SCAN_PARAMS,
        name="forward_final",
    )(step, drive, maps, rate)


def forward_all(step, drive, maps, rate, start):
    tokens, channels = step.shape
    count = tokens // CHUNK
    rows, cols, states, const = scan_specs(channels, count, False)

    def kernel(step_ref, drive_ref, maps_ref, rate_ref, start_ref, y_ref, hs_ref, h_sc):
        @pl.when(pl.program_id(0) == 0)
        def _():
            h_sc[...] = start_ref[...]

        rate_v = rate_ref[...]

        def body(g, h):
            d8, w8 = step_ref[rows_of(g), :], drive_ref[rows_of(g), :]
            out = []
            for k in range(GROUP):
                t = g * GROUP + k
                hs_ref[t] = h.astype(BF16)
                decay = jnp.exp(d8[k : k + 1, :] * rate_v)
                h = decay * h + w8[k : k + 1, :] * across(maps_ref[t, :STATE], channels)
                out.append(
                    jnp.sum(h * across(maps_ref[t, STATE:], channels), axis=0, keepdims=True)
                )
            y_ref[rows_of(g), :] = jnp.concatenate(out, axis=0)
            return h

        h_sc[...] = lax.fori_loop(0, CHUNK // GROUP, body, h_sc[...])

    return pl.pallas_call(
        kernel,
        grid=(count,),
        out_shape=(
            jax.ShapeDtypeStruct((tokens, channels), F32),
            jax.ShapeDtypeStruct((tokens, STATE, channels), BF16),
        ),
        in_specs=[rows, rows, cols(0, 2), const, const],
        out_specs=(rows, states),
        scratch_shapes=[pltpu.VMEM((STATE, channels), F32)],
        compiler_params=SCAN_PARAMS,
        name="forward_all",
    )(step, drive, maps, rate, start)


def backward_first(step, mix_grad, maps, rate):
    tokens, channels = step.shape
    count = tokens // CHUNK
    rows, cols, _, const = scan_specs(channels, count, True)

    def kernel(step_ref, mix_ref, out_map_ref, rate_ref, out_ref):
        @pl.when(pl.program_id(0) == 0)
        def _():
            out_ref[...] = jnp.zeros_like(out_ref)

        rate_v = rate_ref[...]

        def body(n, q):
            g = CHUNK // GROUP - 1 - n
            d8, m8 = step_ref[rows_of(g), :], mix_ref[rows_of(g), :]
            for k in reversed(range(GROUP)):
                decay = jnp.exp(d8[k : k + 1, :] * rate_v)
                q = decay * (q + m8[k : k + 1, :] * across(out_map_ref[g * GROUP + k], channels))
            return q

        out_ref[...] = lax.fori_loop(0, CHUNK // GROUP, body, out_ref[...])

    return pl.pallas_call(
        kernel,
        grid=(count,),
        out_shape=jax.ShapeDtypeStruct(rate.shape, F32),
        in_specs=[rows, rows, cols(1, 1), const],
        out_specs=const,
        compiler_params=SCAN_PARAMS,
        name="backward_first",
    )(step, mix_grad, maps, rate)


def backward_all(step, drive, mix_grad, maps, rate, states_in, start, columns):
    tokens, channels = step.shape
    count = tokens // CHUNK
    rows, cols, states, const = scan_specs(channels, count, True)

    def fold(v):
        total = v[:, :128]
        for i in range(1, channels // 128):
            total = total + v[:, 128 * i : 128 * (i + 1)]
        return total.astype(BF16)

    def kernel(
        step_ref,
        drive_ref,
        mix_ref,
        maps_ref,
        rate_ref,
        hs_ref,
        start_ref,
        sb_ref,
        sr_ref,
        map_ref,
        dd_ref,
        q_sc,
        v_sc,
    ):
        @pl.when(pl.program_id(0) == 0)
        def _():
            q_sc[...] = start_ref[...]
            dd_ref[...] = jnp.zeros_like(dd_ref)

        rate_v = rate_ref[...]

        def body(n, carry):
            q, dd = carry
            g = CHUNK // GROUP - 1 - n
            at = rows_of(g)
            d8, w8, m8 = step_ref[at, :], drive_ref[at, :], mix_ref[at, :]
            sb, sr = [], []
            for k in reversed(range(GROUP)):
                t = g * GROUP + k
                d, w, m = d8[k : k + 1, :], w8[k : k + 1, :], m8[k : k + 1, :]
                b = across(maps_ref[t, :STATE], channels)
                c = across(maps_ref[t, STATE:], channels)
                decay = jnp.exp(d * rate_v)
                kept = decay * hs_ref[t].astype(F32)
                h = kept + w * b
                hbar = q + m * c
                flow = hbar * kept
                q = decay * hbar
                dd = dd + flow * d
                sb.append(jnp.sum(hbar * b, axis=0, keepdims=True))
                sr.append(jnp.sum(flow * rate_v, axis=0, keepdims=True))
                v_sc[t, :STATE] = fold(hbar * w)
                v_sc[t, STATE:] = fold(h * m)
            sb_ref[at, :] = jnp.concatenate(sb[::-1], axis=0)
            sr_ref[at, :] = jnp.concatenate(sr[::-1], axis=0)
            return q, dd

        q, dd = lax.fori_loop(0, CHUNK // GROUP, body, (q_sc[...], dd_ref[...]))
        q_sc[...] = q
        dd_ref[...] = dd

        first = lax.broadcasted_iota(jnp.int32, (256, 2 * columns), 0) < 128
        left = lax.broadcasted_iota(jnp.int32, (256, 2 * columns), 1) < columns
        ones = jnp.where(first == left, 1.0, 0.0).astype(BF16)
        shape = (2 * STATE, columns)
        pick = lax.broadcasted_iota(jnp.int32, shape, 1) == (
            lax.broadcasted_iota(jnp.int32, shape, 0) + columns - 2 * STATE
        )
        many = 32

        def lanes(n, _):
            one = v_sc[rows_of(2 * n, many // 2)].reshape(many * STATE, 128)
            two = v_sc[rows_of(2 * n + 1, many // 2)].reshape(many * STATE, 128)
            total = jnp.dot(
                jnp.concatenate([one, two], axis=1), ones, preferred_element_type=F32
            )
            for i in range(2):
                part = total[:, columns * i : columns * (i + 1)].reshape(many // 2, 2 * STATE, columns)
                map_ref[rows_of(2 * n + i, many // 2), :] = jnp.sum(
                    jnp.where(pick[None], part, 0.0), axis=1
                )
            return 0

        lax.fori_loop(0, CHUNK // many, lanes, 0)

    wide = jax.ShapeDtypeStruct((tokens, channels), F32)
    return pl.pallas_call(
        kernel,
        grid=(count,),
        out_shape=(
            wide,
            wide,
            jax.ShapeDtypeStruct((tokens, columns), F32),
            jax.ShapeDtypeStruct(rate.shape, F32),
        ),
        in_specs=[rows, rows, rows, cols(0, 2), const, states, const],
        out_specs=(
            rows,
            rows,
            pl.BlockSpec((CHUNK, columns), lambda i: (count - 1 - i, 0)),
            const,
        ),
        scratch_shapes=[
            pltpu.VMEM((STATE, channels), F32),
            pltpu.VMEM((CHUNK, 2 * STATE, 128), BF16),
        ],
        compiler_params=SCAN_PARAMS,
        name="backward_all",
    )(step, drive, mix_grad, maps, rate, states_in, start)


def contract(left, right, left_dim, right_dim, kind=F32):
    return lax.dot_general(
        left, right, (((left_dim,), (right_dim,)), ((), ())), preferred_element_type=F32
    ).astype(kind)


def silu_slope(v):
    s = jax.nn.sigmoid(v)
    return s * (1.0 + v * (1.0 - s))


def group_mean(values, lane):
    def mean(low, high):
        inside = jnp.logical_and(lane >= low, lane < high)
        return jnp.sum(jnp.where(inside, values, 0.0), axis=-1, keepdims=True) / (high - low)

    return jnp.where(
        lane < RANK,
        mean(0, RANK),
        jnp.where(lane < RANK + STATE, mean(RANK, RANK + STATE), mean(RANK + STATE, RANK + 2 * STATE)),
    )


def on_device(
    planes,
    block_input,
    documents,
    first_gain,
    inner_weight,
    conv_weight,
    conv_bias,
    select_weight,
    select_gain,
    step_weight,
    step_bias,
    decay_log,
    skip_gain,
    mixer_weight,
    second_gain,
    gate_weight,
    up_weight,
    down_weight,
    cotangent,
):
    tok, width = block_input.shape
    devices = planes * PLANE
    rows = PLANE * tok
    z = lax.axis_index("z")
    own_block = mixer_weight.shape[0]
    inner_block = inner_weight.shape[1]
    channels = planes * own_block
    columns = RANK + 2 * STATE
    taps = conv_weight.shape[0]

    parts = [
        select_weight,
        step_weight.T,
        conv_weight.T,
        conv_bias[:, None],
        step_bias[:, None],
        decay_log.T,
        skip_gain[:, None],
    ]
    used = sum(a.shape[1] for a in parts)
    slab_width = -(-used // 128) * 128
    slab = jnp.pad(jnp.concatenate(parts, axis=1), ((0, 0), (0, slab_width - used)))
    widths = [first_gain.shape[0], second_gain.shape[0], select_gain.shape[0]]
    gains = jnp.concatenate([first_gain, second_gain, select_gain]).astype(F32)
    gains = jnp.pad(gains[None, :], ((0, 7), (0, 128 - sum(widths))))

    x_ext, cot_all, slabs, gains_all, inners = opening(
        planes, block_input, cotangent, slab, gains, inner_weight.T
    )
    cot_all = cot_all.reshape(rows, width)
    route = []
    for k in range(devices):
        half = k // 2
        route.append((k, (2 * (half // PLANE) + k % 2) * PLANE + half % PLANE))
    mixer_here = lax.ppermute(mixer_weight, ("z", "p"), route)
    ffn_own = jnp.concatenate([gate_weight.T, up_weight.T, down_weight])
    mixer_here, ffn_own, _ = lax.optimization_barrier((mixer_here, ffn_own, slabs))
    mixer_w = lax.all_gather(mixer_here, "z", axis=0, tiled=True)
    ffn_w = lax.all_gather(ffn_own, "z", axis=0)

    gains_all = jnp.transpose(gains_all[:, :, 0, :], (1, 0, 2)).reshape(devices, 128)
    first_f = gains_all[:, : widths[0]].reshape(1, width)
    second_f = gains_all[:, widths[0] : widths[0] + widths[1]].reshape(1, width)
    select_f = gains_all[:, widths[0] + widths[1] : sum(widths)].reshape(1, columns)
    slab_all = slabs.reshape(channels, slab_width)
    select_w = slab_all[:, :columns]
    step_w = jnp.pad(slab_all[:, columns : columns + RANK], ((0, 0), (0, columns - RANK)))
    rest = slab_all[:, columns + RANK :].astype(F32).T
    conv_w = [rest[k][None, :] for k in range(taps)]
    conv_b = rest[taps][None, :]
    step_b = rest[taps + 1][None, :]
    rate = -jnp.exp(rest[taps + 2 : taps + 2 + STATE])
    skip = rest[taps + 2 + STATE][None, :]
    inner_w = inners.reshape(2 * channels, width)

    padded = jnp.concatenate([jnp.full((taps - 1,), -1, jnp.int32), documents])
    ids = lax.dynamic_slice_in_dim(padded, z * rows, rows + taps - 1, 0)
    here = ids[taps - 1 :]
    same = [(ids[k : k + rows] == here)[:, None] for k in range(taps)]
    keep = same[taps - 2]

    x_f = x_ext.astype(F32)
    r_one = lax.rsqrt(jnp.mean(x_f * x_f, axis=-1, keepdims=True) + EPSILON)
    normed_one = (x_f * r_one * first_f).astype(BF16)
    conv_input = contract(normed_one, inner_w[:channels], 1, 1, BF16)
    gate_inner = contract(normed_one[HALO:], inner_w[channels:], 1, 1)
    shift = HALO - taps + 1
    total = conv_b
    for k in range(taps):
        tap = conv_input[shift + k : shift + k + rows].astype(F32)
        total = total + conv_w[k] * jnp.where(same[k], tap, 0.0)
    mixed_in = jax.nn.silu(total).astype(BF16)
    proj_part = contract(mixed_in, select_w, 1, 0)
    proj = plane_sum(proj_part.reshape(PLANE, tok, columns), 1, planes).reshape(rows, columns)
    step, step_cut, drive, step_low, maps = prepare(
        proj, select_f, step_w, step_b, mixed_in, keep.astype(F32)
    )
    mixed_f = mixed_in.astype(F32)
    local_final, through = forward_final(step_cut, drive, maps, rate)
    state_in = state_chain(planes, through, local_final, 4, True)
    sums, states = forward_all(step_cut, drive, maps, rate, state_in)
    mix = sums + skip * mixed_f
    gate_silu = jax.nn.silu(gate_inner)
    gated = (mix * gate_silu).astype(BF16)
    mixer_part = contract(gated, mixer_w, 1, 0, BF16)
    resid_mid, normed_two = mixer_join(
        mixer_part.reshape(PLANE, tok, width), block_input, second_f
    )
    normed_two = normed_two.reshape(rows, width)

    two_part, out_part, ffn_hidden, gate_back, up_back = feed_forward(
        normed_two, cot_all, ffn_w
    )
    resid_grad, mixer_back, second_grad, ffn_grads = ffn_join(
        planes,
        two_part.reshape(PLANE, tok, width),
        resid_mid,
        second_f,
        cotangent,
        normed_two,
        cot_all,
        ffn_hidden,
        gate_back,
        up_back,
    )
    mixer_back = mixer_back.reshape(rows, width)

    gated_grad = contract(mixer_back, mixer_w, 1, 1)
    mixer_grad = contract(gated, mixer_back, 0, 0, BF16)
    mixer_sum = lax.psum_scatter(mixer_grad, "z", scatter_dimension=0, tiled=True)
    mixer_out = lax.ppermute(mixer_sum, ("z", "p"), [(b, a) for a, b in route]).astype(F32)
    ffn_grads, _ = lax.optimization_barrier((ffn_grads, mixer_grad))
    ffn_sums = lax.psum_scatter(ffn_grads, "z", scatter_dimension=0, tiled=False)
    units = ffn_sums.shape[0] // 3
    mix_grad = gated_grad * gate_silu
    gate_inner_grad = gated_grad * mix * silu_slope(gate_inner)
    local_back = backward_first(step_cut, mix_grad, maps, rate)
    state_back = state_chain(planes, through, local_back, 5, False)
    map_sum, rate_sum, map_grads, decay_sum = backward_all(
        step_cut, drive, mix_grad, maps, rate, states, state_back, columns
    )
    step_raw_grad = (mixed_f * map_sum + rate_sum) * -jnp.expm1(-step)
    step_back = step_raw_grad.astype(BF16)
    select_part = contract(step_back, step_w, 1, 0) + map_grads
    select_grad = plane_sum(select_part.reshape(PLANE, tok, columns), 7, planes)
    select_grad = select_grad.reshape(rows, columns)
    lane = lax.broadcasted_iota(jnp.int32, (1, columns), 1)
    r_sel = lax.rsqrt(group_mean(proj * proj, lane) + EPSILON)
    scaled = select_grad * select_f
    proj_grad = r_sel * scaled - proj * r_sel * r_sel * r_sel * group_mean(scaled * proj, lane)
    select_gain_grad = jnp.sum(select_grad * proj * r_sel, axis=0) * (1.0 / PLANE)
    proj_back = proj_grad.astype(BF16)
    mixed_grad = step * map_sum + skip * mix_grad + contract(proj_back, select_w, 1, 1)
    pre_grad = mixed_grad * silu_slope(total)
    conv_grads, ext_grad = [], None
    for k in range(taps):
        tap = conv_input[shift + k : shift + k + rows].astype(F32)
        masked = jnp.where(same[k], pre_grad, 0.0)
        conv_grads.append(jnp.sum(masked * tap, axis=0))
        part = jnp.pad(masked * conv_w[k], ((shift + k, taps - 1 - k), (0, 0)))
        ext_grad = part if ext_grad is None else ext_grad + part
    inner_back = jnp.concatenate(
        [ext_grad, jnp.pad(gate_inner_grad, ((HALO, 0), (0, 0)))], axis=1
    ).astype(BF16)
    inner_grad = contract(inner_back, normed_one, 0, 0, BF16)
    one_part = contract(inner_back, inner_w, 1, 0, BF16)
    first_grad = jnp.sum(one_part.astype(F32) * x_f * r_one, axis=0)

    slab_grad = jnp.concatenate(
        [
            contract(mixed_in, proj_back, 0, 0),
            contract(step_back, step_low, 0, 0)[:, :RANK],
            jnp.concatenate(
                [
                    jnp.stack(conv_grads + [jnp.sum(pre_grad, axis=0), jnp.sum(step_raw_grad, axis=0)]),
                    decay_sum * rate,
                    jnp.sum(mix_grad * mixed_f, axis=0)[None, :],
                ]
            ).T,
        ],
        axis=1,
    )
    slab_grad = jnp.pad(slab_grad, ((0, 0), (0, slab_width - used)))
    gain_grad = jnp.concatenate(
        [
            first_grad.reshape(devices, widths[0]),
            second_grad.reshape(devices, widths[1]),
            select_gain_grad.reshape(devices, widths[2]),
        ],
        axis=1,
    )
    gain_grad = jnp.pad(gain_grad, ((0, 0), (0, 128 - sum(widths))))

    input_grad, inner_out, slab_out, gain_out, block_output = closing(
        planes,
        one_part[HALO:].reshape(PLANE, tok, width),
        one_part[:HALO],
        block_input,
        first_f,
        resid_grad,
        inner_grad.reshape(planes, inner_block, width),
        slab_grad.reshape(planes, own_block, slab_width),
        gain_grad.reshape(planes, PLANE, 128),
        out_part.reshape(PLANE, tok, width),
        resid_mid,
    )
    mine = lax.dynamic_index_in_dim(gain_out, lax.axis_index("p"), 0, False)
    small = slab_out[:, columns + RANK :].T
    return (
        block_output,
        input_grad,
        mine[: widths[0]],
        inner_out.T,
        small[:taps],
        small[taps],
        slab_out[:, :columns],
        mine[widths[0] + widths[1] : sum(widths)],
        slab_out[:, columns : columns + RANK].T,
        small[taps + 1],
        small[taps + 2 : taps + 2 + STATE],
        small[taps + 2 + STATE],
        mixer_out,
        mine[widths[0] : widths[0] + widths[1]],
        ffn_sums[:units].astype(F32).T,
        ffn_sums[units : 2 * units].astype(F32).T,
        ffn_sums[2 * units :].astype(F32),
    )


def solution(mesh):
    planes = mesh.devices.size // PLANE
    grid = Mesh(mesh.devices.reshape(planes, PLANE), ("z", "p"))
    seq = ("z", "p")
    by_row, by_column, flat = P(seq, None), P(None, seq), P(seq)

    def program(*args):
        return on_device(planes, *args)

    return jax.shard_map(
        program,
        mesh=grid,
        in_specs=(
            by_row,
            P(),
            flat,
            by_column,
            by_column,
            flat,
            by_row,
            flat,
            by_column,
            flat,
            by_column,
            flat,
            by_row,
            flat,
            by_column,
            by_column,
            by_row,
            by_row,
        ),
        out_specs=(
            by_row,
            by_row,
            flat,
            by_column,
            by_column,
            flat,
            by_row,
            flat,
            by_column,
            flat,
            by_column,
            flat,
            by_row,
            flat,
            by_column,
            by_column,
            by_row,
        ),
        check_vma=False,
    )
```

```python
import jax
import jax.numpy as jnp
import numpy as np
from jax import lax
from jax.experimental import pallas as pl
from jax.experimental.pallas import tpu as pltpu
from jax.sharding import Mesh
from jax.sharding import PartitionSpec as P

STATE = 16
RANK = 96
PLANE = 8
HALO = 16
GROUP = 8
CUT = 1e4
EPSILON = 1e-06
ALL_VMEM = 60 << 20
F32 = jnp.float32
BF16 = jnp.bfloat16
MESH_ID = pl.DeviceIdType.MESH
ANY = pl.BlockSpec(memory_space=pl.ANY)
VMEM = pl.BlockSpec(memory_space=pltpu.VMEM)


def xor(p, k):
    out = p
    for bit in (1, 2, 4):
        if k & bit:
            out = out + bit - 2 * bit * lax.rem(lax.div(out, bit), 2)
    return out


def remote(src, dst, send_sem, recv_sem, z, p):
    return pltpu.make_async_remote_copy(
        src_ref=src,
        dst_ref=dst,
        send_sem=send_sem,
        recv_sem=recv_sem,
        device_id={"z": z, "p": p},
        device_id_type=MESH_ID,
    )


def greet(z, p):
    pl.semaphore_signal(
        pltpu.get_barrier_semaphore(), inc=1, device_id={"z": z, "p": p}, device_id_type=MESH_ID
    )


def comm_params(number, vmem=None):
    return pltpu.CompilerParams(
        collective_id=number, has_side_effects=True, vmem_limit_bytes=vmem
    )


def dma(*shape):
    return pltpu.SemaphoreType.DMA(shape)


def block_route(z, p):
    half = lax.div(PLANE * z + p, 2)
    return lax.rem(half, PLANE), 2 * lax.div(half, PLANE) + lax.rem(p, 2)


def block_source_of(z, p):
    k = 2 * (PLANE * lax.div(z, 2) + p) + lax.rem(z, 2)
    return lax.div(k, PLANE), lax.rem(k, PLANE)


def moves_in(z, p):
    zs, ps = block_source_of(z, p)
    return jnp.logical_or(zs != z, ps != p)


def plane_greet(z, p):
    for k in (1, 2, 4):
        greet(z, xor(p, k))
    return 3


def plane_reduce(
    z, p, part, sbuf, obuf, dbuf, rbuf, s1, r1, s2, r2, finish, rows, during=None, base=0
):
    sib, near, side = xor(p, 1), xor(p, 2), xor(p, 4)
    tok = sbuf.shape[1]
    half = tok // 2
    top, low = pl.ds(0, half), pl.ds(half, half)
    wide = (part.dtype == F32) and (obuf.dtype == F32)
    align = min(rows, 16)

    def block(q):
        return part.at[pl.ds(pl.multiple_of(base + q * tok, align), tok)]

    def piece(q, at):
        return part[pl.ds(pl.multiple_of(base + q * tok + at.start, align), rows), :].astype(F32)

    def chunks(length, body):
        def step(n, _):
            body(pl.ds(pl.multiple_of(n * rows, rows), rows))
            return 0

        lax.fori_loop(0, length // rows, step, 0)

    def put(value):
        return value if wide else value.astype(obuf.dtype)

    first = []
    for i, k in enumerate((6, 2, 4, 0)):
        c = remote(block(xor(sib, k)), sbuf.at[i], s1.at[i], r1.at[i], z, sib)
        c.start()
        first.append(c)
    second = []

    def send(i, src, dst, to):
        c = remote(src, dst, s2.at[i], r2.at[i], z, to)
        c.start()
        second.append(c)
        return c

    for i, k in enumerate((6, 2, 4)):
        first[i].wait_recv()
        q = xor(p, k)

        def add(at, i=i, q=q):
            obuf[i, at] = put(piece(q, at) + sbuf[i, at].astype(F32))

        chunks(tok, add)
        if k == 6:
            far_top = send(0, obuf.at[0, top], dbuf.at[0], near)
            far_low = send(1, obuf.at[0, low], dbuf.at[1], side)
        elif k == 2:
            send(2, obuf.at[1, top], rbuf.at[0, top], near)
        else:
            send(3, obuf.at[2, low], rbuf.at[1, low], side)
    if during is not None:
        during(0)
    far_top.wait_recv()

    def join_top(at):
        obuf[2, at] = put(obuf[2, at].astype(F32) + dbuf[0, at].astype(F32))

    chunks(half, join_top)
    send(4, obuf.at[2, top], rbuf.at[1, top], side)
    far_low.wait_recv()

    def join_low(at):
        down = pl.ds(pl.multiple_of(at.start + half, rows), rows)
        obuf[1, down] = put(obuf[1, down].astype(F32) + dbuf[1, at].astype(F32))

    chunks(half, join_low)
    send(5, obuf.at[1, low], rbuf.at[0, low], near)
    if during is not None:
        during(1)
    first[3].wait_recv()
    for c in second[2:]:
        c.wait_recv()

    def last(at):
        total = piece(p, at) + sbuf[3, at].astype(F32)
        finish(at, total + rbuf[0, at].astype(F32) + rbuf[1, at].astype(F32))

    chunks(tok, last)
    for c in first + second:
        c.wait_send()


class PlaneGather:
    def __init__(self, z, p, own, place, ss, rs, fs, fr, ls):
        self.z, self.p, self.own, self.place = z, p, own, place
        self.ss, self.rs, self.fs, self.fr, self.ls = ss, rs, fs, fr, ls
        self.sent, self.passed = [], []
        half = own.shape[0] // 2
        self.top, self.low = pl.ds(0, half), pl.ds(half, half)

    def send(self, src, dst, to):
        i = len(self.sent)
        c = remote(src, dst, self.ss.at[i], self.rs.at[i], self.z, to)
        c.start()
        self.sent.append(c)

    def pass_on(self, q):
        i = len(self.passed)
        place = self.place(q)
        c = remote(place, place, self.fs.at[i], self.fr.at[i], self.z, xor(self.p, 1))
        c.start()
        self.passed.append(c)

    def start(self):
        p, own = self.p, self.own
        near, side = xor(p, 2), xor(p, 4)
        self.send(own.at[self.top], self.place(p).at[self.top], near)
        self.send(own.at[self.low], self.place(p).at[self.low], side)
        self.send(own.at[self.low], self.place(p).at[self.low], near)
        self.send(own.at[self.top], self.place(p).at[self.top], side)
        self.send(own, self.place(p), xor(p, 1))
        self.local = pltpu.make_async_copy(own, self.place(p), self.ls)
        self.local.start()

    def relay(self):
        near, side = xor(self.p, 2), xor(self.p, 4)
        self.sent[0].wait_recv()
        self.send(self.place(near).at[self.top], self.place(near).at[self.top], side)
        self.sent[1].wait_recv()
        self.send(self.place(side).at[self.low], self.place(side).at[self.low], near)

    def finish(self):
        near, side, far = xor(self.p, 2), xor(self.p, 4), xor(self.p, 6)
        self.sent[2].wait_recv()
        self.pass_on(near)
        self.sent[3].wait_recv()
        self.pass_on(side)
        self.sent[5].wait_recv()
        self.sent[6].wait_recv()
        self.pass_on(far)
        self.sent[4].wait_recv()
        for c in self.passed:
            c.wait_recv()
        for c in self.sent + self.passed:
            c.wait_send()
        self.local.wait()


def plane_gather(z, p, own, place, ss, rs, fs, fr, ls, during=None):
    gather = PlaneGather(z, p, own, place, ss, rs, fs, fr, ls)
    gather.start()
    if during is not None:
        during(2)
    gather.relay()
    gather.finish()


def rows_at(ref, tok, base=0):
    return lambda q: ref.at[pl.ds(pl.multiple_of(base + q * tok, 16), tok)]


GATHER_SEMS = (7, 7, 3, 3)
REDUCE_SEMS = (4, 4, 6, 6)


def ring_gather(planes, z, p, own, out, ss, rs, ls):
    local = pltpu.make_async_copy(own, out.at[z], ls)
    local.start()
    sent = []

    def send(i, src, dst, r):
        c = remote(src, dst, ss.at[i], rs.at[i], lax.rem(z + r, planes), p)
        c.start()
        sent.append(c)
        return c

    if planes != 4:
        for r in range(1, planes):
            send(r, own, out.at[z], r)
        return local, sent, lambda: None
    half = own.shape[0] // 2
    top, low = pl.ds(0, half), pl.ds(half, half)
    up = send(0, own.at[top], out.at[z, top], 1)
    down = send(1, own.at[low], out.at[z, low], 3)
    send(2, own.at[low], out.at[z, low], 1)
    send(3, own.at[top], out.at[z, top], 3)

    def relay():
        before, after = lax.rem(z + 3, 4), lax.rem(z + 1, 4)
        up.wait_recv()
        send(4, out.at[before, top], out.at[before, top], 1)
        down.wait_recv()
        send(5, out.at[after, low], out.at[after, low], 3)

    return local, sent, relay


def ring_finish(local, sent, relayed):
    for i, c in enumerate(sent):
        if not (relayed and i < 2):
            c.wait_recv()
        c.wait_send()
    local.wait()


def ring_reduce(planes, z, p, src, ibuf, fbuf, mbuf, ss, rs):
    half = src.shape[1] // 2
    top, low = pl.ds(0, half), pl.ds(half, half)
    before, after = lax.rem(z + planes - 1, planes), lax.rem(z + 1, planes)
    sent = []

    def send(i, part, dst, r):
        c = remote(part, dst, ss.at[i], rs.at[i], lax.rem(z + r, planes), p)
        c.start()
        sent.append(c)

    if planes == 4:
        far = lax.rem(z + 2, 4)
        send(0, src.at[far, top], fbuf.at[0], 1)
        send(1, src.at[far, low], fbuf.at[1], 3)
        send(2, src.at[after, low], ibuf.at[0, low], 1)
        send(3, src.at[before, top], ibuf.at[1, top], 3)
    else:
        for r in range(1, planes):
            send(r, src.at[lax.rem(z + r, planes)], ibuf.at[r], r)

    def relay():
        if planes == 4:
            sent[0].wait_recv()
            mbuf[0] = (src[after, top].astype(F32) + fbuf[0].astype(F32)).astype(mbuf.dtype)
            send(4, mbuf.at[0], ibuf.at[0, top], 1)
            sent[1].wait_recv()
            mbuf[1] = (src[before, low].astype(F32) + fbuf[1].astype(F32)).astype(mbuf.dtype)
            send(5, mbuf.at[1], ibuf.at[1, low], 3)

    def finish():
        for i, c in enumerate(sent):
            if not (planes == 4 and i < 2):
                c.wait_recv()
            c.wait_send()
        total = src[z].astype(F32)
        for k in range(2) if planes == 4 else range(1, planes):
            total = total + ibuf[k].astype(F32)
        return total

    return relay, finish


def ring_reduce_scratch(planes, block, width, kind=BF16):
    return [
        pltpu.VMEM((2 if planes == 4 else planes, block, width), kind),
        pltpu.VMEM((2, block // 2, width), kind),
        pltpu.VMEM((2, block // 2, width), kind),
        dma(ring_sems(planes)),
        dma(ring_sems(planes)),
    ]


def ring_greet(planes, z, p):
    for r in range(1, planes):
        greet(lax.rem(z + r, planes), p)
    return planes - 1


def ring_sems(planes):
    return max(6, planes)


TRIO = 8


def join_gain(planes, gains_ref, row, per, spread):
    total = spread.shape[1]
    at = lax.broadcasted_iota(jnp.int32, (PLANE, total), 1)
    column = lax.broadcasted_iota(jnp.int32, (PLANE, total), 0)
    joined = jnp.zeros((PLANE, total), F32)
    for k in range(planes):
        piece = jnp.concatenate([gains_ref[q, k, row : row + 1, :] for q in range(PLANE)], axis=0)
        wide = jnp.dot(piece.astype(BF16), spread, preferred_element_type=F32)
        low = (column + PLANE * k) * per
        joined = joined + jnp.where((at >= low) & (at < low + per), wide, 0.0)
    return jnp.sum(joined, axis=0, keepdims=True)


def opening(planes, x, cot, inner, mixer, select, small, gains, ffn):
    tok, width = x.shape
    relayed = planes == 4
    block = mixer.shape[0]
    columns = select.shape[1]
    channels = planes * block
    places, filled = [], 0
    for array in small:
        places.append((filled, filled + array.shape[0]))
        filled += array.shape[0]
    rank = small[0].shape[0]
    states = small[1].shape[0]
    height = rank + 32 + columns
    pers = [g.shape[1] for g in gains]
    spreads = []
    for per, total in ((pers[0], width), (pers[2], columns)):
        spreads.append(
            jnp.asarray(np.arange(128)[:, None] == np.arange(total)[None, :] % per, BF16)
        )
    turn = ffn[0].shape[1] % 128 == 0
    units = ffn[2].shape[0]
    if not turn:
        ffn = [ffn[0].T, ffn[1].T, ffn[2]]

    def kernel(*refs):
        wide_refs, select_ref = refs[:4], refs[4]
        small_refs, gain_refs, refs = refs[5:11], refs[11:14], refs[14:]
        spread_refs, ffn_refs, refs = refs[:2], refs[2:5], refs[5:]
        xg_ref, cots_ref, inners_ref, home_ref = refs[:4]
        select_out, step_ref, rest_ref, first_ref, second_ref, sel_ref, own_ref = refs[4:11]
        refs = refs[11:]
        own_wide, own_small, got_small, smalls, own_gain, gains_all = refs[:6]
        refs = refs[6:]
        near_small, near_gain, near_spread, near_ffn = refs[:6], refs[6:9], refs[9:11], refs[11:13]
        near_select, ffn_out, refs = refs[13], refs[14], refs[15:]
        near_wide, near_down, wide_sems, refs = refs[:4], refs[4], refs[5], refs[6:]
        x_ref, cot_ref, inner_ref, mixer_ref = near_wide
        x_sems, c_sems, refs = refs[:5], refs[5:10], refs[10:]
        hs, hr, gs, gr, gs2, gr2, ins, inr, inl, ps, pr, bs, br, bl, near_sems, out_sems = refs

        z, p = lax.axis_index("z"), lax.axis_index("p")
        column, slot = block_route(z, p)
        from_z, from_p = block_source_of(z, p)
        moves = jnp.logical_or(column != p, slot != z)
        stays = jnp.logical_not(moves)
        after = lax.rem(z + 1, planes)
        for k in range(1, PLANE):
            greet(z, xor(p, k))
        for r in range(1, planes):
            greet(lax.rem(z + r, planes), p)

        @pl.when(moves_in(z, p))
        def _():
            greet(from_z, from_p)

        landing = []
        for i in (2, 0, 1, 3):
            c = pltpu.make_async_copy(wide_refs[i], near_wide[i], wide_sems.at[i])
            c.start()
            landing.append(c)
        down_in = pltpu.make_async_copy(ffn_refs[2], near_down, wide_sems.at[4])
        down_in.start()
        fetched = []
        far_refs = list(small_refs) + list(gain_refs) + [select_ref]
        far_refs += list(spread_refs) + list(ffn_refs[:2])
        near_refs = list(near_small) + list(near_gain) + [near_select]
        near_refs += list(near_spread) + list(near_ffn)
        for i, (src, dst) in enumerate(zip(far_refs, near_refs)):
            c = pltpu.make_async_copy(src, dst, near_sems.at[i])
            c.start()
            fetched.append(c)
        own_wide[...] = jnp.zeros_like(own_wide)
        own_gain[...] = jnp.zeros_like(own_gain)
        pl.semaphore_wait(
            pltpu.get_barrier_semaphore(),
            PLANE - 1 + planes - 1 + moves.astype(jnp.int32),
        )

        for c in landing:
            c.wait()
        local, sent, relay = ring_gather(planes, z, p, inner_ref, inners_ref, ins, inr, inl)

        homes = [
            (own_small, got_small, ps.at[0], pr.at[0]),
            (mixer_ref, home_ref, ps.at[1], pr.at[1]),
        ]

        def homing(items):
            for src, dst, send, recv in items:

                @pl.when(moves)
                def _():
                    remote(src, dst, send, recv, slot, column).start()

                @pl.when(stays)
                def _():
                    pltpu.make_async_copy(src, dst, recv).start()

        def place(q):
            return xg_ref.at[pl.ds(pl.multiple_of(HALO + q * tok, HALO), tok)]

        gain_out, gain_on, block_ring, ffn_sent = [], [], [], []

        def first_sends(_):
            for c in fetched[:10]:
                c.wait()
            for (low, high), ref in zip(places, near_small):
                own_wide[low:high, :] = ref[...].astype(F32)
            own_small[: rank + 32] = own_wide[...].astype(BF16)
            own_small[rank + 32 :] = near_select[...].astype(F32).T.astype(BF16)
            for i, ref in enumerate(near_gain):
                own_gain[i : i + 1, : pers[i]] = ref[...].astype(F32)
            homing(homes[:1])
            for r in range(1, planes):
                c = remote(
                    own_gain, gains_all.at[p, z], gs.at[r], gr.at[r], lax.rem(z + r, planes), p
                )
                c.start()
                gain_out.append(c)
            gains_all[p, z] = own_gain[...]

        x_gather = PlaneGather(z, p, x_ref, place, *x_sems)
        cot_gather = PlaneGather(z, p, cot_ref, rows_at(cots_ref, tok), *c_sems)
        x_gather.start()
        first_sends(0)
        x_gather.relay()
        relay()
        cot_gather.start()
        homing(homes[1:])

        src, dst, _, recv = homes[0]
        pltpu.make_async_copy(src, dst, recv).wait()
        block_ring.extend(ring_gather(planes, z, p, got_small, smalls, bs, br, bl))
        for c in gain_out:
            c.wait_recv()
        for k in range(1, PLANE):
            c = remote(gains_all.at[p], gains_all.at[p], gs2.at[k], gr2.at[k], z, xor(p, k))
            c.start()
            gain_on.append(c)
        x_gather.finish()

        edge = xg_ref.at[pl.ds(PLANE * tok, HALO)]
        front = xg_ref.at[pl.ds(0, HALO)]

        @pl.when(z < planes - 1)
        def _():
            remote(edge, front, hs, hr, after, p).start()

        @pl.when(z == 0)
        def _():
            pltpu.make_async_copy(edge, front, hr).start()

        cot_gather.relay()
        block_ring[2]()
        down_in.wait()
        down_out = pltpu.make_async_copy(
            near_down, own_ref.at[pl.ds(2 * units, units)], out_sems.at[2]
        )
        down_out.start()
        for c in fetched[10:]:
            c.wait()
        for i in range(2):
            if turn:
                ffn_out[i] = near_ffn[i][...].T
            else:
                ffn_out[i] = near_ffn[i][...]
            c = pltpu.make_async_copy(
                ffn_out.at[i], own_ref.at[pl.ds(i * units, units)], out_sems.at[i]
            )
            c.start()
            ffn_sent.append(c)
        for c in gain_on:
            c.wait_recv()
        first_ref[...] = join_gain(planes, gains_all, 0, pers[0], near_spread[0][...])
        second_ref[...] = join_gain(planes, gains_all, 1, pers[1], near_spread[0][...])
        sel_ref[...] = join_gain(planes, gains_all, 2, pers[2], near_spread[1][...])
        cot_gather.finish()
        down_out.wait()
        for c in ffn_sent:
            c.wait()
        pltpu.make_async_copy(edge, front, hr).wait()

        @pl.when(z < planes - 1)
        def _():
            remote(edge, front, hs, hr, after, p).wait_send()

        ring_finish(block_ring[0], block_ring[1], relayed)
        joined = jnp.concatenate([smalls[k].astype(F32) for k in range(planes)], axis=1)
        row = lax.broadcasted_iota(jnp.int32, (rank + 32, channels), 0)
        step_ref[...] = jnp.where(row < rank, joined[: rank + 32], 0.0).astype(BF16)
        rest_ref[...] = joined[rank : rank + 32]
        select_out[...] = joined[rank + 32 :].astype(BF16)
        pltpu.make_async_copy(mixer_ref, home_ref, pr.at[1]).wait()

        @pl.when(moves)
        def _():
            for src, dst, send, recv in homes:
                remote(src, dst, send, recv, slot, column).wait_send()

        for c in gain_out + gain_on:
            c.wait_send()
        ring_finish(local, sent, relayed)

    def shape(*dims, kind=BF16):
        return jax.ShapeDtypeStruct(dims, kind)

    one = pltpu.SemaphoreType.DMA
    return pl.pallas_call(
        kernel,
        out_shape=(
            shape(HALO + PLANE * tok, width),
            shape(PLANE * tok, width),
            shape(planes, *inner.shape),
            shape(*mixer.shape),
            shape(columns, channels),
            shape(rank + 32, channels),
            shape(32, channels, kind=F32),
            shape(1, width, kind=F32),
            shape(1, width, kind=F32),
            shape(1, columns, kind=F32),
            shape(3 * units, width),
        ),
        in_specs=[ANY] * 19,
        out_specs=(ANY,) * 4 + (VMEM,) * 6 + (ANY,),
        scratch_shapes=[
            pltpu.VMEM((rank + 32, block), F32),
            pltpu.VMEM((height, block), BF16),
            pltpu.VMEM((height, block), BF16),
            pltpu.VMEM((planes, height, block), BF16),
            pltpu.VMEM((TRIO, 128), F32),
            pltpu.VMEM((PLANE, planes, TRIO, 128), F32),
            *[pltpu.VMEM(a.shape, a.dtype) for a in (*small, *gains, *spreads, *ffn[:2])],
            pltpu.VMEM(select.shape, BF16),
            pltpu.VMEM((2, units, width), BF16),
            *[pltpu.VMEM(a.shape, a.dtype) for a in (x, cot, inner, mixer, ffn[2])],
            dma(5),
            *[dma(n) for n in GATHER_SEMS],
            one,
            *[dma(n) for n in GATHER_SEMS],
            one,
            one,
            one,
            dma(planes),
            dma(planes),
            dma(PLANE),
            dma(PLANE),
            dma(ring_sems(planes)),
            dma(ring_sems(planes)),
            one,
            dma(2),
            dma(2),
            dma(ring_sems(planes)),
            dma(ring_sems(planes)),
            one,
            dma(14),
            dma(3),
        ],
        compiler_params=comm_params(0, ALL_VMEM),
        name="opening",
    )(x, cot, inner, mixer, select, *small, *gains, *spreads, *ffn)


def plane_sum(part, number, planes, grads=None):
    tok, columns = part.shape[0] // PLANE, part.shape[1]
    beside = [] if grads is None else [grads]

    def kernel(part_ref, *refs):
        grads_ref, refs = refs[: len(beside)], refs[len(beside) :]
        out_ref, refs = refs[0], refs[1:]
        done_ref, refs = refs[: len(beside)], refs[len(beside) :]
        (own, sbuf, obuf, dbuf, rbuf, s1, r1, s2, r2), refs = refs[:9], refs[9:]
        g, ring = refs[:5], refs[5:]
        z, p = lax.axis_index("z"), lax.axis_index("p")
        guests = plane_greet(z, p)
        if beside:
            guests += ring_greet(planes, z, p)
        pl.semaphore_wait(pltpu.get_barrier_semaphore(), guests)
        if beside:
            relay, total = ring_reduce(planes, z, p, grads_ref[0], *ring)

        def finish(at, value):
            own[at] = value

        def during(step):
            if step == 2 and beside:
                relay()

        plane_reduce(
            z, p, part_ref, sbuf, obuf, dbuf, rbuf, s1, r1, s2, r2, finish, tok // 2, during
        )
        plane_gather(z, p, own, rows_at(out_ref, tok), *g, during)
        if beside:
            done_ref[0][...] = total()

    done, ring = (), []
    if beside:
        done = (jax.ShapeDtypeStruct(grads.shape[1:], F32),)
        ring = ring_reduce_scratch(planes, *grads.shape[1:])
    out = pl.pallas_call(
        kernel,
        out_shape=(jax.ShapeDtypeStruct(part.shape, F32),) + done,
        in_specs=[VMEM] * (1 + len(beside)),
        out_specs=(VMEM,) * (1 + len(beside)),
        scratch_shapes=[
            pltpu.VMEM((tok, columns), F32),
            *reduce_scratch(tok, columns, F32),
            *[dma(n) for n in GATHER_SEMS],
            pltpu.SemaphoreType.DMA,
            *ring,
        ],
        compiler_params=comm_params(number, 32 << 20),
        name="plane_sum",
    )(part, *beside)
    return out if beside else out[0]


def reduce_scratch(tok, width, kind=BF16):
    return [
        pltpu.VMEM((4, tok, width), kind),
        pltpu.VMEM((3, tok, width), kind),
        pltpu.VMEM((2, tok // 2, width), kind),
        pltpu.VMEM((2, tok, width), kind),
        *[dma(n) for n in REDUCE_SEMS],
    ]


def mixer_join(part, x, gain):
    tok, width = x.shape

    def kernel(
        part_ref,
        x_ref,
        gain_ref,
        resid_ref,
        out_ref,
        own,
        sbuf,
        obuf,
        dbuf,
        rbuf,
        s1,
        r1,
        s2,
        r2,
        *g,
    ):
        z, p = lax.axis_index("z"), lax.axis_index("p")
        pl.semaphore_wait(pltpu.get_barrier_semaphore(), plane_greet(z, p))

        def finish(at, total):
            v = total + x_ref[at].astype(F32)
            resid_ref[at] = v
            r = lax.rsqrt(jnp.mean(v * v, axis=-1, keepdims=True) + EPSILON)
            own[at] = (v * r * gain_ref[...]).astype(BF16)

        plane_reduce(z, p, part_ref, sbuf, obuf, dbuf, rbuf, s1, r1, s2, r2, finish, 16)
        plane_gather(z, p, own, rows_at(out_ref, tok), *g)

    return pl.pallas_call(
        kernel,
        out_shape=(
            jax.ShapeDtypeStruct((tok, width), F32),
            jax.ShapeDtypeStruct(part.shape, BF16),
        ),
        in_specs=[VMEM] * 3,
        out_specs=(VMEM, VMEM),
        scratch_shapes=[
            pltpu.VMEM((tok, width), BF16),
            *reduce_scratch(tok, width),
            *[dma(n) for n in GATHER_SEMS],
            pltpu.SemaphoreType.DMA,
        ],
        compiler_params=comm_params(2, 32 << 20),
        name="mixer_join",
    )(part, x, gain)


def feed_forward(normed, cot, weights):
    rows, width = normed.shape
    planes, triple, _ = weights.shape
    units = triple // 3
    hidden = planes * units
    block = 256

    def kernel(n_ref, c_ref, w_ref, two_ref, out_ref, h_ref, gb_ref, ub_ref, gw, uw, dw, sem):
        @pl.when(pl.program_id(0) == 0)
        def _():
            copies = []
            for i, dst in enumerate((gw, uw, dw)):
                for k in range(planes):
                    copies.append(
                        pltpu.make_async_copy(
                            w_ref.at[k, pl.ds(i * units, units)],
                            dst.at[pl.ds(k * units, units)],
                            sem.at[i, k],
                        )
                    )
            for c in copies:
                c.start()
            for c in copies:
                c.wait()

        n, c = n_ref[...], c_ref[...]
        gate = contract(n, gw[...], 1, 1)
        up = contract(n, uw[...], 1, 1)
        back = contract(c, dw[...], 1, 1)
        s = jax.nn.sigmoid(gate)
        silu = gate * s
        h = (silu * up).astype(BF16)
        gb = (back * up * (s * (1.0 + gate * (1.0 - s)))).astype(BF16)
        ub = (back * silu).astype(BF16)
        h_ref[...] = h
        gb_ref[...] = gb
        ub_ref[...] = ub
        two_ref[...] = (contract(gb, gw[...], 1, 0) + contract(ub, uw[...], 1, 0)).astype(BF16)
        out_ref[...] = contract(h, dw[...], 1, 0, BF16)

    wide = pl.BlockSpec((block, width), lambda i: (i, 0))
    thin = pl.BlockSpec((block, hidden), lambda i: (i, 0))
    return pl.pallas_call(
        kernel,
        grid=(rows // block,),
        out_shape=(jax.ShapeDtypeStruct((rows, width), BF16),) * 2
        + (jax.ShapeDtypeStruct((rows, hidden), BF16),) * 3,
        in_specs=[wide, wide, ANY],
        out_specs=(wide, wide, thin, thin, thin),
        scratch_shapes=[pltpu.VMEM((hidden, width), BF16)] * 3
        + [pltpu.SemaphoreType.DMA((3, planes))],
        compiler_params=pltpu.CompilerParams(vmem_limit_bytes=ALL_VMEM),
        name="feed_forward",
    )(normed, cot, weights)


def ffn_join(planes, part, resid, gain, cot, normed, cot_all, h, gb, ub):
    tok, width = resid.shape
    hidden = h.shape[1]
    units = hidden // planes
    step_units = 128
    turn = units % 128 == 0

    def kernel(
        part_ref,
        v_ref,
        gain_ref,
        cot_ref,
        n_ref,
        c_ref,
        h_ref,
        gb_ref,
        ub_ref,
        grad_ref,
        out_ref,
        gg_ref,
        w_ref,
        gate_ref,
        own,
        sbuf,
        obuf,
        dbuf,
        rbuf,
        s1,
        r1,
        s2,
        r2,
        *g,
    ):
        g, (gw, uw, dw, wsem), ring = g[:5], g[5:9], g[9:]
        z, p = lax.axis_index("z"), lax.axis_index("p")
        pl.semaphore_wait(
            pltpu.get_barrier_semaphore(), plane_greet(z, p) + ring_greet(planes, z, p)
        )
        gg_ref[...] = jnp.zeros_like(gg_ref)
        copies, rings = [], []
        group = step_units // units

        def weight_grad(dst, left, right):
            for n in range(hidden // step_units):
                at = pl.ds(n * step_units, step_units)
                value = contract(left[:, at], right[...], 0, 0, BF16)
                dst[pl.ds(n * group, group)] = value.reshape(group, units, width)

        def hand_out(i, dst):
            c = pltpu.make_async_copy(
                dst, w_ref.at[:, pl.ds(i * units, units)], wsem.at[i]
            )
            c.start()
            copies.append(c)

        def during(step):
            if step == 0:
                weight_grad(gw, gb_ref, n_ref)
                rings.append(ring_reduce(planes, z, p, gw, *ring))
            if step == 1:
                weight_grad(uw, ub_ref, n_ref)
                hand_out(0, uw)
            if step == 2:
                rings[0][0]()
                weight_grad(dw, h_ref, c_ref)
                hand_out(1, dw)

        def finish(at, u):
            v = v_ref[at]
            r = lax.rsqrt(jnp.mean(v * v, axis=-1, keepdims=True) + EPSILON)
            ug = u * gain_ref[...]
            mid = r * ug - v * (r * r * r) * jnp.mean(ug * v, axis=-1, keepdims=True)
            gg_ref[...] += jnp.sum(u * v * r, axis=0, keepdims=True)
            total = cot_ref[at].astype(F32) + mid
            grad_ref[at] = total
            own[at] = total.astype(BF16)

        plane_reduce(
            z, p, part_ref, sbuf, obuf, dbuf, rbuf, s1, r1, s2, r2, finish, 16, during
        )
        plane_gather(z, p, own, rows_at(out_ref, tok), *g, during)
        for c in copies:
            c.wait()
        total = rings[0][1]()
        gate_ref[...] = total.T if turn else total

    return pl.pallas_call(
        kernel,
        out_shape=(
            jax.ShapeDtypeStruct((tok, width), F32),
            jax.ShapeDtypeStruct(part.shape, BF16),
            jax.ShapeDtypeStruct((1, width), F32),
            jax.ShapeDtypeStruct((planes, 2 * units, width), BF16),
            jax.ShapeDtypeStruct((width, units) if turn else (units, width), F32),
        ),
        in_specs=[VMEM] * 9,
        out_specs=(VMEM, VMEM, VMEM, ANY, VMEM),
        scratch_shapes=[
            pltpu.VMEM((tok, width), BF16),
            *reduce_scratch(tok, width),
            *[dma(n) for n in GATHER_SEMS],
            pltpu.SemaphoreType.DMA,
            *[pltpu.VMEM((planes, units, width), BF16)] * 3,
            dma(2),
            *ring_reduce_scratch(planes, units, width),
        ],
        compiler_params=comm_params(3, 40 << 20),
        name="ffn_join",
    )(part, resid, gain, cot, normed, cot_all, h, gb, ub)


def state_chain(planes, through, local, number, forward):
    def kernel(t_ref, l_ref, out_ref, got, s0, r0, s1, r1):
        z, p = lax.axis_index("z"), lax.axis_index("p")
        for r in range(1, planes):
            greet(lax.rem(z + r, planes), p)
        pl.semaphore_wait(pltpu.get_barrier_semaphore(), planes - 1)
        sent = []
        for r in range(1, planes):
            to = lax.rem(z + r, planes)
            c = remote(t_ref, got.at[z, 0], s0.at[r], r0.at[r], to, p)
            d = remote(l_ref, got.at[z, 1], s1.at[r], r1.at[r], to, p)
            c.start()
            d.start()
            sent += [c, d]
        got[z, 0] = t_ref[...]
        got[z, 1] = l_ref[...]
        for c in sent:
            c.wait()
        state = jnp.zeros_like(l_ref)
        for k in range(planes) if forward else reversed(range(planes)):
            new = got[k, 0] * state + got[k, 1]
            state = jnp.where((k < z) if forward else (k > z), new, state)
        out_ref[...] = state

    return pl.pallas_call(
        kernel,
        out_shape=jax.ShapeDtypeStruct(local.shape, F32),
        in_specs=[VMEM] * 2,
        out_specs=VMEM,
        scratch_shapes=[
            pltpu.VMEM((planes, 2) + local.shape, F32),
            dma(planes),
            dma(planes),
            dma(planes),
            dma(planes),
        ],
        compiler_params=comm_params(number),
        name="state_chain",
    )(through, local)


def closing(planes, part, x, gain, resid_grad, inner_g, slab_g, gain_g, out_part, resid, ffn_g, mixer_g):
    tok, width = x.shape
    block = inner_g.shape[1]
    height, channels = slab_g.shape
    own = channels // planes
    rank = height - 32 - (RANK + 2 * STATE)
    columns = RANK + 2 * STATE
    units = ffn_g.shape[0] // 2
    turn = units % 128 == 0
    operands = (
        part, x, gain, resid_grad, inner_g, slab_g, gain_g, out_part, resid, ffn_g, mixer_g
    )

    def kernel(*refs):
        far, refs = refs[:11], refs[11:]
        out_ref, io_ref, sel_ref, step_ref, rest_ref, go_ref, bo_ref = refs[:7]
        up_ref, down_ref, mo_ref, refs = refs[7], refs[8], refs[9], refs[10:]
        one_bufs, out_bufs, refs = refs[:8], refs[8:16], refs[16:]
        hbuf, hs, hr, refs = refs[0], refs[1], refs[2], refs[3:]
        inner_ring, slab_ring, refs = refs[:5], refs[5:10], refs[10:]
        pieces, homed, mixed, os_, or_, refs = *refs[:5], refs[5:]
        gbuf, gs, gr, gown, gbuf2, gs2, gr2, bown = refs[:8]
        near, near_sems = refs[8:19], refs[19]
        fetched = []
        for i in (4, 0, 6, 5, 10, 7, 9, 1, 2, 3, 8):
            c = pltpu.make_async_copy(far[i], near[i], near_sems.at[i])
            c.start()
            fetched.append(c)
        part_ref, x_ref, gain_ref, rg_ref, ig_ref, sg_ref, gg_ref, fp_ref, rm_ref = near[:9]
        ffn_ref, mix_ref = near[9:]
        z, p = lax.axis_index("z"), lax.axis_index("p")
        column, slot = block_route(z, p)
        to_z, to_p = block_source_of(z, p)
        moves = moves_in(z, p)
        stays = jnp.logical_not(moves)
        gets = jnp.logical_or(column != p, slot != z)
        before = lax.rem(z + planes - 1, planes)
        for k in range(1, PLANE):
            greet(z, xor(p, k))
        for r in range(1, planes):
            greet(lax.rem(z + r, planes), p)

        @pl.when(gets)
        def _():
            greet(slot, column)

        @pl.when(jnp.logical_and(p == PLANE - 1, z < planes - 1))
        def _():
            for q in range(PLANE):
                greet(z + 1, q)

        pl.semaphore_wait(
            pltpu.get_barrier_semaphore(),
            PLANE - 1 + planes - 1 + moves.astype(jnp.int32) + (z > 0).astype(jnp.int32),
        )

        for c in fetched[:5]:
            c.wait()
        relay, inner_total = ring_reduce(planes, z, p, ig_ref, *inner_ring)
        z_sent, p_sent, slab = [], [], []
        for r in range(1, planes):
            to = lax.rem(z + r, planes)
            c = remote(gg_ref.at[to], gbuf.at[z], gs.at[r], gr.at[r], to, p)
            c.start()
            z_sent.append(c)
        halo = remote(part_ref.at[pl.ds(0, HALO)], hbuf.at[p], hs, hr.at[p], before, PLANE - 1)

        @pl.when(z > 0)
        def _():
            halo.start()

        def homing(i, src, dst):
            @pl.when(moves)
            def _():
                remote(src, dst, os_.at[i], or_.at[i], to_z, to_p).start()

            @pl.when(stays)
            def _():
                pltpu.make_async_copy(src, dst, or_.at[i]).start()

        def homing_end(i, src, dst):
            pltpu.make_async_copy(src, dst, or_.at[i]).wait()

            @pl.when(moves)
            def _():
                remote(src, dst, os_.at[i], or_.at[i], to_z, to_p).wait_send()

        homing(1, mix_ref, mixed)

        def during(step):
            if step == 0:
                for k in range(planes):
                    pieces[k] = sg_ref[:, own * k : own * (k + 1)].astype(BF16)
                slab.extend(ring_reduce(planes, z, p, pieces, *slab_ring))
                return
            relay()
            for c in z_sent:
                c.wait()
            total = gg_ref[z]
            for r in range(1, planes):
                total = total + gbuf[lax.rem(z + r, planes)]
            gown[...] = total
            for k in range(1, PLANE):
                c = remote(gown, gbuf2.at[k], gs2.at[k], gr2.at[k], z, xor(p, k))
                c.start()
                p_sent.append(c)

        def finish(at, u):
            out_ref[at] = u

        plane_reduce(z, p, part_ref, *one_bufs, finish, 16, during, HALO)

        for c in fetched[5:]:
            c.wait()

        def later(step):
            if step == 0:
                slab[0]()
                if turn:
                    up_ref[...] = ffn_ref[:units].astype(F32).T
                else:
                    up_ref[...] = ffn_ref[:units].astype(F32)
                down_ref[...] = ffn_ref[units:].astype(F32)
                return
            bown[...] = slab[1]()
            homing(0, bown, homed)

        def output(at, u):
            bo_ref[at] = (rm_ref[at] + u).astype(BF16)

        plane_reduce(z, p, fp_ref, *out_bufs, output, 16, later)

        @pl.when(jnp.logical_and(p == PLANE - 1, z < planes - 1))
        def _():
            for q in range(PLANE):
                pltpu.make_async_copy(
                    part_ref.at[pl.ds(0, HALO)], hbuf.at[q], hr.at[q]
                ).wait()
            add = hbuf[0].astype(F32)
            for q in range(1, PLANE):
                add = add + hbuf[q].astype(F32)
            out_ref[pl.ds(tok - HALO, HALO)] += add

        @pl.when(z > 0)
        def _():
            halo.wait_send()

        def norm(n, _):
            at = pl.ds(pl.multiple_of(n * 16, 16), 16)
            u = out_ref[at]
            v = x_ref[at].astype(F32)
            r = lax.rsqrt(jnp.mean(v * v, axis=-1, keepdims=True) + EPSILON)
            ug = u * gain_ref[...]
            grad = r * ug - v * (r * r * r) * jnp.mean(ug * v, axis=-1, keepdims=True)
            out_ref[at] = rg_ref[at] + grad
            return 0

        lax.fori_loop(0, tok // 16, norm, 0)

        for c in p_sent:
            c.wait()
        total = gown[...]
        for k in range(1, PLANE):
            total = total + gbuf2[k]
        row = lax.broadcasted_iota(jnp.int32, total.shape, 0)
        go_ref[...] = jnp.sum(jnp.where(row == p, total, 0.0), axis=0, keepdims=True)
        homing_end(1, mix_ref, mixed)
        mo_ref[...] = mixed[...].astype(F32)
        homing_end(0, bown, homed)
        sel_ref[...] = homed[:columns, :].T
        step_ref[...] = homed[columns : columns + rank, :]
        rest_ref[...] = homed[columns + rank :, :]
        io_ref[...] = inner_total()

    def shape(*dims, kind=F32):
        return jax.ShapeDtypeStruct(dims, kind)

    one = pltpu.SemaphoreType.DMA
    return pl.pallas_call(
        kernel,
        out_shape=(
            shape(tok, width),
            shape(*inner_g.shape[1:]),
            shape(own, columns),
            shape(rank, own),
            shape(32, own),
            shape(1, 128),
            shape(tok, width, kind=BF16),
            shape(width, units) if turn else shape(units, width),
            shape(units, width),
            shape(*mixer_g.shape),
        ),
        in_specs=[ANY] * 11,
        out_specs=(VMEM,) * 10,
        scratch_shapes=[
            *reduce_scratch(tok, width),
            *reduce_scratch(tok, width),
            pltpu.VMEM((PLANE, HALO, width), BF16),
            one,
            dma(PLANE),
            *ring_reduce_scratch(planes, block, width),
            *ring_reduce_scratch(planes, height, own),
            pltpu.VMEM((planes, height, own), BF16),
            pltpu.VMEM((height, own), F32),
            pltpu.VMEM(mixer_g.shape, BF16),
            dma(2),
            dma(2),
            pltpu.VMEM(gain_g.shape, F32),
            dma(planes),
            dma(planes),
            pltpu.VMEM(gain_g.shape[1:], F32),
            pltpu.VMEM((PLANE,) + gain_g.shape[1:], F32),
            dma(PLANE),
            dma(PLANE),
            pltpu.VMEM((height, own), F32),
            *[pltpu.VMEM(a.shape, a.dtype) for a in operands],
            dma(len(operands)),
        ],
        compiler_params=comm_params(6, 50 << 20),
        name="closing",
    )(*operands)


def hand_over(arrays, moves, shapes):
    count = len(arrays)

    def kernel(*refs):
        ins, outs, sem = refs[:count], refs[count : count + len(moves)], refs[-1]
        copies = []
        for i, (n, start) in enumerate(moves):
            src = ins[n]
            if start is not None:
                src = src.at[pl.ds(start, shapes[i].shape[0])]
            copies.append(pltpu.make_async_copy(src, outs[i], sem.at[i]))
        for c in copies:
            c.start()
        for c in copies:
            c.wait()

    return pl.pallas_call(
        kernel,
        out_shape=tuple(shapes),
        in_specs=[VMEM] * count,
        out_specs=(ANY,) * len(moves),
        scratch_shapes=[dma(len(moves))],
        name="hand_over",
    )(*arrays)


CHUNK = 256


def scan_specs(channels, count, backward):
    def at(i):
        return count - 1 - i if backward else i

    return (
        pl.BlockSpec((CHUNK, channels), lambda i: (at(i), 0)),
        lambda part, size: pl.BlockSpec((CHUNK, size * STATE, 128), lambda i: (at(i), part, 0)),
        pl.BlockSpec((CHUNK, STATE, channels), lambda i: (at(i), 0, 0)),
        pl.BlockSpec((STATE, channels), lambda i: (0, 0)),
    )


def rows_of(g, size=GROUP):
    return pl.ds(pl.multiple_of(g * size, size), size)


def across(maps, channels):
    return jnp.concatenate([maps.astype(F32)] * (channels // 128), axis=1)


SCAN_PARAMS = pltpu.CompilerParams(vmem_limit_bytes=ALL_VMEM)


def prepare(proj, gain, step_w, step_b, mixed, keep):
    tokens, columns = proj.shape
    channels = mixed.shape[1]
    edges = (0, RANK, RANK + STATE, RANK + 2 * STATE)

    def kernel(
        proj_ref, gain_ref, w_ref, b_ref, mixed_ref, keep_ref, step_ref, cut_ref, drive_ref,
        low_ref, maps_ref,
    ):
        row = lax.broadcasted_iota(jnp.int32, (columns, columns), 0)
        col = lax.broadcasted_iota(jnp.int32, (columns, columns), 1)
        mean = jnp.zeros((columns, columns), F32)
        for low, high in zip(edges, edges[1:]):
            inside = (row >= low) & (row < high) & (col >= low) & (col < high)
            mean = mean + jnp.where(inside, 1.0, 0.0)
        mean = mean.astype(BF16)
        lane = lax.broadcasted_iota(jnp.int32, (1, columns), 1)
        share = jnp.where(lane < RANK, 1.0 / RANK, 1.0 / STATE)
        v = proj_ref[...]
        square = v * v
        high = square.astype(BF16)
        rest = (square - high.astype(F32)).astype(BF16)
        total = jnp.dot(high, mean, preferred_element_type=F32) + jnp.dot(
            rest, mean, preferred_element_type=F32
        )
        out = v * lax.rsqrt(total * share + EPSILON) * gain_ref[...]
        low = out.astype(BF16)
        low_ref[...] = low
        raw = contract(low, w_ref[...], 1, 0) + b_ref[...]
        step = jnp.maximum(raw, 0.0) + jnp.log1p(jnp.exp(-jnp.abs(raw)))
        step_ref[...] = step
        drive_ref[...] = step * mixed_ref[...].astype(F32)
        cut_ref[...] = jnp.where(keep_ref[...] > 0.0, step, CUT)

        wide = (2 * STATE, columns)
        pick = lax.broadcasted_iota(jnp.int32, wide, 1) == (
            lax.broadcasted_iota(jnp.int32, wide, 0) + columns - 2 * STATE
        )
        pick = jnp.where(pick, 1.0, 0.0).astype(BF16)
        first = lax.broadcasted_iota(jnp.int32, (2 * columns, 256), 0) < columns
        left = lax.broadcasted_iota(jnp.int32, (2 * columns, 256), 1) < 128
        ones = jnp.where(first == left, 1.0, 0.0).astype(BF16)
        many = 32

        def spread(g, _):
            at = rows_of(g, many)
            rows = low_ref[at, :]
            pairs = []
            for k in range(many // 2):
                pairs.append(
                    jnp.concatenate(
                        [
                            jnp.broadcast_to(rows[k : k + 1], wide) * pick,
                            jnp.broadcast_to(rows[k + many // 2 : k + many // 2 + 1], wide) * pick,
                        ],
                        axis=1,
                    )
                )
            result = jnp.dot(
                jnp.concatenate(pairs, axis=0), ones, preferred_element_type=F32
            ).astype(BF16)
            maps_ref[rows_of(2 * g, many // 2)] = result[:, :128].reshape(many // 2, 2 * STATE, 128)
            maps_ref[rows_of(2 * g + 1, many // 2)] = result[:, 128:].reshape(
                many // 2, 2 * STATE, 128
            )
            return 0

        lax.fori_loop(0, CHUNK // many, spread, 0)

    def tile(size):
        return pl.BlockSpec((CHUNK, size), lambda i: (i, 0))

    def whole(array):
        return pl.BlockSpec(array.shape, lambda i: (0, 0))

    shape = jax.ShapeDtypeStruct((tokens, channels), F32)
    return pl.pallas_call(
        kernel,
        grid=(tokens // CHUNK,),
        out_shape=(
            shape,
            shape,
            shape,
            jax.ShapeDtypeStruct((tokens, columns), BF16),
            jax.ShapeDtypeStruct((tokens, 2 * STATE, 128), BF16),
        ),
        in_specs=[
            tile(columns),
            whole(gain),
            whole(step_w),
            whole(step_b),
            tile(channels),
            tile(1),
        ],
        out_specs=(
            tile(channels),
            tile(channels),
            tile(channels),
            tile(columns),
            pl.BlockSpec((CHUNK, 2 * STATE, 128), lambda i: (i, 0, 0)),
        ),
        compiler_params=SCAN_PARAMS,
        name="prepare",
    )(proj, gain, step_w, step_b, mixed, keep)


def forward_final(step, drive, maps, rate):
    tokens, channels = step.shape
    count = tokens // CHUNK
    rows, cols, _, const = scan_specs(channels, count, False)

    def kernel(step_ref, drive_ref, in_ref, rate_ref, state_ref, through_ref):
        @pl.when(pl.program_id(0) == 0)
        def _():
            state_ref[...] = jnp.zeros_like(state_ref)
            through_ref[...] = jnp.zeros_like(through_ref)

        rate_v = rate_ref[...]

        def body(g, carry):
            h, total = carry
            d8, w8 = step_ref[rows_of(g), :], drive_ref[rows_of(g), :]
            for k in range(GROUP):
                decay = jnp.exp(d8[k : k + 1, :] * rate_v)
                h = decay * h + w8[k : k + 1, :] * across(in_ref[g * GROUP + k], channels)
            return h, total + d8

        h, total = lax.fori_loop(
            0,
            CHUNK // GROUP,
            body,
            (state_ref[...], jnp.zeros((GROUP, channels), F32)),
        )
        state_ref[...] = h
        through_ref[...] += jnp.sum(total, axis=0, keepdims=True)

        @pl.when(pl.program_id(0) == count - 1)
        def _():
            through_ref[...] = jnp.exp(through_ref[...] * rate_v)

    shape = jax.ShapeDtypeStruct(rate.shape, F32)
    return pl.pallas_call(
        kernel,
        grid=(count,),
        out_shape=(shape, shape),
        in_specs=[rows, rows, cols(0, 1), const],
        out_specs=(const, const),
        compiler_params=SCAN_PARAMS,
        name="forward_final",
    )(step, drive, maps, rate)


def forward_all(step, drive, maps, rate, start):
    tokens, channels = step.shape
    count = tokens // CHUNK
    rows, cols, states, const = scan_specs(channels, count, False)

    def kernel(step_ref, drive_ref, maps_ref, rate_ref, start_ref, y_ref, hs_ref, h_sc):
        @pl.when(pl.program_id(0) == 0)
        def _():
            h_sc[...] = start_ref[...]

        rate_v = rate_ref[...]

        def body(g, h):
            d8, w8 = step_ref[rows_of(g), :], drive_ref[rows_of(g), :]
            out = []
            for k in range(GROUP):
                t = g * GROUP + k
                hs_ref[t] = h.astype(BF16)
                decay = jnp.exp(d8[k : k + 1, :] * rate_v)
                h = decay * h + w8[k : k + 1, :] * across(maps_ref[t, :STATE], channels)
                out.append(
                    jnp.sum(h * across(maps_ref[t, STATE:], channels), axis=0, keepdims=True)
                )
            y_ref[rows_of(g), :] = jnp.concatenate(out, axis=0)
            return h

        h_sc[...] = lax.fori_loop(0, CHUNK // GROUP, body, h_sc[...])

    return pl.pallas_call(
        kernel,
        grid=(count,),
        out_shape=(
            jax.ShapeDtypeStruct((tokens, channels), F32),
            jax.ShapeDtypeStruct((tokens, STATE, channels), BF16),
        ),
        in_specs=[rows, rows, cols(0, 2), const, const],
        out_specs=(rows, states),
        scratch_shapes=[pltpu.VMEM((STATE, channels), F32)],
        compiler_params=SCAN_PARAMS,
        name="forward_all",
    )(step, drive, maps, rate, start)


def backward_first(step, mix_grad, maps, rate):
    tokens, channels = step.shape
    count = tokens // CHUNK
    rows, cols, _, const = scan_specs(channels, count, True)

    def kernel(step_ref, mix_ref, out_map_ref, rate_ref, out_ref):
        @pl.when(pl.program_id(0) == 0)
        def _():
            out_ref[...] = jnp.zeros_like(out_ref)

        rate_v = rate_ref[...]

        def body(n, q):
            g = CHUNK // GROUP - 1 - n
            d8, m8 = step_ref[rows_of(g), :], mix_ref[rows_of(g), :]
            for k in reversed(range(GROUP)):
                decay = jnp.exp(d8[k : k + 1, :] * rate_v)
                q = decay * (q + m8[k : k + 1, :] * across(out_map_ref[g * GROUP + k], channels))
            return q

        out_ref[...] = lax.fori_loop(0, CHUNK // GROUP, body, out_ref[...])

    return pl.pallas_call(
        kernel,
        grid=(count,),
        out_shape=jax.ShapeDtypeStruct(rate.shape, F32),
        in_specs=[rows, rows, cols(1, 1), const],
        out_specs=const,
        compiler_params=SCAN_PARAMS,
        name="backward_first",
    )(step, mix_grad, maps, rate)


def backward_all(step, drive, mix_grad, maps, rate, states_in, start, columns):
    tokens, channels = step.shape
    count = tokens // CHUNK
    rows, cols, states, const = scan_specs(channels, count, True)

    def fold(v):
        total = v[:, :128]
        for i in range(1, channels // 128):
            total = total + v[:, 128 * i : 128 * (i + 1)]
        return total.astype(BF16)

    def kernel(
        step_ref,
        drive_ref,
        mix_ref,
        maps_ref,
        rate_ref,
        hs_ref,
        start_ref,
        sb_ref,
        sr_ref,
        map_ref,
        dd_ref,
        q_sc,
        v_sc,
    ):
        @pl.when(pl.program_id(0) == 0)
        def _():
            q_sc[...] = start_ref[...]
            dd_ref[...] = jnp.zeros_like(dd_ref)

        rate_v = rate_ref[...]

        def body(n, carry):
            q, dd = carry
            g = CHUNK // GROUP - 1 - n
            at = rows_of(g)
            d8, w8, m8 = step_ref[at, :], drive_ref[at, :], mix_ref[at, :]
            sb, sr = [], []
            for k in reversed(range(GROUP)):
                t = g * GROUP + k
                d, w, m = d8[k : k + 1, :], w8[k : k + 1, :], m8[k : k + 1, :]
                b = across(maps_ref[t, :STATE], channels)
                c = across(maps_ref[t, STATE:], channels)
                decay = jnp.exp(d * rate_v)
                kept = decay * hs_ref[t].astype(F32)
                h = kept + w * b
                hbar = q + m * c
                flow = hbar * kept
                q = decay * hbar
                dd = dd + flow * d
                sb.append(jnp.sum(hbar * b, axis=0, keepdims=True))
                sr.append(jnp.sum(flow * rate_v, axis=0, keepdims=True))
                v_sc[t, :STATE] = fold(hbar * w)
                v_sc[t, STATE:] = fold(h * m)
            sb_ref[at, :] = jnp.concatenate(sb[::-1], axis=0)
            sr_ref[at, :] = jnp.concatenate(sr[::-1], axis=0)
            return q, dd

        q, dd = lax.fori_loop(0, CHUNK // GROUP, body, (q_sc[...], dd_ref[...]))
        q_sc[...] = q
        dd_ref[...] = dd

        first = lax.broadcasted_iota(jnp.int32, (256, 2 * columns), 0) < 128
        left = lax.broadcasted_iota(jnp.int32, (256, 2 * columns), 1) < columns
        ones = jnp.where(first == left, 1.0, 0.0).astype(BF16)
        shape = (2 * STATE, columns)
        pick = lax.broadcasted_iota(jnp.int32, shape, 1) == (
            lax.broadcasted_iota(jnp.int32, shape, 0) + columns - 2 * STATE
        )
        many = 32

        def lanes(n, _):
            one = v_sc[rows_of(2 * n, many // 2)].reshape(many * STATE, 128)
            two = v_sc[rows_of(2 * n + 1, many // 2)].reshape(many * STATE, 128)
            total = jnp.dot(
                jnp.concatenate([one, two], axis=1), ones, preferred_element_type=F32
            )
            for i in range(2):
                part = total[:, columns * i : columns * (i + 1)].reshape(many // 2, 2 * STATE, columns)
                map_ref[rows_of(2 * n + i, many // 2), :] = jnp.sum(
                    jnp.where(pick[None], part, 0.0), axis=1
                )
            return 0

        lax.fori_loop(0, CHUNK // many, lanes, 0)

    wide = jax.ShapeDtypeStruct((tokens, channels), F32)
    return pl.pallas_call(
        kernel,
        grid=(count,),
        out_shape=(
            wide,
            wide,
            jax.ShapeDtypeStruct((tokens, columns), F32),
            jax.ShapeDtypeStruct(rate.shape, F32),
        ),
        in_specs=[rows, rows, rows, cols(0, 2), const, states, const],
        out_specs=(
            rows,
            rows,
            pl.BlockSpec((CHUNK, columns), lambda i: (count - 1 - i, 0)),
            const,
        ),
        scratch_shapes=[
            pltpu.VMEM((STATE, channels), F32),
            pltpu.VMEM((CHUNK, 2 * STATE, 128), BF16),
        ],
        compiler_params=SCAN_PARAMS,
        name="backward_all",
    )(step, drive, mix_grad, maps, rate, states_in, start)


def contract(left, right, left_dim, right_dim, kind=F32):
    return lax.dot_general(
        left, right, (((left_dim,), (right_dim,)), ((), ())), preferred_element_type=F32
    ).astype(kind)


def silu_slope(v):
    s = jax.nn.sigmoid(v)
    return s * (1.0 + v * (1.0 - s))


def group_mean(values, lane):
    def mean(low, high):
        inside = jnp.logical_and(lane >= low, lane < high)
        return jnp.sum(jnp.where(inside, values, 0.0), axis=-1, keepdims=True) / (high - low)

    return jnp.where(
        lane < RANK,
        mean(0, RANK),
        jnp.where(lane < RANK + STATE, mean(RANK, RANK + STATE), mean(RANK + STATE, RANK + 2 * STATE)),
    )


def on_device(
    planes,
    block_input,
    documents,
    first_gain,
    inner_weight,
    conv_weight,
    conv_bias,
    select_weight,
    select_gain,
    step_weight,
    step_bias,
    decay_log,
    skip_gain,
    mixer_weight,
    second_gain,
    gate_weight,
    up_weight,
    down_weight,
    cotangent,
):
    tok, width = block_input.shape
    devices = planes * PLANE
    rows = PLANE * tok
    z = lax.axis_index("z")
    own_block = mixer_weight.shape[0]
    inner_block = inner_weight.shape[1]
    channels = planes * own_block
    columns = RANK + 2 * STATE
    taps = conv_weight.shape[0]


    (
        x_ext,
        cot_all,
        inners,
        mixer_here,
        select_w,
        step_w,
        rest,
        first_f,
        second_f,
        select_f,
        ffn_own,
    ) = opening(
        planes,
        block_input,
        cotangent,
        inner_weight.T,
        mixer_weight,
        select_weight,
        (
            step_weight,
            decay_log,
            conv_weight,
            conv_bias[None, :],
            step_bias[None, :],
            skip_gain[None, :],
        ),
        (first_gain[None, :], second_gain[None, :], select_gain[None, :]),
        (gate_weight, up_weight, down_weight),
    )
    mixer_w = lax.all_gather(mixer_here, "z", axis=0, tiled=True)
    ffn_w = lax.all_gather(ffn_own, "z", axis=0)
    rate = -jnp.exp(rest[:STATE])
    conv_w = [rest[STATE + k : STATE + k + 1] for k in range(taps)]
    conv_b, step_b, skip = (rest[STATE + taps + k : STATE + taps + k + 1] for k in range(3))
    inner_w = inners.reshape(2 * channels, width)

    padded = jnp.concatenate([jnp.full((taps - 1,), -1, jnp.int32), documents])
    ids = lax.dynamic_slice_in_dim(padded, z * rows, rows + taps - 1, 0)
    here = ids[taps - 1 :]
    same = [(ids[k : k + rows] == here)[:, None] for k in range(taps)]
    keep = same[taps - 2]

    x_f = x_ext.astype(F32)
    r_one = lax.rsqrt(jnp.mean(x_f * x_f, axis=-1, keepdims=True) + EPSILON)
    normed_one = (x_f * r_one * first_f).astype(BF16)
    conv_input = contract(normed_one, inner_w[:channels], 1, 1, BF16)
    gate_inner = contract(normed_one[HALO:], inner_w[channels:], 1, 1)
    shift = HALO - taps + 1
    total = conv_b
    for k in range(taps):
        tap = conv_input[shift + k : shift + k + rows].astype(F32)
        total = total + conv_w[k] * jnp.where(same[k], tap, 0.0)
    mixed_in = jax.nn.silu(total).astype(BF16)
    proj_part = contract(mixed_in, select_w, 1, 1)
    proj = plane_sum(proj_part, 1, planes)
    step, step_cut, drive, step_low, maps = prepare(
        proj, select_f, step_w, step_b, mixed_in, keep.astype(F32)
    )
    mixed_f = mixed_in.astype(F32)
    local_final, through = forward_final(step_cut, drive, maps, rate)
    state_in = state_chain(planes, through, local_final, 4, True)
    sums, states = forward_all(step_cut, drive, maps, rate, state_in)
    mix = sums + skip * mixed_f
    gate_silu = jax.nn.silu(gate_inner)
    gated = (mix * gate_silu).astype(BF16)
    mixer_part = contract(gated, mixer_w, 1, 0, BF16)
    resid_mid, normed_two = mixer_join(
        mixer_part, block_input, second_f
    )

    two_part, out_part, ffn_hidden, gate_back, up_back = feed_forward(
        normed_two, cot_all, ffn_w
    )
    resid_grad, mixer_back, second_grad, ffn_grads, gate_grad = ffn_join(
        planes,
        two_part,
        resid_mid,
        second_f,
        cotangent,
        normed_two,
        cot_all,
        ffn_hidden,
        gate_back,
        up_back,
    )

    gated_grad = contract(mixer_back, mixer_w, 1, 1)
    mixer_grad = contract(gated, mixer_back, 0, 0, BF16)
    mixer_sum = lax.psum_scatter(mixer_grad, "z", scatter_dimension=0, tiled=True)
    ffn_grads, _ = lax.optimization_barrier((ffn_grads, mixer_grad))
    ffn_sums = lax.psum_scatter(ffn_grads, "z", scatter_dimension=0, tiled=False)
    mix_grad = gated_grad * gate_silu
    gate_inner_grad = gated_grad * mix * silu_slope(gate_inner)
    local_back = backward_first(step_cut, mix_grad, maps, rate)
    state_back = state_chain(planes, through, local_back, 5, False)
    map_sum, rate_sum, map_grads, decay_sum = backward_all(
        step_cut, drive, mix_grad, maps, rate, states, state_back, columns
    )
    step_raw_grad = (mixed_f * map_sum + rate_sum) * -jnp.expm1(-step)
    step_back = step_raw_grad.astype(BF16)
    select_part = contract(step_back, step_w, 1, 1) + map_grads
    select_grad = plane_sum(select_part, 7, planes)
    lane = lax.broadcasted_iota(jnp.int32, (1, columns), 1)
    r_sel = lax.rsqrt(group_mean(proj * proj, lane) + EPSILON)
    scaled = select_grad * select_f
    proj_grad = r_sel * scaled - proj * r_sel * r_sel * r_sel * group_mean(scaled * proj, lane)
    select_gain_grad = jnp.sum(select_grad * proj * r_sel, axis=0) * (1.0 / PLANE)
    proj_back = proj_grad.astype(BF16)
    mixed_grad = step * map_sum + skip * mix_grad + contract(proj_back, select_w, 1, 0)
    pre_grad = mixed_grad * silu_slope(total)
    conv_grads, ext_grad = [], None
    for k in range(taps):
        tap = conv_input[shift + k : shift + k + rows].astype(F32)
        masked = jnp.where(same[k], pre_grad, 0.0)
        conv_grads.append(jnp.sum(masked * tap, axis=0))
        part = jnp.pad(masked * conv_w[k], ((shift + k, taps - 1 - k), (0, 0)))
        ext_grad = part if ext_grad is None else ext_grad + part
    inner_back = jnp.concatenate(
        [ext_grad, jnp.pad(gate_inner_grad, ((HALO, 0), (0, 0)))], axis=1
    ).astype(BF16)
    inner_grad = contract(inner_back, normed_one, 0, 0, BF16)
    one_part = contract(inner_back, inner_w, 1, 0, BF16)
    first_grad = jnp.sum(one_part.astype(F32) * x_f * r_one, axis=0)

    slab_grad = jnp.concatenate(
        [
            contract(proj_back, mixed_in, 0, 0),
            contract(step_low, step_back, 0, 0)[:RANK],
            decay_sum * rate,
            jnp.stack(
                conv_grads
                + [
                    jnp.sum(pre_grad, axis=0),
                    jnp.sum(step_raw_grad, axis=0),
                    jnp.sum(mix_grad * mixed_f, axis=0),
                ]
            ),
            jnp.zeros((16 - taps - 3, channels), F32),
        ]
    )
    widths = [first_gain.shape[0], second_gain.shape[0], select_gain.shape[0]]
    gain_grad = jnp.concatenate(
        [
            first_grad.reshape(devices, widths[0]),
            second_grad.reshape(devices, widths[1]),
            select_gain_grad.reshape(devices, widths[2]),
        ],
        axis=1,
    )
    gain_grad = jnp.pad(gain_grad, ((0, 0), (0, 128 - sum(widths))))

    (
        input_grad,
        inner_out,
        select_out,
        step_out,
        rest_out,
        gain_out,
        block_output,
        up_out,
        down_out,
        mixer_out,
    ) = closing(
        planes,
        one_part,
        block_input,
        first_f,
        resid_grad,
        inner_grad.reshape(planes, inner_block, width),
        slab_grad,
        gain_grad.reshape(planes, PLANE, 128),
        out_part,
        resid_mid,
        ffn_sums,
        mixer_sum,
    )
    def shape(*dims, kind=F32):
        return jax.ShapeDtypeStruct(dims, kind)

    mine = gain_out[0]
    (
        block_output,
        input_grad,
        inner_out,
        select_out,
        step_out,
        mixer_out,
        up_out,
        down_out,
        gate_grad,
        decay_out,
        conv_out,
    ) = hand_over(
        (
            block_output,
            input_grad,
            inner_out,
            select_out,
            step_out,
            mixer_out,
            up_out,
            down_out,
            gate_grad,
            rest_out,
        ),
        [(n, None) for n in range(9)] + [(9, 0), (9, STATE)],
        [
            jax.ShapeDtypeStruct(a.shape, a.dtype)
            for a in (
                block_output,
                input_grad,
                inner_out,
                select_out,
                step_out,
                mixer_out,
                up_out,
                down_out,
                gate_grad,
            )
        ]
        + [shape(STATE, own_block), shape(taps, own_block)],
    )
    return (
        block_output,
        input_grad,
        mine[: widths[0]],
        inner_out.T,
        conv_out,
        rest_out[STATE + taps],
        select_out,
        mine[widths[0] + widths[1] : sum(widths)],
        step_out,
        rest_out[STATE + taps + 1],
        decay_out,
        rest_out[STATE + taps + 2],
        mixer_out,
        mine[widths[0] : widths[0] + widths[1]],
        gate_grad if gate_grad.shape[0] == width else gate_grad.T,
        up_out if up_out.shape[0] == width else up_out.T,
        down_out,
    )


def solution(mesh):
    planes = mesh.devices.size // PLANE
    grid = Mesh(mesh.devices.reshape(planes, PLANE), ("z", "p"))
    seq = ("z", "p")
    by_row, by_column, flat = P(seq, None), P(None, seq), P(seq)

    def program(*args):
        return on_device(planes, *args)

    return jax.shard_map(
        program,
        mesh=grid,
        in_specs=(
            by_row,
            P(),
            flat,
            by_column,
            by_column,
            flat,
            by_row,
            flat,
            by_column,
            flat,
            by_column,
            flat,
            by_row,
            flat,
            by_column,
            by_column,
            by_row,
            by_row,
        ),
        out_specs=(
            by_row,
            by_row,
            flat,
            by_column,
            by_column,
            flat,
            by_row,
            flat,
            by_column,
            flat,
            by_column,
            flat,
            by_row,
            flat,
            by_column,
            by_column,
            by_row,
        ),
        check_vma=False,
    )
```

```python
import jax
import jax.numpy as jnp
import numpy as np
from jax import lax
from jax.experimental import pallas as pl
from jax.experimental.pallas import tpu as pltpu
from jax.sharding import Mesh
from jax.sharding import PartitionSpec as P

STATE = 16
RANK = 96
CONV = 4
PLANE = 8
HALO = 16
GROUP = 8
CUT = 1e4
EPSILON = 1e-06
ALL_VMEM = 60 << 20
F32 = jnp.float32
BF16 = jnp.bfloat16
MESH_ID = pl.DeviceIdType.MESH
ANY = pl.BlockSpec(memory_space=pl.ANY)
VMEM = pl.BlockSpec(memory_space=pltpu.VMEM)


def xor(p, k):
    out = p
    for bit in (1, 2, 4):
        if k & bit:
            out = out + bit - 2 * bit * lax.rem(lax.div(out, bit), 2)
    return out


def remote(src, dst, send_sem, recv_sem, z, p):
    return pltpu.make_async_remote_copy(
        src_ref=src,
        dst_ref=dst,
        send_sem=send_sem,
        recv_sem=recv_sem,
        device_id={"z": z, "p": p},
        device_id_type=MESH_ID,
    )


def greet(z, p):
    pl.semaphore_signal(
        pltpu.get_barrier_semaphore(), inc=1, device_id={"z": z, "p": p}, device_id_type=MESH_ID
    )


def comm_params(number, vmem=None):
    return pltpu.CompilerParams(
        collective_id=number, has_side_effects=True, vmem_limit_bytes=vmem
    )


def dma(*shape):
    return pltpu.SemaphoreType.DMA(shape)


def block_route(z, p):
    half = lax.div(PLANE * z + p, 2)
    return lax.rem(half, PLANE), 2 * lax.div(half, PLANE) + lax.rem(p, 2)


def block_source_of(z, p):
    k = 2 * (PLANE * lax.div(z, 2) + p) + lax.rem(z, 2)
    return lax.div(k, PLANE), lax.rem(k, PLANE)


def moves_in(z, p):
    zs, ps = block_source_of(z, p)
    return jnp.logical_or(zs != z, ps != p)


def plane_greet(z, p):
    for k in (1, 2, 4):
        greet(z, xor(p, k))
    return 3


def plane_reduce(
    z, p, part, sbuf, obuf, dbuf, rbuf, s1, r1, s2, r2, finish, rows, during=None, base=0
):
    sib, near, side = xor(p, 1), xor(p, 2), xor(p, 4)
    tok = sbuf.shape[1]
    half = tok // 2
    top, low = pl.ds(0, half), pl.ds(half, half)
    wide = (part.dtype == F32) and (obuf.dtype == F32)
    align = min(rows, 16)

    def block(q):
        return part.at[pl.ds(pl.multiple_of(base + q * tok, align), tok)]

    def piece(q, at):
        return part[pl.ds(pl.multiple_of(base + q * tok + at.start, align), rows), :].astype(F32)

    def chunks(length, body):
        def step(n, _):
            body(pl.ds(pl.multiple_of(n * rows, rows), rows))
            return 0

        lax.fori_loop(0, length // rows, step, 0)

    def put(value):
        return value if wide else value.astype(obuf.dtype)

    first = []
    for i, k in enumerate((6, 2, 4, 0)):
        c = remote(block(xor(sib, k)), sbuf.at[i], s1.at[i], r1.at[i], z, sib)
        c.start()
        first.append(c)
    second = []

    def send(i, src, dst, to):
        c = remote(src, dst, s2.at[i], r2.at[i], z, to)
        c.start()
        second.append(c)
        return c

    for i, k in enumerate((6, 2, 4)):
        first[i].wait_recv()
        q = xor(p, k)

        def add(at, i=i, q=q):
            obuf[i, at] = put(piece(q, at) + sbuf[i, at].astype(F32))

        chunks(tok, add)
        if k == 6:
            far_top = send(0, obuf.at[0, top], dbuf.at[0], near)
            far_low = send(1, obuf.at[0, low], dbuf.at[1], side)
        elif k == 2:
            send(2, obuf.at[1, top], rbuf.at[0, top], near)
        else:
            send(3, obuf.at[2, low], rbuf.at[1, low], side)
    if during is not None:
        during(0)
    far_top.wait_recv()

    def join_top(at):
        obuf[2, at] = put(obuf[2, at].astype(F32) + dbuf[0, at].astype(F32))

    chunks(half, join_top)
    send(4, obuf.at[2, top], rbuf.at[1, top], side)
    far_low.wait_recv()

    def join_low(at):
        down = pl.ds(pl.multiple_of(at.start + half, rows), rows)
        obuf[1, down] = put(obuf[1, down].astype(F32) + dbuf[1, at].astype(F32))

    chunks(half, join_low)
    send(5, obuf.at[1, low], rbuf.at[0, low], near)
    if during is not None:
        during(1)
    first[3].wait_recv()
    for c in second[2:]:
        c.wait_recv()

    def last(at):
        total = piece(p, at) + sbuf[3, at].astype(F32)
        finish(at, total + rbuf[0, at].astype(F32) + rbuf[1, at].astype(F32))

    chunks(tok, last)
    for c in first + second:
        c.wait_send()


class PlaneGather:
    def __init__(self, z, p, own, place, ss, rs, fs, fr, ls):
        self.z, self.p, self.own, self.place = z, p, own, place
        self.ss, self.rs, self.fs, self.fr, self.ls = ss, rs, fs, fr, ls
        self.sent, self.passed = [], []
        half = own.shape[0] // 2
        self.top, self.low = pl.ds(0, half), pl.ds(half, half)

    def send(self, src, dst, to):
        i = len(self.sent)
        c = remote(src, dst, self.ss.at[i], self.rs.at[i], self.z, to)
        c.start()
        self.sent.append(c)

    def pass_on(self, q):
        i = len(self.passed)
        place = self.place(q)
        c = remote(place, place, self.fs.at[i], self.fr.at[i], self.z, xor(self.p, 1))
        c.start()
        self.passed.append(c)

    def start(self):
        p, own = self.p, self.own
        near, side = xor(p, 2), xor(p, 4)
        self.send(own.at[self.top], self.place(p).at[self.top], near)
        self.send(own.at[self.low], self.place(p).at[self.low], side)
        self.send(own.at[self.low], self.place(p).at[self.low], near)
        self.send(own.at[self.top], self.place(p).at[self.top], side)
        self.send(own, self.place(p), xor(p, 1))
        self.local = pltpu.make_async_copy(own, self.place(p), self.ls)
        self.local.start()

    def relay(self):
        near, side = xor(self.p, 2), xor(self.p, 4)
        self.sent[0].wait_recv()
        self.send(self.place(near).at[self.top], self.place(near).at[self.top], side)
        self.sent[1].wait_recv()
        self.send(self.place(side).at[self.low], self.place(side).at[self.low], near)

    def finish(self):
        near, side, far = xor(self.p, 2), xor(self.p, 4), xor(self.p, 6)
        self.sent[2].wait_recv()
        self.pass_on(near)
        self.sent[3].wait_recv()
        self.pass_on(side)
        self.sent[5].wait_recv()
        self.sent[6].wait_recv()
        self.pass_on(far)
        self.sent[4].wait_recv()
        for c in self.passed:
            c.wait_recv()
        for c in self.sent + self.passed:
            c.wait_send()
        self.local.wait()


def plane_gather(z, p, own, place, ss, rs, fs, fr, ls, during=None):
    gather = PlaneGather(z, p, own, place, ss, rs, fs, fr, ls)
    gather.start()
    if during is not None:
        during(2)
    gather.relay()
    gather.finish()


def rows_at(ref, tok, base=0):
    return lambda q: ref.at[pl.ds(pl.multiple_of(base + q * tok, 16), tok)]


GATHER_SEMS = (7, 7, 3, 3)
REDUCE_SEMS = (4, 4, 6, 6)


def ring_gather(planes, z, p, own, out, ss, rs, ls):
    local = pltpu.make_async_copy(own, out.at[z], ls)
    local.start()
    sent = []

    def send(i, src, dst, r):
        c = remote(src, dst, ss.at[i], rs.at[i], lax.rem(z + r, planes), p)
        c.start()
        sent.append(c)
        return c

    if planes != 4:
        for r in range(1, planes):
            send(r, own, out.at[z], r)
        return local, sent, lambda: None
    half = own.shape[0] // 2
    top, low = pl.ds(0, half), pl.ds(half, half)
    up = send(0, own.at[top], out.at[z, top], 1)
    down = send(1, own.at[low], out.at[z, low], 3)
    send(2, own.at[low], out.at[z, low], 1)
    send(3, own.at[top], out.at[z, top], 3)

    def relay():
        before, after = lax.rem(z + 3, 4), lax.rem(z + 1, 4)
        up.wait_recv()
        send(4, out.at[before, top], out.at[before, top], 1)
        down.wait_recv()
        send(5, out.at[after, low], out.at[after, low], 3)

    return local, sent, relay


def ring_finish(local, sent, relayed):
    for i, c in enumerate(sent):
        if not (relayed and i < 2):
            c.wait_recv()
        c.wait_send()
    local.wait()


def ring_reduce(planes, z, p, src, ibuf, fbuf, mbuf, ss, rs):
    half = src.shape[1] // 2
    top, low = pl.ds(0, half), pl.ds(half, half)
    before, after = lax.rem(z + planes - 1, planes), lax.rem(z + 1, planes)
    sent = []

    def send(i, part, dst, r):
        c = remote(part, dst, ss.at[i], rs.at[i], lax.rem(z + r, planes), p)
        c.start()
        sent.append(c)

    if planes == 4:
        far = lax.rem(z + 2, 4)
        send(0, src.at[far, top], fbuf.at[0], 1)
        send(1, src.at[far, low], fbuf.at[1], 3)
        send(2, src.at[after, low], ibuf.at[0, low], 1)
        send(3, src.at[before, top], ibuf.at[1, top], 3)
    else:
        for r in range(1, planes):
            send(r, src.at[lax.rem(z + r, planes)], ibuf.at[r], r)

    def relay():
        if planes == 4:
            sent[0].wait_recv()
            mbuf[0] = (src[after, top].astype(F32) + fbuf[0].astype(F32)).astype(mbuf.dtype)
            send(4, mbuf.at[0], ibuf.at[0, top], 1)
            sent[1].wait_recv()
            mbuf[1] = (src[before, low].astype(F32) + fbuf[1].astype(F32)).astype(mbuf.dtype)
            send(5, mbuf.at[1], ibuf.at[1, low], 3)

    def finish():
        for i, c in enumerate(sent):
            if not (planes == 4 and i < 2):
                c.wait_recv()
            c.wait_send()
        total = src[z].astype(F32)
        for k in range(2) if planes == 4 else range(1, planes):
            total = total + ibuf[k].astype(F32)
        return total

    return relay, finish


def ring_reduce_scratch(planes, block, width, kind=BF16):
    return [
        pltpu.VMEM((2 if planes == 4 else planes, block, width), kind),
        pltpu.VMEM((2, block // 2, width), kind),
        pltpu.VMEM((2, block // 2, width), kind),
        dma(ring_sems(planes)),
        dma(ring_sems(planes)),
    ]


def ring_greet(planes, z, p):
    for r in range(1, planes):
        greet(lax.rem(z + r, planes), p)
    return planes - 1


def ring_sems(planes):
    return max(6, planes)


TRIO = 8


def join_gain(planes, gains_ref, row, per, spread):
    total = spread.shape[1]
    at = lax.broadcasted_iota(jnp.int32, (PLANE, total), 1)
    column = lax.broadcasted_iota(jnp.int32, (PLANE, total), 0)
    joined = jnp.zeros((PLANE, total), F32)
    for k in range(planes):
        piece = jnp.concatenate([gains_ref[q, k, row : row + 1, :] for q in range(PLANE)], axis=0)
        wide = jnp.dot(piece.astype(BF16), spread, preferred_element_type=F32)
        low = (column + PLANE * k) * per
        joined = joined + jnp.where((at >= low) & (at < low + per), wide, 0.0)
    return jnp.sum(joined, axis=0, keepdims=True)


def opening(planes, x, cot, inner, mixer, select, small, gains, ffn):
    tok, width = x.shape
    relayed = planes == 4
    block = mixer.shape[0]
    columns = select.shape[1]
    channels = planes * block
    places, filled = [], 0
    for array in small:
        places.append((filled, filled + array.shape[0]))
        filled += array.shape[0]
    rank = small[0].shape[0]
    states = small[1].shape[0]
    height = rank + 32 + columns
    pers = [g.shape[1] for g in gains]
    spreads = []
    for per, total in ((pers[0], width), (pers[2], columns)):
        spreads.append(
            jnp.asarray(np.arange(128)[:, None] == np.arange(total)[None, :] % per, BF16)
        )
    turn = ffn[0].shape[1] % 128 == 0
    units = ffn[2].shape[0]
    if not turn:
        ffn = [ffn[0].T, ffn[1].T, ffn[2]]

    def kernel(*refs):
        wide_refs, select_ref = refs[:4], refs[4]
        small_refs, gain_refs, refs = refs[5:11], refs[11:14], refs[14:]
        spread_refs, ffn_refs, refs = refs[:2], refs[2:5], refs[5:]
        xg_ref, cots_ref, inners_ref, home_ref = refs[:4]
        select_out, step_ref, rest_ref, first_ref, second_ref, sel_ref, own_ref = refs[4:11]
        refs = refs[11:]
        own_wide, own_small, got_small, smalls, own_gain, gains_all = refs[:6]
        refs = refs[6:]
        near_small, near_gain, near_spread, near_ffn = refs[:6], refs[6:9], refs[9:11], refs[11:13]
        near_select, ffn_out, refs = refs[13], refs[14], refs[15:]
        near_wide, near_down, wide_sems, refs = refs[:4], refs[4], refs[5], refs[6:]
        x_ref, cot_ref, inner_ref, mixer_ref = near_wide
        x_sems, c_sems, refs = refs[:5], refs[5:10], refs[10:]
        hs, hr, gs, gr, gs2, gr2, ins, inr, inl, ps, pr, bs, br, bl, near_sems, out_sems = refs

        z, p = lax.axis_index("z"), lax.axis_index("p")
        column, slot = block_route(z, p)
        from_z, from_p = block_source_of(z, p)
        moves = jnp.logical_or(column != p, slot != z)
        stays = jnp.logical_not(moves)
        after = lax.rem(z + 1, planes)
        for k in range(1, PLANE):
            greet(z, xor(p, k))
        for r in range(1, planes):
            greet(lax.rem(z + r, planes), p)

        @pl.when(moves_in(z, p))
        def _():
            greet(from_z, from_p)

        landing = []
        for i in (2, 0, 1, 3):
            c = pltpu.make_async_copy(wide_refs[i], near_wide[i], wide_sems.at[i])
            c.start()
            landing.append(c)
        down_in = pltpu.make_async_copy(ffn_refs[2], near_down, wide_sems.at[4])
        down_in.start()
        fetched = []
        far_refs = list(small_refs) + list(gain_refs) + [select_ref]
        far_refs += list(spread_refs) + list(ffn_refs[:2])
        near_refs = list(near_small) + list(near_gain) + [near_select]
        near_refs += list(near_spread) + list(near_ffn)
        for i, (src, dst) in enumerate(zip(far_refs, near_refs)):
            c = pltpu.make_async_copy(src, dst, near_sems.at[i])
            c.start()
            fetched.append(c)
        own_wide[...] = jnp.zeros_like(own_wide)
        own_gain[...] = jnp.zeros_like(own_gain)
        pl.semaphore_wait(
            pltpu.get_barrier_semaphore(),
            PLANE - 1 + planes - 1 + moves.astype(jnp.int32),
        )

        for c in landing:
            c.wait()
        local, sent, relay = ring_gather(planes, z, p, inner_ref, inners_ref, ins, inr, inl)

        homes = [
            (own_small, got_small, ps.at[0], pr.at[0]),
            (mixer_ref, home_ref, ps.at[1], pr.at[1]),
        ]

        def homing(items):
            for src, dst, send, recv in items:

                @pl.when(moves)
                def _():
                    remote(src, dst, send, recv, slot, column).start()

                @pl.when(stays)
                def _():
                    pltpu.make_async_copy(src, dst, recv).start()

        def place(q):
            return xg_ref.at[pl.ds(pl.multiple_of(HALO + q * tok, HALO), tok)]

        gain_out, gain_on, block_ring, ffn_sent = [], [], [], []

        def first_sends(_):
            for c in fetched[:10]:
                c.wait()
            for (low, high), ref in zip(places, near_small):
                own_wide[low:high, :] = ref[...].astype(F32)
            own_small[: rank + 32] = own_wide[...].astype(BF16)
            own_small[rank + 32 :] = near_select[...].astype(F32).T.astype(BF16)
            for i, ref in enumerate(near_gain):
                own_gain[i : i + 1, : pers[i]] = ref[...].astype(F32)
            homing(homes[:1])
            for r in range(1, planes):
                c = remote(
                    own_gain, gains_all.at[p, z], gs.at[r], gr.at[r], lax.rem(z + r, planes), p
                )
                c.start()
                gain_out.append(c)
            gains_all[p, z] = own_gain[...]

        x_gather = PlaneGather(z, p, x_ref, place, *x_sems)
        cot_gather = PlaneGather(z, p, cot_ref, rows_at(cots_ref, tok), *c_sems)
        x_gather.start()
        first_sends(0)
        x_gather.relay()
        relay()
        cot_gather.start()
        homing(homes[1:])

        src, dst, _, recv = homes[0]
        pltpu.make_async_copy(src, dst, recv).wait()
        block_ring.extend(ring_gather(planes, z, p, got_small, smalls, bs, br, bl))
        for c in gain_out:
            c.wait_recv()
        for k in range(1, PLANE):
            c = remote(gains_all.at[p], gains_all.at[p], gs2.at[k], gr2.at[k], z, xor(p, k))
            c.start()
            gain_on.append(c)
        x_gather.finish()

        edge = xg_ref.at[pl.ds(PLANE * tok, HALO)]
        front = xg_ref.at[pl.ds(0, HALO)]

        @pl.when(z < planes - 1)
        def _():
            remote(edge, front, hs, hr, after, p).start()

        @pl.when(z == 0)
        def _():
            pltpu.make_async_copy(edge, front, hr).start()

        cot_gather.relay()
        block_ring[2]()
        down_in.wait()
        down_out = pltpu.make_async_copy(
            near_down, own_ref.at[pl.ds(2 * units, units)], out_sems.at[2]
        )
        down_out.start()
        for c in fetched[10:]:
            c.wait()
        for i in range(2):
            if turn:
                ffn_out[i] = near_ffn[i][...].T
            else:
                ffn_out[i] = near_ffn[i][...]
            c = pltpu.make_async_copy(
                ffn_out.at[i], own_ref.at[pl.ds(i * units, units)], out_sems.at[i]
            )
            c.start()
            ffn_sent.append(c)
        for c in gain_on:
            c.wait_recv()
        first_ref[...] = join_gain(planes, gains_all, 0, pers[0], near_spread[0][...])
        second_ref[...] = join_gain(planes, gains_all, 1, pers[1], near_spread[0][...])
        sel_ref[...] = join_gain(planes, gains_all, 2, pers[2], near_spread[1][...])
        cot_gather.finish()
        down_out.wait()
        for c in ffn_sent:
            c.wait()
        pltpu.make_async_copy(edge, front, hr).wait()

        @pl.when(z < planes - 1)
        def _():
            remote(edge, front, hs, hr, after, p).wait_send()

        ring_finish(block_ring[0], block_ring[1], relayed)
        joined = jnp.concatenate([smalls[k].astype(F32) for k in range(planes)], axis=1)
        row = lax.broadcasted_iota(jnp.int32, (rank + 32, channels), 0)
        step_ref[...] = jnp.where(row < rank, joined[: rank + 32], 0.0).astype(BF16)
        rest_ref[...] = joined[rank : rank + 32]
        select_out[...] = joined[rank + 32 :].astype(BF16)
        pltpu.make_async_copy(mixer_ref, home_ref, pr.at[1]).wait()

        @pl.when(moves)
        def _():
            for src, dst, send, recv in homes:
                remote(src, dst, send, recv, slot, column).wait_send()

        for c in gain_out + gain_on:
            c.wait_send()
        ring_finish(local, sent, relayed)

    def shape(*dims, kind=BF16):
        return jax.ShapeDtypeStruct(dims, kind)

    one = pltpu.SemaphoreType.DMA
    return pl.pallas_call(
        kernel,
        out_shape=(
            shape(HALO + PLANE * tok, width),
            shape(PLANE * tok, width),
            shape(planes, *inner.shape),
            shape(*mixer.shape),
            shape(columns, channels),
            shape(rank + 32, channels),
            shape(32, channels, kind=F32),
            shape(1, width, kind=F32),
            shape(1, width, kind=F32),
            shape(1, columns, kind=F32),
            shape(3 * units, width),
        ),
        in_specs=[ANY] * 19,
        out_specs=(ANY,) * 4 + (VMEM,) * 6 + (ANY,),
        scratch_shapes=[
            pltpu.VMEM((rank + 32, block), F32),
            pltpu.VMEM((height, block), BF16),
            pltpu.VMEM((height, block), BF16),
            pltpu.VMEM((planes, height, block), BF16),
            pltpu.VMEM((TRIO, 128), F32),
            pltpu.VMEM((PLANE, planes, TRIO, 128), F32),
            *[pltpu.VMEM(a.shape, a.dtype) for a in (*small, *gains, *spreads, *ffn[:2])],
            pltpu.VMEM(select.shape, BF16),
            pltpu.VMEM((2, units, width), BF16),
            *[pltpu.VMEM(a.shape, a.dtype) for a in (x, cot, inner, mixer, ffn[2])],
            dma(5),
            *[dma(n) for n in GATHER_SEMS],
            one,
            *[dma(n) for n in GATHER_SEMS],
            one,
            one,
            one,
            dma(planes),
            dma(planes),
            dma(PLANE),
            dma(PLANE),
            dma(ring_sems(planes)),
            dma(ring_sems(planes)),
            one,
            dma(2),
            dma(2),
            dma(ring_sems(planes)),
            dma(ring_sems(planes)),
            one,
            dma(14),
            dma(3),
        ],
        compiler_params=comm_params(0, ALL_VMEM),
        name="opening",
    )(x, cot, inner, mixer, select, *small, *gains, *spreads, *ffn)


def plane_sum(part, number):
    tok, columns = part.shape[0] // PLANE, part.shape[1]

    def kernel(part_ref, out_ref, own, *refs):
        bufs, g = refs[:8], refs[8:]
        z, p = lax.axis_index("z"), lax.axis_index("p")
        pl.semaphore_wait(pltpu.get_barrier_semaphore(), plane_greet(z, p))

        def finish(at, value):
            own[at] = value

        plane_reduce(z, p, part_ref, *bufs, finish, tok // 2)
        plane_gather(z, p, own, rows_at(out_ref, tok), *g)

    return pl.pallas_call(
        kernel,
        out_shape=jax.ShapeDtypeStruct(part.shape, F32),
        in_specs=[VMEM],
        out_specs=VMEM,
        scratch_shapes=[
            pltpu.VMEM((tok, columns), F32),
            *reduce_scratch(tok, columns, F32),
            *[dma(n) for n in GATHER_SEMS],
            pltpu.SemaphoreType.DMA,
        ],
        compiler_params=comm_params(number, 32 << 20),
        name="plane_sum",
    )(part)


def reduce_scratch(tok, width, kind=BF16):
    return [
        pltpu.VMEM((4, tok, width), kind),
        pltpu.VMEM((3, tok, width), kind),
        pltpu.VMEM((2, tok // 2, width), kind),
        pltpu.VMEM((2, tok, width), kind),
        *[dma(n) for n in REDUCE_SEMS],
    ]


def mixer_join(part, x, gain):
    tok, width = x.shape

    def kernel(
        part_ref,
        x_ref,
        gain_ref,
        resid_ref,
        out_ref,
        own,
        sbuf,
        obuf,
        dbuf,
        rbuf,
        s1,
        r1,
        s2,
        r2,
        *g,
    ):
        z, p = lax.axis_index("z"), lax.axis_index("p")
        pl.semaphore_wait(pltpu.get_barrier_semaphore(), plane_greet(z, p))

        def finish(at, total):
            v = total + x_ref[at].astype(F32)
            resid_ref[at] = v
            r = lax.rsqrt(jnp.mean(v * v, axis=-1, keepdims=True) + EPSILON)
            own[at] = (v * r * gain_ref[...]).astype(BF16)

        plane_reduce(z, p, part_ref, sbuf, obuf, dbuf, rbuf, s1, r1, s2, r2, finish, 16)
        plane_gather(z, p, own, rows_at(out_ref, tok), *g)

    return pl.pallas_call(
        kernel,
        out_shape=(
            jax.ShapeDtypeStruct((tok, width), F32),
            jax.ShapeDtypeStruct(part.shape, BF16),
        ),
        in_specs=[VMEM] * 3,
        out_specs=(VMEM, VMEM),
        scratch_shapes=[
            pltpu.VMEM((tok, width), BF16),
            *reduce_scratch(tok, width),
            *[dma(n) for n in GATHER_SEMS],
            pltpu.SemaphoreType.DMA,
        ],
        compiler_params=comm_params(2, 32 << 20),
        name="mixer_join",
    )(part, x, gain)


def feed_forward(normed, cot, weights):
    rows, width = normed.shape
    planes, triple, _ = weights.shape
    units = triple // 3
    hidden = planes * units
    block = 256

    def kernel(n_ref, c_ref, w_ref, two_ref, out_ref, h_ref, gb_ref, ub_ref, gw, uw, dw, sem):
        @pl.when(pl.program_id(0) == 0)
        def _():
            copies = []
            for i, dst in enumerate((gw, uw, dw)):
                for k in range(planes):
                    copies.append(
                        pltpu.make_async_copy(
                            w_ref.at[k, pl.ds(i * units, units)],
                            dst.at[pl.ds(k * units, units)],
                            sem.at[i, k],
                        )
                    )
            for c in copies:
                c.start()
            for c in copies:
                c.wait()

        n, c = n_ref[...], c_ref[...]
        gate = contract(n, gw[...], 1, 1)
        up = contract(n, uw[...], 1, 1)
        back = contract(c, dw[...], 1, 1)
        s = jax.nn.sigmoid(gate)
        silu = gate * s
        h = (silu * up).astype(BF16)
        gb = (back * up * (s * (1.0 + gate * (1.0 - s)))).astype(BF16)
        ub = (back * silu).astype(BF16)
        h_ref[...] = h
        gb_ref[...] = gb
        ub_ref[...] = ub
        two_ref[...] = (contract(gb, gw[...], 1, 0) + contract(ub, uw[...], 1, 0)).astype(BF16)
        out_ref[...] = contract(h, dw[...], 1, 0, BF16)

    wide = pl.BlockSpec((block, width), lambda i: (i, 0))
    thin = pl.BlockSpec((block, hidden), lambda i: (i, 0))
    return pl.pallas_call(
        kernel,
        grid=(rows // block,),
        out_shape=(jax.ShapeDtypeStruct((rows, width), BF16),) * 2
        + (jax.ShapeDtypeStruct((rows, hidden), BF16),) * 3,
        in_specs=[wide, wide, ANY],
        out_specs=(wide, wide, thin, thin, thin),
        scratch_shapes=[pltpu.VMEM((hidden, width), BF16)] * 3
        + [pltpu.SemaphoreType.DMA((3, planes))],
        compiler_params=pltpu.CompilerParams(vmem_limit_bytes=ALL_VMEM),
        name="feed_forward",
    )(normed, cot, weights)


def ffn_join(planes, part, resid, gain, cot, normed, cot_all, h, gb, ub):
    tok, width = resid.shape
    hidden = h.shape[1]
    units = hidden // planes
    step_units = 128
    turn = units % 128 == 0

    def kernel(
        part_ref,
        v_ref,
        gain_ref,
        cot_ref,
        n_ref,
        c_ref,
        h_ref,
        gb_ref,
        ub_ref,
        grad_ref,
        out_ref,
        gg_ref,
        w_ref,
        gate_ref,
        near_p,
        near_v,
        near_gain,
        near_cot,
        near_n,
        near_c,
        near_h,
        near_g,
        near_u,
        near_sems,
        own,
        sbuf,
        obuf,
        dbuf,
        rbuf,
        s1,
        r1,
        s2,
        r2,
        *g,
    ):
        g, (gw, uw, dw, wsem), ring = g[:5], g[5:9], g[9:]
        z, p = lax.axis_index("z"), lax.axis_index("p")
        pl.semaphore_wait(
            pltpu.get_barrier_semaphore(), plane_greet(z, p) + ring_greet(planes, z, p)
        )
        gg_ref[...] = jnp.zeros_like(gg_ref)
        copies, rings, fetched = [], [], []
        far = (part_ref, gb_ref, n_ref, ub_ref, h_ref, c_ref, v_ref, gain_ref, cot_ref)
        gb_ref, n_ref, ub_ref, h_ref, c_ref = near_g, near_n, near_u, near_h, near_c
        part_ref, v_ref, gain_ref, cot_ref = near_p, near_v, near_gain, near_cot
        near = (part_ref, gb_ref, n_ref, ub_ref, h_ref, c_ref, v_ref, gain_ref, cot_ref)
        for i, (src, dst) in enumerate(zip(far, near)):
            c = pltpu.make_async_copy(src, dst, near_sems.at[i])
            c.start()
            fetched.append(c)
        fetched[0].wait()
        group = step_units // units

        def weight_grad(dst, left, right):
            for n in range(hidden // step_units):
                at = pl.ds(n * step_units, step_units)
                value = contract(left[:, at], right[...], 0, 0, BF16)
                dst[pl.ds(n * group, group)] = value.reshape(group, units, width)

        def hand_out(i, dst):
            c = pltpu.make_async_copy(
                dst, w_ref.at[:, pl.ds(i * units, units)], wsem.at[i]
            )
            c.start()
            copies.append(c)

        def during(step):
            if step == 0:
                for c in fetched[1:]:
                    c.wait()
                weight_grad(gw, gb_ref, n_ref)
                rings.append(ring_reduce(planes, z, p, gw, *ring))
            if step == 1:
                weight_grad(uw, ub_ref, n_ref)
                hand_out(0, uw)
            if step == 2:
                rings[0][0]()
                weight_grad(dw, h_ref, c_ref)
                hand_out(1, dw)

        def finish(at, u):
            v = v_ref[at]
            r = lax.rsqrt(jnp.mean(v * v, axis=-1, keepdims=True) + EPSILON)
            ug = u * gain_ref[...]
            mid = r * ug - v * (r * r * r) * jnp.mean(ug * v, axis=-1, keepdims=True)
            gg_ref[...] += jnp.sum(u * v * r, axis=0, keepdims=True)
            total = cot_ref[at].astype(F32) + mid
            grad_ref[at] = total
            own[at] = total.astype(BF16)

        plane_reduce(
            z, p, part_ref, sbuf, obuf, dbuf, rbuf, s1, r1, s2, r2, finish, 16, during
        )
        plane_gather(z, p, own, rows_at(out_ref, tok), *g, during)
        for c in copies:
            c.wait()
        total = rings[0][1]()
        gate_ref[...] = total.T if turn else total

    return pl.pallas_call(
        kernel,
        out_shape=(
            jax.ShapeDtypeStruct((tok, width), F32),
            jax.ShapeDtypeStruct(part.shape, BF16),
            jax.ShapeDtypeStruct((1, width), F32),
            jax.ShapeDtypeStruct((planes, 2 * units, width), BF16),
            jax.ShapeDtypeStruct((width, units) if turn else (units, width), F32),
        ),
        in_specs=[ANY] * 9,
        out_specs=(VMEM, ANY, VMEM, ANY, VMEM),
        scratch_shapes=[
            *[
                pltpu.VMEM(a.shape, a.dtype)
                for a in (part, resid, gain, cot, normed, cot_all, h, gb, ub)
            ],
            dma(9),
            pltpu.VMEM((tok, width), BF16),
            *reduce_scratch(tok, width),
            *[dma(n) for n in GATHER_SEMS],
            pltpu.SemaphoreType.DMA,
            *[pltpu.VMEM((planes, units, width), BF16)] * 3,
            dma(2),
            *ring_reduce_scratch(planes, units, width),
        ],
        compiler_params=comm_params(3, 56 << 20),
        name="ffn_join",
    )(part, resid, gain, cot, normed, cot_all, h, gb, ub)


def state_chain(planes, through, local, number, forward):
    def kernel(t_ref, l_ref, out_ref, got, own, s0, r0):
        z, p = lax.axis_index("z"), lax.axis_index("p")
        for r in range(1, planes):
            greet(lax.rem(z + r, planes), p)
        pl.semaphore_wait(pltpu.get_barrier_semaphore(), planes - 1)
        own[0] = t_ref[...].astype(BF16)
        own[1] = l_ref[...].astype(BF16)
        sent = []
        for r in range(1, planes):
            to = lax.rem(z + r, planes)
            c = remote(own, got.at[z], s0.at[r], r0.at[r], to, p)
            c.start()
            sent.append(c)
        for c in sent:
            c.wait()
        got[z] = own[...]
        state = jnp.zeros_like(l_ref)
        for k in range(planes) if forward else reversed(range(planes)):
            new = got[k, 0].astype(F32) * state + got[k, 1].astype(F32)
            state = jnp.where((k < z) if forward else (k > z), new, state)
        out_ref[...] = state

    return pl.pallas_call(
        kernel,
        out_shape=jax.ShapeDtypeStruct(local.shape, F32),
        in_specs=[VMEM] * 2,
        out_specs=VMEM,
        scratch_shapes=[
            pltpu.VMEM((planes, 2) + local.shape, BF16),
            pltpu.VMEM((2,) + local.shape, BF16),
            dma(planes),
            dma(planes),
        ],
        compiler_params=comm_params(number),
        name="state_chain",
    )(through, local)


def gain_spreads(pers, totals):
    spreads, start = [], 0
    for per, total in zip(pers, totals):
        lane = np.arange(128)[:, None]
        spreads.append(jnp.asarray(lane == start + np.arange(total)[None, :] % per, BF16))
        start += per
    return spreads


def closing(
    planes, part, x, gain, resid_grad, inner_g, slab_g, gains_g, out_part, resid, ffn_g, mixer_g
):
    tok, width = x.shape
    block = inner_g.shape[1]
    height, channels = slab_g.shape
    own = channels // planes
    rank = height - 32 - (RANK + 2 * STATE)
    columns = RANK + 2 * STATE
    units = ffn_g.shape[0] // 2
    turn = units % 128 == 0
    devices = planes * PLANE
    pers = [g.shape[1] // devices for g in gains_g]
    spreads = gain_spreads(pers, [g.shape[1] for g in gains_g])
    operands = (
        part, x, gain, resid_grad, inner_g, slab_g, out_part, resid, ffn_g, mixer_g, *gains_g,
        *spreads,
    )

    def shape(*dims, kind=F32):
        return jax.ShapeDtypeStruct(dims, kind)

    outputs = (
        shape(tok, width),
        shape(*inner_g.shape[1:]),
        shape(own, columns),
        shape(rank, own),
        shape(tok, width, kind=BF16),
        shape(width, units) if turn else shape(units, width),
        shape(units, width),
        shape(*mixer_g.shape),
        *[shape(n, own) for n in (STATE, CONV, 1, 1, 1)],
        *[shape(1, per) for per in pers],
    )

    def kernel(*refs):
        far, refs = refs[: len(operands)], refs[len(operands) :]
        far_outs, refs = refs[: len(outputs)], refs[len(outputs) :]
        one_bufs, out_bufs, refs = refs[:8], refs[8:16], refs[16:]
        hbuf, hs, hr, refs = refs[0], refs[1], refs[2], refs[3:]
        inner_ring, slab_ring, refs = refs[:5], refs[5:10], refs[10:]
        pieces, homed, os_, or_, refs = *refs[:4], refs[4:]
        gg_ref, gbuf, gs, gr, gown, gbuf2, gs2, gr2, bown = refs[:9]
        near, refs = refs[9 : 9 + len(operands)], refs[9 + len(operands) :]
        near_sems, refs = refs[0], refs[1:]
        near_outs, out_sems = refs[: len(outputs)], refs[len(outputs)]
        out_ref, io_ref, sel_ref, step_ref, bo_ref, up_ref, down_ref, mo_ref = near_outs[:8]
        row_refs, gain_outs = near_outs[8:13], near_outs[13:]
        written = []

        def write(*which):
            for i in which:
                c = pltpu.make_async_copy(near_outs[i], far_outs[i], out_sems.at[i])
                c.start()
                written.append(c)

        fetched = []
        for i in (4, 0, 10, 11, 12, 13, 14, 15, 5, 6, 8, 9, 1, 2, 3, 7):
            c = pltpu.make_async_copy(far[i], near[i], near_sems.at[i])
            c.start()
            fetched.append(c)
        part_ref, x_ref, gain_ref, rg_ref, ig_ref, sg_ref, fp_ref, rm_ref = near[:8]
        ffn_ref, mix_ref = near[8:10]
        z, p = lax.axis_index("z"), lax.axis_index("p")
        column, slot = block_route(z, p)
        to_z, to_p = block_source_of(z, p)
        moves = moves_in(z, p)
        stays = jnp.logical_not(moves)
        gets = jnp.logical_or(column != p, slot != z)
        before = lax.rem(z + planes - 1, planes)
        for k in range(1, PLANE):
            greet(z, xor(p, k))
        for r in range(1, planes):
            greet(lax.rem(z + r, planes), p)

        @pl.when(gets)
        def _():
            greet(slot, column)

        @pl.when(jnp.logical_and(p == PLANE - 1, z < planes - 1))
        def _():
            for q in range(PLANE):
                greet(z + 1, q)

        pl.semaphore_wait(
            pltpu.get_barrier_semaphore(),
            PLANE - 1 + planes - 1 + moves.astype(jnp.int32) + (z > 0).astype(jnp.int32),
        )

        fetched[0].wait()
        relay, inner_total = ring_reduce(planes, z, p, ig_ref, *inner_ring)
        for c in fetched[1:9]:
            c.wait()
        z_sent, p_sent, slab = [], [], []
        halo = remote(part_ref.at[pl.ds(0, HALO)], hbuf.at[p], hs, hr.at[p], before, PLANE - 1)

        @pl.when(z > 0)
        def _():
            halo.start()

        def homing(i, src, dst):
            @pl.when(moves)
            def _():
                remote(src, dst, os_.at[i], or_.at[i], to_z, to_p).start()

            @pl.when(stays)
            def _():
                pltpu.make_async_copy(src, dst, or_.at[i]).start()

        def homing_end(i, src, dst):
            pltpu.make_async_copy(src, dst, or_.at[i]).wait()

            @pl.when(moves)
            def _():
                remote(src, dst, os_.at[i], or_.at[i], to_z, to_p).wait_send()


        def during(step):
            if step == 0:
                for k in range(planes):
                    pieces[k] = sg_ref[:, own * k : own * (k + 1)].astype(BF16)
                slab.extend(ring_reduce(planes, z, p, pieces, *slab_ring))
                packed = jnp.zeros((devices, 128), F32)
                for i, per in enumerate(pers):
                    value = near[10 + i][...]
                    at = lax.broadcasted_iota(jnp.int32, (devices, value.shape[1]), 1)
                    low = lax.broadcasted_iota(jnp.int32, at.shape, 0) * per
                    value = jnp.where((at >= low) & (at < low + per), value, 0.0)
                    high = value.astype(BF16)
                    rest = (value - high.astype(F32)).astype(BF16)
                    spread = near[13 + i][...]
                    packed = packed + contract(high, spread, 1, 1) + contract(rest, spread, 1, 1)
                gg_ref[...] = packed.reshape(planes, PLANE, 128)
                for r in range(1, planes):
                    to = lax.rem(z + r, planes)
                    c = remote(gg_ref.at[to], gbuf.at[z], gs.at[r], gr.at[r], to, p)
                    c.start()
                    z_sent.append(c)
                return
            relay()
            for c in z_sent:
                c.wait()
            total = gg_ref[z]
            for r in range(1, planes):
                total = total + gbuf[lax.rem(z + r, planes)]
            gown[...] = total
            for k in range(1, PLANE):
                c = remote(gown, gbuf2.at[k], gs2.at[k], gr2.at[k], z, xor(p, k))
                c.start()
                p_sent.append(c)

        def finish(at, u):
            out_ref[at] = u

        plane_reduce(z, p, part_ref, *one_bufs, finish, 16, during, HALO)

        for c in fetched[9:]:
            c.wait()

        def later(step):
            if step == 0:
                slab[0]()
                if turn:
                    up_ref[...] = ffn_ref[:units].astype(F32).T
                else:
                    up_ref[...] = ffn_ref[:units].astype(F32)
                down_ref[...] = ffn_ref[units:].astype(F32)
                mo_ref[...] = mix_ref[...].astype(F32)
                write(5, 6, 7)
                return
            bown[...] = slab[1]()
            homing(0, bown, homed)

        def output(at, u):
            bo_ref[at] = (rm_ref[at] + u).astype(BF16)

        plane_reduce(z, p, fp_ref, *out_bufs, output, 16, later)
        write(4)

        @pl.when(jnp.logical_and(p == PLANE - 1, z < planes - 1))
        def _():
            for q in range(PLANE):
                pltpu.make_async_copy(
                    part_ref.at[pl.ds(0, HALO)], hbuf.at[q], hr.at[q]
                ).wait()
            add = hbuf[0].astype(F32)
            for q in range(1, PLANE):
                add = add + hbuf[q].astype(F32)
            out_ref[pl.ds(tok - HALO, HALO)] += add

        @pl.when(z > 0)
        def _():
            halo.wait_send()

        def norm(n, _):
            at = pl.ds(pl.multiple_of(n * 16, 16), 16)
            u = out_ref[at]
            v = x_ref[at].astype(F32)
            r = lax.rsqrt(jnp.mean(v * v, axis=-1, keepdims=True) + EPSILON)
            ug = u * gain_ref[...]
            grad = r * ug - v * (r * r * r) * jnp.mean(ug * v, axis=-1, keepdims=True)
            out_ref[at] = rg_ref[at] + grad
            return 0

        lax.fori_loop(0, tok // 16, norm, 0)
        write(0)

        for c in p_sent:
            c.wait()
        total = gown[...]
        for k in range(1, PLANE):
            total = total + gbuf2[k]
        row = lax.broadcasted_iota(jnp.int32, total.shape, 0)
        mine = jnp.sum(jnp.where(row == p, total, 0.0), axis=0, keepdims=True)
        start = 0
        for ref, per in zip(gain_outs, pers):
            ref[...] = mine[:, start : start + per]
            start += per
        homing_end(0, bown, homed)
        sel_ref[...] = homed[:columns, :].T
        step_ref[...] = homed[columns : columns + rank, :]
        start = columns + rank
        for ref in row_refs:
            ref[...] = homed[start : start + ref.shape[0], :]
            start += ref.shape[0]
        write(2, 3, *range(8, len(outputs)))
        io_ref[...] = inner_total()
        write(1)
        for c in written:
            c.wait()

    one = pltpu.SemaphoreType.DMA
    return pl.pallas_call(
        kernel,
        out_shape=outputs,
        in_specs=[ANY] * len(operands),
        out_specs=(ANY,) * len(outputs),
        scratch_shapes=[
            *reduce_scratch(tok, width),
            *reduce_scratch(tok, width),
            pltpu.VMEM((PLANE, HALO, width), BF16),
            one,
            dma(PLANE),
            *ring_reduce_scratch(planes, block, width),
            *ring_reduce_scratch(planes, height, own),
            pltpu.VMEM((planes, height, own), BF16),
            pltpu.VMEM((height, own), F32),
            dma(2),
            dma(2),
            pltpu.VMEM((planes, PLANE, 128), F32),
            pltpu.VMEM((planes, PLANE, 128), F32),
            dma(planes),
            dma(planes),
            pltpu.VMEM((PLANE, 128), F32),
            pltpu.VMEM((PLANE, PLANE, 128), F32),
            dma(PLANE),
            dma(PLANE),
            pltpu.VMEM((height, own), F32),
            *[pltpu.VMEM(a.shape, a.dtype) for a in operands],
            dma(len(operands)),
            *[pltpu.VMEM(a.shape, a.dtype) for a in outputs],
            dma(len(outputs)),
        ],
        compiler_params=comm_params(6, ALL_VMEM),
        name="closing",
    )(*operands)


def hand_over(arrays):
    count = len(arrays)

    def kernel(*refs):
        ins, outs, near = refs[:count], refs[count : 2 * count], refs[2 * count : 3 * count]
        in_sems, out_sems = refs[3 * count :]
        fetched, copies = [], []
        for i in range(count):
            c = pltpu.make_async_copy(ins[i], near[i], in_sems.at[i])
            c.start()
            fetched.append(c)
        for i in range(count):
            fetched[i].wait()
            c = pltpu.make_async_copy(near[i], outs[i], out_sems.at[i])
            c.start()
            copies.append(c)
        for c in copies:
            c.wait()

    return pl.pallas_call(
        kernel,
        out_shape=tuple(jax.ShapeDtypeStruct(a.shape, a.dtype) for a in arrays),
        in_specs=[ANY] * count,
        out_specs=(ANY,) * count,
        scratch_shapes=[
            *[pltpu.VMEM(a.shape, a.dtype) for a in arrays],
            dma(count),
            dma(count),
        ],
        compiler_params=SCAN_PARAMS,
        name="hand_over",
    )(*arrays)


CHUNK = 256


def scan_specs(channels, count, backward):
    def at(i):
        return count - 1 - i if backward else i

    return (
        pl.BlockSpec((CHUNK, channels), lambda i: (at(i), 0)),
        lambda part, size: pl.BlockSpec((CHUNK, size * STATE, 128), lambda i: (at(i), part, 0)),
        pl.BlockSpec((CHUNK, STATE, channels), lambda i: (at(i), 0, 0)),
        pl.BlockSpec((STATE, channels), lambda i: (0, 0)),
    )


def rows_of(g, size=GROUP):
    return pl.ds(pl.multiple_of(g * size, size), size)


def across(maps, channels):
    return jnp.concatenate([maps.astype(F32)] * (channels // 128), axis=1)


SCAN_PARAMS = pltpu.CompilerParams(vmem_limit_bytes=ALL_VMEM)


def prepare(proj, gain, step_w, step_b, mixed, keep):
    tokens, columns = proj.shape
    channels = mixed.shape[1]

    def kernel(
        proj_ref, gain_ref, w_ref, b_ref, mixed_ref, keep_ref, step_ref, slope_ref, cut_ref, drive_ref,
        low_ref, maps_ref,
    ):
        v = proj_ref[...]
        mean = group_mean(v * v, group_sums(columns))
        out = v * lax.rsqrt(mean + EPSILON) * gain_ref[...]
        low = out.astype(BF16)
        low_ref[...] = low
        raw = contract(low, w_ref[...], 1, 0) + b_ref[...]
        step = jnp.maximum(raw, 0.0) + jnp.log1p(jnp.exp(-jnp.abs(raw)))
        step_ref[...] = step
        slope_ref[...] = jax.nn.sigmoid(raw)
        drive_ref[...] = step * mixed_ref[...].astype(F32)
        cut_ref[...] = jnp.where(keep_ref[:, CONV - 2 : CONV - 1] > 0.0, step, CUT)

        wide = (2 * STATE, columns)
        pick = lax.broadcasted_iota(jnp.int32, wide, 1) == (
            lax.broadcasted_iota(jnp.int32, wide, 0) + columns - 2 * STATE
        )
        pick = jnp.where(pick, 1.0, 0.0).astype(BF16)
        first = lax.broadcasted_iota(jnp.int32, (2 * columns, 256), 0) < columns
        left = lax.broadcasted_iota(jnp.int32, (2 * columns, 256), 1) < 128
        ones = jnp.where(first == left, 1.0, 0.0).astype(BF16)
        many = 32

        def spread(g, _):
            at = rows_of(g, many)
            rows = low_ref[at, :]
            pairs = []
            for k in range(many // 2):
                pairs.append(
                    jnp.concatenate(
                        [
                            jnp.broadcast_to(rows[k : k + 1], wide) * pick,
                            jnp.broadcast_to(rows[k + many // 2 : k + many // 2 + 1], wide) * pick,
                        ],
                        axis=1,
                    )
                )
            result = jnp.dot(
                jnp.concatenate(pairs, axis=0), ones, preferred_element_type=F32
            ).astype(BF16)
            maps_ref[rows_of(2 * g, many // 2)] = result[:, :128].reshape(many // 2, 2 * STATE, 128)
            maps_ref[rows_of(2 * g + 1, many // 2)] = result[:, 128:].reshape(
                many // 2, 2 * STATE, 128
            )
            return 0

        lax.fori_loop(0, CHUNK // many, spread, 0)

    def tile(size):
        return pl.BlockSpec((CHUNK, size), lambda i: (i, 0))

    def whole(array):
        return pl.BlockSpec(array.shape, lambda i: (0, 0))

    shape = jax.ShapeDtypeStruct((tokens, channels), F32)
    return pl.pallas_call(
        kernel,
        grid=(tokens // CHUNK,),
        out_shape=(
            shape,
            shape,
            shape,
            shape,
            jax.ShapeDtypeStruct((tokens, columns), BF16),
            jax.ShapeDtypeStruct((tokens, 2 * STATE, 128), BF16),
        ),
        in_specs=[
            tile(columns),
            whole(gain),
            whole(step_w),
            whole(step_b),
            tile(channels),
            tile(CONV),
        ],
        out_specs=(
            tile(channels),
            tile(channels),
            tile(channels),
            tile(channels),
            tile(columns),
            pl.BlockSpec((CHUNK, 2 * STATE, 128), lambda i: (i, 0, 0)),
        ),
        compiler_params=SCAN_PARAMS,
        name="prepare",
    )(proj, gain, step_w, step_b, mixed, keep)


def forward_final(step, drive, maps, rate):
    tokens, channels = step.shape
    count = tokens // CHUNK
    rows, cols, _, const = scan_specs(channels, count, False)

    def kernel(step_ref, drive_ref, in_ref, rate_ref, state_ref, through_ref):
        @pl.when(pl.program_id(0) == 0)
        def _():
            state_ref[...] = jnp.zeros_like(state_ref)
            through_ref[...] = jnp.zeros_like(through_ref)

        rate_v = rate_ref[...]

        def body(g, carry):
            h, total = carry
            d8, w8 = step_ref[rows_of(g), :], drive_ref[rows_of(g), :]
            for k in range(GROUP):
                decay = jnp.exp(d8[k : k + 1, :] * rate_v)
                h = decay * h + w8[k : k + 1, :] * across(in_ref[g * GROUP + k], channels)
            return h, total + d8

        h, total = lax.fori_loop(
            0,
            CHUNK // GROUP,
            body,
            (state_ref[...], jnp.zeros((GROUP, channels), F32)),
        )
        state_ref[...] = h
        through_ref[...] += jnp.sum(total, axis=0, keepdims=True)

        @pl.when(pl.program_id(0) == count - 1)
        def _():
            through_ref[...] = jnp.exp(through_ref[...] * rate_v)

    shape = jax.ShapeDtypeStruct(rate.shape, F32)
    return pl.pallas_call(
        kernel,
        grid=(count,),
        out_shape=(shape, shape),
        in_specs=[rows, rows, cols(0, 1), const],
        out_specs=(const, const),
        compiler_params=SCAN_PARAMS,
        name="forward_final",
    )(step, drive, maps, rate)


def forward_all(step, drive, maps, rate, start):
    tokens, channels = step.shape
    count = tokens // CHUNK
    rows, cols, states, const = scan_specs(channels, count, False)

    def kernel(step_ref, drive_ref, maps_ref, rate_ref, start_ref, y_ref, hs_ref, h_sc):
        @pl.when(pl.program_id(0) == 0)
        def _():
            h_sc[...] = start_ref[...]

        rate_v = rate_ref[...]

        def body(g, h):
            d8, w8 = step_ref[rows_of(g), :], drive_ref[rows_of(g), :]
            out = []
            for k in range(GROUP):
                t = g * GROUP + k
                hs_ref[t] = h.astype(BF16)
                decay = jnp.exp(d8[k : k + 1, :] * rate_v)
                h = decay * h + w8[k : k + 1, :] * across(maps_ref[t, :STATE], channels)
                out.append(
                    jnp.sum(h * across(maps_ref[t, STATE:], channels), axis=0, keepdims=True)
                )
            y_ref[rows_of(g), :] = jnp.concatenate(out, axis=0)
            return h

        h_sc[...] = lax.fori_loop(0, CHUNK // GROUP, body, h_sc[...])

    return pl.pallas_call(
        kernel,
        grid=(count,),
        out_shape=(
            jax.ShapeDtypeStruct((tokens, channels), F32),
            jax.ShapeDtypeStruct((tokens, STATE, channels), BF16),
        ),
        in_specs=[rows, rows, cols(0, 2), const, const],
        out_specs=(rows, states),
        scratch_shapes=[pltpu.VMEM((STATE, channels), F32)],
        compiler_params=SCAN_PARAMS,
        name="forward_all",
    )(step, drive, maps, rate, start)


def backward_first(step, mix_grad, maps, rate):
    tokens, channels = step.shape
    count = tokens // CHUNK
    rows, cols, _, const = scan_specs(channels, count, True)

    def kernel(step_ref, mix_ref, out_map_ref, rate_ref, out_ref):
        @pl.when(pl.program_id(0) == 0)
        def _():
            out_ref[...] = jnp.zeros_like(out_ref)

        rate_v = rate_ref[...]

        def body(n, q):
            g = CHUNK // GROUP - 1 - n
            d8, m8 = step_ref[rows_of(g), :], mix_ref[rows_of(g), :]
            for k in reversed(range(GROUP)):
                decay = jnp.exp(d8[k : k + 1, :] * rate_v)
                q = decay * (q + m8[k : k + 1, :] * across(out_map_ref[g * GROUP + k], channels))
            return q

        out_ref[...] = lax.fori_loop(0, CHUNK // GROUP, body, out_ref[...])

    return pl.pallas_call(
        kernel,
        grid=(count,),
        out_shape=jax.ShapeDtypeStruct(rate.shape, F32),
        in_specs=[rows, rows, cols(1, 1), const],
        out_specs=const,
        compiler_params=SCAN_PARAMS,
        name="backward_first",
    )(step, mix_grad, maps, rate)


def backward_all(step, drive, mix_grad, maps, rate, states_in, start, slope, mixed, step_w):
    tokens, channels = step.shape
    columns = step_w.shape[0]
    count = tokens // CHUNK
    rows, cols, states, const = scan_specs(channels, count, True)

    def fold(v):
        total = v[:, :128]
        for i in range(1, channels // 128):
            total = total + v[:, 128 * i : 128 * (i + 1)]
        return total.astype(BF16)

    def kernel(
        step_ref,
        drive_ref,
        mix_ref,
        maps_ref,
        rate_ref,
        hs_ref,
        start_ref,
        slope_ref,
        mixed_ref,
        sw_ref,
        sb_ref,
        back_ref,
        part_ref,
        extra_ref,
        q_sc,
        dd_sc,
        sr_ref,
        v_sc,
    ):
        @pl.when(pl.program_id(0) == 0)
        def _():
            q_sc[...] = start_ref[...]
            dd_sc[...] = jnp.zeros_like(dd_sc)
            extra_ref[...] = jnp.zeros_like(extra_ref)

        rate_v = rate_ref[...]

        def body(n, carry):
            q, dd = carry
            g = CHUNK // GROUP - 1 - n
            at = rows_of(g)
            d8, w8, m8 = step_ref[at, :], drive_ref[at, :], mix_ref[at, :]
            sb, sr = [], []
            for k in reversed(range(GROUP)):
                t = g * GROUP + k
                d, w, m = d8[k : k + 1, :], w8[k : k + 1, :], m8[k : k + 1, :]
                b = across(maps_ref[t, :STATE], channels)
                c = across(maps_ref[t, STATE:], channels)
                decay = jnp.exp(d * rate_v)
                kept = decay * hs_ref[t].astype(F32)
                h = kept + w * b
                hbar = q + m * c
                flow = hbar * kept
                q = decay * hbar
                dd = dd + flow * d
                sb.append(jnp.sum(hbar * b, axis=0, keepdims=True))
                sr.append(jnp.sum(flow * rate_v, axis=0, keepdims=True))
                v_sc[t, :STATE] = fold(hbar * w)
                v_sc[t, STATE:] = fold(h * m)
            sb_ref[at, :] = jnp.concatenate(sb[::-1], axis=0)
            sr_ref[at, :] = jnp.concatenate(sr[::-1], axis=0)
            return q, dd

        q, dd = lax.fori_loop(0, CHUNK // GROUP, body, (q_sc[...], dd_sc[...]))
        q_sc[...] = q
        dd_sc[...] = dd

        first = lax.broadcasted_iota(jnp.int32, (256, 2 * columns), 0) < 128
        left = lax.broadcasted_iota(jnp.int32, (256, 2 * columns), 1) < columns
        ones = jnp.where(first == left, 1.0, 0.0).astype(BF16)
        shape = (2 * STATE, columns)
        pick = lax.broadcasted_iota(jnp.int32, shape, 1) == (
            lax.broadcasted_iota(jnp.int32, shape, 0) + columns - 2 * STATE
        )
        many = 32

        def lanes(n, _):
            one = v_sc[rows_of(2 * n, many // 2)].reshape(many * STATE, 128)
            two = v_sc[rows_of(2 * n + 1, many // 2)].reshape(many * STATE, 128)
            total = jnp.dot(
                jnp.concatenate([one, two], axis=1), ones, preferred_element_type=F32
            )
            halves = []
            for i in range(2):
                part = total[:, columns * i : columns * (i + 1)].reshape(many // 2, 2 * STATE, columns)
                halves.append(jnp.sum(jnp.where(pick[None], part, 0.0), axis=1))
            at = rows_of(n, many)
            mixed_v = mixed_ref[at, :].astype(F32)
            raw = (mixed_v * sb_ref[at, :] + sr_ref[at, :]) * slope_ref[at, :]
            back = raw.astype(BF16)
            back_ref[at, :] = back
            part_ref[at, :] = contract(back, sw_ref[...], 1, 1) + jnp.concatenate(halves, axis=0)
            extra_ref[STATE : STATE + 1, :] += jnp.sum(raw, axis=0, keepdims=True)
            extra_ref[STATE + 1 : STATE + 2, :] += jnp.sum(
                mix_ref[at, :] * mixed_v, axis=0, keepdims=True
            )
            return 0

        lax.fori_loop(0, CHUNK // many, lanes, 0)

        @pl.when(pl.program_id(0) == count - 1)
        def _():
            extra_ref[:STATE, :] = dd_sc[...] * rate_v

    wide = jax.ShapeDtypeStruct((tokens, channels), F32)
    return pl.pallas_call(
        kernel,
        grid=(count,),
        out_shape=(
            wide,
            jax.ShapeDtypeStruct((tokens, channels), BF16),
            jax.ShapeDtypeStruct((tokens, columns), F32),
            jax.ShapeDtypeStruct((STATE + 8, channels), F32),
        ),
        in_specs=[rows, rows, rows, cols(0, 2), const, states, const, rows, rows]
        + [pl.BlockSpec(step_w.shape, lambda i: (0, 0))],
        out_specs=(
            rows,
            rows,
            pl.BlockSpec((CHUNK, columns), lambda i: (count - 1 - i, 0)),
            pl.BlockSpec((STATE + 8, channels), lambda i: (0, 0)),
        ),
        scratch_shapes=[
            pltpu.VMEM((STATE, channels), F32),
            pltpu.VMEM((STATE, channels), F32),
            pltpu.VMEM((CHUNK, channels), F32),
            pltpu.VMEM((CHUNK, 2 * STATE, 128), BF16),
        ],
        compiler_params=SCAN_PARAMS,
        name="backward_all",
    )(step, drive, mix_grad, maps, rate, states_in, start, slope, mixed, step_w)


def silu_slope(v):
    s = jax.nn.sigmoid(v)
    return s * (1.0 + v * (1.0 - s))


def turn_back(mixer_back, mixer_w, gated, gate_inner, mix):
    rows, width = mixer_back.shape
    channels = gated.shape[1]

    def kernel(b_ref, w_ref, g_ref, i_ref, m_ref, mix_ref, gate_ref, grad_ref, acc):
        back = b_ref[...]
        gated_grad = contract(back, w_ref[...], 1, 1)
        gate = i_ref[...]
        s = jax.nn.sigmoid(gate)
        mix_ref[...] = gated_grad * (gate * s)
        gate_ref[...] = (gated_grad * m_ref[...] * (s * (1.0 + gate * (1.0 - s)))).astype(BF16)

        @pl.when(pl.program_id(0) == 0)
        def _():
            acc[...] = jnp.zeros_like(acc)

        acc[...] += contract(g_ref[...], back, 0, 0)

        @pl.when(pl.program_id(0) == rows // CHUNK - 1)
        def _():
            grad_ref[...] = acc[...].astype(BF16)

    thin = pl.BlockSpec((CHUNK, channels), lambda i: (i, 0))
    const = pl.BlockSpec((channels, width), lambda i: (0, 0))
    return pl.pallas_call(
        kernel,
        grid=(rows // CHUNK,),
        out_shape=(
            jax.ShapeDtypeStruct((rows, channels), F32),
            jax.ShapeDtypeStruct((rows, channels), BF16),
            jax.ShapeDtypeStruct((channels, width), BF16),
        ),
        in_specs=[pl.BlockSpec((CHUNK, width), lambda i: (i, 0)), const, thin, thin, thin],
        out_specs=(thin, thin, const),
        scratch_shapes=[pltpu.VMEM((channels, width), F32)],
        compiler_params=SCAN_PARAMS,
        name="turn_back",
    )(mixer_back, mixer_w, gated, gate_inner, mix)


def group_sums(columns):
    row = lax.broadcasted_iota(jnp.int32, (columns, columns), 0)
    col = lax.broadcasted_iota(jnp.int32, (columns, columns), 1)
    edges = (0, RANK, RANK + STATE, RANK + 2 * STATE)
    mean = jnp.zeros((columns, columns), F32)
    for low, high in zip(edges, edges[1:]):
        inside = (row >= low) & (row < high) & (col >= low) & (col < high)
        mean = mean + jnp.where(inside, 1.0, 0.0)
    return mean.astype(BF16)


def group_mean(values, sums):
    lane = lax.broadcasted_iota(jnp.int32, (1, values.shape[1]), 1)
    high = values.astype(BF16)
    rest = (values - high.astype(F32)).astype(BF16)
    total = jnp.dot(high, sums, preferred_element_type=F32) + jnp.dot(
        rest, sums, preferred_element_type=F32
    )
    return total * jnp.where(lane < RANK, 1.0 / RANK, 1.0 / STATE)


def unwind(
    select_grad, proj, gain, select_w, step, map_sum, mix_grad, rest, conv_input, masks,
    gate_back, normed, inner_w, mixed, step_low, step_back, first, extra,
):
    rows, channels = step.shape
    columns = proj.shape[1]
    width = normed.shape[1]
    taps = CONV
    piece = 128
    ops = (
        select_grad, proj, gain, select_w, rest, masks, step, map_sum, mix_grad, conv_input,
        gate_back, inner_w, normed, mixed, step_low, step_back, first, extra,
    )

    def kernel(*refs):
        far, refs = refs[: len(ops)], refs[len(ops) :]
        one_ref, inner_ref, slab_ref, first_ref, gain_ref = refs[:5]
        near, refs = refs[5 : 5 + len(ops)], refs[5 + len(ops) :]
        back, conv_f, pre, ext, one_v, inner_v, sems, outs = refs
        fetched = []
        for i in range(len(ops)):
            c = pltpu.make_async_copy(far[i], near[i], sems.at[i])
            c.start()
            fetched.append(c)
        (
            sg_ref, pr_ref, g_ref, sw_ref, rest_ref, mask_ref, st_ref, ms_ref, mg_ref, ci_ref,
            gb_ref, iw_ref, n_ref, mx_ref, sl_ref, sb_ref, f_ref, e_ref,
        ) = near
        for c in fetched[:4]:
            c.wait()
        sums = group_sums(columns)
        v, u = pr_ref[...], sg_ref[...]
        r = lax.rsqrt(group_mean(v * v, sums) + EPSILON)
        scaled = u * g_ref[...]
        grad = r * scaled - v * (r * r * r) * group_mean(scaled * v, sums)
        gain_ref[...] = jnp.sum(u * v * r, axis=0, keepdims=True) * (1.0 / PLANE)
        back[...] = grad.astype(BF16)
        for c in fetched[4:10]:
            c.wait()
        conv_f[...] = ci_ref[...].astype(F32)
        pre[rows:, :] = jnp.zeros((8, channels), F32)
        weights = [rest_ref[STATE + k : STATE + k + 1, :] for k in range(taps)]
        bias = rest_ref[STATE + taps : STATE + taps + 1, :]
        skip = rest_ref[STATE + taps + 2 : STATE + taps + 3, :]

        def first_pass(n, carry):
            at = rows_of(n, piece)
            window = conv_f[pl.ds(pl.multiple_of(HALO - 8 + n * piece, 8), piece + 8), :]
            mask = mask_ref[at, :]
            total = bias
            seen = []
            for k in range(taps):
                tap = window[8 - taps + 1 + k : 8 - taps + 1 + k + piece]
                if k < taps - 1:
                    tap = tap * mask[:, k : k + 1]
                seen.append(tap)
                total = total + weights[k] * tap
            mixed_grad = (
                st_ref[at, :] * ms_ref[at, :]
                + skip * mg_ref[at, :]
                + jnp.dot(back[at, :], sw_ref[...], preferred_element_type=F32)
            )
            value = mixed_grad * silu_slope(total)
            pre[at, :] = value
            new = [c + jnp.sum(value * t, axis=0, keepdims=True) for c, t in zip(carry, seen)]
            return (*new, carry[taps] + jnp.sum(value, axis=0, keepdims=True))

        zero = jnp.zeros((1, channels), F32)
        conv_sums = lax.fori_loop(0, rows // piece, first_pass, (zero,) * (taps + 1))

        def second_pass(n, _):
            window = pre[pl.ds(pl.multiple_of(n * piece, 8), piece + 8), :]
            mask = mask_ref[pl.ds(pl.multiple_of(n * piece, 8), piece + 8), :]
            total = None
            for k in range(taps):
                part = window
                if k < taps - 1:
                    part = part * mask[:, k : k + 1]
                part = part[taps - 1 - k : taps - 1 - k + piece] * weights[k]
                total = part if total is None else total + part
            ext[pl.ds(pl.multiple_of(HALO + n * piece, 16), piece), :channels] = total.astype(BF16)
            return 0

        lax.fori_loop(0, rows // piece, second_pass, 0)
        window = pre[0:8, :]
        at = lax.broadcasted_iota(jnp.int32, (HALO, channels), 0)
        ahead = jnp.zeros((HALO, channels), F32)
        for k in range(taps - 1):
            part = window * mask_ref[0:8, k : k + 1] * weights[k]
            for t in range(taps - 1 - k):
                row = HALO - taps + 1 + k + t
                ahead = ahead + jnp.where(at == row, part[t : t + 1], 0.0)
        ext[0:HALO, :channels] = ahead.astype(BF16)
        ext[0:HALO, channels:] = jnp.zeros((HALO, channels), BF16)
        for c in fetched[10:]:
            c.wait()
        ext[HALO:, channels:] = gb_ref[...]

        copies = []
        third = 2 * channels // 6
        for n in range(6):
            inner_v[pl.ds(n * third, third), :] = contract(
                ext[:, n * third : (n + 1) * third], n_ref[...], 0, 0, BF16
            )
        c = pltpu.make_async_copy(inner_v, inner_ref, outs.at[0])
        c.start()
        copies.append(c)
        part_rows = (rows + HALO) // 5

        def last_pass(n, total):
            at = rows_of(n, part_rows)
            value = jnp.dot(ext[at, :], iw_ref[...], preferred_element_type=F32).astype(BF16)
            one_v[at, :] = value
            return total + jnp.sum(
                value.astype(F32) * n_ref[at, :].astype(F32), axis=0, keepdims=True
            )

        total = lax.fori_loop(0, 5, last_pass, jnp.zeros((1, width), F32))
        c = pltpu.make_async_copy(one_v, one_ref, outs.at[1])
        c.start()
        copies.append(c)
        first_ref[...] = total / f_ref[...]
        slab_ref[:columns, :] = contract(back[...], mx_ref[...], 0, 0)
        slab_ref[columns : columns + RANK, :] = contract(sl_ref[...], sb_ref[...], 0, 0)[:RANK]
        others = jnp.concatenate(
            [e_ref[:STATE]]
            + list(conv_sums)
            + [e_ref[STATE : STATE + 2], jnp.zeros((16 - taps - 3, channels), F32)],
            axis=0,
        )
        slab_ref[columns + RANK :, :] = others
        for c in copies:
            c.wait()

    one = jax.ShapeDtypeStruct((rows + HALO, width), BF16)
    inner = jax.ShapeDtypeStruct((2 * channels, width), BF16)
    return pl.pallas_call(
        kernel,
        out_shape=(
            one,
            inner,
            jax.ShapeDtypeStruct((columns + RANK + 32, channels), F32),
            jax.ShapeDtypeStruct((1, width), F32),
            jax.ShapeDtypeStruct((1, columns), F32),
        ),
        in_specs=[ANY] * len(ops),
        out_specs=(ANY, ANY, VMEM, VMEM, VMEM),
        scratch_shapes=[
            *[pltpu.VMEM(a.shape, a.dtype) for a in ops],
            pltpu.VMEM((rows, columns), BF16),
            pltpu.VMEM((rows + HALO, channels), F32),
            pltpu.VMEM((rows + 8, channels), F32),
            pltpu.VMEM((rows + HALO, 2 * channels), BF16),
            pltpu.VMEM(one.shape, BF16),
            pltpu.VMEM(inner.shape, BF16),
            dma(len(ops)),
            dma(2),
        ],
        compiler_params=SCAN_PARAMS,
        name="unwind",
    )(*ops)


def contract(left, right, left_dim, right_dim, kind=F32):
    return lax.dot_general(
        left, right, (((left_dim,), (right_dim,)), ((), ())), preferred_element_type=F32
    ).astype(kind)


def on_device(
    planes,
    block_input,
    documents,
    first_gain,
    inner_weight,
    conv_weight,
    conv_bias,
    select_weight,
    select_gain,
    step_weight,
    step_bias,
    decay_log,
    skip_gain,
    mixer_weight,
    second_gain,
    gate_weight,
    up_weight,
    down_weight,
    cotangent,
):
    tok, width = block_input.shape
    devices = planes * PLANE
    rows = PLANE * tok
    z = lax.axis_index("z")
    own_block = mixer_weight.shape[0]
    inner_block = inner_weight.shape[1]
    channels = planes * own_block
    columns = RANK + 2 * STATE
    taps = conv_weight.shape[0]


    (
        x_ext,
        cot_all,
        inners,
        mixer_here,
        select_w,
        step_w,
        rest,
        first_f,
        second_f,
        select_f,
        ffn_own,
    ) = opening(
        planes,
        block_input,
        cotangent,
        inner_weight.T,
        mixer_weight,
        select_weight,
        (
            step_weight,
            decay_log,
            conv_weight,
            conv_bias[None, :],
            step_bias[None, :],
            skip_gain[None, :],
        ),
        (first_gain[None, :], second_gain[None, :], select_gain[None, :]),
        (gate_weight, up_weight, down_weight),
    )
    mixer_w = lax.all_gather(mixer_here, "z", axis=0, tiled=True)
    ffn_w = lax.all_gather(ffn_own, "z", axis=0)
    rate = -jnp.exp(rest[:STATE])
    conv_w = [rest[STATE + k : STATE + k + 1] for k in range(taps)]
    conv_b, step_b, skip = (rest[STATE + taps + k : STATE + taps + k + 1] for k in range(3))
    inner_w = inners.reshape(2 * channels, width)

    padded = jnp.concatenate([jnp.full((taps - 1,), -1, jnp.int32), documents])
    ids = lax.dynamic_slice_in_dim(padded, z * rows, rows + taps - 1, 0)
    here = ids[taps - 1 :]
    same = [(ids[k : k + rows] == here)[:, None] for k in range(taps)]
    masks = jnp.concatenate([m.astype(F32) for m in same], axis=1)
    masks = jnp.pad(masks, ((0, 8), (0, 0)))

    x_f = x_ext.astype(F32)
    r_one = lax.rsqrt(jnp.mean(x_f * x_f, axis=-1, keepdims=True) + EPSILON)
    normed_one = (x_f * r_one * first_f).astype(BF16)
    conv_input = contract(normed_one, inner_w[:channels], 1, 1, BF16)
    gate_inner = contract(normed_one[HALO:], inner_w[channels:], 1, 1)
    shift = HALO - taps + 1
    total = conv_b
    for k in range(taps):
        tap = conv_input[shift + k : shift + k + rows].astype(F32)
        total = total + conv_w[k] * jnp.where(same[k], tap, 0.0)
    mixed_in = jax.nn.silu(total).astype(BF16)
    proj_part = contract(mixed_in, select_w, 1, 1)
    proj = plane_sum(proj_part, 1)
    step, slope, step_cut, drive, step_low, maps = prepare(
        proj, select_f, step_w, step_b, mixed_in, masks
    )
    mixed_f = mixed_in.astype(F32)
    local_final, through = forward_final(step_cut, drive, maps, rate)
    state_in = state_chain(planes, through, local_final, 4, True)
    sums, states = forward_all(step_cut, drive, maps, rate, state_in)
    mix = sums + skip * mixed_f
    gate_silu = jax.nn.silu(gate_inner)
    gated = (mix * gate_silu).astype(BF16)
    mixer_part = contract(gated, mixer_w, 1, 0, BF16)
    resid_mid, normed_two = mixer_join(
        mixer_part, block_input, second_f
    )

    two_part, out_part, ffn_hidden, gate_back, up_back = feed_forward(
        normed_two, cot_all, ffn_w
    )
    resid_grad, mixer_back, second_grad, ffn_grads, gate_grad = ffn_join(
        planes,
        two_part,
        resid_mid,
        second_f,
        cotangent,
        normed_two,
        cot_all,
        ffn_hidden,
        gate_back,
        up_back,
    )

    mix_grad, gate_back, mixer_grad = turn_back(mixer_back, mixer_w, gated, gate_inner, mix)
    mixer_sum = lax.psum_scatter(mixer_grad, "z", scatter_dimension=0, tiled=True)
    route = []
    for k in range(devices):
        half = k // 2
        route.append(((2 * (half // PLANE) + k % 2) * PLANE + half % PLANE, k))
    ffn_grads, _ = lax.optimization_barrier((ffn_grads, mixer_grad))
    ffn_sums = lax.psum_scatter(ffn_grads, "z", scatter_dimension=0, tiled=False)
    local_back = backward_first(step_cut, mix_grad, maps, rate)
    state_back = state_chain(planes, through, local_back, 5, False)
    map_sum, step_back, select_part, extra = backward_all(
        step_cut, drive, mix_grad, maps, rate, states, state_back, slope, mixed_in, step_w
    )
    mixer_sum, select_part = lax.optimization_barrier((mixer_sum, select_part))
    mixer_home = lax.ppermute(mixer_sum, ("z", "p"), route)
    select_grad = plane_sum(select_part, 7)
    one_part, inner_grad, slab_grad, first_grad, select_gain_grad = unwind(
        select_grad,
        proj,
        select_f,
        select_w,
        step,
        map_sum,
        mix_grad,
        rest,
        conv_input,
        masks,
        gate_back,
        normed_one,
        inner_w,
        mixed_in,
        step_low,
        step_back,
        first_f,
        extra,
    )
    results = closing(
        planes,
        one_part,
        block_input,
        first_f,
        resid_grad,
        inner_grad.reshape(planes, inner_block, width),
        slab_grad,
        (first_grad, second_grad, select_gain_grad),
        out_part,
        resid_mid,
        ffn_sums,
        mixer_home,
    )
    (
        input_grad,
        inner_out,
        select_out,
        step_out,
        block_output,
        up_out,
        down_out,
        mixer_out,
        decay_out,
        conv_out,
        conv_b_out,
        step_b_out,
        skip_out,
        first_out,
        second_out,
        gain_out,
        gate_out,
    ) = hand_over((*results, gate_grad))
    return (
        block_output,
        input_grad,
        first_out[0],
        inner_out.T,
        conv_out,
        conv_b_out[0],
        select_out,
        gain_out[0],
        step_out,
        step_b_out[0],
        decay_out,
        skip_out[0],
        mixer_out,
        second_out[0],
        gate_out if gate_out.shape[0] == width else gate_out.T,
        up_out if up_out.shape[0] == width else up_out.T,
        down_out,
    )


def solution(mesh):
    planes = mesh.devices.size // PLANE
    grid = Mesh(mesh.devices.reshape(planes, PLANE), ("z", "p"))
    seq = ("z", "p")
    by_row, by_column, flat = P(seq, None), P(None, seq), P(seq)

    def program(*args):
        return on_device(planes, *args)

    return jax.shard_map(
        program,
        mesh=grid,
        in_specs=(
            by_row,
            P(),
            flat,
            by_column,
            by_column,
            flat,
            by_row,
            flat,
            by_column,
            flat,
            by_column,
            flat,
            by_row,
            flat,
            by_column,
            by_column,
            by_row,
            by_row,
        ),
        out_specs=(
            by_row,
            by_row,
            flat,
            by_column,
            by_column,
            flat,
            by_row,
            flat,
            by_column,
            flat,
            by_column,
            flat,
            by_row,
            flat,
            by_column,
            by_column,
            by_row,
        ),
        check_vma=False,
    )
```

```python
import jax
import jax.numpy as jnp
import numpy as np
from jax import lax
from jax.experimental import pallas as pl
from jax.experimental.pallas import tpu as pltpu
from jax.sharding import Mesh
from jax.sharding import PartitionSpec as P

STATE = 16
RANK = 96
CONV = 4
PLANE = 8
HALO = 16
GROUP = 8
CUT = 1e4
EPSILON = 1e-06
ALL_VMEM = 60 << 20
F32 = jnp.float32
BF16 = jnp.bfloat16
MESH_ID = pl.DeviceIdType.MESH
ANY = pl.BlockSpec(memory_space=pl.ANY)
VMEM = pl.BlockSpec(memory_space=pltpu.VMEM)


def xor(p, k):
    out = p
    for bit in (1, 2, 4):
        if k & bit:
            out = out + bit - 2 * bit * lax.rem(lax.div(out, bit), 2)
    return out


def remote(src, dst, send_sem, recv_sem, z, p):
    return pltpu.make_async_remote_copy(
        src_ref=src,
        dst_ref=dst,
        send_sem=send_sem,
        recv_sem=recv_sem,
        device_id={"z": z, "p": p},
        device_id_type=MESH_ID,
    )


def greet(z, p):
    pl.semaphore_signal(
        pltpu.get_barrier_semaphore(), inc=1, device_id={"z": z, "p": p}, device_id_type=MESH_ID
    )


def comm_params(number, vmem=None):
    return pltpu.CompilerParams(
        collective_id=number, has_side_effects=True, vmem_limit_bytes=vmem
    )


def dma(*shape):
    return pltpu.SemaphoreType.DMA(shape)


def block_route(z, p):
    half = lax.div(PLANE * z + p, 2)
    return lax.rem(half, PLANE), 2 * lax.div(half, PLANE) + lax.rem(p, 2)


def block_source_of(z, p):
    k = 2 * (PLANE * lax.div(z, 2) + p) + lax.rem(z, 2)
    return lax.div(k, PLANE), lax.rem(k, PLANE)


def moves_in(z, p):
    zs, ps = block_source_of(z, p)
    return jnp.logical_or(zs != z, ps != p)


def plane_greet(z, p):
    for k in (1, 2, 4):
        greet(z, xor(p, k))
    return 3


def plane_reduce(
    z, p, part, sbuf, obuf, dbuf, rbuf, s1, r1, s2, r2, finish, rows, during=None, base=0
):
    sib, near, side = xor(p, 1), xor(p, 2), xor(p, 4)
    tok = sbuf.shape[1]
    half = tok // 2
    top, low = pl.ds(0, half), pl.ds(half, half)
    wide = (part.dtype == F32) and (obuf.dtype == F32)
    align = min(rows, 16)

    def block(q):
        return part.at[pl.ds(pl.multiple_of(base + q * tok, align), tok)]

    def piece(q, at):
        return part[pl.ds(pl.multiple_of(base + q * tok + at.start, align), rows), :].astype(F32)

    def chunks(length, body):
        def step(n, _):
            body(pl.ds(pl.multiple_of(n * rows, rows), rows))
            return 0

        lax.fori_loop(0, length // rows, step, 0)

    def put(value):
        return value if wide else value.astype(obuf.dtype)

    first = []
    for i, k in enumerate((6, 2, 4, 0)):
        c = remote(block(xor(sib, k)), sbuf.at[i], s1.at[i], r1.at[i], z, sib)
        c.start()
        first.append(c)
    second = []

    def send(i, src, dst, to):
        c = remote(src, dst, s2.at[i], r2.at[i], z, to)
        c.start()
        second.append(c)
        return c

    for i, k in enumerate((6, 2, 4)):
        first[i].wait_recv()
        q = xor(p, k)

        def add(at, i=i, q=q):
            obuf[i, at] = put(piece(q, at) + sbuf[i, at].astype(F32))

        chunks(tok, add)
        if k == 6:
            far_top = send(0, obuf.at[0, top], dbuf.at[0], near)
            far_low = send(1, obuf.at[0, low], dbuf.at[1], side)
        elif k == 2:
            send(2, obuf.at[1, top], rbuf.at[0, top], near)
        else:
            send(3, obuf.at[2, low], rbuf.at[1, low], side)
    if during is not None:
        during(0)
    far_top.wait_recv()

    def join_top(at):
        obuf[2, at] = put(obuf[2, at].astype(F32) + dbuf[0, at].astype(F32))

    chunks(half, join_top)
    send(4, obuf.at[2, top], rbuf.at[1, top], side)
    far_low.wait_recv()

    def join_low(at):
        down = pl.ds(pl.multiple_of(at.start + half, rows), rows)
        obuf[1, down] = put(obuf[1, down].astype(F32) + dbuf[1, at].astype(F32))

    chunks(half, join_low)
    send(5, obuf.at[1, low], rbuf.at[0, low], near)
    if during is not None:
        during(1)
    first[3].wait_recv()
    for c in second[2:]:
        c.wait_recv()

    def last(at):
        total = piece(p, at) + sbuf[3, at].astype(F32)
        finish(at, total + rbuf[0, at].astype(F32) + rbuf[1, at].astype(F32))

    chunks(tok, last)
    for c in first + second:
        c.wait_send()


class PlaneGather:
    def __init__(self, z, p, own, place, ss, rs, fs, fr, ls):
        self.z, self.p, self.own, self.place = z, p, own, place
        self.ss, self.rs, self.fs, self.fr, self.ls = ss, rs, fs, fr, ls
        self.sent, self.passed = [], []
        half = own.shape[0] // 2
        self.top, self.low = pl.ds(0, half), pl.ds(half, half)

    def send(self, src, dst, to):
        i = len(self.sent)
        c = remote(src, dst, self.ss.at[i], self.rs.at[i], self.z, to)
        c.start()
        self.sent.append(c)

    def pass_on(self, q):
        i = len(self.passed)
        place = self.place(q)
        c = remote(place, place, self.fs.at[i], self.fr.at[i], self.z, xor(self.p, 1))
        c.start()
        self.passed.append(c)

    def start(self):
        p, own = self.p, self.own
        near, side = xor(p, 2), xor(p, 4)
        self.send(own.at[self.top], self.place(p).at[self.top], near)
        self.send(own.at[self.low], self.place(p).at[self.low], side)
        self.send(own.at[self.low], self.place(p).at[self.low], near)
        self.send(own.at[self.top], self.place(p).at[self.top], side)
        self.send(own, self.place(p), xor(p, 1))
        self.local = pltpu.make_async_copy(own, self.place(p), self.ls)
        self.local.start()

    def relay(self):
        near, side = xor(self.p, 2), xor(self.p, 4)
        self.sent[0].wait_recv()
        self.send(self.place(near).at[self.top], self.place(near).at[self.top], side)
        self.sent[1].wait_recv()
        self.send(self.place(side).at[self.low], self.place(side).at[self.low], near)

    def finish(self):
        near, side, far = xor(self.p, 2), xor(self.p, 4), xor(self.p, 6)
        self.sent[2].wait_recv()
        self.pass_on(near)
        self.sent[3].wait_recv()
        self.pass_on(side)
        self.sent[5].wait_recv()
        self.sent[6].wait_recv()
        self.pass_on(far)
        self.sent[4].wait_recv()
        for c in self.passed:
            c.wait_recv()
        for c in self.sent + self.passed:
            c.wait_send()
        self.local.wait()


def plane_gather(z, p, own, place, ss, rs, fs, fr, ls, during=None):
    gather = PlaneGather(z, p, own, place, ss, rs, fs, fr, ls)
    gather.start()
    if during is not None:
        during(2)
    gather.relay()
    gather.finish()


def rows_at(ref, tok, base=0):
    return lambda q: ref.at[pl.ds(pl.multiple_of(base + q * tok, 16), tok)]


GATHER_SEMS = (7, 7, 3, 3)
REDUCE_SEMS = (4, 4, 6, 6)


def ring_gather(planes, z, p, own, out, ss, rs, ls):
    local = pltpu.make_async_copy(own, out.at[z], ls)
    local.start()
    sent = []

    def send(i, src, dst, r):
        c = remote(src, dst, ss.at[i], rs.at[i], lax.rem(z + r, planes), p)
        c.start()
        sent.append(c)
        return c

    if planes != 4:
        for r in range(1, planes):
            send(r, own, out.at[z], r)
        return local, sent, lambda: None
    half = own.shape[0] // 2
    top, low = pl.ds(0, half), pl.ds(half, half)
    up = send(0, own.at[top], out.at[z, top], 1)
    down = send(1, own.at[low], out.at[z, low], 3)

    def relay():
        before, after = lax.rem(z + 3, 4), lax.rem(z + 1, 4)
        send(2, own.at[low], out.at[z, low], 1)
        send(3, own.at[top], out.at[z, top], 3)
        up.wait_recv()
        send(4, out.at[before, top], out.at[before, top], 1)
        down.wait_recv()
        send(5, out.at[after, low], out.at[after, low], 3)

    return local, sent, relay


def ring_finish(local, sent, relayed):
    for i, c in enumerate(sent):
        if not (relayed and i < 2):
            c.wait_recv()
        c.wait_send()
    local.wait()


def ring_reduce(planes, z, p, src, ibuf, fbuf, mbuf, ss, rs, hold=False):
    half = src.shape[1] // 2
    top, low = pl.ds(0, half), pl.ds(half, half)
    before, after = lax.rem(z + planes - 1, planes), lax.rem(z + 1, planes)
    sent = []

    def send(i, part, dst, r):
        c = remote(part, dst, ss.at[i], rs.at[i], lax.rem(z + r, planes), p)
        c.start()
        sent.append(c)

    def near():
        send(2, src.at[after, low], ibuf.at[0, low], 1)
        send(3, src.at[before, top], ibuf.at[1, top], 3)

    if planes == 4:
        far = lax.rem(z + 2, 4)
        send(0, src.at[far, top], fbuf.at[0], 1)
        send(1, src.at[far, low], fbuf.at[1], 3)
        if not hold:
            near()
    else:
        for r in range(1, planes):
            send(r, src.at[lax.rem(z + r, planes)], ibuf.at[r], r)

    def relay():
        if planes == 4:
            if hold:
                near()
            sent[0].wait_recv()
            mbuf[0] = (src[after, top].astype(F32) + fbuf[0].astype(F32)).astype(mbuf.dtype)
            send(4, mbuf.at[0], ibuf.at[0, top], 1)
            sent[1].wait_recv()
            mbuf[1] = (src[before, low].astype(F32) + fbuf[1].astype(F32)).astype(mbuf.dtype)
            send(5, mbuf.at[1], ibuf.at[1, low], 3)

    def finish():
        for i, c in enumerate(sent):
            if not (planes == 4 and i < 2):
                c.wait_recv()
            c.wait_send()
        total = src[z].astype(F32)
        for k in range(2) if planes == 4 else range(1, planes):
            total = total + ibuf[k].astype(F32)
        return total

    return relay, finish


def ring_reduce_scratch(planes, block, width, kind=BF16):
    return [
        pltpu.VMEM((2 if planes == 4 else planes, block, width), kind),
        pltpu.VMEM((2, block // 2, width), kind),
        pltpu.VMEM((2, block // 2, width), kind),
        dma(ring_sems(planes)),
        dma(ring_sems(planes)),
    ]


def ring_greet(planes, z, p):
    for r in range(1, planes):
        greet(lax.rem(z + r, planes), p)
    return planes - 1


def ring_sems(planes):
    return max(6, planes)


TRIO = 8


def join_gain(planes, gains_ref, row, per, spread):
    total = spread.shape[1]
    at = lax.broadcasted_iota(jnp.int32, (PLANE, total), 1)
    column = lax.broadcasted_iota(jnp.int32, (PLANE, total), 0)
    joined = jnp.zeros((PLANE, total), F32)
    for k in range(planes):
        piece = jnp.concatenate([gains_ref[q, k, row : row + 1, :] for q in range(PLANE)], axis=0)
        wide = jnp.dot(piece.astype(BF16), spread, preferred_element_type=F32)
        low = (column + PLANE * k) * per
        joined = joined + jnp.where((at >= low) & (at < low + per), wide, 0.0)
    return jnp.sum(joined, axis=0, keepdims=True)


def opening(planes, x, cot, inner, mixer, select, small, gains, ffn):
    tok, width = x.shape
    relayed = planes == 4
    block = mixer.shape[0]
    columns = select.shape[1]
    channels = planes * block
    places, filled = [], 0
    for array in small:
        places.append((filled, filled + array.shape[0]))
        filled += array.shape[0]
    rank = small[0].shape[0]
    states = small[1].shape[0]
    height = rank + 32 + columns
    pers = [g.shape[1] for g in gains]
    spreads = []
    for per, total in ((pers[0], width), (pers[2], columns)):
        spreads.append(
            jnp.asarray(np.arange(128)[:, None] == np.arange(total)[None, :] % per, BF16)
        )
    turn = ffn[0].shape[1] % 128 == 0
    units = ffn[2].shape[0]
    if not turn:
        ffn = [ffn[0].T, ffn[1].T, ffn[2]]

    def kernel(*refs):
        wide_refs, select_ref = refs[:4], refs[4]
        small_refs, gain_refs, refs = refs[5:11], refs[11:14], refs[14:]
        spread_refs, ffn_refs, refs = refs[:2], refs[2:5], refs[5:]
        xg_ref, cots_ref, inners_ref, home_ref = refs[:4]
        select_out, step_ref, rest_ref, first_ref, second_ref, sel_ref, own_ref = refs[4:11]
        refs = refs[11:]
        own_wide, own_small, got_small, smalls, own_gain, gains_all = refs[:6]
        refs = refs[6:]
        near_small, near_gain, near_spread, near_ffn = refs[:6], refs[6:9], refs[9:11], refs[11:13]
        near_select, ffn_out, refs = refs[13], refs[14], refs[15:]
        near_wide, near_down, wide_sems, refs = refs[:4], refs[4], refs[5], refs[6:]
        x_ref, cot_ref, inner_ref, mixer_ref = near_wide
        x_sems, c_sems, refs = refs[:5], refs[5:10], refs[10:]
        hs, hr, gs, gr, gs2, gr2, ins, inr, inl, ps, pr, bs, br, bl, near_sems, out_sems = refs

        z, p = lax.axis_index("z"), lax.axis_index("p")
        column, slot = block_route(z, p)
        from_z, from_p = block_source_of(z, p)
        moves = jnp.logical_or(column != p, slot != z)
        stays = jnp.logical_not(moves)
        after = lax.rem(z + 1, planes)
        for k in range(1, PLANE):
            greet(z, xor(p, k))
        for r in range(1, planes):
            greet(lax.rem(z + r, planes), p)

        @pl.when(moves_in(z, p))
        def _():
            greet(from_z, from_p)

        landing = []
        for i in (2, 0, 1, 3):
            c = pltpu.make_async_copy(wide_refs[i], near_wide[i], wide_sems.at[i])
            c.start()
            landing.append(c)
        down_in = pltpu.make_async_copy(ffn_refs[2], near_down, wide_sems.at[4])
        down_in.start()
        fetched = []
        far_refs = list(small_refs) + list(gain_refs) + [select_ref]
        far_refs += list(spread_refs) + list(ffn_refs[:2])
        near_refs = list(near_small) + list(near_gain) + [near_select]
        near_refs += list(near_spread) + list(near_ffn)
        for i, (src, dst) in enumerate(zip(far_refs, near_refs)):
            c = pltpu.make_async_copy(src, dst, near_sems.at[i])
            c.start()
            fetched.append(c)
        own_wide[...] = jnp.zeros_like(own_wide)
        own_gain[...] = jnp.zeros_like(own_gain)
        pl.semaphore_wait(
            pltpu.get_barrier_semaphore(),
            PLANE - 1 + planes - 1 + moves.astype(jnp.int32),
        )

        for c in landing:
            c.wait()
        local, sent, relay = ring_gather(planes, z, p, inner_ref, inners_ref, ins, inr, inl)

        homes = [
            (own_small, got_small, ps.at[0], pr.at[0]),
            (mixer_ref, home_ref, ps.at[1], pr.at[1]),
        ]

        def homing(items):
            for src, dst, send, recv in items:

                @pl.when(moves)
                def _():
                    remote(src, dst, send, recv, slot, column).start()

                @pl.when(stays)
                def _():
                    pltpu.make_async_copy(src, dst, recv).start()

        def place(q):
            return xg_ref.at[pl.ds(pl.multiple_of(HALO + q * tok, HALO), tok)]

        gain_out, gain_on, block_ring, ffn_sent = [], [], [], []

        def first_sends(_):
            for c in fetched[:10]:
                c.wait()
            for (low, high), ref in zip(places, near_small):
                own_wide[low:high, :] = ref[...].astype(F32)
            own_small[: rank + 32] = own_wide[...].astype(BF16)
            own_small[rank + 32 :] = near_select[...].astype(F32).T.astype(BF16)
            for i, ref in enumerate(near_gain):
                own_gain[i : i + 1, : pers[i]] = ref[...].astype(F32)
            homing(homes[:1])
            for r in range(1, planes):
                c = remote(
                    own_gain, gains_all.at[p, z], gs.at[r], gr.at[r], lax.rem(z + r, planes), p
                )
                c.start()
                gain_out.append(c)
            gains_all[p, z] = own_gain[...]

        x_gather = PlaneGather(z, p, x_ref, place, *x_sems)
        cot_gather = PlaneGather(z, p, cot_ref, rows_at(cots_ref, tok), *c_sems)
        x_gather.start()
        first_sends(0)
        x_gather.relay()
        relay()
        cot_gather.start()
        homing(homes[1:])

        src, dst, _, recv = homes[0]
        pltpu.make_async_copy(src, dst, recv).wait()
        block_ring.extend(ring_gather(planes, z, p, got_small, smalls, bs, br, bl))
        for c in gain_out:
            c.wait_recv()
        for k in range(1, PLANE):
            c = remote(gains_all.at[p], gains_all.at[p], gs2.at[k], gr2.at[k], z, xor(p, k))
            c.start()
            gain_on.append(c)
        x_gather.finish()

        edge = xg_ref.at[pl.ds(PLANE * tok, HALO)]
        front = xg_ref.at[pl.ds(0, HALO)]

        @pl.when(z < planes - 1)
        def _():
            remote(edge, front, hs, hr, after, p).start()

        @pl.when(z == 0)
        def _():
            pltpu.make_async_copy(edge, front, hr).start()

        cot_gather.relay()
        block_ring[2]()
        down_in.wait()
        down_out = pltpu.make_async_copy(
            near_down, own_ref.at[pl.ds(2 * units, units)], out_sems.at[2]
        )
        down_out.start()
        for c in fetched[10:]:
            c.wait()
        for i in range(2):
            if turn:
                ffn_out[i] = near_ffn[i][...].T
            else:
                ffn_out[i] = near_ffn[i][...]
            c = pltpu.make_async_copy(
                ffn_out.at[i], own_ref.at[pl.ds(i * units, units)], out_sems.at[i]
            )
            c.start()
            ffn_sent.append(c)
        for c in gain_on:
            c.wait_recv()
        first_ref[...] = join_gain(planes, gains_all, 0, pers[0], near_spread[0][...])
        second_ref[...] = join_gain(planes, gains_all, 1, pers[1], near_spread[0][...])
        sel_ref[...] = join_gain(planes, gains_all, 2, pers[2], near_spread[1][...])
        cot_gather.finish()
        down_out.wait()
        for c in ffn_sent:
            c.wait()
        pltpu.make_async_copy(edge, front, hr).wait()

        @pl.when(z < planes - 1)
        def _():
            remote(edge, front, hs, hr, after, p).wait_send()

        ring_finish(block_ring[0], block_ring[1], relayed)
        joined = jnp.concatenate([smalls[k].astype(F32) for k in range(planes)], axis=1)
        row = lax.broadcasted_iota(jnp.int32, (rank + 32, channels), 0)
        step_ref[...] = jnp.where(row < rank, joined[: rank + 32], 0.0).astype(BF16)
        rest_ref[...] = joined[rank : rank + 32]
        select_out[...] = joined[rank + 32 :].astype(BF16)
        pltpu.make_async_copy(mixer_ref, home_ref, pr.at[1]).wait()

        @pl.when(moves)
        def _():
            for src, dst, send, recv in homes:
                remote(src, dst, send, recv, slot, column).wait_send()

        for c in gain_out + gain_on:
            c.wait_send()
        ring_finish(local, sent, relayed)

    def shape(*dims, kind=BF16):
        return jax.ShapeDtypeStruct(dims, kind)

    one = pltpu.SemaphoreType.DMA
    return pl.pallas_call(
        kernel,
        out_shape=(
            shape(HALO + PLANE * tok, width),
            shape(PLANE * tok, width),
            shape(planes, *inner.shape),
            shape(*mixer.shape),
            shape(columns, channels),
            shape(rank + 32, channels),
            shape(32, channels, kind=F32),
            shape(1, width, kind=F32),
            shape(1, width, kind=F32),
            shape(1, columns, kind=F32),
            shape(3 * units, width),
        ),
        in_specs=[ANY] * 19,
        out_specs=(ANY,) * 4 + (VMEM,) * 6 + (ANY,),
        scratch_shapes=[
            pltpu.VMEM((rank + 32, block), F32),
            pltpu.VMEM((height, block), BF16),
            pltpu.VMEM((height, block), BF16),
            pltpu.VMEM((planes, height, block), BF16),
            pltpu.VMEM((TRIO, 128), F32),
            pltpu.VMEM((PLANE, planes, TRIO, 128), F32),
            *[pltpu.VMEM(a.shape, a.dtype) for a in (*small, *gains, *spreads, *ffn[:2])],
            pltpu.VMEM(select.shape, BF16),
            pltpu.VMEM((2, units, width), BF16),
            *[pltpu.VMEM(a.shape, a.dtype) for a in (x, cot, inner, mixer, ffn[2])],
            dma(5),
            *[dma(n) for n in GATHER_SEMS],
            one,
            *[dma(n) for n in GATHER_SEMS],
            one,
            one,
            one,
            dma(planes),
            dma(planes),
            dma(PLANE),
            dma(PLANE),
            dma(ring_sems(planes)),
            dma(ring_sems(planes)),
            one,
            dma(2),
            dma(2),
            dma(ring_sems(planes)),
            dma(ring_sems(planes)),
            one,
            dma(14),
            dma(3),
        ],
        compiler_params=comm_params(0, ALL_VMEM),
        name="opening",
    )(x, cot, inner, mixer, select, *small, *gains, *spreads, *ffn)


def plane_sum(part, number):
    tok, columns = part.shape[0] // PLANE, part.shape[1]

    def kernel(part_ref, out_ref, own, *refs):
        bufs, g = refs[:8], refs[8:]
        z, p = lax.axis_index("z"), lax.axis_index("p")
        pl.semaphore_wait(pltpu.get_barrier_semaphore(), plane_greet(z, p))

        def finish(at, value):
            own[at] = value

        plane_reduce(z, p, part_ref, *bufs, finish, tok // 2)
        plane_gather(z, p, own, rows_at(out_ref, tok), *g)

    return pl.pallas_call(
        kernel,
        out_shape=jax.ShapeDtypeStruct(part.shape, F32),
        in_specs=[VMEM],
        out_specs=VMEM,
        scratch_shapes=[
            pltpu.VMEM((tok, columns), F32),
            *reduce_scratch(tok, columns, F32),
            *[dma(n) for n in GATHER_SEMS],
            pltpu.SemaphoreType.DMA,
        ],
        compiler_params=comm_params(number, 32 << 20),
        name="plane_sum",
    )(part)


def reduce_scratch(tok, width, kind=BF16):
    return [
        pltpu.VMEM((4, tok, width), kind),
        pltpu.VMEM((3, tok, width), kind),
        pltpu.VMEM((2, tok // 2, width), kind),
        pltpu.VMEM((2, tok, width), kind),
        *[dma(n) for n in REDUCE_SEMS],
    ]


def mixer_join(part, x, gain):
    tok, width = x.shape

    def kernel(
        part_ref,
        x_ref,
        gain_ref,
        resid_ref,
        out_ref,
        own,
        sbuf,
        obuf,
        dbuf,
        rbuf,
        s1,
        r1,
        s2,
        r2,
        *g,
    ):
        z, p = lax.axis_index("z"), lax.axis_index("p")
        pl.semaphore_wait(pltpu.get_barrier_semaphore(), plane_greet(z, p))

        def finish(at, total):
            v = total + x_ref[at].astype(F32)
            resid_ref[at] = v
            r = lax.rsqrt(jnp.mean(v * v, axis=-1, keepdims=True) + EPSILON)
            own[at] = (v * r * gain_ref[...]).astype(BF16)

        plane_reduce(z, p, part_ref, sbuf, obuf, dbuf, rbuf, s1, r1, s2, r2, finish, 16)
        plane_gather(z, p, own, rows_at(out_ref, tok), *g)

    return pl.pallas_call(
        kernel,
        out_shape=(
            jax.ShapeDtypeStruct((tok, width), F32),
            jax.ShapeDtypeStruct(part.shape, BF16),
        ),
        in_specs=[VMEM] * 3,
        out_specs=(VMEM, VMEM),
        scratch_shapes=[
            pltpu.VMEM((tok, width), BF16),
            *reduce_scratch(tok, width),
            *[dma(n) for n in GATHER_SEMS],
            pltpu.SemaphoreType.DMA,
        ],
        compiler_params=comm_params(2, 32 << 20),
        name="mixer_join",
    )(part, x, gain)


def feed_forward(normed, cot, weights):
    rows, width = normed.shape
    planes, triple, _ = weights.shape
    units = triple // 3
    hidden = planes * units
    block = 512

    def kernel(n_ref, c_ref, w_ref, two_ref, out_ref, h_ref, gb_ref, ub_ref, gw, uw, dw, sem):
        @pl.when(pl.program_id(0) == 0)
        def _():
            copies = []
            for i, dst in enumerate((gw, uw, dw)):
                for k in range(planes):
                    copies.append(
                        pltpu.make_async_copy(
                            w_ref.at[k, pl.ds(i * units, units)],
                            dst.at[pl.ds(k * units, units)],
                            sem.at[i, k],
                        )
                    )
            for c in copies:
                c.start()
            for c in copies:
                c.wait()

        n, c = n_ref[...], c_ref[...]
        gate = contract(n, gw[...], 1, 1)
        up = contract(n, uw[...], 1, 1)
        back = contract(c, dw[...], 1, 1)
        s = jax.nn.sigmoid(gate)
        silu = gate * s
        h = (silu * up).astype(BF16)
        gb = (back * up * (s * (1.0 + gate * (1.0 - s)))).astype(BF16)
        ub = (back * silu).astype(BF16)
        h_ref[...] = h
        gb_ref[...] = gb
        ub_ref[...] = ub
        two_ref[...] = (contract(gb, gw[...], 1, 0) + contract(ub, uw[...], 1, 0)).astype(BF16)
        out_ref[...] = contract(h, dw[...], 1, 0, BF16)

    wide = pl.BlockSpec((block, width), lambda i: (i, 0))
    thin = pl.BlockSpec((block, hidden), lambda i: (i, 0))
    return pl.pallas_call(
        kernel,
        grid=(rows // block,),
        out_shape=(jax.ShapeDtypeStruct((rows, width), BF16),) * 2
        + (jax.ShapeDtypeStruct((rows, hidden), BF16),) * 3,
        in_specs=[wide, wide, ANY],
        out_specs=(wide, wide, thin, thin, thin),
        scratch_shapes=[pltpu.VMEM((hidden, width), BF16)] * 3
        + [pltpu.SemaphoreType.DMA((3, planes))],
        compiler_params=pltpu.CompilerParams(vmem_limit_bytes=ALL_VMEM),
        name="feed_forward",
    )(normed, cot, weights)


def ffn_join(planes, part, resid, gain, cot, normed, cot_all, h, gb, ub):
    tok, width = resid.shape
    hidden = h.shape[1]
    units = hidden // planes
    step_units = 256
    turn = units % 128 == 0

    def kernel(
        part_ref,
        v_ref,
        gain_ref,
        cot_ref,
        n_ref,
        c_ref,
        h_ref,
        gb_ref,
        ub_ref,
        grad_ref,
        out_ref,
        gg_ref,
        w_ref,
        gate_ref,
        near_p,
        near_v,
        near_gain,
        near_cot,
        near_n,
        near_c,
        near_h,
        near_g,
        near_u,
        near_sems,
        own,
        sbuf,
        obuf,
        dbuf,
        rbuf,
        s1,
        r1,
        s2,
        r2,
        *g,
    ):
        g, (gw, uw, dw, wsem), ring = g[:5], g[5:9], g[9:]
        z, p = lax.axis_index("z"), lax.axis_index("p")
        pl.semaphore_wait(
            pltpu.get_barrier_semaphore(), plane_greet(z, p) + ring_greet(planes, z, p)
        )
        gg_ref[...] = jnp.zeros_like(gg_ref)
        copies, rings, fetched = [], [], []
        far = (part_ref, gb_ref, n_ref, ub_ref, h_ref, c_ref, v_ref, gain_ref, cot_ref)
        gb_ref, n_ref, ub_ref, h_ref, c_ref = near_g, near_n, near_u, near_h, near_c
        part_ref, v_ref, gain_ref, cot_ref = near_p, near_v, near_gain, near_cot
        near = (part_ref, gb_ref, n_ref, ub_ref, h_ref, c_ref, v_ref, gain_ref, cot_ref)
        for i, (src, dst) in enumerate(zip(far, near)):
            c = pltpu.make_async_copy(src, dst, near_sems.at[i])
            c.start()
            fetched.append(c)
        fetched[0].wait()
        group = step_units // units

        def weight_grad(dst, left, right):
            for n in range(hidden // step_units):
                at = pl.ds(n * step_units, step_units)
                value = contract(left[:, at], right[...], 0, 0, BF16)
                dst[pl.ds(n * group, group)] = value.reshape(group, units, width)

        def hand_out(i, dst):
            c = pltpu.make_async_copy(
                dst, w_ref.at[:, pl.ds(i * units, units)], wsem.at[i]
            )
            c.start()
            copies.append(c)

        def during(step):
            if step == 0:
                for c in fetched[1:]:
                    c.wait()
                weight_grad(gw, gb_ref, n_ref)
                rings.append(ring_reduce(planes, z, p, gw, *ring))
            if step == 1:
                weight_grad(uw, ub_ref, n_ref)
                hand_out(0, uw)
            if step == 2:
                rings[0][0]()
                weight_grad(dw, h_ref, c_ref)
                hand_out(1, dw)

        def finish(at, u):
            v = v_ref[at]
            r = lax.rsqrt(jnp.mean(v * v, axis=-1, keepdims=True) + EPSILON)
            ug = u * gain_ref[...]
            mid = r * ug - v * (r * r * r) * jnp.mean(ug * v, axis=-1, keepdims=True)
            gg_ref[...] += jnp.sum(u * v * r, axis=0, keepdims=True)
            total = cot_ref[at].astype(F32) + mid
            grad_ref[at] = total
            own[at] = total.astype(BF16)

        plane_reduce(
            z, p, part_ref, sbuf, obuf, dbuf, rbuf, s1, r1, s2, r2, finish, 16, during
        )
        plane_gather(z, p, own, rows_at(out_ref, tok), *g, during)
        for c in copies:
            c.wait()
        total = rings[0][1]()
        gate_ref[...] = total.T if turn else total

    return pl.pallas_call(
        kernel,
        out_shape=(
            jax.ShapeDtypeStruct((tok, width), F32),
            jax.ShapeDtypeStruct(part.shape, BF16),
            jax.ShapeDtypeStruct((1, width), F32),
            jax.ShapeDtypeStruct((planes, 2 * units, width), BF16),
            jax.ShapeDtypeStruct((width, units) if turn else (units, width), F32),
        ),
        in_specs=[ANY] * 9,
        out_specs=(VMEM, ANY, VMEM, ANY, VMEM),
        scratch_shapes=[
            *[
                pltpu.VMEM(a.shape, a.dtype)
                for a in (part, resid, gain, cot, normed, cot_all, h, gb, ub)
            ],
            dma(9),
            pltpu.VMEM((tok, width), BF16),
            *reduce_scratch(tok, width),
            *[dma(n) for n in GATHER_SEMS],
            pltpu.SemaphoreType.DMA,
            *[pltpu.VMEM((planes, units, width), BF16)] * 3,
            dma(2),
            *ring_reduce_scratch(planes, units, width),
        ],
        compiler_params=comm_params(3, 56 << 20),
        name="ffn_join",
    )(part, resid, gain, cot, normed, cot_all, h, gb, ub)


def state_chain(planes, through, local, number, forward, left=None, right=None):
    beside = [] if left is None else [left, right]

    def kernel(t_ref, l_ref, *refs):
        far, refs = refs[: len(beside)], refs[len(beside) :]
        out_ref, refs = refs[0], refs[1:]
        if beside:
            grad_ref, got, own, s0, r0, near_l, near_r, sems = refs
            fetched = []
            for i, dst in enumerate((near_l, near_r)):
                c = pltpu.make_async_copy(far[i], dst, sems.at[i])
                c.start()
                fetched.append(c)
        else:
            got, own, s0, r0 = refs
        z, p = lax.axis_index("z"), lax.axis_index("p")
        for r in range(1, planes):
            greet(lax.rem(z + r, planes), p)
        own[0] = t_ref[...].astype(BF16)
        own[1] = l_ref[...].astype(BF16)
        pl.semaphore_wait(pltpu.get_barrier_semaphore(), planes - 1)
        sent = []
        for r in range(1, planes):
            to = lax.rem(z + r, planes)
            c = remote(own, got.at[z], s0.at[r], r0.at[r], to, p)
            c.start()
            sent.append(c)
        if beside:
            for c in fetched:
                c.wait()
            grad_ref[...] = contract(near_l[...], near_r[...], 0, 0, BF16)
        for c in sent:
            c.wait()
        got[z] = own[...]
        state = jnp.zeros_like(l_ref)
        for k in range(planes) if forward else reversed(range(planes)):
            new = got[k, 0].astype(F32) * state + got[k, 1].astype(F32)
            state = jnp.where((k < z) if forward else (k > z), new, state)
        out_ref[...] = state

    shapes, extra = (jax.ShapeDtypeStruct(local.shape, F32),), []
    if beside:
        shapes += (jax.ShapeDtypeStruct((left.shape[1], right.shape[1]), BF16),)
        extra = [*[pltpu.VMEM(a.shape, a.dtype) for a in beside], dma(2)]
    out = pl.pallas_call(
        kernel,
        out_shape=shapes,
        in_specs=[VMEM] * 2 + [ANY] * len(beside),
        out_specs=(VMEM,) * len(shapes),
        scratch_shapes=[
            pltpu.VMEM((planes, 2) + local.shape, BF16),
            pltpu.VMEM((2,) + local.shape, BF16),
            dma(planes),
            dma(planes),
            *extra,
        ],
        compiler_params=comm_params(number, (56 << 20) if beside else None),
        name="state_chain",
    )(through, local, *beside)
    return out if beside else out[0]


def gain_spreads(pers, totals):
    spreads, start = [], 0
    for per, total in zip(pers, totals):
        lane = np.arange(128)[:, None]
        spreads.append(jnp.asarray(lane == start + np.arange(total)[None, :] % per, BF16))
        start += per
    return spreads


def closing(
    planes, part, x, gain, resid_grad, inner_g, slab_g, gains_g, out_part, resid, ffn_g, mixer_g
):
    tok, width = x.shape
    block = inner_g.shape[1]
    height, channels = slab_g.shape
    own = channels // planes
    rank = height - 32 - (RANK + 2 * STATE)
    columns = RANK + 2 * STATE
    units = ffn_g.shape[0] // 2
    turn = units % 128 == 0
    devices = planes * PLANE
    pers = [g.shape[1] // devices for g in gains_g]
    spreads = gain_spreads(pers, [g.shape[1] for g in gains_g])
    operands = (
        part, x, gain, resid_grad, inner_g, slab_g, out_part, resid, ffn_g, mixer_g, *gains_g,
        *spreads,
    )

    def shape(*dims, kind=F32):
        return jax.ShapeDtypeStruct(dims, kind)

    outputs = (
        shape(tok, width),
        shape(*inner_g.shape[1:]),
        shape(own, columns),
        shape(rank, own),
        shape(tok, width, kind=BF16),
        shape(width, units) if turn else shape(units, width),
        shape(units, width),
        shape(*mixer_g.shape),
        *[shape(n, own) for n in (STATE, CONV, 1, 1, 1)],
        *[shape(1, per) for per in pers],
    )

    def kernel(*refs):
        far, refs = refs[: len(operands)], refs[len(operands) :]
        far_outs, refs = refs[: len(outputs)], refs[len(outputs) :]
        one_bufs, out_bufs, refs = refs[:8], refs[8:16], refs[16:]
        hbuf, hs, hr, refs = refs[0], refs[1], refs[2], refs[3:]
        inner_ring, slab_ring, refs = refs[:5], refs[5:10], refs[10:]
        pieces, homed, mixed, os_, or_, refs = *refs[:5], refs[5:]
        gg_ref, gbuf, gs, gr, gown, gbuf2, gs2, gr2, bown = refs[:9]
        near, refs = refs[9 : 9 + len(operands)], refs[9 + len(operands) :]
        near_sems, refs = refs[0], refs[1:]
        near_outs, out_sems = refs[: len(outputs)], refs[len(outputs)]
        out_ref, io_ref, sel_ref, step_ref, bo_ref, up_ref, down_ref, mo_ref = near_outs[:8]
        row_refs, gain_outs = near_outs[8:13], near_outs[13:]
        written = []

        def write(*which):
            for i in which:
                c = pltpu.make_async_copy(near_outs[i], far_outs[i], out_sems.at[i])
                c.start()
                written.append(c)

        fetched = []
        for i in (4, 0, 10, 11, 12, 13, 14, 15, 5, 6, 8, 9, 1, 2, 3, 7):
            c = pltpu.make_async_copy(far[i], near[i], near_sems.at[i])
            c.start()
            fetched.append(c)
        part_ref, x_ref, gain_ref, rg_ref, ig_ref, sg_ref, fp_ref, rm_ref = near[:8]
        ffn_ref, mix_ref = near[8:10]
        z, p = lax.axis_index("z"), lax.axis_index("p")
        column, slot = block_route(z, p)
        to_z, to_p = block_source_of(z, p)
        moves = moves_in(z, p)
        stays = jnp.logical_not(moves)
        gets = jnp.logical_or(column != p, slot != z)
        before = lax.rem(z + planes - 1, planes)
        for k in range(1, PLANE):
            greet(z, xor(p, k))
        for r in range(1, planes):
            greet(lax.rem(z + r, planes), p)

        @pl.when(gets)
        def _():
            greet(slot, column)

        @pl.when(jnp.logical_and(p == PLANE - 1, z < planes - 1))
        def _():
            for q in range(PLANE):
                greet(z + 1, q)

        pl.semaphore_wait(
            pltpu.get_barrier_semaphore(),
            PLANE - 1 + planes - 1 + moves.astype(jnp.int32) + (z > 0).astype(jnp.int32),
        )

        fetched[0].wait()
        relay, inner_total = ring_reduce(planes, z, p, ig_ref, *inner_ring, hold=True)
        for c in fetched[1:9]:
            c.wait()
        z_sent, p_sent, slab = [], [], []
        halo = remote(part_ref.at[pl.ds(0, HALO)], hbuf.at[p], hs, hr.at[p], before, PLANE - 1)

        @pl.when(z > 0)
        def _():
            halo.start()

        def homing(i, src, dst):
            @pl.when(moves)
            def _():
                remote(src, dst, os_.at[i], or_.at[i], to_z, to_p).start()

            @pl.when(stays)
            def _():
                pltpu.make_async_copy(src, dst, or_.at[i]).start()

        def homing_end(i, src, dst):
            pltpu.make_async_copy(src, dst, or_.at[i]).wait()

            @pl.when(moves)
            def _():
                remote(src, dst, os_.at[i], or_.at[i], to_z, to_p).wait_send()


        def during(step):
            if step == 0:
                for k in range(planes):
                    pieces[k] = sg_ref[:, own * k : own * (k + 1)].astype(BF16)
                slab.extend(ring_reduce(planes, z, p, pieces, *slab_ring))
                packed = jnp.zeros((devices, 128), F32)
                for i, per in enumerate(pers):
                    value = near[10 + i][...]
                    at = lax.broadcasted_iota(jnp.int32, (devices, value.shape[1]), 1)
                    low = lax.broadcasted_iota(jnp.int32, at.shape, 0) * per
                    value = jnp.where((at >= low) & (at < low + per), value, 0.0)
                    high = value.astype(BF16)
                    rest = (value - high.astype(F32)).astype(BF16)
                    spread = near[13 + i][...]
                    packed = packed + contract(high, spread, 1, 1) + contract(rest, spread, 1, 1)
                gg_ref[...] = packed.reshape(planes, PLANE, 128)
                for r in range(1, planes):
                    to = lax.rem(z + r, planes)
                    c = remote(gg_ref.at[to], gbuf.at[z], gs.at[r], gr.at[r], to, p)
                    c.start()
                    z_sent.append(c)
                return
            relay()
            for c in z_sent:
                c.wait()
            total = gg_ref[z]
            for r in range(1, planes):
                total = total + gbuf[lax.rem(z + r, planes)]
            gown[...] = total
            for k in range(1, PLANE):
                c = remote(gown, gbuf2.at[k], gs2.at[k], gr2.at[k], z, xor(p, k))
                c.start()
                p_sent.append(c)

        def finish(at, u):
            out_ref[at] = u

        plane_reduce(z, p, part_ref, *one_bufs, finish, 16, during, HALO)

        for c in fetched[9:]:
            c.wait()

        def later(step):
            if step == 0:
                slab[0]()
                if turn:
                    up_ref[...] = ffn_ref[:units].astype(F32).T
                else:
                    up_ref[...] = ffn_ref[:units].astype(F32)
                down_ref[...] = ffn_ref[units:].astype(F32)
                write(5, 6)
                homing(1, mix_ref, mixed)
                return
            bown[...] = slab[1]()
            homing(0, bown, homed)

        def output(at, u):
            bo_ref[at] = (rm_ref[at] + u).astype(BF16)

        plane_reduce(z, p, fp_ref, *out_bufs, output, 16, later)
        write(4)

        @pl.when(jnp.logical_and(p == PLANE - 1, z < planes - 1))
        def _():
            for q in range(PLANE):
                pltpu.make_async_copy(
                    part_ref.at[pl.ds(0, HALO)], hbuf.at[q], hr.at[q]
                ).wait()
            add = hbuf[0].astype(F32)
            for q in range(1, PLANE):
                add = add + hbuf[q].astype(F32)
            out_ref[pl.ds(tok - HALO, HALO)] += add

        @pl.when(z > 0)
        def _():
            halo.wait_send()

        def norm(n, _):
            at = pl.ds(pl.multiple_of(n * 16, 16), 16)
            u = out_ref[at]
            v = x_ref[at].astype(F32)
            r = lax.rsqrt(jnp.mean(v * v, axis=-1, keepdims=True) + EPSILON)
            ug = u * gain_ref[...]
            grad = r * ug - v * (r * r * r) * jnp.mean(ug * v, axis=-1, keepdims=True)
            out_ref[at] = rg_ref[at] + grad
            return 0

        lax.fori_loop(0, tok // 16, norm, 0)
        write(0)

        for c in p_sent:
            c.wait()
        total = gown[...]
        for k in range(1, PLANE):
            total = total + gbuf2[k]
        row = lax.broadcasted_iota(jnp.int32, total.shape, 0)
        mine = jnp.sum(jnp.where(row == p, total, 0.0), axis=0, keepdims=True)
        start = 0
        for ref, per in zip(gain_outs, pers):
            ref[...] = mine[:, start : start + per]
            start += per
        homing_end(1, mix_ref, mixed)
        mo_ref[...] = mixed[...].astype(F32)
        write(7)
        homing_end(0, bown, homed)
        sel_ref[...] = homed[:columns, :].T
        step_ref[...] = homed[columns : columns + rank, :]
        start = columns + rank
        for ref in row_refs:
            ref[...] = homed[start : start + ref.shape[0], :]
            start += ref.shape[0]
        write(2, 3, *range(8, len(outputs)))
        io_ref[...] = inner_total()
        write(1)
        for c in written:
            c.wait()

    one = pltpu.SemaphoreType.DMA
    return pl.pallas_call(
        kernel,
        out_shape=outputs,
        in_specs=[ANY] * len(operands),
        out_specs=(ANY,) * len(outputs),
        scratch_shapes=[
            *reduce_scratch(tok, width),
            *reduce_scratch(tok, width),
            pltpu.VMEM((PLANE, HALO, width), BF16),
            one,
            dma(PLANE),
            *ring_reduce_scratch(planes, block, width),
            *ring_reduce_scratch(planes, height, own),
            pltpu.VMEM((planes, height, own), BF16),
            pltpu.VMEM((height, own), F32),
            pltpu.VMEM(mixer_g.shape, BF16),
            dma(2),
            dma(2),
            pltpu.VMEM((planes, PLANE, 128), F32),
            pltpu.VMEM((planes, PLANE, 128), F32),
            dma(planes),
            dma(planes),
            pltpu.VMEM((PLANE, 128), F32),
            pltpu.VMEM((PLANE, PLANE, 128), F32),
            dma(PLANE),
            dma(PLANE),
            pltpu.VMEM((height, own), F32),
            *[pltpu.VMEM(a.shape, a.dtype) for a in operands],
            dma(len(operands)),
            *[pltpu.VMEM(a.shape, a.dtype) for a in outputs],
            dma(len(outputs)),
        ],
        compiler_params=comm_params(6, ALL_VMEM),
        name="closing",
    )(*operands)


def hand_over(arrays):
    count = len(arrays)

    def kernel(*refs):
        ins, outs, near = refs[:count], refs[count : 2 * count], refs[2 * count : 3 * count]
        in_sems, out_sems = refs[3 * count :]
        fetched, copies = [], []
        for i in range(count):
            c = pltpu.make_async_copy(ins[i], near[i], in_sems.at[i])
            c.start()
            fetched.append(c)
        for i in range(count):
            fetched[i].wait()
            c = pltpu.make_async_copy(near[i], outs[i], out_sems.at[i])
            c.start()
            copies.append(c)
        for c in copies:
            c.wait()

    return pl.pallas_call(
        kernel,
        out_shape=tuple(jax.ShapeDtypeStruct(a.shape, a.dtype) for a in arrays),
        in_specs=[ANY] * count,
        out_specs=(ANY,) * count,
        scratch_shapes=[
            *[pltpu.VMEM(a.shape, a.dtype) for a in arrays],
            dma(count),
            dma(count),
        ],
        compiler_params=SCAN_PARAMS,
        name="hand_over",
    )(*arrays)


CHUNK = 256


def scan_specs(channels, count, backward):
    def at(i):
        return count - 1 - i if backward else i

    return (
        pl.BlockSpec((CHUNK, channels), lambda i: (at(i), 0)),
        lambda part, size: pl.BlockSpec((CHUNK, size * STATE, 128), lambda i: (at(i), part, 0)),
        pl.BlockSpec((CHUNK, STATE, channels), lambda i: (at(i), 0, 0)),
        pl.BlockSpec((STATE, channels), lambda i: (0, 0)),
    )


def rows_of(g, size=GROUP):
    return pl.ds(pl.multiple_of(g * size, size), size)


def across(maps, channels):
    return jnp.concatenate([maps.astype(F32)] * (channels // 128), axis=1)


SCAN_PARAMS = pltpu.CompilerParams(vmem_limit_bytes=ALL_VMEM)


def prepare(proj, gain, step_w, step_b, mixed, keep):
    tokens, columns = proj.shape
    channels = mixed.shape[1]

    def kernel(
        proj_ref, gain_ref, w_ref, b_ref, mixed_ref, keep_ref, step_ref, slope_ref, cut_ref, drive_ref,
        low_ref, maps_ref,
    ):
        v = proj_ref[...]
        mean = group_mean(v * v, group_sums(columns))
        out = v * lax.rsqrt(mean + EPSILON) * gain_ref[...]
        low = out.astype(BF16)
        low_ref[...] = low
        raw = contract(low, w_ref[...], 1, 0) + b_ref[...]
        step = jnp.maximum(raw, 0.0) + jnp.log1p(jnp.exp(-jnp.abs(raw)))
        step_ref[...] = step
        slope_ref[...] = jax.nn.sigmoid(raw)
        drive_ref[...] = step * mixed_ref[...].astype(F32)
        cut_ref[...] = jnp.where(keep_ref[:, CONV - 2 : CONV - 1] > 0.0, step, CUT)

        wide = (2 * STATE, columns)
        pick = lax.broadcasted_iota(jnp.int32, wide, 1) == (
            lax.broadcasted_iota(jnp.int32, wide, 0) + columns - 2 * STATE
        )
        pick = jnp.where(pick, 1.0, 0.0).astype(BF16)
        first = lax.broadcasted_iota(jnp.int32, (2 * columns, 256), 0) < columns
        left = lax.broadcasted_iota(jnp.int32, (2 * columns, 256), 1) < 128
        ones = jnp.where(first == left, 1.0, 0.0).astype(BF16)
        many = 32

        def spread(g, _):
            at = rows_of(g, many)
            rows = low_ref[at, :]
            pairs = []
            for k in range(many // 2):
                pairs.append(
                    jnp.concatenate(
                        [
                            jnp.broadcast_to(rows[k : k + 1], wide) * pick,
                            jnp.broadcast_to(rows[k + many // 2 : k + many // 2 + 1], wide) * pick,
                        ],
                        axis=1,
                    )
                )
            result = jnp.dot(
                jnp.concatenate(pairs, axis=0), ones, preferred_element_type=F32
            ).astype(BF16)
            maps_ref[rows_of(2 * g, many // 2)] = result[:, :128].reshape(many // 2, 2 * STATE, 128)
            maps_ref[rows_of(2 * g + 1, many // 2)] = result[:, 128:].reshape(
                many // 2, 2 * STATE, 128
            )
            return 0

        lax.fori_loop(0, CHUNK // many, spread, 0)

    def tile(size):
        return pl.BlockSpec((CHUNK, size), lambda i: (i, 0))

    def whole(array):
        return pl.BlockSpec(array.shape, lambda i: (0, 0))

    shape = jax.ShapeDtypeStruct((tokens, channels), F32)
    return pl.pallas_call(
        kernel,
        grid=(tokens // CHUNK,),
        out_shape=(
            shape,
            shape,
            shape,
            shape,
            jax.ShapeDtypeStruct((tokens, columns), BF16),
            jax.ShapeDtypeStruct((tokens, 2 * STATE, 128), BF16),
        ),
        in_specs=[
            tile(columns),
            whole(gain),
            whole(step_w),
            whole(step_b),
            tile(channels),
            tile(CONV),
        ],
        out_specs=(
            tile(channels),
            tile(channels),
            tile(channels),
            tile(channels),
            tile(columns),
            pl.BlockSpec((CHUNK, 2 * STATE, 128), lambda i: (i, 0, 0)),
        ),
        compiler_params=SCAN_PARAMS,
        name="prepare",
    )(proj, gain, step_w, step_b, mixed, keep)


def forward_final(step, drive, maps, rate):
    tokens, channels = step.shape
    count = tokens // CHUNK
    rows, cols, _, const = scan_specs(channels, count, False)

    def kernel(step_ref, drive_ref, in_ref, rate_ref, state_ref, through_ref):
        @pl.when(pl.program_id(0) == 0)
        def _():
            state_ref[...] = jnp.zeros_like(state_ref)
            through_ref[...] = jnp.zeros_like(through_ref)

        rate_v = rate_ref[...]

        def body(g, carry):
            h, total = carry
            d8, w8 = step_ref[rows_of(g), :], drive_ref[rows_of(g), :]
            for k in range(GROUP):
                decay = jnp.exp(d8[k : k + 1, :] * rate_v)
                h = decay * h + w8[k : k + 1, :] * across(in_ref[g * GROUP + k], channels)
            return h, total + d8

        h, total = lax.fori_loop(
            0,
            CHUNK // GROUP,
            body,
            (state_ref[...], jnp.zeros((GROUP, channels), F32)),
        )
        state_ref[...] = h
        through_ref[...] += jnp.sum(total, axis=0, keepdims=True)

        @pl.when(pl.program_id(0) == count - 1)
        def _():
            through_ref[...] = jnp.exp(through_ref[...] * rate_v)

    shape = jax.ShapeDtypeStruct(rate.shape, F32)
    return pl.pallas_call(
        kernel,
        grid=(count,),
        out_shape=(shape, shape),
        in_specs=[rows, rows, cols(0, 1), const],
        out_specs=(const, const),
        compiler_params=SCAN_PARAMS,
        name="forward_final",
    )(step, drive, maps, rate)


def forward_all(step, drive, maps, rate, start):
    tokens, channels = step.shape
    count = tokens // CHUNK
    rows, cols, states, const = scan_specs(channels, count, False)

    def kernel(step_ref, drive_ref, maps_ref, rate_ref, start_ref, y_ref, hs_ref, h_sc):
        @pl.when(pl.program_id(0) == 0)
        def _():
            h_sc[...] = start_ref[...]

        rate_v = rate_ref[...]

        def body(g, h):
            d8, w8 = step_ref[rows_of(g), :], drive_ref[rows_of(g), :]
            out = []
            for k in range(GROUP):
                t = g * GROUP + k
                hs_ref[t] = h.astype(BF16)
                decay = jnp.exp(d8[k : k + 1, :] * rate_v)
                h = decay * h + w8[k : k + 1, :] * across(maps_ref[t, :STATE], channels)
                out.append(
                    jnp.sum(h * across(maps_ref[t, STATE:], channels), axis=0, keepdims=True)
                )
            y_ref[rows_of(g), :] = jnp.concatenate(out, axis=0)
            return h

        h_sc[...] = lax.fori_loop(0, CHUNK // GROUP, body, h_sc[...])

    return pl.pallas_call(
        kernel,
        grid=(count,),
        out_shape=(
            jax.ShapeDtypeStruct((tokens, channels), F32),
            jax.ShapeDtypeStruct((tokens, STATE, channels), BF16),
            jax.ShapeDtypeStruct(rate.shape, F32),
        ),
        in_specs=[rows, rows, cols(0, 2), const, const],
        out_specs=(rows, states, const),
        compiler_params=SCAN_PARAMS,
        name="forward_all",
    )(step, drive, maps, rate, start)


def backward_first(step, mix_grad, maps, rate):
    tokens, channels = step.shape
    count = tokens // CHUNK
    rows, cols, _, const = scan_specs(channels, count, True)

    def kernel(step_ref, mix_ref, out_map_ref, rate_ref, out_ref):
        @pl.when(pl.program_id(0) == 0)
        def _():
            out_ref[...] = jnp.zeros_like(out_ref)

        rate_v = rate_ref[...]

        def body(n, q):
            g = CHUNK // GROUP - 1 - n
            d8, m8 = step_ref[rows_of(g), :], mix_ref[rows_of(g), :]
            for k in reversed(range(GROUP)):
                decay = jnp.exp(d8[k : k + 1, :] * rate_v)
                q = decay * (q + m8[k : k + 1, :] * across(out_map_ref[g * GROUP + k], channels))
            return q

        out_ref[...] = lax.fori_loop(0, CHUNK // GROUP, body, out_ref[...])

    return pl.pallas_call(
        kernel,
        grid=(count,),
        out_shape=jax.ShapeDtypeStruct(rate.shape, F32),
        in_specs=[rows, rows, cols(1, 1), const],
        out_specs=const,
        compiler_params=SCAN_PARAMS,
        name="backward_first",
    )(step, mix_grad, maps, rate)


def backward_all(
    step, drive, mix_grad, maps, rate, states_in, state_out, start, slope, mixed, step_w
):
    tokens, channels = step.shape
    columns = step_w.shape[0]
    count = tokens // CHUNK
    rows, cols, states, const = scan_specs(channels, count, True)

    def fold(v):
        total = v[:, :128]
        for i in range(1, channels // 128):
            total = total + v[:, 128 * i : 128 * (i + 1)]
        return total.astype(BF16)

    def kernel(
        step_ref,
        drive_ref,
        mix_ref,
        maps_ref,
        rate_ref,
        hs_ref,
        end_ref,
        start_ref,
        slope_ref,
        mixed_ref,
        sw_ref,
        sb_ref,
        back_ref,
        part_ref,
        extra_ref,
        q_sc,
        dd_sc,
        h_sc,
        sr_ref,
        v_sc,
    ):
        @pl.when(pl.program_id(0) == 0)
        def _():
            q_sc[...] = start_ref[...]
            h_sc[...] = end_ref[...]
            dd_sc[...] = jnp.zeros_like(dd_sc)
            extra_ref[...] = jnp.zeros_like(extra_ref)

        rate_v = rate_ref[...]

        def body(n, carry):
            q, dd, h = carry
            g = CHUNK // GROUP - 1 - n
            at = rows_of(g)
            d8, w8, m8 = step_ref[at, :], drive_ref[at, :], mix_ref[at, :]
            sb, sr = [], []
            for k in reversed(range(GROUP)):
                t = g * GROUP + k
                d, w, m = d8[k : k + 1, :], w8[k : k + 1, :], m8[k : k + 1, :]
                b = across(maps_ref[t, :STATE], channels)
                c = across(maps_ref[t, STATE:], channels)
                decay = jnp.exp(d * rate_v)
                ahead = hs_ref[t].astype(F32)
                kept = decay * ahead
                hbar = q + m * c
                flow = hbar * kept
                q = decay * hbar
                dd = dd + flow * d
                sb.append(jnp.sum(hbar * b, axis=0, keepdims=True))
                sr.append(jnp.sum(flow * rate_v, axis=0, keepdims=True))
                v_sc[t, :STATE] = fold(hbar * w)
                v_sc[t, STATE:] = fold(h * m)
                h = ahead
            sb_ref[at, :] = jnp.concatenate(sb[::-1], axis=0)
            sr_ref[at, :] = jnp.concatenate(sr[::-1], axis=0)
            return q, dd, h

        q, dd, h = lax.fori_loop(0, CHUNK // GROUP, body, (q_sc[...], dd_sc[...], h_sc[...]))
        q_sc[...] = q
        h_sc[...] = h
        dd_sc[...] = dd

        first = lax.broadcasted_iota(jnp.int32, (256, 2 * columns), 0) < 128
        left = lax.broadcasted_iota(jnp.int32, (256, 2 * columns), 1) < columns
        ones = jnp.where(first == left, 1.0, 0.0).astype(BF16)
        shape = (2 * STATE, columns)
        pick = lax.broadcasted_iota(jnp.int32, shape, 1) == (
            lax.broadcasted_iota(jnp.int32, shape, 0) + columns - 2 * STATE
        )
        many = 32

        def lanes(n, _):
            one = v_sc[rows_of(2 * n, many // 2)].reshape(many * STATE, 128)
            two = v_sc[rows_of(2 * n + 1, many // 2)].reshape(many * STATE, 128)
            total = jnp.dot(
                jnp.concatenate([one, two], axis=1), ones, preferred_element_type=F32
            )
            halves = []
            for i in range(2):
                part = total[:, columns * i : columns * (i + 1)].reshape(many // 2, 2 * STATE, columns)
                halves.append(jnp.sum(jnp.where(pick[None], part, 0.0), axis=1))
            at = rows_of(n, many)
            mixed_v = mixed_ref[at, :].astype(F32)
            raw = (mixed_v * sb_ref[at, :] + sr_ref[at, :]) * slope_ref[at, :]
            back = raw.astype(BF16)
            back_ref[at, :] = back
            part_ref[at, :] = contract(back, sw_ref[...], 1, 1) + jnp.concatenate(halves, axis=0)
            extra_ref[STATE : STATE + 1, :] += jnp.sum(raw, axis=0, keepdims=True)
            extra_ref[STATE + 1 : STATE + 2, :] += jnp.sum(
                mix_ref[at, :] * mixed_v, axis=0, keepdims=True
            )
            return 0

        lax.fori_loop(0, CHUNK // many, lanes, 0)

        @pl.when(pl.program_id(0) == count - 1)
        def _():
            extra_ref[:STATE, :] = dd_sc[...] * rate_v

    wide = jax.ShapeDtypeStruct((tokens, channels), F32)
    return pl.pallas_call(
        kernel,
        grid=(count,),
        out_shape=(
            wide,
            jax.ShapeDtypeStruct((tokens, channels), BF16),
            jax.ShapeDtypeStruct((tokens, columns), F32),
            jax.ShapeDtypeStruct((STATE + 8, channels), F32),
        ),
        in_specs=[rows, rows, rows, cols(0, 2), const, states, const, const, rows, rows]
        + [pl.BlockSpec(step_w.shape, lambda i: (0, 0))],
        out_specs=(
            rows,
            rows,
            pl.BlockSpec((CHUNK, columns), lambda i: (count - 1 - i, 0)),
            pl.BlockSpec((STATE + 8, channels), lambda i: (0, 0)),
        ),
        scratch_shapes=[
            pltpu.VMEM((STATE, channels), F32),
            pltpu.VMEM((STATE, channels), F32),
            pltpu.VMEM((STATE, channels), F32),
            pltpu.VMEM((CHUNK, channels), F32),
            pltpu.VMEM((CHUNK, 2 * STATE, 128), BF16),
        ],
        compiler_params=SCAN_PARAMS,
        name="backward_all",
    )(step, drive, mix_grad, maps, rate, states_in, state_out, start, slope, mixed, step_w)


def silu_slope(v):
    s = jax.nn.sigmoid(v)
    return s * (1.0 + v * (1.0 - s))


def turn_back(mixer_back, mixer_w, gate_inner, mix):
    rows, width = mixer_back.shape
    channels = mix.shape[1]

    def kernel(b_ref, w_ref, i_ref, m_ref, mix_ref, gate_ref):
        gated_grad = contract(b_ref[...], w_ref[...], 1, 1)
        gate = i_ref[...]
        s = jax.nn.sigmoid(gate)
        mix_ref[...] = gated_grad * (gate * s)
        gate_ref[...] = (gated_grad * m_ref[...] * (s * (1.0 + gate * (1.0 - s)))).astype(BF16)

    thin = pl.BlockSpec((CHUNK, channels), lambda i: (i, 0))
    const = pl.BlockSpec((channels, width), lambda i: (0, 0))
    return pl.pallas_call(
        kernel,
        grid=(rows // CHUNK,),
        out_shape=(
            jax.ShapeDtypeStruct((rows, channels), F32),
            jax.ShapeDtypeStruct((rows, channels), BF16),
        ),
        in_specs=[pl.BlockSpec((CHUNK, width), lambda i: (i, 0)), const, thin, thin],
        out_specs=(thin, thin),
        compiler_params=SCAN_PARAMS,
        name="turn_back",
    )(mixer_back, mixer_w, gate_inner, mix)


def group_sums(columns):
    row = lax.broadcasted_iota(jnp.int32, (columns, columns), 0)
    col = lax.broadcasted_iota(jnp.int32, (columns, columns), 1)
    edges = (0, RANK, RANK + STATE, RANK + 2 * STATE)
    mean = jnp.zeros((columns, columns), F32)
    for low, high in zip(edges, edges[1:]):
        inside = (row >= low) & (row < high) & (col >= low) & (col < high)
        mean = mean + jnp.where(inside, 1.0, 0.0)
    return mean.astype(BF16)


def group_mean(values, sums):
    lane = lax.broadcasted_iota(jnp.int32, (1, values.shape[1]), 1)
    high = values.astype(BF16)
    rest = (values - high.astype(F32)).astype(BF16)
    total = jnp.dot(high, sums, preferred_element_type=F32) + jnp.dot(
        rest, sums, preferred_element_type=F32
    )
    return total * jnp.where(lane < RANK, 1.0 / RANK, 1.0 / STATE)


def unwind(
    select_grad, proj, gain, select_w, step, map_sum, mix_grad, rest, conv_input, masks,
    gate_back, normed, inner_w, mixed, step_low, step_back, first, extra,
):
    rows, channels = step.shape
    columns = proj.shape[1]
    width = normed.shape[1]
    taps = CONV
    piece = 128
    ops = (
        select_grad, proj, gain, select_w, rest, masks, step, map_sum, mix_grad, conv_input,
        gate_back, inner_w, normed, mixed, step_low, step_back, first, extra,
    )

    def kernel(*refs):
        far, refs = refs[: len(ops)], refs[len(ops) :]
        one_ref, inner_ref, slab_ref, first_ref, gain_ref = refs[:5]
        near, refs = refs[5 : 5 + len(ops)], refs[5 + len(ops) :]
        back, conv_f, pre, ext, one_v, inner_v, sems, outs = refs
        fetched = []
        for i in range(len(ops)):
            c = pltpu.make_async_copy(far[i], near[i], sems.at[i])
            c.start()
            fetched.append(c)
        (
            sg_ref, pr_ref, g_ref, sw_ref, rest_ref, mask_ref, st_ref, ms_ref, mg_ref, ci_ref,
            gb_ref, iw_ref, n_ref, mx_ref, sl_ref, sb_ref, f_ref, e_ref,
        ) = near
        for c in fetched[:4]:
            c.wait()
        sums = group_sums(columns)
        v, u = pr_ref[...], sg_ref[...]
        r = lax.rsqrt(group_mean(v * v, sums) + EPSILON)
        scaled = u * g_ref[...]
        grad = r * scaled - v * (r * r * r) * group_mean(scaled * v, sums)
        gain_ref[...] = jnp.sum(u * v * r, axis=0, keepdims=True) * (1.0 / PLANE)
        back[...] = grad.astype(BF16)
        for c in fetched[4:10]:
            c.wait()
        conv_f[...] = ci_ref[...].astype(F32)
        pre[rows:, :] = jnp.zeros((8, channels), F32)
        weights = [rest_ref[STATE + k : STATE + k + 1, :] for k in range(taps)]
        bias = rest_ref[STATE + taps : STATE + taps + 1, :]
        skip = rest_ref[STATE + taps + 2 : STATE + taps + 3, :]

        def first_pass(n, carry):
            at = rows_of(n, piece)
            window = conv_f[pl.ds(pl.multiple_of(HALO - 8 + n * piece, 8), piece + 8), :]
            mask = mask_ref[at, :]
            total = bias
            seen = []
            for k in range(taps):
                tap = window[8 - taps + 1 + k : 8 - taps + 1 + k + piece]
                if k < taps - 1:
                    tap = tap * mask[:, k : k + 1]
                seen.append(tap)
                total = total + weights[k] * tap
            mixed_grad = (
                st_ref[at, :] * ms_ref[at, :]
                + skip * mg_ref[at, :]
                + jnp.dot(back[at, :], sw_ref[...], preferred_element_type=F32)
            )
            value = mixed_grad * silu_slope(total)
            pre[at, :] = value
            new = [c + jnp.sum(value * t, axis=0, keepdims=True) for c, t in zip(carry, seen)]
            return (*new, carry[taps] + jnp.sum(value, axis=0, keepdims=True))

        zero = jnp.zeros((1, channels), F32)
        conv_sums = lax.fori_loop(0, rows // piece, first_pass, (zero,) * (taps + 1))

        def second_pass(n, _):
            window = pre[pl.ds(pl.multiple_of(n * piece, 8), piece + 8), :]
            mask = mask_ref[pl.ds(pl.multiple_of(n * piece, 8), piece + 8), :]
            total = None
            for k in range(taps):
                part = window
                if k < taps - 1:
                    part = part * mask[:, k : k + 1]
                part = part[taps - 1 - k : taps - 1 - k + piece] * weights[k]
                total = part if total is None else total + part
            ext[pl.ds(pl.multiple_of(HALO + n * piece, 16), piece), :channels] = total.astype(BF16)
            return 0

        lax.fori_loop(0, rows // piece, second_pass, 0)
        window = pre[0:8, :]
        at = lax.broadcasted_iota(jnp.int32, (HALO, channels), 0)
        ahead = jnp.zeros((HALO, channels), F32)
        for k in range(taps - 1):
            part = window * mask_ref[0:8, k : k + 1] * weights[k]
            for t in range(taps - 1 - k):
                row = HALO - taps + 1 + k + t
                ahead = ahead + jnp.where(at == row, part[t : t + 1], 0.0)
        ext[0:HALO, :channels] = ahead.astype(BF16)
        ext[0:HALO, channels:] = jnp.zeros((HALO, channels), BF16)
        for c in fetched[10:]:
            c.wait()
        ext[HALO:, channels:] = gb_ref[...]

        copies = []
        third = 2 * channels // 3
        for n in range(3):
            inner_v[pl.ds(n * third, third), :] = contract(
                ext[:, n * third : (n + 1) * third], n_ref[...], 0, 0, BF16
            )
        c = pltpu.make_async_copy(inner_v, inner_ref, outs.at[0])
        c.start()
        copies.append(c)
        part_rows = (rows + HALO) // 5

        def last_pass(n, total):
            at = rows_of(n, part_rows)
            value = jnp.dot(ext[at, :], iw_ref[...], preferred_element_type=F32).astype(BF16)
            one_v[at, :] = value
            return total + jnp.sum(
                value.astype(F32) * n_ref[at, :].astype(F32), axis=0, keepdims=True
            )

        total = lax.fori_loop(0, 5, last_pass, jnp.zeros((1, width), F32))
        c = pltpu.make_async_copy(one_v, one_ref, outs.at[1])
        c.start()
        copies.append(c)
        first_ref[...] = total / f_ref[...]
        slab_ref[:columns, :] = contract(back[...], mx_ref[...], 0, 0)
        slab_ref[columns : columns + RANK, :] = contract(sl_ref[...], sb_ref[...], 0, 0)[:RANK]
        others = jnp.concatenate(
            [e_ref[:STATE]]
            + list(conv_sums)
            + [e_ref[STATE : STATE + 2], jnp.zeros((16 - taps - 3, channels), F32)],
            axis=0,
        )
        slab_ref[columns + RANK :, :] = others
        for c in copies:
            c.wait()

    one = jax.ShapeDtypeStruct((rows + HALO, width), BF16)
    inner = jax.ShapeDtypeStruct((2 * channels, width), BF16)
    return pl.pallas_call(
        kernel,
        out_shape=(
            one,
            inner,
            jax.ShapeDtypeStruct((columns + RANK + 32, channels), F32),
            jax.ShapeDtypeStruct((1, width), F32),
            jax.ShapeDtypeStruct((1, columns), F32),
        ),
        in_specs=[ANY] * len(ops),
        out_specs=(ANY, ANY, VMEM, VMEM, VMEM),
        scratch_shapes=[
            *[pltpu.VMEM(a.shape, a.dtype) for a in ops],
            pltpu.VMEM((rows, columns), BF16),
            pltpu.VMEM((rows + HALO, channels), F32),
            pltpu.VMEM((rows + 8, channels), F32),
            pltpu.VMEM((rows + HALO, 2 * channels), BF16),
            pltpu.VMEM(one.shape, BF16),
            pltpu.VMEM(inner.shape, BF16),
            dma(len(ops)),
            dma(2),
        ],
        compiler_params=SCAN_PARAMS,
        name="unwind",
    )(*ops)


def contract(left, right, left_dim, right_dim, kind=F32):
    return lax.dot_general(
        left, right, (((left_dim,), (right_dim,)), ((), ())), preferred_element_type=F32
    ).astype(kind)


def on_device(
    planes,
    block_input,
    documents,
    first_gain,
    inner_weight,
    conv_weight,
    conv_bias,
    select_weight,
    select_gain,
    step_weight,
    step_bias,
    decay_log,
    skip_gain,
    mixer_weight,
    second_gain,
    gate_weight,
    up_weight,
    down_weight,
    cotangent,
):
    tok, width = block_input.shape
    devices = planes * PLANE
    rows = PLANE * tok
    z = lax.axis_index("z")
    own_block = mixer_weight.shape[0]
    inner_block = inner_weight.shape[1]
    channels = planes * own_block
    columns = RANK + 2 * STATE
    taps = conv_weight.shape[0]


    (
        x_ext,
        cot_all,
        inners,
        mixer_here,
        select_w,
        step_w,
        rest,
        first_f,
        second_f,
        select_f,
        ffn_own,
    ) = opening(
        planes,
        block_input,
        cotangent,
        inner_weight.T,
        mixer_weight,
        select_weight,
        (
            step_weight,
            decay_log,
            conv_weight,
            conv_bias[None, :],
            step_bias[None, :],
            skip_gain[None, :],
        ),
        (first_gain[None, :], second_gain[None, :], select_gain[None, :]),
        (gate_weight, up_weight, down_weight),
    )
    mixer_w = lax.all_gather(mixer_here, "z", axis=0, tiled=True)
    ffn_w = lax.all_gather(ffn_own, "z", axis=0)
    rate = -jnp.exp(rest[:STATE])
    conv_w = [rest[STATE + k : STATE + k + 1] for k in range(taps)]
    conv_b, step_b, skip = (rest[STATE + taps + k : STATE + taps + k + 1] for k in range(3))
    inner_w = inners.reshape(2 * channels, width)

    padded = jnp.concatenate([jnp.full((taps - 1,), -1, jnp.int32), documents])
    ids = lax.dynamic_slice_in_dim(padded, z * rows, rows + taps - 1, 0)
    here = ids[taps - 1 :]
    same = [(ids[k : k + rows] == here)[:, None] for k in range(taps)]
    masks = jnp.concatenate([m.astype(F32) for m in same], axis=1)
    masks = jnp.pad(masks, ((0, 8), (0, 0)))

    x_f = x_ext.astype(F32)
    r_one = lax.rsqrt(jnp.mean(x_f * x_f, axis=-1, keepdims=True) + EPSILON)
    normed_one = (x_f * r_one * first_f).astype(BF16)
    conv_input = contract(normed_one, inner_w[:channels], 1, 1, BF16)
    gate_inner = contract(normed_one[HALO:], inner_w[channels:], 1, 1)
    shift = HALO - taps + 1
    total = conv_b
    for k in range(taps):
        tap = conv_input[shift + k : shift + k + rows].astype(F32)
        total = total + conv_w[k] * jnp.where(same[k], tap, 0.0)
    mixed_in = jax.nn.silu(total).astype(BF16)
    proj_part = contract(mixed_in, select_w, 1, 1)
    proj = plane_sum(proj_part, 1)
    step, slope, step_cut, drive, step_low, maps = prepare(
        proj, select_f, step_w, step_b, mixed_in, masks
    )
    mixed_f = mixed_in.astype(F32)
    local_final, through = forward_final(step_cut, drive, maps, rate)
    state_in = state_chain(planes, through, local_final, 4, True)
    sums, states, state_out = forward_all(step_cut, drive, maps, rate, state_in)
    mix = sums + skip * mixed_f
    gate_silu = jax.nn.silu(gate_inner)
    gated = (mix * gate_silu).astype(BF16)
    mixer_part = contract(gated, mixer_w, 1, 0, BF16)
    resid_mid, normed_two = mixer_join(
        mixer_part, block_input, second_f
    )

    two_part, out_part, ffn_hidden, gate_back, up_back = feed_forward(
        normed_two, cot_all, ffn_w
    )
    resid_grad, mixer_back, second_grad, ffn_grads, gate_grad = ffn_join(
        planes,
        two_part,
        resid_mid,
        second_f,
        cotangent,
        normed_two,
        cot_all,
        ffn_hidden,
        gate_back,
        up_back,
    )

    mix_grad, gate_back = turn_back(mixer_back, mixer_w, gate_inner, mix)
    ffn_sums = lax.psum_scatter(ffn_grads, "z", scatter_dimension=0, tiled=False)
    local_back = backward_first(step_cut, mix_grad, maps, rate)
    state_back, mixer_grad = state_chain(
        planes, through, local_back, 5, False, gated, mixer_back
    )
    map_sum, step_back, select_part, extra = backward_all(
        step_cut,
        drive,
        mix_grad,
        maps,
        rate,
        states,
        state_out,
        state_back,
        slope,
        mixed_in,
        step_w,
    )
    mixer_grad, ffn_sums, select_part = lax.optimization_barrier(
        (mixer_grad, ffn_sums, select_part)
    )
    mixer_sum = lax.psum_scatter(mixer_grad, "z", scatter_dimension=0, tiled=True)
    select_grad = plane_sum(select_part, 7)
    one_part, inner_grad, slab_grad, first_grad, select_gain_grad = unwind(
        select_grad,
        proj,
        select_f,
        select_w,
        step,
        map_sum,
        mix_grad,
        rest,
        conv_input,
        masks,
        gate_back,
        normed_one,
        inner_w,
        mixed_in,
        step_low,
        step_back,
        first_f,
        extra,
    )
    results = closing(
        planes,
        one_part,
        block_input,
        first_f,
        resid_grad,
        inner_grad.reshape(planes, inner_block, width),
        slab_grad,
        (first_grad, second_grad, select_gain_grad),
        out_part,
        resid_mid,
        ffn_sums,
        mixer_sum,
    )
    (
        input_grad,
        inner_out,
        select_out,
        step_out,
        block_output,
        up_out,
        down_out,
        mixer_out,
        decay_out,
        conv_out,
        conv_b_out,
        step_b_out,
        skip_out,
        first_out,
        second_out,
        gain_out,
        gate_out,
    ) = hand_over((*results, gate_grad))
    return (
        block_output,
        input_grad,
        first_out[0],
        inner_out.T,
        conv_out,
        conv_b_out[0],
        select_out,
        gain_out[0],
        step_out,
        step_b_out[0],
        decay_out,
        skip_out[0],
        mixer_out,
        second_out[0],
        gate_out if gate_out.shape[0] == width else gate_out.T,
        up_out if up_out.shape[0] == width else up_out.T,
        down_out,
    )


def solution(mesh):
    planes = mesh.devices.size // PLANE
    grid = Mesh(mesh.devices.reshape(planes, PLANE), ("z", "p"))
    seq = ("z", "p")
    by_row, by_column, flat = P(seq, None), P(None, seq), P(seq)

    def program(*args):
        return on_device(planes, *args)

    return jax.shard_map(
        program,
        mesh=grid,
        in_specs=(
            by_row,
            P(),
            flat,
            by_column,
            by_column,
            flat,
            by_row,
            flat,
            by_column,
            flat,
            by_column,
            flat,
            by_row,
            flat,
            by_column,
            by_column,
            by_row,
            by_row,
        ),
        out_specs=(
            by_row,
            by_row,
            flat,
            by_column,
            by_column,
            flat,
            by_row,
            flat,
            by_column,
            flat,
            by_column,
            flat,
            by_row,
            flat,
            by_column,
            by_column,
            by_row,
        ),
        check_vma=False,
    )
```

```python
import jax
import jax.numpy as jnp
import numpy as np
from jax import lax
from jax.experimental import pallas as pl
from jax.experimental.pallas import tpu as pltpu
from jax.sharding import Mesh
from jax.sharding import PartitionSpec as P

STATE = 16
RANK = 96
CONV = 4
PLANE = 8
HALO = 16
GROUP = 8
CUT = 1e4
EPSILON = 1e-06
ALL_VMEM = 60 << 20
F32 = jnp.float32
BF16 = jnp.bfloat16
MESH_ID = pl.DeviceIdType.MESH
ANY = pl.BlockSpec(memory_space=pl.ANY)
VMEM = pl.BlockSpec(memory_space=pltpu.VMEM)


def xor(p, k):
    out = p
    for bit in (1, 2, 4):
        if k & bit:
            out = out + bit - 2 * bit * lax.rem(lax.div(out, bit), 2)
    return out


def remote(src, dst, send_sem, recv_sem, z, p):
    return pltpu.make_async_remote_copy(
        src_ref=src,
        dst_ref=dst,
        send_sem=send_sem,
        recv_sem=recv_sem,
        device_id={"z": z, "p": p},
        device_id_type=MESH_ID,
    )


def greet(z, p):
    pl.semaphore_signal(
        pltpu.get_barrier_semaphore(), inc=1, device_id={"z": z, "p": p}, device_id_type=MESH_ID
    )


def comm_params(number, vmem=None):
    return pltpu.CompilerParams(
        collective_id=number, has_side_effects=True, vmem_limit_bytes=vmem
    )


def dma(*shape):
    return pltpu.SemaphoreType.DMA(shape)


def block_route(z, p):
    half = lax.div(PLANE * z + p, 2)
    return lax.rem(half, PLANE), 2 * lax.div(half, PLANE) + lax.rem(p, 2)


def block_source_of(z, p):
    k = 2 * (PLANE * lax.div(z, 2) + p) + lax.rem(z, 2)
    return lax.div(k, PLANE), lax.rem(k, PLANE)


def moves_in(z, p):
    zs, ps = block_source_of(z, p)
    return jnp.logical_or(zs != z, ps != p)


def plane_greet(z, p):
    for k in (1, 2, 4):
        greet(z, xor(p, k))
    return 3


def plane_reduce(
    z, p, part, sbuf, obuf, dbuf, rbuf, s1, r1, s2, r2, finish, rows, during=None, base=0
):
    sib, near, side = xor(p, 1), xor(p, 2), xor(p, 4)
    tok = sbuf.shape[1]
    half = tok // 2
    top, low = pl.ds(0, half), pl.ds(half, half)
    wide = (part.dtype == F32) and (obuf.dtype == F32)
    align = min(rows, 16)

    def block(q):
        return part.at[pl.ds(pl.multiple_of(base + q * tok, align), tok)]

    def piece(q, at):
        return part[pl.ds(pl.multiple_of(base + q * tok + at.start, align), rows), :].astype(F32)

    def chunks(length, body):
        def step(n, _):
            body(pl.ds(pl.multiple_of(n * rows, rows), rows))
            return 0

        lax.fori_loop(0, length // rows, step, 0)

    def put(value):
        return value if wide else value.astype(obuf.dtype)

    first = []
    for i, k in enumerate((6, 2, 4, 0)):
        c = remote(block(xor(sib, k)), sbuf.at[i], s1.at[i], r1.at[i], z, sib)
        c.start()
        first.append(c)
    second = []

    def send(i, src, dst, to):
        c = remote(src, dst, s2.at[i], r2.at[i], z, to)
        c.start()
        second.append(c)
        return c

    for i, k in enumerate((6, 2, 4)):
        first[i].wait_recv()
        q = xor(p, k)

        def add(at, i=i, q=q):
            obuf[i, at] = put(piece(q, at) + sbuf[i, at].astype(F32))

        chunks(tok, add)
        if k == 6:
            far_top = send(0, obuf.at[0, top], dbuf.at[0], near)
            far_low = send(1, obuf.at[0, low], dbuf.at[1], side)
        elif k == 2:
            send(2, obuf.at[1, top], rbuf.at[0, top], near)
        else:
            send(3, obuf.at[2, low], rbuf.at[1, low], side)
    if during is not None:
        during(0)
    far_top.wait_recv()

    def join_top(at):
        obuf[2, at] = put(obuf[2, at].astype(F32) + dbuf[0, at].astype(F32))

    chunks(half, join_top)
    send(4, obuf.at[2, top], rbuf.at[1, top], side)
    far_low.wait_recv()

    def join_low(at):
        down = pl.ds(pl.multiple_of(at.start + half, rows), rows)
        obuf[1, down] = put(obuf[1, down].astype(F32) + dbuf[1, at].astype(F32))

    chunks(half, join_low)
    send(5, obuf.at[1, low], rbuf.at[0, low], near)
    if during is not None:
        during(1)
    first[3].wait_recv()
    for c in second[2:]:
        c.wait_recv()

    def last(at):
        total = piece(p, at) + sbuf[3, at].astype(F32)
        finish(at, total + rbuf[0, at].astype(F32) + rbuf[1, at].astype(F32))

    chunks(tok, last)
    for c in first + second:
        c.wait_send()


class PlaneGather:
    def __init__(self, z, p, own, place, ss, rs, fs, fr, ls):
        self.z, self.p, self.own, self.place = z, p, own, place
        self.ss, self.rs, self.fs, self.fr, self.ls = ss, rs, fs, fr, ls
        self.sent, self.passed = [], []
        half = own.shape[0] // 2
        self.top, self.low = pl.ds(0, half), pl.ds(half, half)

    def send(self, src, dst, to):
        i = len(self.sent)
        c = remote(src, dst, self.ss.at[i], self.rs.at[i], self.z, to)
        c.start()
        self.sent.append(c)

    def pass_on(self, q):
        i = len(self.passed)
        place = self.place(q)
        c = remote(place, place, self.fs.at[i], self.fr.at[i], self.z, xor(self.p, 1))
        c.start()
        self.passed.append(c)

    def start(self):
        p, own = self.p, self.own
        near, side = xor(p, 2), xor(p, 4)
        self.send(own.at[self.top], self.place(p).at[self.top], near)
        self.send(own.at[self.low], self.place(p).at[self.low], side)
        self.send(own.at[self.low], self.place(p).at[self.low], near)
        self.send(own.at[self.top], self.place(p).at[self.top], side)
        self.send(own, self.place(p), xor(p, 1))
        self.local = pltpu.make_async_copy(own, self.place(p), self.ls)
        self.local.start()

    def relay(self):
        near, side = xor(self.p, 2), xor(self.p, 4)
        self.sent[0].wait_recv()
        self.send(self.place(near).at[self.top], self.place(near).at[self.top], side)
        self.sent[1].wait_recv()
        self.send(self.place(side).at[self.low], self.place(side).at[self.low], near)

    def finish(self):
        near, side, far = xor(self.p, 2), xor(self.p, 4), xor(self.p, 6)
        self.sent[2].wait_recv()
        self.pass_on(near)
        self.sent[3].wait_recv()
        self.pass_on(side)
        self.sent[5].wait_recv()
        self.sent[6].wait_recv()
        self.pass_on(far)
        self.sent[4].wait_recv()
        for c in self.passed:
            c.wait_recv()
        for c in self.sent + self.passed:
            c.wait_send()
        self.local.wait()


def plane_gather(z, p, own, place, ss, rs, fs, fr, ls, during=None):
    gather = PlaneGather(z, p, own, place, ss, rs, fs, fr, ls)
    gather.start()
    if during is not None:
        during(2)
    gather.relay()
    gather.finish()


def rows_at(ref, tok, base=0):
    return lambda q: ref.at[pl.ds(pl.multiple_of(base + q * tok, 16), tok)]


GATHER_SEMS = (7, 7, 3, 3)
REDUCE_SEMS = (4, 4, 6, 6)


def ring_gather(planes, z, p, own, out, ss, rs, ls):
    local = pltpu.make_async_copy(own, out.at[z], ls)
    local.start()
    sent = []

    def send(i, src, dst, r):
        c = remote(src, dst, ss.at[i], rs.at[i], lax.rem(z + r, planes), p)
        c.start()
        sent.append(c)
        return c

    if planes != 4:
        for r in range(1, planes):
            send(r, own, out.at[z], r)
        return local, sent, lambda: None
    half = own.shape[0] // 2
    top, low = pl.ds(0, half), pl.ds(half, half)
    up = send(0, own.at[top], out.at[z, top], 1)
    down = send(1, own.at[low], out.at[z, low], 3)

    def relay():
        before, after = lax.rem(z + 3, 4), lax.rem(z + 1, 4)
        send(2, own.at[low], out.at[z, low], 1)
        send(3, own.at[top], out.at[z, top], 3)
        up.wait_recv()
        send(4, out.at[before, top], out.at[before, top], 1)
        down.wait_recv()
        send(5, out.at[after, low], out.at[after, low], 3)

    return local, sent, relay


def ring_finish(local, sent, relayed):
    for i, c in enumerate(sent):
        if not (relayed and i < 2):
            c.wait_recv()
        c.wait_send()
    local.wait()


def ring_reduce(planes, z, p, src, ibuf, fbuf, mbuf, ss, rs, hold=False):
    half = src.shape[1] // 2
    top, low = pl.ds(0, half), pl.ds(half, half)
    before, after = lax.rem(z + planes - 1, planes), lax.rem(z + 1, planes)
    sent = []

    def send(i, part, dst, r):
        c = remote(part, dst, ss.at[i], rs.at[i], lax.rem(z + r, planes), p)
        c.start()
        sent.append(c)

    def near():
        send(2, src.at[after, low], ibuf.at[0, low], 1)
        send(3, src.at[before, top], ibuf.at[1, top], 3)

    if planes == 4:
        far = lax.rem(z + 2, 4)
        send(0, src.at[far, top], fbuf.at[0], 1)
        send(1, src.at[far, low], fbuf.at[1], 3)
        if not hold:
            near()
    else:
        for r in range(1, planes):
            send(r, src.at[lax.rem(z + r, planes)], ibuf.at[r], r)

    def relay():
        if planes == 4:
            if hold:
                near()
            sent[0].wait_recv()
            mbuf[0] = (src[after, top].astype(F32) + fbuf[0].astype(F32)).astype(mbuf.dtype)
            send(4, mbuf.at[0], ibuf.at[0, top], 1)
            sent[1].wait_recv()
            mbuf[1] = (src[before, low].astype(F32) + fbuf[1].astype(F32)).astype(mbuf.dtype)
            send(5, mbuf.at[1], ibuf.at[1, low], 3)

    def finish():
        for i, c in enumerate(sent):
            if not (planes == 4 and i < 2):
                c.wait_recv()
            c.wait_send()
        total = src[z].astype(F32)
        for k in range(2) if planes == 4 else range(1, planes):
            total = total + ibuf[k].astype(F32)
        return total

    return relay, finish


def ring_reduce_scratch(planes, block, width, kind=BF16):
    return [
        pltpu.VMEM((2 if planes == 4 else planes, block, width), kind),
        pltpu.VMEM((2, block // 2, width), kind),
        pltpu.VMEM((2, block // 2, width), kind),
        dma(ring_sems(planes)),
        dma(ring_sems(planes)),
    ]


def ring_greet(planes, z, p):
    for r in range(1, planes):
        greet(lax.rem(z + r, planes), p)
    return planes - 1


def ring_sems(planes):
    return max(6, planes)


TRIO = 8


def join_gain(planes, gains_ref, row, per, spread):
    total = spread.shape[1]
    at = lax.broadcasted_iota(jnp.int32, (PLANE, total), 1)
    column = lax.broadcasted_iota(jnp.int32, (PLANE, total), 0)
    joined = jnp.zeros((PLANE, total), F32)
    for k in range(planes):
        piece = jnp.concatenate([gains_ref[q, k, row : row + 1, :] for q in range(PLANE)], axis=0)
        wide = jnp.dot(piece.astype(BF16), spread, preferred_element_type=F32)
        low = (column + PLANE * k) * per
        joined = joined + jnp.where((at >= low) & (at < low + per), wide, 0.0)
    return jnp.sum(joined, axis=0, keepdims=True)


def opening(planes, x, cot, inner, mixer, select, small, gains, ffn):
    tok, width = x.shape
    relayed = planes == 4
    block = mixer.shape[0]
    columns = select.shape[1]
    channels = planes * block
    places, filled = [], 0
    for array in small:
        places.append((filled, filled + array.shape[0]))
        filled += array.shape[0]
    rank = small[0].shape[0]
    states = small[1].shape[0]
    height = rank + 32 + columns
    pers = [g.shape[1] for g in gains]
    spreads = []
    for per, total in ((pers[0], width), (pers[2], columns)):
        spreads.append(
            jnp.asarray(np.arange(128)[:, None] == np.arange(total)[None, :] % per, BF16)
        )
    turn = ffn[0].shape[1] % 128 == 0
    units = ffn[2].shape[0]
    if not turn:
        ffn = [ffn[0].T, ffn[1].T, ffn[2]]

    def kernel(*refs):
        wide_refs, select_ref = refs[:4], refs[4]
        small_refs, gain_refs, refs = refs[5:11], refs[11:14], refs[14:]
        spread_refs, ffn_refs, refs = refs[:2], refs[2:5], refs[5:]
        xg_ref, cots_ref, inners_ref, home_ref = refs[:4]
        select_out, step_ref, rest_ref, first_ref, second_ref, sel_ref, own_ref = refs[4:11]
        refs = refs[11:]
        own_wide, own_small, got_small, smalls, own_gain, gains_all = refs[:6]
        refs = refs[6:]
        near_small, near_gain, near_spread, near_ffn = refs[:6], refs[6:9], refs[9:11], refs[11:13]
        near_select, ffn_out, refs = refs[13], refs[14], refs[15:]
        near_wide, near_down, wide_sems, refs = refs[:4], refs[4], refs[5], refs[6:]
        x_ref, cot_ref, inner_ref, mixer_ref = near_wide
        x_sems, c_sems, refs = refs[:5], refs[5:10], refs[10:]
        hs, hr, gs, gr, gs2, gr2, ins, inr, inl, ps, pr, bs, br, bl, near_sems, out_sems = refs

        z, p = lax.axis_index("z"), lax.axis_index("p")
        column, slot = block_route(z, p)
        from_z, from_p = block_source_of(z, p)
        moves = jnp.logical_or(column != p, slot != z)
        stays = jnp.logical_not(moves)
        after = lax.rem(z + 1, planes)
        for k in range(1, PLANE):
            greet(z, xor(p, k))
        for r in range(1, planes):
            greet(lax.rem(z + r, planes), p)

        @pl.when(moves_in(z, p))
        def _():
            greet(from_z, from_p)

        landing = []
        for i in (2, 0, 1, 3):
            c = pltpu.make_async_copy(wide_refs[i], near_wide[i], wide_sems.at[i])
            c.start()
            landing.append(c)
        down_in = pltpu.make_async_copy(ffn_refs[2], near_down, wide_sems.at[4])
        down_in.start()
        fetched = []
        far_refs = list(small_refs) + list(gain_refs) + [select_ref]
        far_refs += list(spread_refs) + list(ffn_refs[:2])
        near_refs = list(near_small) + list(near_gain) + [near_select]
        near_refs += list(near_spread) + list(near_ffn)
        for i, (src, dst) in enumerate(zip(far_refs, near_refs)):
            c = pltpu.make_async_copy(src, dst, near_sems.at[i])
            c.start()
            fetched.append(c)
        own_wide[...] = jnp.zeros_like(own_wide)
        own_gain[...] = jnp.zeros_like(own_gain)
        pl.semaphore_wait(
            pltpu.get_barrier_semaphore(),
            PLANE - 1 + planes - 1 + moves.astype(jnp.int32),
        )

        for c in landing:
            c.wait()
        local, sent, relay = ring_gather(planes, z, p, inner_ref, inners_ref, ins, inr, inl)

        homes = [
            (own_small, got_small, ps.at[0], pr.at[0]),
            (mixer_ref, home_ref, ps.at[1], pr.at[1]),
        ]

        def homing(items):
            for src, dst, send, recv in items:

                @pl.when(moves)
                def _():
                    remote(src, dst, send, recv, slot, column).start()

                @pl.when(stays)
                def _():
                    pltpu.make_async_copy(src, dst, recv).start()

        def place(q):
            return xg_ref.at[pl.ds(pl.multiple_of(HALO + q * tok, HALO), tok)]

        gain_out, gain_on, block_ring, ffn_sent = [], [], [], []

        def first_sends(_):
            for c in fetched[:10]:
                c.wait()
            for (low, high), ref in zip(places, near_small):
                own_wide[low:high, :] = ref[...].astype(F32)
            own_small[: rank + 32] = own_wide[...].astype(BF16)
            own_small[rank + 32 :] = near_select[...].astype(F32).T.astype(BF16)
            for i, ref in enumerate(near_gain):
                own_gain[i : i + 1, : pers[i]] = ref[...].astype(F32)
            homing(homes[:1])
            for r in range(1, planes):
                c = remote(
                    own_gain, gains_all.at[p, z], gs.at[r], gr.at[r], lax.rem(z + r, planes), p
                )
                c.start()
                gain_out.append(c)
            gains_all[p, z] = own_gain[...]

        x_gather = PlaneGather(z, p, x_ref, place, *x_sems)
        cot_gather = PlaneGather(z, p, cot_ref, rows_at(cots_ref, tok), *c_sems)
        x_gather.start()
        first_sends(0)
        x_gather.relay()
        relay()
        cot_gather.start()
        homing(homes[1:])

        src, dst, _, recv = homes[0]
        pltpu.make_async_copy(src, dst, recv).wait()
        block_ring.extend(ring_gather(planes, z, p, got_small, smalls, bs, br, bl))
        for c in gain_out:
            c.wait_recv()
        for k in range(1, PLANE):
            c = remote(gains_all.at[p], gains_all.at[p], gs2.at[k], gr2.at[k], z, xor(p, k))
            c.start()
            gain_on.append(c)
        x_gather.finish()

        edge = xg_ref.at[pl.ds(PLANE * tok, HALO)]
        front = xg_ref.at[pl.ds(0, HALO)]

        @pl.when(z < planes - 1)
        def _():
            remote(edge, front, hs, hr, after, p).start()

        @pl.when(z == 0)
        def _():
            pltpu.make_async_copy(edge, front, hr).start()

        cot_gather.relay()
        block_ring[2]()
        down_in.wait()
        down_out = pltpu.make_async_copy(
            near_down, own_ref.at[pl.ds(2 * units, units)], out_sems.at[2]
        )
        down_out.start()
        for c in fetched[10:]:
            c.wait()
        for i in range(2):
            if turn:
                ffn_out[i] = near_ffn[i][...].T
            else:
                ffn_out[i] = near_ffn[i][...]
            c = pltpu.make_async_copy(
                ffn_out.at[i], own_ref.at[pl.ds(i * units, units)], out_sems.at[i]
            )
            c.start()
            ffn_sent.append(c)
        for c in gain_on:
            c.wait_recv()
        first_ref[...] = join_gain(planes, gains_all, 0, pers[0], near_spread[0][...])
        second_ref[...] = join_gain(planes, gains_all, 1, pers[1], near_spread[0][...])
        sel_ref[...] = join_gain(planes, gains_all, 2, pers[2], near_spread[1][...])
        cot_gather.finish()
        down_out.wait()
        for c in ffn_sent:
            c.wait()
        pltpu.make_async_copy(edge, front, hr).wait()

        @pl.when(z < planes - 1)
        def _():
            remote(edge, front, hs, hr, after, p).wait_send()

        ring_finish(block_ring[0], block_ring[1], relayed)
        joined = jnp.concatenate([smalls[k].astype(F32) for k in range(planes)], axis=1)
        row = lax.broadcasted_iota(jnp.int32, (rank + 32, channels), 0)
        step_ref[...] = jnp.where(row < rank, joined[: rank + 32], 0.0).astype(BF16)
        rest_ref[...] = joined[rank : rank + 32]
        select_out[...] = joined[rank + 32 :].astype(BF16)
        pltpu.make_async_copy(mixer_ref, home_ref, pr.at[1]).wait()

        @pl.when(moves)
        def _():
            for src, dst, send, recv in homes:
                remote(src, dst, send, recv, slot, column).wait_send()

        for c in gain_out + gain_on:
            c.wait_send()
        ring_finish(local, sent, relayed)

    def shape(*dims, kind=BF16):
        return jax.ShapeDtypeStruct(dims, kind)

    one = pltpu.SemaphoreType.DMA
    return pl.pallas_call(
        kernel,
        out_shape=(
            shape(HALO + PLANE * tok, width),
            shape(PLANE * tok, width),
            shape(planes, *inner.shape),
            shape(*mixer.shape),
            shape(columns, channels),
            shape(rank + 32, channels),
            shape(32, channels, kind=F32),
            shape(1, width, kind=F32),
            shape(1, width, kind=F32),
            shape(1, columns, kind=F32),
            shape(3 * units, width),
        ),
        in_specs=[ANY] * 19,
        out_specs=(ANY,) * 4 + (VMEM,) * 6 + (ANY,),
        scratch_shapes=[
            pltpu.VMEM((rank + 32, block), F32),
            pltpu.VMEM((height, block), BF16),
            pltpu.VMEM((height, block), BF16),
            pltpu.VMEM((planes, height, block), BF16),
            pltpu.VMEM((TRIO, 128), F32),
            pltpu.VMEM((PLANE, planes, TRIO, 128), F32),
            *[pltpu.VMEM(a.shape, a.dtype) for a in (*small, *gains, *spreads, *ffn[:2])],
            pltpu.VMEM(select.shape, BF16),
            pltpu.VMEM((2, units, width), BF16),
            *[pltpu.VMEM(a.shape, a.dtype) for a in (x, cot, inner, mixer, ffn[2])],
            dma(5),
            *[dma(n) for n in GATHER_SEMS],
            one,
            *[dma(n) for n in GATHER_SEMS],
            one,
            one,
            one,
            dma(planes),
            dma(planes),
            dma(PLANE),
            dma(PLANE),
            dma(ring_sems(planes)),
            dma(ring_sems(planes)),
            one,
            dma(2),
            dma(2),
            dma(ring_sems(planes)),
            dma(ring_sems(planes)),
            one,
            dma(14),
            dma(3),
        ],
        compiler_params=comm_params(0, ALL_VMEM),
        name="opening",
    )(x, cot, inner, mixer, select, *small, *gains, *spreads, *ffn)


def plane_sum(part, number, kind=F32):
    tok, columns = part.shape[0] // PLANE, part.shape[1]

    def kernel(part_ref, out_ref, own, *refs):
        bufs, g = refs[:8], refs[8:]
        z, p = lax.axis_index("z"), lax.axis_index("p")
        pl.semaphore_wait(pltpu.get_barrier_semaphore(), plane_greet(z, p))

        def finish(at, value):
            own[at] = value.astype(kind)

        plane_reduce(z, p, part_ref, *bufs, finish, tok // 2)
        plane_gather(z, p, own, rows_at(out_ref, tok), *g)

    return pl.pallas_call(
        kernel,
        out_shape=jax.ShapeDtypeStruct(part.shape, kind),
        in_specs=[VMEM],
        out_specs=VMEM,
        scratch_shapes=[
            pltpu.VMEM((tok, columns), kind),
            pltpu.VMEM((4, tok, columns), F32),
            *reduce_scratch(tok, columns, kind)[1:],
            *[dma(n) for n in GATHER_SEMS],
            pltpu.SemaphoreType.DMA,
        ],
        compiler_params=comm_params(number, 32 << 20),
        name="plane_sum",
    )(part)


def reduce_scratch(tok, width, kind=BF16):
    return [
        pltpu.VMEM((4, tok, width), kind),
        pltpu.VMEM((3, tok, width), kind),
        pltpu.VMEM((2, tok // 2, width), kind),
        pltpu.VMEM((2, tok, width), kind),
        *[dma(n) for n in REDUCE_SEMS],
    ]


def mixer_join(part, x, gain):
    tok, width = x.shape

    def kernel(
        part_ref,
        x_ref,
        gain_ref,
        resid_ref,
        out_ref,
        own,
        sbuf,
        obuf,
        dbuf,
        rbuf,
        s1,
        r1,
        s2,
        r2,
        *g,
    ):
        z, p = lax.axis_index("z"), lax.axis_index("p")
        pl.semaphore_wait(pltpu.get_barrier_semaphore(), plane_greet(z, p))

        def finish(at, total):
            v = total + x_ref[at].astype(F32)
            resid_ref[at] = v
            r = lax.rsqrt(jnp.mean(v * v, axis=-1, keepdims=True) + EPSILON)
            own[at] = (v * r * gain_ref[...]).astype(BF16)

        plane_reduce(z, p, part_ref, sbuf, obuf, dbuf, rbuf, s1, r1, s2, r2, finish, 16)
        plane_gather(z, p, own, rows_at(out_ref, tok), *g)

    return pl.pallas_call(
        kernel,
        out_shape=(
            jax.ShapeDtypeStruct((tok, width), F32),
            jax.ShapeDtypeStruct(part.shape, BF16),
        ),
        in_specs=[VMEM] * 3,
        out_specs=(VMEM, VMEM),
        scratch_shapes=[
            pltpu.VMEM((tok, width), BF16),
            *reduce_scratch(tok, width),
            *[dma(n) for n in GATHER_SEMS],
            pltpu.SemaphoreType.DMA,
        ],
        compiler_params=comm_params(2, 32 << 20),
        name="mixer_join",
    )(part, x, gain)


def feed_forward(normed, cot, weights):
    rows, width = normed.shape
    planes, triple, _ = weights.shape
    units = triple // 3
    hidden = planes * units
    block = 512

    def kernel(n_ref, c_ref, w_ref, two_ref, out_ref, h_ref, gb_ref, ub_ref, gw, uw, dw, sem):
        @pl.when(pl.program_id(0) == 0)
        def _():
            copies = []
            for i, dst in enumerate((gw, uw, dw)):
                for k in range(planes):
                    copies.append(
                        pltpu.make_async_copy(
                            w_ref.at[k, pl.ds(i * units, units)],
                            dst.at[pl.ds(k * units, units)],
                            sem.at[i, k],
                        )
                    )
            for c in copies:
                c.start()
            for c in copies:
                c.wait()

        n, c = n_ref[...], c_ref[...]
        gate = contract(n, gw[...], 1, 1)
        up = contract(n, uw[...], 1, 1)
        back = contract(c, dw[...], 1, 1)
        s = jax.nn.sigmoid(gate)
        silu = gate * s
        h = (silu * up).astype(BF16)
        gb = (back * up * (s * (1.0 + gate * (1.0 - s)))).astype(BF16)
        ub = (back * silu).astype(BF16)
        h_ref[...] = h
        gb_ref[...] = gb
        ub_ref[...] = ub
        two_ref[...] = (contract(gb, gw[...], 1, 0) + contract(ub, uw[...], 1, 0)).astype(BF16)
        out_ref[...] = contract(h, dw[...], 1, 0, BF16)

    wide = pl.BlockSpec((block, width), lambda i: (i, 0))
    thin = pl.BlockSpec((block, hidden), lambda i: (i, 0))
    return pl.pallas_call(
        kernel,
        grid=(rows // block,),
        out_shape=(jax.ShapeDtypeStruct((rows, width), BF16),) * 2
        + (jax.ShapeDtypeStruct((rows, hidden), BF16),) * 3,
        in_specs=[wide, wide, ANY],
        out_specs=(wide, wide, thin, thin, thin),
        scratch_shapes=[pltpu.VMEM((hidden, width), BF16)] * 3
        + [pltpu.SemaphoreType.DMA((3, planes))],
        compiler_params=pltpu.CompilerParams(vmem_limit_bytes=ALL_VMEM),
        name="feed_forward",
    )(normed, cot, weights)


def ffn_join(planes, part, resid, gain, cot, normed, cot_all, h, gb, ub):
    tok, width = resid.shape
    hidden = h.shape[1]
    units = hidden // planes
    step_units = 256
    turn = units % 128 == 0

    def kernel(
        part_ref,
        v_ref,
        gain_ref,
        cot_ref,
        n_ref,
        c_ref,
        h_ref,
        gb_ref,
        ub_ref,
        grad_ref,
        out_ref,
        gg_ref,
        w_ref,
        gate_ref,
        near_p,
        near_v,
        near_gain,
        near_cot,
        near_n,
        near_c,
        near_h,
        near_g,
        near_u,
        near_sems,
        own,
        sbuf,
        obuf,
        dbuf,
        rbuf,
        s1,
        r1,
        s2,
        r2,
        *g,
    ):
        g, (gw, uw, dw, wsem), ring = g[:5], g[5:9], g[9:]
        z, p = lax.axis_index("z"), lax.axis_index("p")
        pl.semaphore_wait(
            pltpu.get_barrier_semaphore(), plane_greet(z, p) + ring_greet(planes, z, p)
        )
        gg_ref[...] = jnp.zeros_like(gg_ref)
        copies, rings, fetched = [], [], []
        far = (part_ref, gb_ref, n_ref, ub_ref, h_ref, c_ref, v_ref, gain_ref, cot_ref)
        gb_ref, n_ref, ub_ref, h_ref, c_ref = near_g, near_n, near_u, near_h, near_c
        part_ref, v_ref, gain_ref, cot_ref = near_p, near_v, near_gain, near_cot
        near = (part_ref, gb_ref, n_ref, ub_ref, h_ref, c_ref, v_ref, gain_ref, cot_ref)
        for i, (src, dst) in enumerate(zip(far, near)):
            c = pltpu.make_async_copy(src, dst, near_sems.at[i])
            c.start()
            fetched.append(c)
        fetched[0].wait()
        group = step_units // units

        def weight_grad(dst, left, right):
            for n in range(hidden // step_units):
                at = pl.ds(n * step_units, step_units)
                value = contract(left[:, at], right[...], 0, 0, BF16)
                dst[pl.ds(n * group, group)] = value.reshape(group, units, width)

        def hand_out(i, dst):
            c = pltpu.make_async_copy(
                dst, w_ref.at[:, pl.ds(i * units, units)], wsem.at[i]
            )
            c.start()
            copies.append(c)

        def during(step):
            if step == 0:
                for c in fetched[1:]:
                    c.wait()
                weight_grad(gw, gb_ref, n_ref)
                rings.append(ring_reduce(planes, z, p, gw, *ring))
            if step == 1:
                weight_grad(uw, ub_ref, n_ref)
                hand_out(0, uw)
            if step == 2:
                rings[0][0]()
                weight_grad(dw, h_ref, c_ref)
                hand_out(1, dw)

        def finish(at, u):
            v = v_ref[at]
            r = lax.rsqrt(jnp.mean(v * v, axis=-1, keepdims=True) + EPSILON)
            ug = u * gain_ref[...]
            mid = r * ug - v * (r * r * r) * jnp.mean(ug * v, axis=-1, keepdims=True)
            gg_ref[...] += jnp.sum(u * v * r, axis=0, keepdims=True)
            total = cot_ref[at].astype(F32) + mid
            grad_ref[at] = total
            own[at] = total.astype(BF16)

        plane_reduce(
            z, p, part_ref, sbuf, obuf, dbuf, rbuf, s1, r1, s2, r2, finish, 16, during
        )
        plane_gather(z, p, own, rows_at(out_ref, tok), *g, during)
        for c in copies:
            c.wait()
        total = rings[0][1]()
        gate_ref[...] = total.T if turn else total

    return pl.pallas_call(
        kernel,
        out_shape=(
            jax.ShapeDtypeStruct((tok, width), F32),
            jax.ShapeDtypeStruct(part.shape, BF16),
            jax.ShapeDtypeStruct((1, width), F32),
            jax.ShapeDtypeStruct((planes, 2 * units, width), BF16),
            jax.ShapeDtypeStruct((width, units) if turn else (units, width), F32),
        ),
        in_specs=[ANY] * 9,
        out_specs=(VMEM, ANY, VMEM, ANY, VMEM),
        scratch_shapes=[
            *[
                pltpu.VMEM(a.shape, a.dtype)
                for a in (part, resid, gain, cot, normed, cot_all, h, gb, ub)
            ],
            dma(9),
            pltpu.VMEM((tok, width), BF16),
            *reduce_scratch(tok, width),
            *[dma(n) for n in GATHER_SEMS],
            pltpu.SemaphoreType.DMA,
            *[pltpu.VMEM((planes, units, width), BF16)] * 3,
            dma(2),
            *ring_reduce_scratch(planes, units, width),
        ],
        compiler_params=comm_params(3, 56 << 20),
        name="ffn_join",
    )(part, resid, gain, cot, normed, cot_all, h, gb, ub)


def state_chain(planes, through, local, number, forward, left=None, right=None):
    beside = [] if left is None else [left, right]

    def kernel(t_ref, l_ref, *refs):
        far, refs = refs[: len(beside)], refs[len(beside) :]
        out_ref, refs = refs[0], refs[1:]
        if beside:
            grad_ref, got, own, s0, r0, near_l, near_r, sems = refs
            fetched = []
            for i, dst in enumerate((near_l, near_r)):
                c = pltpu.make_async_copy(far[i], dst, sems.at[i])
                c.start()
                fetched.append(c)
        else:
            got, own, s0, r0 = refs
        z, p = lax.axis_index("z"), lax.axis_index("p")
        for r in range(1, planes):
            greet(lax.rem(z + r, planes), p)
        own[0] = t_ref[...].astype(BF16)
        own[1] = l_ref[...].astype(BF16)
        pl.semaphore_wait(pltpu.get_barrier_semaphore(), planes - 1)
        sent = []
        for r in range(1, planes):
            to = lax.rem(z + r, planes)
            c = remote(own, got.at[z], s0.at[r], r0.at[r], to, p)
            c.start()
            sent.append(c)
        if beside:
            for c in fetched:
                c.wait()
            grad_ref[...] = contract(near_l[...], near_r[...], 0, 0, BF16)
        for c in sent:
            c.wait()
        got[z] = own[...]
        state = jnp.zeros_like(l_ref)
        for k in range(planes) if forward else reversed(range(planes)):
            new = got[k, 0].astype(F32) * state + got[k, 1].astype(F32)
            state = jnp.where((k < z) if forward else (k > z), new, state)
        out_ref[...] = state

    shapes, extra = (jax.ShapeDtypeStruct(local.shape, F32),), []
    if beside:
        shapes += (jax.ShapeDtypeStruct((left.shape[1], right.shape[1]), BF16),)
        extra = [*[pltpu.VMEM(a.shape, a.dtype) for a in beside], dma(2)]
    out = pl.pallas_call(
        kernel,
        out_shape=shapes,
        in_specs=[VMEM] * 2 + [ANY] * len(beside),
        out_specs=(VMEM,) * len(shapes),
        scratch_shapes=[
            pltpu.VMEM((planes, 2) + local.shape, BF16),
            pltpu.VMEM((2,) + local.shape, BF16),
            dma(planes),
            dma(planes),
            *extra,
        ],
        compiler_params=comm_params(number, (56 << 20) if beside else None),
        name="state_chain",
    )(through, local, *beside)
    return out if beside else out[0]


def gain_spreads(pers, totals):
    spreads, start = [], 0
    for per, total in zip(pers, totals):
        lane = np.arange(128)[:, None]
        spreads.append(jnp.asarray(lane == start + np.arange(total)[None, :] % per, BF16))
        start += per
    return spreads


def closing(
    planes, part, x, gain, resid_grad, inner_g, slab_g, gains_g, out_part, resid, ffn_g, mixer_g
):
    tok, width = x.shape
    block = inner_g.shape[1]
    height, channels = slab_g.shape
    own = channels // planes
    rank = height - 32 - (RANK + 2 * STATE)
    columns = RANK + 2 * STATE
    units = ffn_g.shape[0] // 2
    turn = units % 128 == 0
    devices = planes * PLANE
    pers = [g.shape[1] // devices for g in gains_g]
    spreads = gain_spreads(pers, [g.shape[1] for g in gains_g])
    operands = (
        part, x, gain, resid_grad, inner_g, slab_g, out_part, resid, ffn_g, mixer_g, *gains_g,
        *spreads,
    )

    def shape(*dims, kind=F32):
        return jax.ShapeDtypeStruct(dims, kind)

    outputs = (
        shape(tok, width),
        shape(*inner_g.shape[1:]),
        shape(own, columns),
        shape(rank, own),
        shape(tok, width, kind=BF16),
        shape(width, units) if turn else shape(units, width),
        shape(units, width),
        shape(*mixer_g.shape),
        *[shape(n, own) for n in (STATE, CONV, 1, 1, 1)],
        *[shape(1, per) for per in pers],
    )

    def kernel(*refs):
        far, refs = refs[: len(operands)], refs[len(operands) :]
        far_outs, refs = refs[: len(outputs)], refs[len(outputs) :]
        one_bufs, out_bufs, refs = refs[:8], refs[8:16], refs[16:]
        hbuf, hsum, hgot, hs, hr, refs = *refs[:5], refs[5:]
        inner_ring, slab_ring, refs = refs[:5], refs[5:10], refs[10:]
        pieces, homed, mixed, os_, or_, refs = *refs[:5], refs[5:]
        gg_ref, gbuf, gs, gr, gown, gbuf2, gs2, gr2, bown = refs[:9]
        near, refs = refs[9 : 9 + len(operands)], refs[9 + len(operands) :]
        near_sems, refs = refs[0], refs[1:]
        near_outs, out_sems = refs[: len(outputs)], refs[len(outputs)]
        out_ref, io_ref, sel_ref, step_ref, bo_ref, up_ref, down_ref, mo_ref = near_outs[:8]
        row_refs, gain_outs = near_outs[8:13], near_outs[13:]
        written = []

        def write(*which):
            for i in which:
                c = pltpu.make_async_copy(near_outs[i], far_outs[i], out_sems.at[i])
                c.start()
                written.append(c)

        fetched = []
        for i in (4, 0, 10, 11, 12, 13, 14, 15, 5, 6, 8, 9, 1, 2, 3, 7):
            c = pltpu.make_async_copy(far[i], near[i], near_sems.at[i])
            c.start()
            fetched.append(c)
        part_ref, x_ref, gain_ref, rg_ref, ig_ref, sg_ref, fp_ref, rm_ref = near[:8]
        ffn_ref, mix_ref = near[8:10]
        z, p = lax.axis_index("z"), lax.axis_index("p")
        column, slot = block_route(z, p)
        to_z, to_p = block_source_of(z, p)
        moves = moves_in(z, p)
        stays = jnp.logical_not(moves)
        gets = jnp.logical_or(column != p, slot != z)
        before = lax.rem(z + planes - 1, planes)
        for k in range(1, PLANE):
            greet(z, xor(p, k))
        for r in range(1, planes):
            greet(lax.rem(z + r, planes), p)

        @pl.when(gets)
        def _():
            greet(slot, column)

        pl.semaphore_wait(
            pltpu.get_barrier_semaphore(),
            PLANE - 1 + planes - 1 + moves.astype(jnp.int32),
        )

        fetched[0].wait()
        relay, inner_total = ring_reduce(planes, z, p, ig_ref, *inner_ring, hold=True)
        for c in fetched[1:9]:
            c.wait()
        z_sent, p_sent, slab = [], [], []
        halo = remote(part_ref.at[pl.ds(0, HALO)], hbuf.at[p], hs.at[0], hr.at[p], z, PLANE - 1)
        halo_on = remote(hsum, hgot, hs.at[1], hr.at[PLANE], before, PLANE - 1)
        inside = jnp.logical_and(z > 0, p < PLANE - 1)
        gathers = jnp.logical_and(z > 0, p == PLANE - 1)

        @pl.when(inside)
        def _():
            halo.start()

        def homing(i, src, dst):
            @pl.when(moves)
            def _():
                remote(src, dst, os_.at[i], or_.at[i], to_z, to_p).start()

            @pl.when(stays)
            def _():
                pltpu.make_async_copy(src, dst, or_.at[i]).start()

        def homing_end(i, src, dst):
            pltpu.make_async_copy(src, dst, or_.at[i]).wait()

            @pl.when(moves)
            def _():
                remote(src, dst, os_.at[i], or_.at[i], to_z, to_p).wait_send()


        def during(step):
            if step == 0:
                for k in range(planes):
                    pieces[k] = sg_ref[:, own * k : own * (k + 1)].astype(BF16)
                slab.extend(ring_reduce(planes, z, p, pieces, *slab_ring))
                packed = jnp.zeros((devices, 128), F32)
                for i, per in enumerate(pers):
                    value = near[10 + i][...]
                    at = lax.broadcasted_iota(jnp.int32, (devices, value.shape[1]), 1)
                    low = lax.broadcasted_iota(jnp.int32, at.shape, 0) * per
                    value = jnp.where((at >= low) & (at < low + per), value, 0.0)
                    high = value.astype(BF16)
                    rest = (value - high.astype(F32)).astype(BF16)
                    spread = near[13 + i][...]
                    packed = packed + contract(high, spread, 1, 1) + contract(rest, spread, 1, 1)
                gg_ref[...] = packed.reshape(planes, PLANE, 128)
                for r in range(1, planes):
                    to = lax.rem(z + r, planes)
                    c = remote(gg_ref.at[to], gbuf.at[z], gs.at[r], gr.at[r], to, p)
                    c.start()
                    z_sent.append(c)
                return
            relay()

            @pl.when(gathers)
            def _():
                add = part_ref[pl.ds(0, HALO), :].astype(F32)
                for q in range(PLANE - 1):
                    pltpu.make_async_copy(
                        part_ref.at[pl.ds(0, HALO)], hbuf.at[q], hr.at[q]
                    ).wait()
                    add = add + hbuf[q].astype(F32)
                hsum[...] = add.astype(BF16)
                halo_on.start()

            for c in z_sent:
                c.wait()
            total = gg_ref[z]
            for r in range(1, planes):
                total = total + gbuf[lax.rem(z + r, planes)]
            gown[...] = total
            for k in range(1, PLANE):
                c = remote(gown, gbuf2.at[k], gs2.at[k], gr2.at[k], z, xor(p, k))
                c.start()
                p_sent.append(c)

        def finish(at, u):
            out_ref[at] = u

        plane_reduce(z, p, part_ref, *one_bufs, finish, 16, during, HALO)

        for c in fetched[9:]:
            c.wait()

        def later(step):
            if step == 0:
                slab[0]()
                if turn:
                    up_ref[...] = ffn_ref[:units].astype(F32).T
                else:
                    up_ref[...] = ffn_ref[:units].astype(F32)
                down_ref[...] = ffn_ref[units:].astype(F32)
                write(5, 6)
                homing(1, mix_ref, mixed)
                return
            bown[...] = slab[1]().astype(BF16)
            homing(0, bown, homed)

        def output(at, u):
            bo_ref[at] = (rm_ref[at] + u).astype(BF16)

        plane_reduce(z, p, fp_ref, *out_bufs, output, 16, later)
        write(4)

        @pl.when(jnp.logical_and(p == PLANE - 1, z < planes - 1))
        def _():
            pltpu.make_async_copy(hsum, hgot, hr.at[PLANE]).wait()
            out_ref[pl.ds(tok - HALO, HALO)] += hgot[...].astype(F32)

        @pl.when(inside)
        def _():
            halo.wait_send()

        @pl.when(gathers)
        def _():
            halo_on.wait_send()

        def norm(n, _):
            at = pl.ds(pl.multiple_of(n * 16, 16), 16)
            u = out_ref[at]
            v = x_ref[at].astype(F32)
            r = lax.rsqrt(jnp.mean(v * v, axis=-1, keepdims=True) + EPSILON)
            ug = u * gain_ref[...]
            grad = r * ug - v * (r * r * r) * jnp.mean(ug * v, axis=-1, keepdims=True)
            out_ref[at] = rg_ref[at] + grad
            return 0

        lax.fori_loop(0, tok // 16, norm, 0)
        write(0)

        for c in p_sent:
            c.wait()
        total = gown[...]
        for k in range(1, PLANE):
            total = total + gbuf2[k]
        row = lax.broadcasted_iota(jnp.int32, total.shape, 0)
        mine = jnp.sum(jnp.where(row == p, total, 0.0), axis=0, keepdims=True)
        start = 0
        for ref, per in zip(gain_outs, pers):
            ref[...] = mine[:, start : start + per]
            start += per
        homing_end(1, mix_ref, mixed)
        mo_ref[...] = mixed[...].astype(F32)
        write(7)
        homing_end(0, bown, homed)
        small = homed[...].astype(F32)
        sel_ref[...] = small[:columns, :].T
        step_ref[...] = small[columns : columns + rank, :]
        start = columns + rank
        for ref in row_refs:
            ref[...] = small[start : start + ref.shape[0], :]
            start += ref.shape[0]
        write(2, 3, *range(8, len(outputs)))
        io_ref[...] = inner_total()
        write(1)
        for c in written:
            c.wait()

    one = pltpu.SemaphoreType.DMA
    return pl.pallas_call(
        kernel,
        out_shape=outputs,
        in_specs=[ANY] * len(operands),
        out_specs=(ANY,) * len(outputs),
        scratch_shapes=[
            *reduce_scratch(tok, width),
            *reduce_scratch(tok, width),
            pltpu.VMEM((PLANE, HALO, width), BF16),
            pltpu.VMEM((HALO, width), BF16),
            pltpu.VMEM((HALO, width), BF16),
            dma(2),
            dma(PLANE + 1),
            *ring_reduce_scratch(planes, block, width),
            *ring_reduce_scratch(planes, height, own),
            pltpu.VMEM((planes, height, own), BF16),
            pltpu.VMEM((height, own), BF16),
            pltpu.VMEM(mixer_g.shape, BF16),
            dma(2),
            dma(2),
            pltpu.VMEM((planes, PLANE, 128), F32),
            pltpu.VMEM((planes, PLANE, 128), F32),
            dma(planes),
            dma(planes),
            pltpu.VMEM((PLANE, 128), F32),
            pltpu.VMEM((PLANE, PLANE, 128), F32),
            dma(PLANE),
            dma(PLANE),
            pltpu.VMEM((height, own), BF16),
            *[pltpu.VMEM(a.shape, a.dtype) for a in operands],
            dma(len(operands)),
            *[pltpu.VMEM(a.shape, a.dtype) for a in outputs],
            dma(len(outputs)),
        ],
        compiler_params=comm_params(6, ALL_VMEM),
        name="closing",
    )(*operands)


def hand_over(arrays):
    count = len(arrays)

    def kernel(*refs):
        ins, outs, near = refs[:count], refs[count : 2 * count], refs[2 * count : 3 * count]
        in_sems, out_sems = refs[3 * count :]
        fetched, copies = [], []
        for i in range(count):
            c = pltpu.make_async_copy(ins[i], near[i], in_sems.at[i])
            c.start()
            fetched.append(c)
        for i in range(count):
            fetched[i].wait()
            c = pltpu.make_async_copy(near[i], outs[i], out_sems.at[i])
            c.start()
            copies.append(c)
        for c in copies:
            c.wait()

    return pl.pallas_call(
        kernel,
        out_shape=tuple(jax.ShapeDtypeStruct(a.shape, a.dtype) for a in arrays),
        in_specs=[ANY] * count,
        out_specs=(ANY,) * count,
        scratch_shapes=[
            *[pltpu.VMEM(a.shape, a.dtype) for a in arrays],
            dma(count),
            dma(count),
        ],
        compiler_params=SCAN_PARAMS,
        name="hand_over",
    )(*arrays)


CHUNK = 256


def scan_specs(channels, count, backward):
    def at(i):
        return count - 1 - i if backward else i

    return (
        pl.BlockSpec((CHUNK, channels), lambda i: (at(i), 0)),
        lambda part, size: pl.BlockSpec((CHUNK, size * STATE, 128), lambda i: (at(i), part, 0)),
        pl.BlockSpec((CHUNK, STATE, channels), lambda i: (at(i), 0, 0)),
        pl.BlockSpec((STATE, channels), lambda i: (0, 0)),
    )


def rows_of(g, size=GROUP):
    return pl.ds(pl.multiple_of(g * size, size), size)


def across(maps, channels):
    return jnp.concatenate([maps.astype(F32)] * (channels // 128), axis=1)


SCAN_PARAMS = pltpu.CompilerParams(vmem_limit_bytes=ALL_VMEM)


def prepare(proj, gain, step_w, step_b, mixed, keep):
    tokens, columns = proj.shape
    channels = mixed.shape[1]

    def kernel(
        proj_ref, gain_ref, w_ref, b_ref, mixed_ref, keep_ref, step_ref, slope_ref, cut_ref, drive_ref,
        low_ref, maps_ref,
    ):
        v = proj_ref[...]
        mean = group_mean(v * v, group_sums(columns))
        out = v * lax.rsqrt(mean + EPSILON) * gain_ref[...]
        low = out.astype(BF16)
        low_ref[...] = low
        raw = contract(low, w_ref[...], 1, 0) + b_ref[...]
        step = jnp.maximum(raw, 0.0) + jnp.log1p(jnp.exp(-jnp.abs(raw)))
        step_ref[...] = step
        slope_ref[...] = jax.nn.sigmoid(raw)
        drive_ref[...] = step * mixed_ref[...].astype(F32)
        cut_ref[...] = jnp.where(keep_ref[:, CONV - 2 : CONV - 1] > 0.0, step, CUT)

        wide = (2 * STATE, columns)
        pick = lax.broadcasted_iota(jnp.int32, wide, 1) == (
            lax.broadcasted_iota(jnp.int32, wide, 0) + columns - 2 * STATE
        )
        pick = jnp.where(pick, 1.0, 0.0).astype(BF16)
        first = lax.broadcasted_iota(jnp.int32, (2 * columns, 256), 0) < columns
        left = lax.broadcasted_iota(jnp.int32, (2 * columns, 256), 1) < 128
        ones = jnp.where(first == left, 1.0, 0.0).astype(BF16)
        many = 32

        def spread(g, _):
            at = rows_of(g, many)
            rows = low_ref[at, :]
            pairs = []
            for k in range(many // 2):
                pairs.append(
                    jnp.concatenate(
                        [
                            jnp.broadcast_to(rows[k : k + 1], wide) * pick,
                            jnp.broadcast_to(rows[k + many // 2 : k + many // 2 + 1], wide) * pick,
                        ],
                        axis=1,
                    )
                )
            result = jnp.dot(
                jnp.concatenate(pairs, axis=0), ones, preferred_element_type=F32
            ).astype(BF16)
            maps_ref[rows_of(2 * g, many // 2)] = result[:, :128].reshape(many // 2, 2 * STATE, 128)
            maps_ref[rows_of(2 * g + 1, many // 2)] = result[:, 128:].reshape(
                many // 2, 2 * STATE, 128
            )
            return 0

        lax.fori_loop(0, CHUNK // many, spread, 0)

    def tile(size):
        return pl.BlockSpec((CHUNK, size), lambda i: (i, 0))

    def whole(array):
        return pl.BlockSpec(array.shape, lambda i: (0, 0))

    shape = jax.ShapeDtypeStruct((tokens, channels), F32)
    return pl.pallas_call(
        kernel,
        grid=(tokens // CHUNK,),
        out_shape=(
            shape,
            shape,
            shape,
            shape,
            jax.ShapeDtypeStruct((tokens, columns), BF16),
            jax.ShapeDtypeStruct((tokens, 2 * STATE, 128), BF16),
        ),
        in_specs=[
            tile(columns),
            whole(gain),
            whole(step_w),
            whole(step_b),
            tile(channels),
            tile(CONV),
        ],
        out_specs=(
            tile(channels),
            tile(channels),
            tile(channels),
            tile(channels),
            tile(columns),
            pl.BlockSpec((CHUNK, 2 * STATE, 128), lambda i: (i, 0, 0)),
        ),
        compiler_params=SCAN_PARAMS,
        name="prepare",
    )(proj, gain, step_w, step_b, mixed, keep)


def forward_final(step, drive, maps, rate):
    tokens, channels = step.shape
    count = tokens // CHUNK
    rows, cols, _, const = scan_specs(channels, count, False)

    def kernel(step_ref, drive_ref, in_ref, rate_ref, state_ref, through_ref):
        @pl.when(pl.program_id(0) == 0)
        def _():
            state_ref[...] = jnp.zeros_like(state_ref)
            through_ref[...] = jnp.zeros_like(through_ref)

        rate_v = rate_ref[...]

        def body(g, carry):
            h, total = carry
            d8, w8 = step_ref[rows_of(g), :], drive_ref[rows_of(g), :]
            for k in range(GROUP):
                decay = jnp.exp(d8[k : k + 1, :] * rate_v)
                h = decay * h + w8[k : k + 1, :] * across(in_ref[g * GROUP + k], channels)
            return h, total + d8

        h, total = lax.fori_loop(
            0,
            CHUNK // GROUP,
            body,
            (state_ref[...], jnp.zeros((GROUP, channels), F32)),
        )
        state_ref[...] = h
        through_ref[...] += jnp.sum(total, axis=0, keepdims=True)

        @pl.when(pl.program_id(0) == count - 1)
        def _():
            through_ref[...] = jnp.exp(through_ref[...] * rate_v)

    shape = jax.ShapeDtypeStruct(rate.shape, F32)
    return pl.pallas_call(
        kernel,
        grid=(count,),
        out_shape=(shape, shape),
        in_specs=[rows, rows, cols(0, 1), const],
        out_specs=(const, const),
        compiler_params=SCAN_PARAMS,
        name="forward_final",
    )(step, drive, maps, rate)


def forward_all(step, drive, maps, rate, start):
    tokens, channels = step.shape
    count = tokens // CHUNK
    rows, cols, states, const = scan_specs(channels, count, False)

    def kernel(step_ref, drive_ref, maps_ref, rate_ref, start_ref, y_ref, hs_ref, h_sc):
        @pl.when(pl.program_id(0) == 0)
        def _():
            h_sc[...] = start_ref[...]

        rate_v = rate_ref[...]

        def body(g, h):
            d8, w8 = step_ref[rows_of(g), :], drive_ref[rows_of(g), :]
            out = []
            for k in range(GROUP):
                t = g * GROUP + k
                hs_ref[t] = h.astype(BF16)
                decay = jnp.exp(d8[k : k + 1, :] * rate_v)
                h = decay * h + w8[k : k + 1, :] * across(maps_ref[t, :STATE], channels)
                out.append(
                    jnp.sum(h * across(maps_ref[t, STATE:], channels), axis=0, keepdims=True)
                )
            y_ref[rows_of(g), :] = jnp.concatenate(out, axis=0)
            return h

        h_sc[...] = lax.fori_loop(0, CHUNK // GROUP, body, h_sc[...])

    return pl.pallas_call(
        kernel,
        grid=(count,),
        out_shape=(
            jax.ShapeDtypeStruct((tokens, channels), F32),
            jax.ShapeDtypeStruct((tokens, STATE, channels), BF16),
            jax.ShapeDtypeStruct(rate.shape, F32),
        ),
        in_specs=[rows, rows, cols(0, 2), const, const],
        out_specs=(rows, states, const),
        compiler_params=SCAN_PARAMS,
        name="forward_all",
    )(step, drive, maps, rate, start)


def backward_first(step, mix_grad, maps, rate):
    tokens, channels = step.shape
    count = tokens // CHUNK
    rows, cols, _, const = scan_specs(channels, count, True)

    def kernel(step_ref, mix_ref, out_map_ref, rate_ref, out_ref):
        @pl.when(pl.program_id(0) == 0)
        def _():
            out_ref[...] = jnp.zeros_like(out_ref)

        rate_v = rate_ref[...]

        def body(n, q):
            g = CHUNK // GROUP - 1 - n
            d8, m8 = step_ref[rows_of(g), :], mix_ref[rows_of(g), :]
            for k in reversed(range(GROUP)):
                decay = jnp.exp(d8[k : k + 1, :] * rate_v)
                q = decay * (q + m8[k : k + 1, :] * across(out_map_ref[g * GROUP + k], channels))
            return q

        out_ref[...] = lax.fori_loop(0, CHUNK // GROUP, body, out_ref[...])

    return pl.pallas_call(
        kernel,
        grid=(count,),
        out_shape=jax.ShapeDtypeStruct(rate.shape, F32),
        in_specs=[rows, rows, cols(1, 1), const],
        out_specs=const,
        compiler_params=SCAN_PARAMS,
        name="backward_first",
    )(step, mix_grad, maps, rate)


def backward_all(
    step, drive, mix_grad, maps, rate, states_in, state_out, start, slope, mixed, step_w
):
    tokens, channels = step.shape
    columns = step_w.shape[0]
    count = tokens // CHUNK
    rows, cols, states, const = scan_specs(channels, count, True)

    def fold(v):
        total = v[:, :128]
        for i in range(1, channels // 128):
            total = total + v[:, 128 * i : 128 * (i + 1)]
        return total.astype(BF16)

    def kernel(
        step_ref,
        drive_ref,
        mix_ref,
        maps_ref,
        rate_ref,
        hs_ref,
        end_ref,
        start_ref,
        slope_ref,
        mixed_ref,
        sw_ref,
        sb_ref,
        back_ref,
        part_ref,
        extra_ref,
        q_sc,
        dd_sc,
        h_sc,
        sr_ref,
        v_sc,
    ):
        @pl.when(pl.program_id(0) == 0)
        def _():
            q_sc[...] = start_ref[...]
            h_sc[...] = end_ref[...]
            dd_sc[...] = jnp.zeros_like(dd_sc)
            extra_ref[...] = jnp.zeros_like(extra_ref)

        rate_v = rate_ref[...]

        def body(n, carry):
            q, dd, h = carry
            g = CHUNK // GROUP - 1 - n
            at = rows_of(g)
            d8, w8, m8 = step_ref[at, :], drive_ref[at, :], mix_ref[at, :]
            sb, sr = [], []
            for k in reversed(range(GROUP)):
                t = g * GROUP + k
                d, w, m = d8[k : k + 1, :], w8[k : k + 1, :], m8[k : k + 1, :]
                b = across(maps_ref[t, :STATE], channels)
                c = across(maps_ref[t, STATE:], channels)
                decay = jnp.exp(d * rate_v)
                ahead = hs_ref[t].astype(F32)
                kept = decay * ahead
                hbar = q + m * c
                flow = hbar * kept
                q = decay * hbar
                dd = dd + flow * d
                sb.append(jnp.sum(hbar * b, axis=0, keepdims=True))
                sr.append(jnp.sum(flow * rate_v, axis=0, keepdims=True))
                v_sc[t, :STATE] = fold(hbar * w)
                v_sc[t, STATE:] = fold(h * m)
                h = ahead
            sb_ref[at, :] = jnp.concatenate(sb[::-1], axis=0)
            sr_ref[at, :] = jnp.concatenate(sr[::-1], axis=0)
            return q, dd, h

        q, dd, h = lax.fori_loop(0, CHUNK // GROUP, body, (q_sc[...], dd_sc[...], h_sc[...]))
        q_sc[...] = q
        h_sc[...] = h
        dd_sc[...] = dd

        first = lax.broadcasted_iota(jnp.int32, (256, 2 * columns), 0) < 128
        left = lax.broadcasted_iota(jnp.int32, (256, 2 * columns), 1) < columns
        ones = jnp.where(first == left, 1.0, 0.0).astype(BF16)
        shape = (2 * STATE, columns)
        pick = lax.broadcasted_iota(jnp.int32, shape, 1) == (
            lax.broadcasted_iota(jnp.int32, shape, 0) + columns - 2 * STATE
        )
        many = 32

        def lanes(n, _):
            one = v_sc[rows_of(2 * n, many // 2)].reshape(many * STATE, 128)
            two = v_sc[rows_of(2 * n + 1, many // 2)].reshape(many * STATE, 128)
            total = jnp.dot(
                jnp.concatenate([one, two], axis=1), ones, preferred_element_type=F32
            )
            halves = []
            for i in range(2):
                part = total[:, columns * i : columns * (i + 1)].reshape(many // 2, 2 * STATE, columns)
                halves.append(jnp.sum(jnp.where(pick[None], part, 0.0), axis=1))
            at = rows_of(n, many)
            mixed_v = mixed_ref[at, :].astype(F32)
            raw = (mixed_v * sb_ref[at, :] + sr_ref[at, :]) * slope_ref[at, :]
            back = raw.astype(BF16)
            back_ref[at, :] = back
            part_ref[at, :] = contract(back, sw_ref[...], 1, 1) + jnp.concatenate(halves, axis=0)
            extra_ref[STATE : STATE + 1, :] += jnp.sum(raw, axis=0, keepdims=True)
            extra_ref[STATE + 1 : STATE + 2, :] += jnp.sum(
                mix_ref[at, :] * mixed_v, axis=0, keepdims=True
            )
            return 0

        lax.fori_loop(0, CHUNK // many, lanes, 0)

        @pl.when(pl.program_id(0) == count - 1)
        def _():
            extra_ref[:STATE, :] = dd_sc[...] * rate_v

    wide = jax.ShapeDtypeStruct((tokens, channels), F32)
    return pl.pallas_call(
        kernel,
        grid=(count,),
        out_shape=(
            wide,
            jax.ShapeDtypeStruct((tokens, channels), BF16),
            jax.ShapeDtypeStruct((tokens, columns), F32),
            jax.ShapeDtypeStruct((STATE + 8, channels), F32),
        ),
        in_specs=[rows, rows, rows, cols(0, 2), const, states, const, const, rows, rows]
        + [pl.BlockSpec(step_w.shape, lambda i: (0, 0))],
        out_specs=(
            rows,
            rows,
            pl.BlockSpec((CHUNK, columns), lambda i: (count - 1 - i, 0)),
            pl.BlockSpec((STATE + 8, channels), lambda i: (0, 0)),
        ),
        scratch_shapes=[
            pltpu.VMEM((STATE, channels), F32),
            pltpu.VMEM((STATE, channels), F32),
            pltpu.VMEM((STATE, channels), F32),
            pltpu.VMEM((CHUNK, channels), F32),
            pltpu.VMEM((CHUNK, 2 * STATE, 128), BF16),
        ],
        compiler_params=SCAN_PARAMS,
        name="backward_all",
    )(step, drive, mix_grad, maps, rate, states_in, state_out, start, slope, mixed, step_w)


def silu_slope(v):
    s = jax.nn.sigmoid(v)
    return s * (1.0 + v * (1.0 - s))


def turn_back(mixer_back, mixer_w, gate_inner, mix):
    rows, width = mixer_back.shape
    channels = mix.shape[1]

    def kernel(b_ref, w_ref, i_ref, m_ref, mix_ref, gate_ref):
        gated_grad = contract(b_ref[...], w_ref[...], 1, 1)
        gate = i_ref[...]
        s = jax.nn.sigmoid(gate)
        mix_ref[...] = gated_grad * (gate * s)
        gate_ref[...] = (gated_grad * m_ref[...] * (s * (1.0 + gate * (1.0 - s)))).astype(BF16)

    thin = pl.BlockSpec((CHUNK, channels), lambda i: (i, 0))
    const = pl.BlockSpec((channels, width), lambda i: (0, 0))
    return pl.pallas_call(
        kernel,
        grid=(rows // CHUNK,),
        out_shape=(
            jax.ShapeDtypeStruct((rows, channels), F32),
            jax.ShapeDtypeStruct((rows, channels), BF16),
        ),
        in_specs=[pl.BlockSpec((CHUNK, width), lambda i: (i, 0)), const, thin, thin],
        out_specs=(thin, thin),
        compiler_params=SCAN_PARAMS,
        name="turn_back",
    )(mixer_back, mixer_w, gate_inner, mix)


def group_sums(columns):
    row = lax.broadcasted_iota(jnp.int32, (columns, columns), 0)
    col = lax.broadcasted_iota(jnp.int32, (columns, columns), 1)
    edges = (0, RANK, RANK + STATE, RANK + 2 * STATE)
    mean = jnp.zeros((columns, columns), F32)
    for low, high in zip(edges, edges[1:]):
        inside = (row >= low) & (row < high) & (col >= low) & (col < high)
        mean = mean + jnp.where(inside, 1.0, 0.0)
    return mean.astype(BF16)


def group_mean(values, sums):
    lane = lax.broadcasted_iota(jnp.int32, (1, values.shape[1]), 1)
    high = values.astype(BF16)
    rest = (values - high.astype(F32)).astype(BF16)
    total = jnp.dot(high, sums, preferred_element_type=F32) + jnp.dot(
        rest, sums, preferred_element_type=F32
    )
    return total * jnp.where(lane < RANK, 1.0 / RANK, 1.0 / STATE)


def unwind(
    select_grad, proj, gain, select_w, step, map_sum, mix_grad, rest, conv_input, masks,
    gate_back, normed, inner_w, mixed, step_low, step_back, first, extra,
):
    rows, channels = step.shape
    columns = proj.shape[1]
    width = normed.shape[1]
    taps = CONV
    piece = 128
    ops = (
        select_grad, proj, gain, select_w, rest, masks, step, map_sum, mix_grad, conv_input,
        gate_back, inner_w, normed, mixed, step_low, step_back, first, extra,
    )

    def kernel(*refs):
        far, refs = refs[: len(ops)], refs[len(ops) :]
        one_ref, inner_ref, slab_ref, first_ref, gain_ref = refs[:5]
        near, refs = refs[5 : 5 + len(ops)], refs[5 + len(ops) :]
        back, conv_f, pre, ext, one_v, inner_v, sems, outs = refs
        fetched = []
        for i in range(len(ops)):
            c = pltpu.make_async_copy(far[i], near[i], sems.at[i])
            c.start()
            fetched.append(c)
        (
            sg_ref, pr_ref, g_ref, sw_ref, rest_ref, mask_ref, st_ref, ms_ref, mg_ref, ci_ref,
            gb_ref, iw_ref, n_ref, mx_ref, sl_ref, sb_ref, f_ref, e_ref,
        ) = near
        for c in fetched[:4]:
            c.wait()
        sums = group_sums(columns)
        v, u = pr_ref[...], sg_ref[...].astype(F32)
        r = lax.rsqrt(group_mean(v * v, sums) + EPSILON)
        scaled = u * g_ref[...]
        grad = r * scaled - v * (r * r * r) * group_mean(scaled * v, sums)
        gain_ref[...] = jnp.sum(u * v * r, axis=0, keepdims=True) * (1.0 / PLANE)
        back[...] = grad.astype(BF16)
        for c in fetched[4:10]:
            c.wait()
        conv_f[...] = ci_ref[...].astype(F32)
        pre[rows:, :] = jnp.zeros((8, channels), F32)
        weights = [rest_ref[STATE + k : STATE + k + 1, :] for k in range(taps)]
        bias = rest_ref[STATE + taps : STATE + taps + 1, :]
        skip = rest_ref[STATE + taps + 2 : STATE + taps + 3, :]

        def first_pass(n, carry):
            at = rows_of(n, piece)
            window = conv_f[pl.ds(pl.multiple_of(HALO - 8 + n * piece, 8), piece + 8), :]
            mask = mask_ref[at, :]
            total = bias
            seen = []
            for k in range(taps):
                tap = window[8 - taps + 1 + k : 8 - taps + 1 + k + piece]
                if k < taps - 1:
                    tap = tap * mask[:, k : k + 1]
                seen.append(tap)
                total = total + weights[k] * tap
            mixed_grad = (
                st_ref[at, :] * ms_ref[at, :]
                + skip * mg_ref[at, :]
                + jnp.dot(back[at, :], sw_ref[...], preferred_element_type=F32)
            )
            value = mixed_grad * silu_slope(total)
            pre[at, :] = value
            new = [c + jnp.sum(value * t, axis=0, keepdims=True) for c, t in zip(carry, seen)]
            return (*new, carry[taps] + jnp.sum(value, axis=0, keepdims=True))

        zero = jnp.zeros((1, channels), F32)
        conv_sums = lax.fori_loop(0, rows // piece, first_pass, (zero,) * (taps + 1))

        def second_pass(n, _):
            window = pre[pl.ds(pl.multiple_of(n * piece, 8), piece + 8), :]
            mask = mask_ref[pl.ds(pl.multiple_of(n * piece, 8), piece + 8), :]
            total = None
            for k in range(taps):
                part = window
                if k < taps - 1:
                    part = part * mask[:, k : k + 1]
                part = part[taps - 1 - k : taps - 1 - k + piece] * weights[k]
                total = part if total is None else total + part
            ext[pl.ds(pl.multiple_of(HALO + n * piece, 16), piece), :channels] = total.astype(BF16)
            return 0

        lax.fori_loop(0, rows // piece, second_pass, 0)
        window = pre[0:8, :]
        at = lax.broadcasted_iota(jnp.int32, (HALO, channels), 0)
        ahead = jnp.zeros((HALO, channels), F32)
        for k in range(taps - 1):
            part = window * mask_ref[0:8, k : k + 1] * weights[k]
            for t in range(taps - 1 - k):
                row = HALO - taps + 1 + k + t
                ahead = ahead + jnp.where(at == row, part[t : t + 1], 0.0)
        ext[0:HALO, :channels] = ahead.astype(BF16)
        ext[0:HALO, channels:] = jnp.zeros((HALO, channels), BF16)
        for c in fetched[10:]:
            c.wait()
        ext[HALO:, channels:] = gb_ref[...]

        copies = []
        third = 2 * channels // 3
        for n in range(3):
            inner_v[pl.ds(n * third, third), :] = contract(
                ext[:, n * third : (n + 1) * third], n_ref[...], 0, 0, BF16
            )
        c = pltpu.make_async_copy(inner_v, inner_ref, outs.at[0])
        c.start()
        copies.append(c)
        part_rows = (rows + HALO) // 5

        def last_pass(n, total):
            at = rows_of(n, part_rows)
            value = jnp.dot(ext[at, :], iw_ref[...], preferred_element_type=F32).astype(BF16)
            one_v[at, :] = value
            return total + jnp.sum(
                value.astype(F32) * n_ref[at, :].astype(F32), axis=0, keepdims=True
            )

        total = lax.fori_loop(0, 5, last_pass, jnp.zeros((1, width), F32))
        c = pltpu.make_async_copy(one_v, one_ref, outs.at[1])
        c.start()
        copies.append(c)
        first_ref[...] = total / f_ref[...]
        slab_ref[:columns, :] = contract(back[...], mx_ref[...], 0, 0)
        slab_ref[columns : columns + RANK, :] = contract(sl_ref[...], sb_ref[...], 0, 0)[:RANK]
        others = jnp.concatenate(
            [e_ref[:STATE]]
            + list(conv_sums)
            + [e_ref[STATE : STATE + 2], jnp.zeros((16 - taps - 3, channels), F32)],
            axis=0,
        )
        slab_ref[columns + RANK :, :] = others
        for c in copies:
            c.wait()

    one = jax.ShapeDtypeStruct((rows + HALO, width), BF16)
    inner = jax.ShapeDtypeStruct((2 * channels, width), BF16)
    return pl.pallas_call(
        kernel,
        out_shape=(
            one,
            inner,
            jax.ShapeDtypeStruct((columns + RANK + 32, channels), F32),
            jax.ShapeDtypeStruct((1, width), F32),
            jax.ShapeDtypeStruct((1, columns), F32),
        ),
        in_specs=[ANY] * len(ops),
        out_specs=(ANY, ANY, VMEM, VMEM, VMEM),
        scratch_shapes=[
            *[pltpu.VMEM(a.shape, a.dtype) for a in ops],
            pltpu.VMEM((rows, columns), BF16),
            pltpu.VMEM((rows + HALO, channels), F32),
            pltpu.VMEM((rows + 8, channels), F32),
            pltpu.VMEM((rows + HALO, 2 * channels), BF16),
            pltpu.VMEM(one.shape, BF16),
            pltpu.VMEM(inner.shape, BF16),
            dma(len(ops)),
            dma(2),
        ],
        compiler_params=SCAN_PARAMS,
        name="unwind",
    )(*ops)


def contract(left, right, left_dim, right_dim, kind=F32):
    return lax.dot_general(
        left, right, (((left_dim,), (right_dim,)), ((), ())), preferred_element_type=F32
    ).astype(kind)


def on_device(
    planes,
    block_input,
    documents,
    first_gain,
    inner_weight,
    conv_weight,
    conv_bias,
    select_weight,
    select_gain,
    step_weight,
    step_bias,
    decay_log,
    skip_gain,
    mixer_weight,
    second_gain,
    gate_weight,
    up_weight,
    down_weight,
    cotangent,
):
    tok, width = block_input.shape
    devices = planes * PLANE
    rows = PLANE * tok
    z = lax.axis_index("z")
    own_block = mixer_weight.shape[0]
    inner_block = inner_weight.shape[1]
    channels = planes * own_block
    columns = RANK + 2 * STATE
    taps = conv_weight.shape[0]


    (
        x_ext,
        cot_all,
        inners,
        mixer_here,
        select_w,
        step_w,
        rest,
        first_f,
        second_f,
        select_f,
        ffn_own,
    ) = opening(
        planes,
        block_input,
        cotangent,
        inner_weight.T,
        mixer_weight,
        select_weight,
        (
            step_weight,
            decay_log,
            conv_weight,
            conv_bias[None, :],
            step_bias[None, :],
            skip_gain[None, :],
        ),
        (first_gain[None, :], second_gain[None, :], select_gain[None, :]),
        (gate_weight, up_weight, down_weight),
    )
    mixer_w = lax.all_gather(mixer_here, "z", axis=0, tiled=True)
    ffn_w = lax.all_gather(ffn_own, "z", axis=0)
    rate = -jnp.exp(rest[:STATE])
    conv_w = [rest[STATE + k : STATE + k + 1] for k in range(taps)]
    conv_b, step_b, skip = (rest[STATE + taps + k : STATE + taps + k + 1] for k in range(3))
    inner_w = inners.reshape(2 * channels, width)

    padded = jnp.concatenate([jnp.full((taps - 1,), -1, jnp.int32), documents])
    ids = lax.dynamic_slice_in_dim(padded, z * rows, rows + taps - 1, 0)
    here = ids[taps - 1 :]
    same = [(ids[k : k + rows] == here)[:, None] for k in range(taps)]
    masks = jnp.concatenate([m.astype(F32) for m in same], axis=1)
    masks = jnp.pad(masks, ((0, 8), (0, 0)))

    x_f = x_ext.astype(F32)
    r_one = lax.rsqrt(jnp.mean(x_f * x_f, axis=-1, keepdims=True) + EPSILON)
    normed_one = (x_f * r_one * first_f).astype(BF16)
    conv_input = contract(normed_one, inner_w[:channels], 1, 1, BF16)
    gate_inner = contract(normed_one[HALO:], inner_w[channels:], 1, 1)
    shift = HALO - taps + 1
    total = conv_b
    for k in range(taps):
        tap = conv_input[shift + k : shift + k + rows].astype(F32)
        total = total + conv_w[k] * jnp.where(same[k], tap, 0.0)
    mixed_in = jax.nn.silu(total).astype(BF16)
    proj_part = contract(mixed_in, select_w, 1, 1)
    proj = plane_sum(proj_part, 1)
    step, slope, step_cut, drive, step_low, maps = prepare(
        proj, select_f, step_w, step_b, mixed_in, masks
    )
    mixed_f = mixed_in.astype(F32)
    local_final, through = forward_final(step_cut, drive, maps, rate)
    state_in = state_chain(planes, through, local_final, 4, True)
    sums, states, state_out = forward_all(step_cut, drive, maps, rate, state_in)
    mix = sums + skip * mixed_f
    gate_silu = jax.nn.silu(gate_inner)
    gated = (mix * gate_silu).astype(BF16)
    mixer_part = contract(gated, mixer_w, 1, 0, BF16)
    resid_mid, normed_two = mixer_join(
        mixer_part, block_input, second_f
    )

    two_part, out_part, ffn_hidden, gate_back, up_back = feed_forward(
        normed_two, cot_all, ffn_w
    )
    resid_grad, mixer_back, second_grad, ffn_grads, gate_grad = ffn_join(
        planes,
        two_part,
        resid_mid,
        second_f,
        cotangent,
        normed_two,
        cot_all,
        ffn_hidden,
        gate_back,
        up_back,
    )

    mix_grad, gate_back = turn_back(mixer_back, mixer_w, gate_inner, mix)
    ffn_sums = lax.psum_scatter(ffn_grads, "z", scatter_dimension=0, tiled=False)
    local_back = backward_first(step_cut, mix_grad, maps, rate)
    state_back, mixer_grad = state_chain(
        planes, through, local_back, 5, False, gated, mixer_back
    )
    map_sum, step_back, select_part, extra = backward_all(
        step_cut,
        drive,
        mix_grad,
        maps,
        rate,
        states,
        state_out,
        state_back,
        slope,
        mixed_in,
        step_w,
    )
    mixer_grad, ffn_sums, select_part = lax.optimization_barrier(
        (mixer_grad, ffn_sums, select_part)
    )
    mixer_sum = lax.psum_scatter(mixer_grad, "z", scatter_dimension=0, tiled=True)
    select_grad = plane_sum(select_part, 7, BF16)
    one_part, inner_grad, slab_grad, first_grad, select_gain_grad = unwind(
        select_grad,
        proj,
        select_f,
        select_w,
        step,
        map_sum,
        mix_grad,
        rest,
        conv_input,
        masks,
        gate_back,
        normed_one,
        inner_w,
        mixed_in,
        step_low,
        step_back,
        first_f,
        extra,
    )
    results = closing(
        planes,
        one_part,
        block_input,
        first_f,
        resid_grad,
        inner_grad.reshape(planes, inner_block, width),
        slab_grad,
        (first_grad, second_grad, select_gain_grad),
        out_part,
        resid_mid,
        ffn_sums,
        mixer_sum,
    )
    (
        input_grad,
        inner_out,
        select_out,
        step_out,
        block_output,
        up_out,
        down_out,
        mixer_out,
        decay_out,
        conv_out,
        conv_b_out,
        step_b_out,
        skip_out,
        first_out,
        second_out,
        gain_out,
        gate_out,
    ) = hand_over((*results, gate_grad))
    return (
        block_output,
        input_grad,
        first_out[0],
        inner_out.T,
        conv_out,
        conv_b_out[0],
        select_out,
        gain_out[0],
        step_out,
        step_b_out[0],
        decay_out,
        skip_out[0],
        mixer_out,
        second_out[0],
        gate_out if gate_out.shape[0] == width else gate_out.T,
        up_out if up_out.shape[0] == width else up_out.T,
        down_out,
    )


def solution(mesh):
    planes = mesh.devices.size // PLANE
    grid = Mesh(mesh.devices.reshape(planes, PLANE), ("z", "p"))
    seq = ("z", "p")
    by_row, by_column, flat = P(seq, None), P(None, seq), P(seq)

    def program(*args):
        return on_device(planes, *args)

    return jax.shard_map(
        program,
        mesh=grid,
        in_specs=(
            by_row,
            P(),
            flat,
            by_column,
            by_column,
            flat,
            by_row,
            flat,
            by_column,
            flat,
            by_column,
            flat,
            by_row,
            flat,
            by_column,
            by_column,
            by_row,
            by_row,
        ),
        out_specs=(
            by_row,
            by_row,
            flat,
            by_column,
            by_column,
            flat,
            by_row,
            flat,
            by_column,
            flat,
            by_column,
            flat,
            by_row,
            flat,
            by_column,
            by_column,
            by_row,
        ),
        check_vma=False,
    )
```

```python
import jax
import jax.numpy as jnp
import numpy as np
from jax import lax
from jax.experimental import pallas as pl
from jax.experimental.pallas import tpu as pltpu
from jax.sharding import Mesh
from jax.sharding import PartitionSpec as P

STATE = 16
RANK = 96
CONV = 4
PLANE = 8
HALO = 16
GROUP = 8
CUT = 1e4
EPSILON = 1e-06
ALL_VMEM = 60 << 20
F32 = jnp.float32
BF16 = jnp.bfloat16
MESH_ID = pl.DeviceIdType.MESH
ANY = pl.BlockSpec(memory_space=pl.ANY)
VMEM = pl.BlockSpec(memory_space=pltpu.VMEM)


def xor(p, k):
    out = p
    for bit in (1, 2, 4):
        if k & bit:
            out = out + bit - 2 * bit * lax.rem(lax.div(out, bit), 2)
    return out


def remote(src, dst, send_sem, recv_sem, z, p):
    return pltpu.make_async_remote_copy(
        src_ref=src,
        dst_ref=dst,
        send_sem=send_sem,
        recv_sem=recv_sem,
        device_id={"z": z, "p": p},
        device_id_type=MESH_ID,
    )


def greet(z, p):
    pl.semaphore_signal(
        pltpu.get_barrier_semaphore(), inc=1, device_id={"z": z, "p": p}, device_id_type=MESH_ID
    )


def comm_params(number, vmem=None):
    return pltpu.CompilerParams(
        collective_id=number, has_side_effects=True, vmem_limit_bytes=vmem
    )


def dma(*shape):
    return pltpu.SemaphoreType.DMA(shape)


def block_route(z, p):
    half = lax.div(PLANE * z + p, 2)
    return lax.rem(half, PLANE), 2 * lax.div(half, PLANE) + lax.rem(p, 2)


def block_source_of(z, p):
    k = 2 * (PLANE * lax.div(z, 2) + p) + lax.rem(z, 2)
    return lax.div(k, PLANE), lax.rem(k, PLANE)


def moves_in(z, p):
    zs, ps = block_source_of(z, p)
    return jnp.logical_or(zs != z, ps != p)


def plane_greet(z, p):
    for k in (1, 2, 4):
        greet(z, xor(p, k))
    return 3


def plane_reduce(
    z, p, part, sbuf, obuf, dbuf, rbuf, s1, r1, s2, r2, finish, rows, during=None, base=0
):
    sib, near, side = xor(p, 1), xor(p, 2), xor(p, 4)
    tok = sbuf.shape[1]
    half = tok // 2
    top, low = pl.ds(0, half), pl.ds(half, half)
    wide = (part.dtype == F32) and (obuf.dtype == F32)
    align = min(rows, 16)

    def block(q):
        return part.at[pl.ds(pl.multiple_of(base + q * tok, align), tok)]

    def piece(q, at):
        return part[pl.ds(pl.multiple_of(base + q * tok + at.start, align), rows), :].astype(F32)

    def chunks(length, body):
        def step(n, _):
            body(pl.ds(pl.multiple_of(n * rows, rows), rows))
            return 0

        lax.fori_loop(0, length // rows, step, 0)

    def put(value):
        return value if wide else value.astype(obuf.dtype)

    first = []
    for i, k in enumerate((6, 2, 4, 0)):
        c = remote(block(xor(sib, k)), sbuf.at[i], s1.at[i], r1.at[i], z, sib)
        c.start()
        first.append(c)
    second = []

    def send(i, src, dst, to):
        c = remote(src, dst, s2.at[i], r2.at[i], z, to)
        c.start()
        second.append(c)
        return c

    for i, k in enumerate((6, 2, 4)):
        first[i].wait_recv()
        q = xor(p, k)

        def add(at, i=i, q=q):
            obuf[i, at] = put(piece(q, at) + sbuf[i, at].astype(F32))

        chunks(tok, add)
        if k == 6:
            far_top = send(0, obuf.at[0, top], dbuf.at[0], near)
            far_low = send(1, obuf.at[0, low], dbuf.at[1], side)
        elif k == 2:
            send(2, obuf.at[1, top], rbuf.at[0, top], near)
        else:
            send(3, obuf.at[2, low], rbuf.at[1, low], side)
    if during is not None:
        during(0)
    far_top.wait_recv()

    def join_top(at):
        obuf[2, at] = put(obuf[2, at].astype(F32) + dbuf[0, at].astype(F32))

    chunks(half, join_top)
    send(4, obuf.at[2, top], rbuf.at[1, top], side)
    far_low.wait_recv()

    def join_low(at):
        down = pl.ds(pl.multiple_of(at.start + half, rows), rows)
        obuf[1, down] = put(obuf[1, down].astype(F32) + dbuf[1, at].astype(F32))

    chunks(half, join_low)
    send(5, obuf.at[1, low], rbuf.at[0, low], near)
    if during is not None:
        during(1)
    first[3].wait_recv()
    for c in second[2:]:
        c.wait_recv()

    def last(at):
        total = piece(p, at) + sbuf[3, at].astype(F32)
        finish(at, total + rbuf[0, at].astype(F32) + rbuf[1, at].astype(F32))

    chunks(tok, last)
    for c in first + second:
        c.wait_send()


class PlaneGather:
    def __init__(self, z, p, own, place, ss, rs, fs, fr, ls):
        self.z, self.p, self.own, self.place = z, p, own, place
        self.ss, self.rs, self.fs, self.fr, self.ls = ss, rs, fs, fr, ls
        self.sent, self.passed = [], []
        half = own.shape[0] // 2
        self.top, self.low = pl.ds(0, half), pl.ds(half, half)

    def send(self, src, dst, to):
        i = len(self.sent)
        c = remote(src, dst, self.ss.at[i], self.rs.at[i], self.z, to)
        c.start()
        self.sent.append(c)

    def pass_on(self, q):
        i = len(self.passed)
        place = self.place(q)
        c = remote(place, place, self.fs.at[i], self.fr.at[i], self.z, xor(self.p, 1))
        c.start()
        self.passed.append(c)

    def start(self):
        p, own = self.p, self.own
        near, side = xor(p, 2), xor(p, 4)
        self.send(own.at[self.top], self.place(p).at[self.top], near)
        self.send(own.at[self.low], self.place(p).at[self.low], side)
        self.send(own.at[self.low], self.place(p).at[self.low], near)
        self.send(own.at[self.top], self.place(p).at[self.top], side)
        self.send(own, self.place(p), xor(p, 1))
        self.local = pltpu.make_async_copy(own, self.place(p), self.ls)
        self.local.start()

    def relay(self):
        near, side = xor(self.p, 2), xor(self.p, 4)
        self.sent[0].wait_recv()
        self.send(self.place(near).at[self.top], self.place(near).at[self.top], side)
        self.sent[1].wait_recv()
        self.send(self.place(side).at[self.low], self.place(side).at[self.low], near)

    def finish(self):
        near, side, far = xor(self.p, 2), xor(self.p, 4), xor(self.p, 6)
        self.sent[2].wait_recv()
        self.pass_on(near)
        self.sent[3].wait_recv()
        self.pass_on(side)
        self.sent[5].wait_recv()
        self.sent[6].wait_recv()
        self.pass_on(far)
        self.sent[4].wait_recv()
        for c in self.passed:
            c.wait_recv()
        for c in self.sent + self.passed:
            c.wait_send()
        self.local.wait()


def plane_gather(z, p, own, place, ss, rs, fs, fr, ls, during=None):
    gather = PlaneGather(z, p, own, place, ss, rs, fs, fr, ls)
    gather.start()
    if during is not None:
        during(2)
    gather.relay()
    gather.finish()


def rows_at(ref, tok, base=0):
    return lambda q: ref.at[pl.ds(pl.multiple_of(base + q * tok, 16), tok)]


GATHER_SEMS = (7, 7, 3, 3)
REDUCE_SEMS = (4, 4, 6, 6)


def ring_gather(planes, z, p, own, out, ss, rs, ls):
    local = pltpu.make_async_copy(own, out.at[z], ls)
    local.start()
    sent = []

    def send(i, src, dst, r):
        c = remote(src, dst, ss.at[i], rs.at[i], lax.rem(z + r, planes), p)
        c.start()
        sent.append(c)
        return c

    if planes != 4:
        for r in range(1, planes):
            send(r, own, out.at[z], r)
        return local, sent, lambda: None
    half = own.shape[0] // 2
    top, low = pl.ds(0, half), pl.ds(half, half)
    up = send(0, own.at[top], out.at[z, top], 1)
    down = send(1, own.at[low], out.at[z, low], 3)

    def relay():
        before, after = lax.rem(z + 3, 4), lax.rem(z + 1, 4)
        send(2, own.at[low], out.at[z, low], 1)
        send(3, own.at[top], out.at[z, top], 3)
        up.wait_recv()
        send(4, out.at[before, top], out.at[before, top], 1)
        down.wait_recv()
        send(5, out.at[after, low], out.at[after, low], 3)

    return local, sent, relay


def ring_finish(local, sent, relayed):
    for i, c in enumerate(sent):
        if not (relayed and i < 2):
            c.wait_recv()
        c.wait_send()
    local.wait()


def ring_reduce(planes, z, p, src, ibuf, fbuf, mbuf, ss, rs, hold=False):
    half = src.shape[1] // 2
    top, low = pl.ds(0, half), pl.ds(half, half)
    before, after = lax.rem(z + planes - 1, planes), lax.rem(z + 1, planes)
    sent = []

    def send(i, part, dst, r):
        c = remote(part, dst, ss.at[i], rs.at[i], lax.rem(z + r, planes), p)
        c.start()
        sent.append(c)

    def near():
        send(2, src.at[after, low], ibuf.at[0, low], 1)
        send(3, src.at[before, top], ibuf.at[1, top], 3)

    if planes == 4:
        far = lax.rem(z + 2, 4)
        send(0, src.at[far, top], fbuf.at[0], 1)
        send(1, src.at[far, low], fbuf.at[1], 3)
        if not hold:
            near()
    else:
        for r in range(1, planes):
            send(r, src.at[lax.rem(z + r, planes)], ibuf.at[r], r)

    def relay():
        if planes == 4:
            if hold:
                near()
            sent[0].wait_recv()
            mbuf[0] = (src[after, top].astype(F32) + fbuf[0].astype(F32)).astype(mbuf.dtype)
            send(4, mbuf.at[0], ibuf.at[0, top], 1)
            sent[1].wait_recv()
            mbuf[1] = (src[before, low].astype(F32) + fbuf[1].astype(F32)).astype(mbuf.dtype)
            send(5, mbuf.at[1], ibuf.at[1, low], 3)

    def finish():
        for i, c in enumerate(sent):
            if not (planes == 4 and i < 2):
                c.wait_recv()
            c.wait_send()
        total = src[z].astype(F32)
        for k in range(2) if planes == 4 else range(1, planes):
            total = total + ibuf[k].astype(F32)
        return total

    return relay, finish


def ring_reduce_scratch(planes, block, width, kind=BF16):
    return [
        pltpu.VMEM((2 if planes == 4 else planes, block, width), kind),
        pltpu.VMEM((2, block // 2, width), kind),
        pltpu.VMEM((2, block // 2, width), kind),
        dma(ring_sems(planes)),
        dma(ring_sems(planes)),
    ]


def ring_greet(planes, z, p):
    for r in range(1, planes):
        greet(lax.rem(z + r, planes), p)
    return planes - 1


def ring_sems(planes):
    return max(6, planes)


TRIO = 8


def join_gain(planes, gains_ref, row, per, spread):
    total = spread.shape[1]
    at = lax.broadcasted_iota(jnp.int32, (PLANE, total), 1)
    column = lax.broadcasted_iota(jnp.int32, (PLANE, total), 0)
    joined = jnp.zeros((PLANE, total), F32)
    for k in range(planes):
        piece = jnp.concatenate([gains_ref[q, k, row : row + 1, :] for q in range(PLANE)], axis=0)
        wide = jnp.dot(piece.astype(BF16), spread, preferred_element_type=F32)
        low = (column + PLANE * k) * per
        joined = joined + jnp.where((at >= low) & (at < low + per), wide, 0.0)
    return jnp.sum(joined, axis=0, keepdims=True)


def opening(planes, x, cot, inner, mixer, select, small, gains, ffn):
    tok, width = x.shape
    relayed = planes == 4
    block = mixer.shape[0]
    columns = select.shape[1]
    channels = planes * block
    places, filled = [], 0
    for array in small:
        places.append((filled, filled + array.shape[0]))
        filled += array.shape[0]
    rank = small[0].shape[0]
    states = small[1].shape[0]
    height = rank + 32 + columns
    pers = [g.shape[1] for g in gains]
    spreads = []
    for per, total in ((pers[0], width), (pers[2], columns)):
        spreads.append(
            jnp.asarray(np.arange(128)[:, None] == np.arange(total)[None, :] % per, BF16)
        )
    turn = ffn[0].shape[1] % 128 == 0
    units = ffn[2].shape[0]
    if not turn:
        ffn = [ffn[0].T, ffn[1].T, ffn[2]]

    def kernel(*refs):
        wide_refs, select_ref = refs[:4], refs[4]
        small_refs, gain_refs, refs = refs[5:11], refs[11:14], refs[14:]
        spread_refs, ffn_refs, refs = refs[:2], refs[2:5], refs[5:]
        xg_ref, cots_ref, inners_ref, home_ref = refs[:4]
        select_out, step_ref, rest_ref, first_ref, second_ref, sel_ref, own_ref = refs[4:11]
        refs = refs[11:]
        own_wide, own_small, got_small, smalls, own_gain, gains_all = refs[:6]
        refs = refs[6:]
        near_small, near_gain, near_spread, near_ffn = refs[:6], refs[6:9], refs[9:11], refs[11:13]
        near_select, ffn_out, refs = refs[13], refs[14], refs[15:]
        near_wide, near_down, wide_sems, refs = refs[:4], refs[4], refs[5], refs[6:]
        x_ref, cot_ref, inner_ref, mixer_ref = near_wide
        x_sems, c_sems, refs = refs[:5], refs[5:10], refs[10:]
        hs, hr, gs, gr, gs2, gr2, ins, inr, inl, ps, pr, bs, br, bl, near_sems, out_sems = refs

        z, p = lax.axis_index("z"), lax.axis_index("p")
        column, slot = block_route(z, p)
        from_z, from_p = block_source_of(z, p)
        moves = jnp.logical_or(column != p, slot != z)
        stays = jnp.logical_not(moves)
        after = lax.rem(z + 1, planes)
        for k in range(1, PLANE):
            greet(z, xor(p, k))
        for r in range(1, planes):
            greet(lax.rem(z + r, planes), p)

        @pl.when(moves_in(z, p))
        def _():
            greet(from_z, from_p)

        landing = []
        for i in (2, 0, 1, 3):
            c = pltpu.make_async_copy(wide_refs[i], near_wide[i], wide_sems.at[i])
            c.start()
            landing.append(c)
        down_in = pltpu.make_async_copy(ffn_refs[2], near_down, wide_sems.at[4])
        down_in.start()
        fetched = []
        far_refs = list(small_refs) + list(gain_refs) + [select_ref]
        far_refs += list(spread_refs) + list(ffn_refs[:2])
        near_refs = list(near_small) + list(near_gain) + [near_select]
        near_refs += list(near_spread) + list(near_ffn)
        for i, (src, dst) in enumerate(zip(far_refs, near_refs)):
            c = pltpu.make_async_copy(src, dst, near_sems.at[i])
            c.start()
            fetched.append(c)
        own_wide[...] = jnp.zeros_like(own_wide)
        own_gain[...] = jnp.zeros_like(own_gain)
        pl.semaphore_wait(
            pltpu.get_barrier_semaphore(),
            PLANE - 1 + planes - 1 + moves.astype(jnp.int32),
        )

        for c in landing:
            c.wait()
        local, sent, relay = ring_gather(planes, z, p, inner_ref, inners_ref, ins, inr, inl)

        homes = [
            (own_small, got_small, ps.at[0], pr.at[0]),
            (mixer_ref, home_ref, ps.at[1], pr.at[1]),
        ]

        def homing(items):
            for src, dst, send, recv in items:

                @pl.when(moves)
                def _():
                    remote(src, dst, send, recv, slot, column).start()

                @pl.when(stays)
                def _():
                    pltpu.make_async_copy(src, dst, recv).start()

        def place(q):
            return xg_ref.at[pl.ds(pl.multiple_of(HALO + q * tok, HALO), tok)]

        gain_out, gain_on, block_ring, ffn_sent = [], [], [], []

        def first_sends(_):
            for c in fetched[:10]:
                c.wait()
            for (low, high), ref in zip(places, near_small):
                own_wide[low:high, :] = ref[...].astype(F32)
            own_small[: rank + 32] = own_wide[...].astype(BF16)
            own_small[rank + 32 :] = near_select[...].astype(F32).T.astype(BF16)
            for i, ref in enumerate(near_gain):
                own_gain[i : i + 1, : pers[i]] = ref[...].astype(F32)
            homing(homes[:1])
            for r in range(1, planes):
                c = remote(
                    own_gain, gains_all.at[p, z], gs.at[r], gr.at[r], lax.rem(z + r, planes), p
                )
                c.start()
                gain_out.append(c)
            gains_all[p, z] = own_gain[...]

        x_gather = PlaneGather(z, p, x_ref, place, *x_sems)
        cot_gather = PlaneGather(z, p, cot_ref, rows_at(cots_ref, tok), *c_sems)
        x_gather.start()
        first_sends(0)
        x_gather.relay()
        relay()
        cot_gather.start()
        homing(homes[1:])

        src, dst, _, recv = homes[0]
        pltpu.make_async_copy(src, dst, recv).wait()
        block_ring.extend(ring_gather(planes, z, p, got_small, smalls, bs, br, bl))
        for c in gain_out:
            c.wait_recv()
        for k in range(1, PLANE):
            c = remote(gains_all.at[p], gains_all.at[p], gs2.at[k], gr2.at[k], z, xor(p, k))
            c.start()
            gain_on.append(c)
        x_gather.finish()

        edge = xg_ref.at[pl.ds(PLANE * tok, HALO)]
        front = xg_ref.at[pl.ds(0, HALO)]

        @pl.when(z < planes - 1)
        def _():
            remote(edge, front, hs, hr, after, p).start()

        @pl.when(z == 0)
        def _():
            pltpu.make_async_copy(edge, front, hr).start()

        cot_gather.relay()
        block_ring[2]()
        down_in.wait()
        down_out = pltpu.make_async_copy(
            near_down, own_ref.at[pl.ds(2 * units, units)], out_sems.at[2]
        )
        down_out.start()
        for c in fetched[10:]:
            c.wait()
        for i in range(2):
            if turn:
                ffn_out[i] = near_ffn[i][...].T
            else:
                ffn_out[i] = near_ffn[i][...]
            c = pltpu.make_async_copy(
                ffn_out.at[i], own_ref.at[pl.ds(i * units, units)], out_sems.at[i]
            )
            c.start()
            ffn_sent.append(c)
        for c in gain_on:
            c.wait_recv()
        first_ref[...] = join_gain(planes, gains_all, 0, pers[0], near_spread[0][...])
        second_ref[...] = join_gain(planes, gains_all, 1, pers[1], near_spread[0][...])
        sel_ref[...] = join_gain(planes, gains_all, 2, pers[2], near_spread[1][...])
        cot_gather.finish()
        down_out.wait()
        for c in ffn_sent:
            c.wait()
        pltpu.make_async_copy(edge, front, hr).wait()

        @pl.when(z < planes - 1)
        def _():
            remote(edge, front, hs, hr, after, p).wait_send()

        ring_finish(block_ring[0], block_ring[1], relayed)
        joined = jnp.concatenate([smalls[k].astype(F32) for k in range(planes)], axis=1)
        row = lax.broadcasted_iota(jnp.int32, (rank + 32, channels), 0)
        step_ref[...] = jnp.where(row < rank, joined[: rank + 32], 0.0).astype(BF16)
        rest_ref[...] = joined[rank : rank + 32]
        select_out[...] = joined[rank + 32 :].astype(BF16)
        pltpu.make_async_copy(mixer_ref, home_ref, pr.at[1]).wait()

        @pl.when(moves)
        def _():
            for src, dst, send, recv in homes:
                remote(src, dst, send, recv, slot, column).wait_send()

        for c in gain_out + gain_on:
            c.wait_send()
        ring_finish(local, sent, relayed)

    def shape(*dims, kind=BF16):
        return jax.ShapeDtypeStruct(dims, kind)

    one = pltpu.SemaphoreType.DMA
    return pl.pallas_call(
        kernel,
        out_shape=(
            shape(HALO + PLANE * tok, width),
            shape(PLANE * tok, width),
            shape(planes, *inner.shape),
            shape(*mixer.shape),
            shape(columns, channels),
            shape(rank + 32, channels),
            shape(32, channels, kind=F32),
            shape(1, width, kind=F32),
            shape(1, width, kind=F32),
            shape(1, columns, kind=F32),
            shape(3 * units, width),
        ),
        in_specs=[ANY] * 19,
        out_specs=(ANY,) * 4 + (VMEM,) * 6 + (ANY,),
        scratch_shapes=[
            pltpu.VMEM((rank + 32, block), F32),
            pltpu.VMEM((height, block), BF16),
            pltpu.VMEM((height, block), BF16),
            pltpu.VMEM((planes, height, block), BF16),
            pltpu.VMEM((TRIO, 128), F32),
            pltpu.VMEM((PLANE, planes, TRIO, 128), F32),
            *[pltpu.VMEM(a.shape, a.dtype) for a in (*small, *gains, *spreads, *ffn[:2])],
            pltpu.VMEM(select.shape, BF16),
            pltpu.VMEM((2, units, width), BF16),
            *[pltpu.VMEM(a.shape, a.dtype) for a in (x, cot, inner, mixer, ffn[2])],
            dma(5),
            *[dma(n) for n in GATHER_SEMS],
            one,
            *[dma(n) for n in GATHER_SEMS],
            one,
            one,
            one,
            dma(planes),
            dma(planes),
            dma(PLANE),
            dma(PLANE),
            dma(ring_sems(planes)),
            dma(ring_sems(planes)),
            one,
            dma(2),
            dma(2),
            dma(ring_sems(planes)),
            dma(ring_sems(planes)),
            one,
            dma(14),
            dma(3),
        ],
        compiler_params=comm_params(0, ALL_VMEM),
        name="opening",
    )(x, cot, inner, mixer, select, *small, *gains, *spreads, *ffn)


def plane_sum(part, number, kind=F32):
    tok, columns = part.shape[0] // PLANE, part.shape[1]

    def kernel(part_ref, out_ref, own, *refs):
        bufs, g = refs[:8], refs[8:]
        z, p = lax.axis_index("z"), lax.axis_index("p")
        pl.semaphore_wait(pltpu.get_barrier_semaphore(), plane_greet(z, p))

        def finish(at, value):
            own[at] = value.astype(kind)

        plane_reduce(z, p, part_ref, *bufs, finish, tok // 2)
        plane_gather(z, p, own, rows_at(out_ref, tok), *g)

    return pl.pallas_call(
        kernel,
        out_shape=jax.ShapeDtypeStruct(part.shape, kind),
        in_specs=[VMEM],
        out_specs=VMEM,
        scratch_shapes=[
            pltpu.VMEM((tok, columns), kind),
            pltpu.VMEM((4, tok, columns), F32),
            *reduce_scratch(tok, columns, kind)[1:],
            *[dma(n) for n in GATHER_SEMS],
            pltpu.SemaphoreType.DMA,
        ],
        compiler_params=comm_params(number, 32 << 20),
        name="plane_sum",
    )(part)


def reduce_scratch(tok, width, kind=BF16):
    return [
        pltpu.VMEM((4, tok, width), kind),
        pltpu.VMEM((3, tok, width), kind),
        pltpu.VMEM((2, tok // 2, width), kind),
        pltpu.VMEM((2, tok, width), kind),
        *[dma(n) for n in REDUCE_SEMS],
    ]


def mixer_join(part, x, gain):
    tok, width = x.shape

    def kernel(
        part_ref,
        x_ref,
        gain_ref,
        resid_ref,
        out_ref,
        own,
        sbuf,
        obuf,
        dbuf,
        rbuf,
        s1,
        r1,
        s2,
        r2,
        *g,
    ):
        z, p = lax.axis_index("z"), lax.axis_index("p")
        pl.semaphore_wait(pltpu.get_barrier_semaphore(), plane_greet(z, p))

        def finish(at, total):
            v = total + x_ref[at].astype(F32)
            resid_ref[at] = v
            r = lax.rsqrt(jnp.mean(v * v, axis=-1, keepdims=True) + EPSILON)
            own[at] = (v * r * gain_ref[...]).astype(BF16)

        plane_reduce(z, p, part_ref, sbuf, obuf, dbuf, rbuf, s1, r1, s2, r2, finish, 16)
        plane_gather(z, p, own, rows_at(out_ref, tok), *g)

    return pl.pallas_call(
        kernel,
        out_shape=(
            jax.ShapeDtypeStruct((tok, width), F32),
            jax.ShapeDtypeStruct(part.shape, BF16),
        ),
        in_specs=[VMEM] * 3,
        out_specs=(VMEM, VMEM),
        scratch_shapes=[
            pltpu.VMEM((tok, width), BF16),
            *reduce_scratch(tok, width),
            *[dma(n) for n in GATHER_SEMS],
            pltpu.SemaphoreType.DMA,
        ],
        compiler_params=comm_params(2, 32 << 20),
        name="mixer_join",
    )(part, x, gain)


def feed_forward(normed, cot, weights):
    rows, width = normed.shape
    planes, triple, _ = weights.shape
    units = triple // 3
    hidden = planes * units
    block = 512

    def kernel(n_ref, c_ref, w_ref, two_ref, out_ref, h_ref, gb_ref, ub_ref, gw, uw, dw, sem):
        @pl.when(pl.program_id(0) == 0)
        def _():
            copies = []
            for i, dst in enumerate((gw, uw, dw)):
                for k in range(planes):
                    copies.append(
                        pltpu.make_async_copy(
                            w_ref.at[k, pl.ds(i * units, units)],
                            dst.at[pl.ds(k * units, units)],
                            sem.at[i, k],
                        )
                    )
            for c in copies:
                c.start()
            for c in copies:
                c.wait()

        n, c = n_ref[...], c_ref[...]
        gate = contract(n, gw[...], 1, 1)
        up = contract(n, uw[...], 1, 1)
        back = contract(c, dw[...], 1, 1)
        s = jax.nn.sigmoid(gate)
        silu = gate * s
        h = (silu * up).astype(BF16)
        gb = (back * up * (s * (1.0 + gate * (1.0 - s)))).astype(BF16)
        ub = (back * silu).astype(BF16)
        h_ref[...] = h
        gb_ref[...] = gb
        ub_ref[...] = ub
        two_ref[...] = (contract(gb, gw[...], 1, 0) + contract(ub, uw[...], 1, 0)).astype(BF16)
        out_ref[...] = contract(h, dw[...], 1, 0, BF16)

    wide = pl.BlockSpec((block, width), lambda i: (i, 0))
    thin = pl.BlockSpec((block, hidden), lambda i: (i, 0))
    return pl.pallas_call(
        kernel,
        grid=(rows // block,),
        out_shape=(jax.ShapeDtypeStruct((rows, width), BF16),) * 2
        + (jax.ShapeDtypeStruct((rows, hidden), BF16),) * 3,
        in_specs=[wide, wide, ANY],
        out_specs=(wide, wide, thin, thin, thin),
        scratch_shapes=[pltpu.VMEM((hidden, width), BF16)] * 3
        + [pltpu.SemaphoreType.DMA((3, planes))],
        compiler_params=pltpu.CompilerParams(vmem_limit_bytes=ALL_VMEM),
        name="feed_forward",
    )(normed, cot, weights)


def ffn_join(planes, part, resid, gain, cot, normed, cot_all, h, gb, ub):
    tok, width = resid.shape
    hidden = h.shape[1]
    units = hidden // planes
    step_units = 256
    turn = units % 128 == 0

    def kernel(
        part_ref,
        v_ref,
        gain_ref,
        cot_ref,
        n_ref,
        c_ref,
        h_ref,
        gb_ref,
        ub_ref,
        grad_ref,
        out_ref,
        gg_ref,
        w_ref,
        gate_ref,
        near_p,
        near_v,
        near_gain,
        near_cot,
        near_n,
        near_c,
        near_h,
        near_g,
        near_u,
        near_sems,
        own,
        sbuf,
        obuf,
        dbuf,
        rbuf,
        s1,
        r1,
        s2,
        r2,
        *g,
    ):
        g, (gw, uw, dw, wsem), ring = g[:5], g[5:9], g[9:]
        z, p = lax.axis_index("z"), lax.axis_index("p")
        pl.semaphore_wait(
            pltpu.get_barrier_semaphore(), plane_greet(z, p) + ring_greet(planes, z, p)
        )
        gg_ref[...] = jnp.zeros_like(gg_ref)
        copies, rings, fetched = [], [], []
        far = (part_ref, gb_ref, n_ref, ub_ref, h_ref, c_ref, v_ref, gain_ref, cot_ref)
        gb_ref, n_ref, ub_ref, h_ref, c_ref = near_g, near_n, near_u, near_h, near_c
        part_ref, v_ref, gain_ref, cot_ref = near_p, near_v, near_gain, near_cot
        near = (part_ref, gb_ref, n_ref, ub_ref, h_ref, c_ref, v_ref, gain_ref, cot_ref)
        for i, (src, dst) in enumerate(zip(far, near)):
            c = pltpu.make_async_copy(src, dst, near_sems.at[i])
            c.start()
            fetched.append(c)
        fetched[0].wait()
        group = step_units // units

        def weight_grad(dst, left, right):
            for n in range(hidden // step_units):
                at = pl.ds(n * step_units, step_units)
                value = contract(left[:, at], right[...], 0, 0, BF16)
                dst[pl.ds(n * group, group)] = value.reshape(group, units, width)

        def hand_out(i, dst):
            c = pltpu.make_async_copy(
                dst, w_ref.at[:, pl.ds(i * units, units)], wsem.at[i]
            )
            c.start()
            copies.append(c)

        def during(step):
            if step == 0:
                for c in fetched[1:]:
                    c.wait()
                weight_grad(gw, gb_ref, n_ref)
                rings.append(ring_reduce(planes, z, p, gw, *ring))
            if step == 1:
                weight_grad(uw, ub_ref, n_ref)
                hand_out(0, uw)
            if step == 2:
                rings[0][0]()
                weight_grad(dw, h_ref, c_ref)
                hand_out(1, dw)

        def finish(at, u):
            v = v_ref[at]
            r = lax.rsqrt(jnp.mean(v * v, axis=-1, keepdims=True) + EPSILON)
            ug = u * gain_ref[...]
            mid = r * ug - v * (r * r * r) * jnp.mean(ug * v, axis=-1, keepdims=True)
            gg_ref[...] += jnp.sum(u * v * r, axis=0, keepdims=True)
            total = cot_ref[at].astype(F32) + mid
            grad_ref[at] = total
            own[at] = total.astype(BF16)

        plane_reduce(
            z, p, part_ref, sbuf, obuf, dbuf, rbuf, s1, r1, s2, r2, finish, 16, during
        )
        plane_gather(z, p, own, rows_at(out_ref, tok), *g, during)
        for c in copies:
            c.wait()
        total = rings[0][1]()
        gate_ref[...] = total.T if turn else total

    return pl.pallas_call(
        kernel,
        out_shape=(
            jax.ShapeDtypeStruct((tok, width), F32),
            jax.ShapeDtypeStruct(part.shape, BF16),
            jax.ShapeDtypeStruct((1, width), F32),
            jax.ShapeDtypeStruct((planes, 2 * units, width), BF16),
            jax.ShapeDtypeStruct((width, units) if turn else (units, width), F32),
        ),
        in_specs=[ANY] * 9,
        out_specs=(VMEM, ANY, VMEM, ANY, VMEM),
        scratch_shapes=[
            *[
                pltpu.VMEM(a.shape, a.dtype)
                for a in (part, resid, gain, cot, normed, cot_all, h, gb, ub)
            ],
            dma(9),
            pltpu.VMEM((tok, width), BF16),
            *reduce_scratch(tok, width),
            *[dma(n) for n in GATHER_SEMS],
            pltpu.SemaphoreType.DMA,
            *[pltpu.VMEM((planes, units, width), BF16)] * 3,
            dma(2),
            *ring_reduce_scratch(planes, units, width),
        ],
        compiler_params=comm_params(3, 56 << 20),
        name="ffn_join",
    )(part, resid, gain, cot, normed, cot_all, h, gb, ub)


def state_chain(planes, through, local, number, forward, left=None, right=None):
    beside = [] if left is None else [left, right]

    def kernel(t_ref, l_ref, *refs):
        far, refs = refs[: len(beside)], refs[len(beside) :]
        out_ref, refs = refs[0], refs[1:]
        if beside:
            grad_ref, got, own, s0, r0, near_l, near_r, sems = refs
            fetched = []
            for i, dst in enumerate((near_l, near_r)):
                c = pltpu.make_async_copy(far[i], dst, sems.at[i])
                c.start()
                fetched.append(c)
        else:
            got, own, s0, r0 = refs
        z, p = lax.axis_index("z"), lax.axis_index("p")
        for r in range(1, planes):
            greet(lax.rem(z + r, planes), p)
        own[0] = t_ref[...].astype(BF16)
        own[1] = l_ref[...].astype(BF16)
        pl.semaphore_wait(pltpu.get_barrier_semaphore(), planes - 1)
        sent = []
        for r in range(1, planes):
            to = lax.rem(z + r, planes)
            c = remote(own, got.at[z], s0.at[r], r0.at[r], to, p)
            c.start()
            sent.append(c)
        if beside:
            for c in fetched:
                c.wait()
            grad_ref[...] = contract(near_l[...], near_r[...], 0, 0, BF16)
        for c in sent:
            c.wait()
        got[z] = own[...]
        state = jnp.zeros_like(l_ref)
        for k in range(planes) if forward else reversed(range(planes)):
            new = got[k, 0].astype(F32) * state + got[k, 1].astype(F32)
            state = jnp.where((k < z) if forward else (k > z), new, state)
        out_ref[...] = state

    shapes, extra = (jax.ShapeDtypeStruct(local.shape, F32),), []
    if beside:
        shapes += (jax.ShapeDtypeStruct((left.shape[1], right.shape[1]), BF16),)
        extra = [*[pltpu.VMEM(a.shape, a.dtype) for a in beside], dma(2)]
    out = pl.pallas_call(
        kernel,
        out_shape=shapes,
        in_specs=[VMEM] * 2 + [ANY] * len(beside),
        out_specs=(VMEM,) * len(shapes),
        scratch_shapes=[
            pltpu.VMEM((planes, 2) + local.shape, BF16),
            pltpu.VMEM((2,) + local.shape, BF16),
            dma(planes),
            dma(planes),
            *extra,
        ],
        compiler_params=comm_params(number, (56 << 20) if beside else None),
        name="state_chain",
    )(through, local, *beside)
    return out if beside else out[0]


def gain_spreads(pers, totals):
    spreads, start = [], 0
    for per, total in zip(pers, totals):
        lane = np.arange(128)[:, None]
        spreads.append(jnp.asarray(lane == start + np.arange(total)[None, :] % per, BF16))
        start += per
    return spreads


def closing(
    planes, part, x, gain, resid_grad, inner_g, slab_g, gains_g, out_part, resid, ffn_g, mixer_g
):
    tok, width = x.shape
    block = inner_g.shape[1]
    height, channels = slab_g.shape
    own = channels // planes
    rank = height - 32 - (RANK + 2 * STATE)
    columns = RANK + 2 * STATE
    units = ffn_g.shape[0] // 2
    turn = units % 128 == 0
    devices = planes * PLANE
    pers = [g.shape[1] // devices for g in gains_g]
    spreads = gain_spreads(pers, [g.shape[1] for g in gains_g])
    operands = (
        part, x, gain, resid_grad, inner_g, slab_g, out_part, resid, ffn_g, mixer_g, *gains_g,
        *spreads,
    )

    def shape(*dims, kind=F32):
        return jax.ShapeDtypeStruct(dims, kind)

    outputs = (
        shape(tok, width),
        shape(*inner_g.shape[1:]),
        shape(own, columns),
        shape(rank, own),
        shape(tok, width, kind=BF16),
        shape(width, units) if turn else shape(units, width),
        shape(units, width),
        shape(*mixer_g.shape),
        *[shape(n, own) for n in (STATE, CONV, 1, 1, 1)],
        *[shape(1, per) for per in pers],
    )

    def kernel(*refs):
        far, refs = refs[: len(operands)], refs[len(operands) :]
        far_outs, refs = refs[: len(outputs)], refs[len(outputs) :]
        one_bufs, out_bufs, refs = refs[:8], refs[8:16], refs[16:]
        hbuf, hsum, hgot, hs, hr, refs = *refs[:5], refs[5:]
        inner_ring, slab_ring, refs = refs[:5], refs[5:10], refs[10:]
        pieces, homed, mixed, os_, or_, refs = *refs[:5], refs[5:]
        gg_ref, gbuf, gs, gr, gown, gbuf2, gs2, gr2, bown = refs[:9]
        near, refs = refs[9 : 9 + len(operands)], refs[9 + len(operands) :]
        near_sems, refs = refs[0], refs[1:]
        near_outs, out_sems = refs[: len(outputs)], refs[len(outputs)]
        out_ref, io_ref, sel_ref, step_ref, bo_ref, up_ref, down_ref, mo_ref = near_outs[:8]
        row_refs, gain_outs = near_outs[8:13], near_outs[13:]
        written = []

        def write(*which):
            for i in which:
                c = pltpu.make_async_copy(near_outs[i], far_outs[i], out_sems.at[i])
                c.start()
                written.append(c)

        fetched = []
        for i in (4, 0, 10, 11, 12, 13, 14, 15, 5, 6, 8, 9, 1, 2, 3, 7):
            c = pltpu.make_async_copy(far[i], near[i], near_sems.at[i])
            c.start()
            fetched.append(c)
        part_ref, x_ref, gain_ref, rg_ref, ig_ref, sg_ref, fp_ref, rm_ref = near[:8]
        ffn_ref, mix_ref = near[8:10]
        z, p = lax.axis_index("z"), lax.axis_index("p")
        column, slot = block_route(z, p)
        to_z, to_p = block_source_of(z, p)
        moves = moves_in(z, p)
        stays = jnp.logical_not(moves)
        gets = jnp.logical_or(column != p, slot != z)
        before = lax.rem(z + planes - 1, planes)
        for k in range(1, PLANE):
            greet(z, xor(p, k))
        for r in range(1, planes):
            greet(lax.rem(z + r, planes), p)

        @pl.when(gets)
        def _():
            greet(slot, column)

        pl.semaphore_wait(
            pltpu.get_barrier_semaphore(),
            PLANE - 1 + planes - 1 + moves.astype(jnp.int32),
        )

        fetched[0].wait()
        relay, inner_total = ring_reduce(planes, z, p, ig_ref, *inner_ring, hold=True)
        for c in fetched[1:9]:
            c.wait()
        z_sent, p_sent, slab = [], [], []
        halo = remote(part_ref.at[pl.ds(0, HALO)], hbuf.at[p], hs.at[0], hr.at[p], z, PLANE - 1)
        halo_on = remote(hsum, hgot, hs.at[1], hr.at[PLANE], before, PLANE - 1)
        inside = jnp.logical_and(z > 0, p < PLANE - 1)
        gathers = jnp.logical_and(z > 0, p == PLANE - 1)

        @pl.when(inside)
        def _():
            halo.start()

        def homing(i, src, dst):
            @pl.when(moves)
            def _():
                remote(src, dst, os_.at[i], or_.at[i], to_z, to_p).start()

            @pl.when(stays)
            def _():
                pltpu.make_async_copy(src, dst, or_.at[i]).start()

        def homing_end(i, src, dst):
            pltpu.make_async_copy(src, dst, or_.at[i]).wait()

            @pl.when(moves)
            def _():
                remote(src, dst, os_.at[i], or_.at[i], to_z, to_p).wait_send()


        def during(step):
            if step == 0:
                for k in range(planes):
                    pieces[k] = sg_ref[:, own * k : own * (k + 1)].astype(BF16)
                slab.extend(ring_reduce(planes, z, p, pieces, *slab_ring))
                packed = jnp.zeros((devices, 128), F32)
                for i, per in enumerate(pers):
                    value = near[10 + i][...]
                    at = lax.broadcasted_iota(jnp.int32, (devices, value.shape[1]), 1)
                    low = lax.broadcasted_iota(jnp.int32, at.shape, 0) * per
                    value = jnp.where((at >= low) & (at < low + per), value, 0.0)
                    high = value.astype(BF16)
                    rest = (value - high.astype(F32)).astype(BF16)
                    spread = near[13 + i][...]
                    packed = packed + contract(high, spread, 1, 1) + contract(rest, spread, 1, 1)
                gg_ref[...] = packed.reshape(planes, PLANE, 128)
                for r in range(1, planes):
                    to = lax.rem(z + r, planes)
                    c = remote(gg_ref.at[to], gbuf.at[z], gs.at[r], gr.at[r], to, p)
                    c.start()
                    z_sent.append(c)
                return
            relay()

            @pl.when(gathers)
            def _():
                add = part_ref[pl.ds(0, HALO), :].astype(F32)
                for q in range(PLANE - 1):
                    pltpu.make_async_copy(
                        part_ref.at[pl.ds(0, HALO)], hbuf.at[q], hr.at[q]
                    ).wait()
                    add = add + hbuf[q].astype(F32)
                hsum[...] = add.astype(BF16)
                halo_on.start()

            for c in z_sent:
                c.wait()
            total = gg_ref[z]
            for r in range(1, planes):
                total = total + gbuf[lax.rem(z + r, planes)]
            gown[...] = total
            for k in range(1, PLANE):
                c = remote(gown, gbuf2.at[k], gs2.at[k], gr2.at[k], z, xor(p, k))
                c.start()
                p_sent.append(c)

        def finish(at, u):
            out_ref[at] = u

        plane_reduce(z, p, part_ref, *one_bufs, finish, 16, during, HALO)

        for c in fetched[9:]:
            c.wait()

        def later(step):
            if step == 0:
                slab[0]()
                if turn:
                    up_ref[...] = ffn_ref[:units].astype(F32).T
                else:
                    up_ref[...] = ffn_ref[:units].astype(F32)
                down_ref[...] = ffn_ref[units:].astype(F32)
                write(5, 6)
                homing(1, mix_ref, mixed)
                return
            bown[...] = slab[1]().astype(BF16)
            homing(0, bown, homed)

        def output(at, u):
            bo_ref[at] = (rm_ref[at] + u).astype(BF16)

        plane_reduce(z, p, fp_ref, *out_bufs, output, 16, later)
        write(4)

        @pl.when(jnp.logical_and(p == PLANE - 1, z < planes - 1))
        def _():
            pltpu.make_async_copy(hsum, hgot, hr.at[PLANE]).wait()
            out_ref[pl.ds(tok - HALO, HALO)] += hgot[...].astype(F32)

        @pl.when(inside)
        def _():
            halo.wait_send()

        @pl.when(gathers)
        def _():
            halo_on.wait_send()

        def norm(n, _):
            at = pl.ds(pl.multiple_of(n * 16, 16), 16)
            u = out_ref[at]
            v = x_ref[at].astype(F32)
            r = lax.rsqrt(jnp.mean(v * v, axis=-1, keepdims=True) + EPSILON)
            ug = u * gain_ref[...]
            grad = r * ug - v * (r * r * r) * jnp.mean(ug * v, axis=-1, keepdims=True)
            out_ref[at] = rg_ref[at] + grad
            return 0

        lax.fori_loop(0, tok // 16, norm, 0)
        write(0)

        for c in p_sent:
            c.wait()
        total = gown[...]
        for k in range(1, PLANE):
            total = total + gbuf2[k]
        row = lax.broadcasted_iota(jnp.int32, total.shape, 0)
        mine = jnp.sum(jnp.where(row == p, total, 0.0), axis=0, keepdims=True)
        start = 0
        for ref, per in zip(gain_outs, pers):
            ref[...] = mine[:, start : start + per]
            start += per
        homing_end(1, mix_ref, mixed)
        mo_ref[...] = mixed[...].astype(F32)
        write(7)
        homing_end(0, bown, homed)
        small = homed[...].astype(F32)
        sel_ref[...] = small[:columns, :].T
        step_ref[...] = small[columns : columns + rank, :]
        start = columns + rank
        for ref in row_refs:
            ref[...] = small[start : start + ref.shape[0], :]
            start += ref.shape[0]
        write(2, 3, *range(8, len(outputs)))
        io_ref[...] = inner_total()
        write(1)
        for c in written:
            c.wait()

    one = pltpu.SemaphoreType.DMA
    return pl.pallas_call(
        kernel,
        out_shape=outputs,
        in_specs=[ANY] * len(operands),
        out_specs=(ANY,) * len(outputs),
        scratch_shapes=[
            *reduce_scratch(tok, width),
            *reduce_scratch(tok, width),
            pltpu.VMEM((PLANE, HALO, width), BF16),
            pltpu.VMEM((HALO, width), BF16),
            pltpu.VMEM((HALO, width), BF16),
            dma(2),
            dma(PLANE + 1),
            *ring_reduce_scratch(planes, block, width),
            *ring_reduce_scratch(planes, height, own),
            pltpu.VMEM((planes, height, own), BF16),
            pltpu.VMEM((height, own), BF16),
            pltpu.VMEM(mixer_g.shape, BF16),
            dma(2),
            dma(2),
            pltpu.VMEM((planes, PLANE, 128), F32),
            pltpu.VMEM((planes, PLANE, 128), F32),
            dma(planes),
            dma(planes),
            pltpu.VMEM((PLANE, 128), F32),
            pltpu.VMEM((PLANE, PLANE, 128), F32),
            dma(PLANE),
            dma(PLANE),
            pltpu.VMEM((height, own), BF16),
            *[pltpu.VMEM(a.shape, a.dtype) for a in operands],
            dma(len(operands)),
            *[pltpu.VMEM(a.shape, a.dtype) for a in outputs],
            dma(len(outputs)),
        ],
        compiler_params=comm_params(6, ALL_VMEM),
        name="closing",
    )(*operands)


def hand_over(arrays):
    count = len(arrays)

    def kernel(*refs):
        ins, outs, near = refs[:count], refs[count : 2 * count], refs[2 * count : 3 * count]
        in_sems, out_sems = refs[3 * count :]
        fetched, copies = [], []
        for i in range(count):
            c = pltpu.make_async_copy(ins[i], near[i], in_sems.at[i])
            c.start()
            fetched.append(c)
        for i in range(count):
            fetched[i].wait()
            c = pltpu.make_async_copy(near[i], outs[i], out_sems.at[i])
            c.start()
            copies.append(c)
        for c in copies:
            c.wait()

    return pl.pallas_call(
        kernel,
        out_shape=tuple(jax.ShapeDtypeStruct(a.shape, a.dtype) for a in arrays),
        in_specs=[ANY] * count,
        out_specs=(ANY,) * count,
        scratch_shapes=[
            *[pltpu.VMEM(a.shape, a.dtype) for a in arrays],
            dma(count),
            dma(count),
        ],
        compiler_params=SCAN_PARAMS,
        name="hand_over",
    )(*arrays)


CHUNK = 256


def scan_specs(channels, count, backward):
    def at(i):
        return count - 1 - i if backward else i

    return (
        pl.BlockSpec((CHUNK, channels), lambda i: (at(i), 0)),
        lambda part, size: pl.BlockSpec((CHUNK, size * STATE, 128), lambda i: (at(i), part, 0)),
        pl.BlockSpec((CHUNK, STATE, channels), lambda i: (at(i), 0, 0)),
        pl.BlockSpec((STATE, channels), lambda i: (0, 0)),
    )


def rows_of(g, size=GROUP):
    return pl.ds(pl.multiple_of(g * size, size), size)


def across(maps, channels):
    return jnp.concatenate([maps.astype(F32)] * (channels // 128), axis=1)


SCAN_PARAMS = pltpu.CompilerParams(vmem_limit_bytes=ALL_VMEM)


def prepare(proj, gain, step_w, step_b, mixed, keep):
    tokens, columns = proj.shape
    channels = mixed.shape[1]

    def kernel(
        proj_ref, gain_ref, w_ref, b_ref, mixed_ref, keep_ref, step_ref, slope_ref, cut_ref, drive_ref,
        low_ref, maps_ref,
    ):
        v = proj_ref[...]
        mean = group_mean(v * v, group_sums(columns))
        out = v * lax.rsqrt(mean + EPSILON) * gain_ref[...]
        low = out.astype(BF16)
        low_ref[...] = low
        raw = contract(low, w_ref[...], 1, 0) + b_ref[...]
        step = jnp.maximum(raw, 0.0) + jnp.log1p(jnp.exp(-jnp.abs(raw)))
        step_ref[...] = step
        slope_ref[...] = jax.nn.sigmoid(raw)
        drive_ref[...] = step * mixed_ref[...].astype(F32)
        cut_ref[...] = jnp.where(keep_ref[:, CONV - 2 : CONV - 1] > 0.0, step, CUT)

        wide = (2 * STATE, columns)
        pick = lax.broadcasted_iota(jnp.int32, wide, 1) == (
            lax.broadcasted_iota(jnp.int32, wide, 0) + columns - 2 * STATE
        )
        pick = jnp.where(pick, 1.0, 0.0).astype(BF16)
        first = lax.broadcasted_iota(jnp.int32, (2 * columns, 256), 0) < columns
        left = lax.broadcasted_iota(jnp.int32, (2 * columns, 256), 1) < 128
        ones = jnp.where(first == left, 1.0, 0.0).astype(BF16)
        many = 32

        def spread(g, _):
            at = rows_of(g, many)
            rows = low_ref[at, :]
            pairs = []
            for k in range(many // 2):
                pairs.append(
                    jnp.concatenate(
                        [
                            jnp.broadcast_to(rows[k : k + 1], wide) * pick,
                            jnp.broadcast_to(rows[k + many // 2 : k + many // 2 + 1], wide) * pick,
                        ],
                        axis=1,
                    )
                )
            result = jnp.dot(
                jnp.concatenate(pairs, axis=0), ones, preferred_element_type=F32
            ).astype(BF16)
            maps_ref[rows_of(2 * g, many // 2)] = result[:, :128].reshape(many // 2, 2 * STATE, 128)
            maps_ref[rows_of(2 * g + 1, many // 2)] = result[:, 128:].reshape(
                many // 2, 2 * STATE, 128
            )
            return 0

        lax.fori_loop(0, CHUNK // many, spread, 0)

    def tile(size):
        return pl.BlockSpec((CHUNK, size), lambda i: (i, 0))

    def whole(array):
        return pl.BlockSpec(array.shape, lambda i: (0, 0))

    shape = jax.ShapeDtypeStruct((tokens, channels), F32)
    return pl.pallas_call(
        kernel,
        grid=(tokens // CHUNK,),
        out_shape=(
            shape,
            shape,
            shape,
            shape,
            jax.ShapeDtypeStruct((tokens, columns), BF16),
            jax.ShapeDtypeStruct((tokens, 2 * STATE, 128), BF16),
        ),
        in_specs=[
            tile(columns),
            whole(gain),
            whole(step_w),
            whole(step_b),
            tile(channels),
            tile(CONV),
        ],
        out_specs=(
            tile(channels),
            tile(channels),
            tile(channels),
            tile(channels),
            tile(columns),
            pl.BlockSpec((CHUNK, 2 * STATE, 128), lambda i: (i, 0, 0)),
        ),
        compiler_params=SCAN_PARAMS,
        name="prepare",
    )(proj, gain, step_w, step_b, mixed, keep)


def forward_final(step, drive, maps, rate):
    tokens, channels = step.shape
    count = tokens // CHUNK
    rows, cols, _, const = scan_specs(channels, count, False)

    def kernel(step_ref, drive_ref, in_ref, rate_ref, state_ref, through_ref):
        @pl.when(pl.program_id(0) == 0)
        def _():
            state_ref[...] = jnp.zeros_like(state_ref)
            through_ref[...] = jnp.zeros_like(through_ref)

        rate_v = rate_ref[...]

        def body(g, carry):
            h, total = carry
            d8, w8 = step_ref[rows_of(g), :], drive_ref[rows_of(g), :]
            for k in range(GROUP):
                decay = jnp.exp(d8[k : k + 1, :] * rate_v)
                h = decay * h + w8[k : k + 1, :] * across(in_ref[g * GROUP + k], channels)
            return h, total + d8

        h, total = lax.fori_loop(
            0,
            CHUNK // GROUP,
            body,
            (state_ref[...], jnp.zeros((GROUP, channels), F32)),
        )
        state_ref[...] = h
        through_ref[...] += jnp.sum(total, axis=0, keepdims=True)

        @pl.when(pl.program_id(0) == count - 1)
        def _():
            through_ref[...] = jnp.exp(through_ref[...] * rate_v)

    shape = jax.ShapeDtypeStruct(rate.shape, F32)
    return pl.pallas_call(
        kernel,
        grid=(count,),
        out_shape=(shape, shape),
        in_specs=[rows, rows, cols(0, 1), const],
        out_specs=(const, const),
        compiler_params=SCAN_PARAMS,
        name="forward_final",
    )(step, drive, maps, rate)


def forward_all(step, drive, maps, rate, start):
    tokens, channels = step.shape
    count = tokens // CHUNK
    rows, cols, states, const = scan_specs(channels, count, False)

    def kernel(step_ref, drive_ref, maps_ref, rate_ref, start_ref, y_ref, hs_ref, h_sc):
        @pl.when(pl.program_id(0) == 0)
        def _():
            h_sc[...] = start_ref[...]

        rate_v = rate_ref[...]

        def body(g, h):
            d8, w8 = step_ref[rows_of(g), :], drive_ref[rows_of(g), :]
            out = []
            for k in range(GROUP):
                t = g * GROUP + k
                hs_ref[t] = h.astype(BF16)
                decay = jnp.exp(d8[k : k + 1, :] * rate_v)
                h = decay * h + w8[k : k + 1, :] * across(maps_ref[t, :STATE], channels)
                out.append(
                    jnp.sum(h * across(maps_ref[t, STATE:], channels), axis=0, keepdims=True)
                )
            y_ref[rows_of(g), :] = jnp.concatenate(out, axis=0)
            return h

        h_sc[...] = lax.fori_loop(0, CHUNK // GROUP, body, h_sc[...])

    return pl.pallas_call(
        kernel,
        grid=(count,),
        out_shape=(
            jax.ShapeDtypeStruct((tokens, channels), F32),
            jax.ShapeDtypeStruct((tokens, STATE, channels), BF16),
            jax.ShapeDtypeStruct(rate.shape, F32),
        ),
        in_specs=[rows, rows, cols(0, 2), const, const],
        out_specs=(rows, states, const),
        compiler_params=SCAN_PARAMS,
        name="forward_all",
    )(step, drive, maps, rate, start)


def backward_first(step, mix_grad, maps, rate):
    tokens, channels = step.shape
    count = tokens // CHUNK
    rows, cols, _, const = scan_specs(channels, count, True)

    def kernel(step_ref, mix_ref, out_map_ref, rate_ref, out_ref):
        @pl.when(pl.program_id(0) == 0)
        def _():
            out_ref[...] = jnp.zeros_like(out_ref)

        rate_v = rate_ref[...]

        def body(n, q):
            g = CHUNK // GROUP - 1 - n
            d8, m8 = step_ref[rows_of(g), :], mix_ref[rows_of(g), :]
            for k in reversed(range(GROUP)):
                decay = jnp.exp(d8[k : k + 1, :] * rate_v)
                q = decay * (q + m8[k : k + 1, :] * across(out_map_ref[g * GROUP + k], channels))
            return q

        out_ref[...] = lax.fori_loop(0, CHUNK // GROUP, body, out_ref[...])

    return pl.pallas_call(
        kernel,
        grid=(count,),
        out_shape=jax.ShapeDtypeStruct(rate.shape, F32),
        in_specs=[rows, rows, cols(1, 1), const],
        out_specs=const,
        compiler_params=SCAN_PARAMS,
        name="backward_first",
    )(step, mix_grad, maps, rate)


def backward_all(
    step, drive, mix_grad, maps, rate, states_in, state_out, start, slope, mixed, step_w
):
    tokens, channels = step.shape
    columns = step_w.shape[0]
    count = tokens // CHUNK
    rows, cols, states, const = scan_specs(channels, count, True)

    def fold(v):
        total = v[:, :128]
        for i in range(1, channels // 128):
            total = total + v[:, 128 * i : 128 * (i + 1)]
        return total.astype(BF16)

    def kernel(
        step_ref,
        drive_ref,
        mix_ref,
        maps_ref,
        rate_ref,
        hs_ref,
        end_ref,
        start_ref,
        slope_ref,
        mixed_ref,
        sw_ref,
        sb_ref,
        back_ref,
        part_ref,
        extra_ref,
        q_sc,
        dd_sc,
        h_sc,
        sr_ref,
        v_sc,
    ):
        @pl.when(pl.program_id(0) == 0)
        def _():
            q_sc[...] = start_ref[...]
            h_sc[...] = end_ref[...]
            dd_sc[...] = jnp.zeros_like(dd_sc)
            extra_ref[...] = jnp.zeros_like(extra_ref)

        rate_v = rate_ref[...]

        def body(n, carry):
            q, dd, h = carry
            g = CHUNK // GROUP - 1 - n
            at = rows_of(g)
            d8, w8, m8 = step_ref[at, :], drive_ref[at, :], mix_ref[at, :]
            sb, sr = [], []
            for k in reversed(range(GROUP)):
                t = g * GROUP + k
                d, w, m = d8[k : k + 1, :], w8[k : k + 1, :], m8[k : k + 1, :]
                b = across(maps_ref[t, :STATE], channels)
                c = across(maps_ref[t, STATE:], channels)
                decay = jnp.exp(d * rate_v)
                ahead = hs_ref[t].astype(F32)
                kept = decay * ahead
                hbar = q + m * c
                flow = hbar * kept
                q = decay * hbar
                dd = dd + flow * d
                sb.append(jnp.sum(hbar * b, axis=0, keepdims=True))
                sr.append(jnp.sum(flow * rate_v, axis=0, keepdims=True))
                v_sc[t, :STATE] = fold(hbar * w)
                v_sc[t, STATE:] = fold(h * m)
                h = ahead
            sb_ref[at, :] = jnp.concatenate(sb[::-1], axis=0)
            sr_ref[at, :] = jnp.concatenate(sr[::-1], axis=0)
            return q, dd, h

        q, dd, h = lax.fori_loop(0, CHUNK // GROUP, body, (q_sc[...], dd_sc[...], h_sc[...]))
        q_sc[...] = q
        h_sc[...] = h
        dd_sc[...] = dd

        first = lax.broadcasted_iota(jnp.int32, (256, 2 * columns), 0) < 128
        left = lax.broadcasted_iota(jnp.int32, (256, 2 * columns), 1) < columns
        ones = jnp.where(first == left, 1.0, 0.0).astype(BF16)
        shape = (2 * STATE, columns)
        pick = lax.broadcasted_iota(jnp.int32, shape, 1) == (
            lax.broadcasted_iota(jnp.int32, shape, 0) + columns - 2 * STATE
        )
        many = 64

        def lanes(n, _):
            one = v_sc[rows_of(2 * n, many // 2)].reshape(many * STATE, 128)
            two = v_sc[rows_of(2 * n + 1, many // 2)].reshape(many * STATE, 128)
            total = jnp.dot(
                jnp.concatenate([one, two], axis=1), ones, preferred_element_type=F32
            )
            halves = []
            for i in range(2):
                part = total[:, columns * i : columns * (i + 1)].reshape(many // 2, 2 * STATE, columns)
                halves.append(jnp.sum(jnp.where(pick[None], part, 0.0), axis=1))
            at = rows_of(n, many)
            mixed_v = mixed_ref[at, :].astype(F32)
            raw = (mixed_v * sb_ref[at, :] + sr_ref[at, :]) * slope_ref[at, :]
            back = raw.astype(BF16)
            back_ref[at, :] = back
            part_ref[at, :] = contract(back, sw_ref[...], 1, 1) + jnp.concatenate(halves, axis=0)
            extra_ref[STATE : STATE + 1, :] += jnp.sum(raw, axis=0, keepdims=True)
            extra_ref[STATE + 1 : STATE + 2, :] += jnp.sum(
                mix_ref[at, :] * mixed_v, axis=0, keepdims=True
            )
            return 0

        lax.fori_loop(0, CHUNK // many, lanes, 0)

        @pl.when(pl.program_id(0) == count - 1)
        def _():
            extra_ref[:STATE, :] = dd_sc[...] * rate_v

    wide = jax.ShapeDtypeStruct((tokens, channels), F32)
    return pl.pallas_call(
        kernel,
        grid=(count,),
        out_shape=(
            wide,
            jax.ShapeDtypeStruct((tokens, channels), BF16),
            jax.ShapeDtypeStruct((tokens, columns), F32),
            jax.ShapeDtypeStruct((STATE + 8, channels), F32),
        ),
        in_specs=[rows, rows, rows, cols(0, 2), const, states, const, const, rows, rows]
        + [pl.BlockSpec(step_w.shape, lambda i: (0, 0))],
        out_specs=(
            rows,
            rows,
            pl.BlockSpec((CHUNK, columns), lambda i: (count - 1 - i, 0)),
            pl.BlockSpec((STATE + 8, channels), lambda i: (0, 0)),
        ),
        scratch_shapes=[
            pltpu.VMEM((STATE, channels), F32),
            pltpu.VMEM((STATE, channels), F32),
            pltpu.VMEM((STATE, channels), F32),
            pltpu.VMEM((CHUNK, channels), F32),
            pltpu.VMEM((CHUNK, 2 * STATE, 128), BF16),
        ],
        compiler_params=SCAN_PARAMS,
        name="backward_all",
    )(step, drive, mix_grad, maps, rate, states_in, state_out, start, slope, mixed, step_w)


def silu_slope(v):
    s = jax.nn.sigmoid(v)
    return s * (1.0 + v * (1.0 - s))


def turn_back(mixer_back, mixer_w, gate_inner, mix):
    rows, width = mixer_back.shape
    channels = mix.shape[1]

    def kernel(b_ref, w_ref, i_ref, m_ref, mix_ref, gate_ref):
        gated_grad = contract(b_ref[...], w_ref[...], 1, 1)
        gate = i_ref[...]
        s = jax.nn.sigmoid(gate)
        mix_ref[...] = gated_grad * (gate * s)
        gate_ref[...] = (gated_grad * m_ref[...] * (s * (1.0 + gate * (1.0 - s)))).astype(BF16)

    thin = pl.BlockSpec((CHUNK, channels), lambda i: (i, 0))
    const = pl.BlockSpec((channels, width), lambda i: (0, 0))
    return pl.pallas_call(
        kernel,
        grid=(rows // CHUNK,),
        out_shape=(
            jax.ShapeDtypeStruct((rows, channels), F32),
            jax.ShapeDtypeStruct((rows, channels), BF16),
        ),
        in_specs=[pl.BlockSpec((CHUNK, width), lambda i: (i, 0)), const, thin, thin],
        out_specs=(thin, thin),
        compiler_params=SCAN_PARAMS,
        name="turn_back",
    )(mixer_back, mixer_w, gate_inner, mix)


def group_sums(columns):
    row = lax.broadcasted_iota(jnp.int32, (columns, columns), 0)
    col = lax.broadcasted_iota(jnp.int32, (columns, columns), 1)
    edges = (0, RANK, RANK + STATE, RANK + 2 * STATE)
    mean = jnp.zeros((columns, columns), F32)
    for low, high in zip(edges, edges[1:]):
        inside = (row >= low) & (row < high) & (col >= low) & (col < high)
        mean = mean + jnp.where(inside, 1.0, 0.0)
    return mean.astype(BF16)


def group_mean(values, sums):
    lane = lax.broadcasted_iota(jnp.int32, (1, values.shape[1]), 1)
    high = values.astype(BF16)
    rest = (values - high.astype(F32)).astype(BF16)
    total = jnp.dot(high, sums, preferred_element_type=F32) + jnp.dot(
        rest, sums, preferred_element_type=F32
    )
    return total * jnp.where(lane < RANK, 1.0 / RANK, 1.0 / STATE)


def unwind(
    select_grad, proj, gain, select_w, step, map_sum, mix_grad, rest, conv_input, masks,
    gate_back, normed, inner_w, mixed, step_low, step_back, first, extra,
):
    rows, channels = step.shape
    columns = proj.shape[1]
    width = normed.shape[1]
    taps = CONV
    piece = 128
    ops = (
        select_grad, proj, gain, select_w, rest, masks, step, map_sum, mix_grad, conv_input,
        gate_back, inner_w, normed, mixed, step_low, step_back, first, extra,
    )

    def kernel(*refs):
        far, refs = refs[: len(ops)], refs[len(ops) :]
        one_ref, inner_ref, slab_ref, first_ref, gain_ref = refs[:5]
        near, refs = refs[5 : 5 + len(ops)], refs[5 + len(ops) :]
        back, conv_f, pre, ext, one_v, inner_v, sems, outs = refs
        fetched = []
        for i in range(len(ops)):
            c = pltpu.make_async_copy(far[i], near[i], sems.at[i])
            c.start()
            fetched.append(c)
        (
            sg_ref, pr_ref, g_ref, sw_ref, rest_ref, mask_ref, st_ref, ms_ref, mg_ref, ci_ref,
            gb_ref, iw_ref, n_ref, mx_ref, sl_ref, sb_ref, f_ref, e_ref,
        ) = near
        for c in fetched[:4]:
            c.wait()
        sums = group_sums(columns)
        v, u = pr_ref[...], sg_ref[...].astype(F32)
        r = lax.rsqrt(group_mean(v * v, sums) + EPSILON)
        scaled = u * g_ref[...]
        grad = r * scaled - v * (r * r * r) * group_mean(scaled * v, sums)
        gain_ref[...] = jnp.sum(u * v * r, axis=0, keepdims=True) * (1.0 / PLANE)
        back[...] = grad.astype(BF16)
        for c in fetched[4:10]:
            c.wait()
        conv_f[...] = ci_ref[...].astype(F32)
        pre[rows:, :] = jnp.zeros((8, channels), F32)
        weights = [rest_ref[STATE + k : STATE + k + 1, :] for k in range(taps)]
        bias = rest_ref[STATE + taps : STATE + taps + 1, :]
        skip = rest_ref[STATE + taps + 2 : STATE + taps + 3, :]

        def first_pass(n, carry):
            at = rows_of(n, piece)
            window = conv_f[pl.ds(pl.multiple_of(HALO - 8 + n * piece, 8), piece + 8), :]
            mask = mask_ref[at, :]
            total = bias
            seen = []
            for k in range(taps):
                tap = window[8 - taps + 1 + k : 8 - taps + 1 + k + piece]
                if k < taps - 1:
                    tap = tap * mask[:, k : k + 1]
                seen.append(tap)
                total = total + weights[k] * tap
            mixed_grad = (
                st_ref[at, :] * ms_ref[at, :]
                + skip * mg_ref[at, :]
                + jnp.dot(back[at, :], sw_ref[...], preferred_element_type=F32)
            )
            value = mixed_grad * silu_slope(total)
            pre[at, :] = value
            new = [c + jnp.sum(value * t, axis=0, keepdims=True) for c, t in zip(carry, seen)]
            return (*new, carry[taps] + jnp.sum(value, axis=0, keepdims=True))

        zero = jnp.zeros((1, channels), F32)
        conv_sums = lax.fori_loop(0, rows // piece, first_pass, (zero,) * (taps + 1))

        def second_pass(n, _):
            window = pre[pl.ds(pl.multiple_of(n * piece, 8), piece + 8), :]
            mask = mask_ref[pl.ds(pl.multiple_of(n * piece, 8), piece + 8), :]
            total = None
            for k in range(taps):
                part = window
                if k < taps - 1:
                    part = part * mask[:, k : k + 1]
                part = part[taps - 1 - k : taps - 1 - k + piece] * weights[k]
                total = part if total is None else total + part
            ext[pl.ds(pl.multiple_of(HALO + n * piece, 16), piece), :channels] = total.astype(BF16)
            return 0

        lax.fori_loop(0, rows // piece, second_pass, 0)
        window = pre[0:8, :]
        at = lax.broadcasted_iota(jnp.int32, (HALO, channels), 0)
        ahead = jnp.zeros((HALO, channels), F32)
        for k in range(taps - 1):
            part = window * mask_ref[0:8, k : k + 1] * weights[k]
            for t in range(taps - 1 - k):
                row = HALO - taps + 1 + k + t
                ahead = ahead + jnp.where(at == row, part[t : t + 1], 0.0)
        ext[0:HALO, :channels] = ahead.astype(BF16)
        ext[0:HALO, channels:] = jnp.zeros((HALO, channels), BF16)
        for c in fetched[10:]:
            c.wait()
        ext[HALO:, channels:] = gb_ref[...]

        copies = []
        third = 2 * channels // 3
        for n in range(3):
            inner_v[pl.ds(n * third, third), :] = contract(
                ext[:, n * third : (n + 1) * third], n_ref[...], 0, 0, BF16
            )
        c = pltpu.make_async_copy(inner_v, inner_ref, outs.at[0])
        c.start()
        copies.append(c)
        part_rows = (rows + HALO) // 5

        def last_pass(n, total):
            at = rows_of(n, part_rows)
            value = jnp.dot(ext[at, :], iw_ref[...], preferred_element_type=F32).astype(BF16)
            one_v[at, :] = value
            return total + jnp.sum(
                value.astype(F32) * n_ref[at, :].astype(F32), axis=0, keepdims=True
            )

        total = lax.fori_loop(0, 5, last_pass, jnp.zeros((1, width), F32))
        c = pltpu.make_async_copy(one_v, one_ref, outs.at[1])
        c.start()
        copies.append(c)
        first_ref[...] = total / f_ref[...]
        slab_ref[:columns, :] = contract(back[...], mx_ref[...], 0, 0)
        slab_ref[columns : columns + RANK, :] = contract(sl_ref[...], sb_ref[...], 0, 0)[:RANK]
        others = jnp.concatenate(
            [e_ref[:STATE]]
            + list(conv_sums)
            + [e_ref[STATE : STATE + 2], jnp.zeros((16 - taps - 3, channels), F32)],
            axis=0,
        )
        slab_ref[columns + RANK :, :] = others
        for c in copies:
            c.wait()

    one = jax.ShapeDtypeStruct((rows + HALO, width), BF16)
    inner = jax.ShapeDtypeStruct((2 * channels, width), BF16)
    return pl.pallas_call(
        kernel,
        out_shape=(
            one,
            inner,
            jax.ShapeDtypeStruct((columns + RANK + 32, channels), F32),
            jax.ShapeDtypeStruct((1, width), F32),
            jax.ShapeDtypeStruct((1, columns), F32),
        ),
        in_specs=[ANY] * len(ops),
        out_specs=(ANY, ANY, VMEM, VMEM, VMEM),
        scratch_shapes=[
            *[pltpu.VMEM(a.shape, a.dtype) for a in ops],
            pltpu.VMEM((rows, columns), BF16),
            pltpu.VMEM((rows + HALO, channels), F32),
            pltpu.VMEM((rows + 8, channels), F32),
            pltpu.VMEM((rows + HALO, 2 * channels), BF16),
            pltpu.VMEM(one.shape, BF16),
            pltpu.VMEM(inner.shape, BF16),
            dma(len(ops)),
            dma(2),
        ],
        compiler_params=SCAN_PARAMS,
        name="unwind",
    )(*ops)


def contract(left, right, left_dim, right_dim, kind=F32):
    return lax.dot_general(
        left, right, (((left_dim,), (right_dim,)), ((), ())), preferred_element_type=F32
    ).astype(kind)


def on_device(
    planes,
    block_input,
    documents,
    first_gain,
    inner_weight,
    conv_weight,
    conv_bias,
    select_weight,
    select_gain,
    step_weight,
    step_bias,
    decay_log,
    skip_gain,
    mixer_weight,
    second_gain,
    gate_weight,
    up_weight,
    down_weight,
    cotangent,
):
    tok, width = block_input.shape
    devices = planes * PLANE
    rows = PLANE * tok
    z = lax.axis_index("z")
    own_block = mixer_weight.shape[0]
    inner_block = inner_weight.shape[1]
    channels = planes * own_block
    columns = RANK + 2 * STATE
    taps = conv_weight.shape[0]


    (
        x_ext,
        cot_all,
        inners,
        mixer_here,
        select_w,
        step_w,
        rest,
        first_f,
        second_f,
        select_f,
        ffn_own,
    ) = opening(
        planes,
        block_input,
        cotangent,
        inner_weight.T,
        mixer_weight,
        select_weight,
        (
            step_weight,
            decay_log,
            conv_weight,
            conv_bias[None, :],
            step_bias[None, :],
            skip_gain[None, :],
        ),
        (first_gain[None, :], second_gain[None, :], select_gain[None, :]),
        (gate_weight, up_weight, down_weight),
    )
    mixer_w = lax.all_gather(mixer_here, "z", axis=0, tiled=True)
    ffn_w = lax.all_gather(ffn_own, "z", axis=0)
    rate = -jnp.exp(rest[:STATE])
    conv_w = [rest[STATE + k : STATE + k + 1] for k in range(taps)]
    conv_b, step_b, skip = (rest[STATE + taps + k : STATE + taps + k + 1] for k in range(3))
    inner_w = inners.reshape(2 * channels, width)

    padded = jnp.concatenate([jnp.full((taps - 1,), -1, jnp.int32), documents])
    ids = lax.dynamic_slice_in_dim(padded, z * rows, rows + taps - 1, 0)
    here = ids[taps - 1 :]
    same = [(ids[k : k + rows] == here)[:, None] for k in range(taps)]
    masks = jnp.concatenate([m.astype(F32) for m in same], axis=1)
    masks = jnp.pad(masks, ((0, 8), (0, 0)))

    x_f = x_ext.astype(F32)
    r_one = lax.rsqrt(jnp.mean(x_f * x_f, axis=-1, keepdims=True) + EPSILON)
    normed_one = (x_f * r_one * first_f).astype(BF16)
    conv_input = contract(normed_one, inner_w[:channels], 1, 1, BF16)
    gate_inner = contract(normed_one[HALO:], inner_w[channels:], 1, 1)
    shift = HALO - taps + 1
    total = conv_b
    for k in range(taps):
        tap = conv_input[shift + k : shift + k + rows].astype(F32)
        total = total + conv_w[k] * jnp.where(same[k], tap, 0.0)
    mixed_in = jax.nn.silu(total).astype(BF16)
    proj_part = contract(mixed_in, select_w, 1, 1)
    proj = plane_sum(proj_part, 1)
    step, slope, step_cut, drive, step_low, maps = prepare(
        proj, select_f, step_w, step_b, mixed_in, masks
    )
    mixed_f = mixed_in.astype(F32)
    local_final, through = forward_final(step_cut, drive, maps, rate)
    state_in = state_chain(planes, through, local_final, 4, True)
    sums, states, state_out = forward_all(step_cut, drive, maps, rate, state_in)
    mix = sums + skip * mixed_f
    gate_silu = jax.nn.silu(gate_inner)
    gated = (mix * gate_silu).astype(BF16)
    mixer_part = contract(gated, mixer_w, 1, 0, BF16)
    resid_mid, normed_two = mixer_join(
        mixer_part, block_input, second_f
    )

    two_part, out_part, ffn_hidden, gate_back, up_back = feed_forward(
        normed_two, cot_all, ffn_w
    )
    resid_grad, mixer_back, second_grad, ffn_grads, gate_grad = ffn_join(
        planes,
        two_part,
        resid_mid,
        second_f,
        cotangent,
        normed_two,
        cot_all,
        ffn_hidden,
        gate_back,
        up_back,
    )

    mix_grad, gate_back = turn_back(mixer_back, mixer_w, gate_inner, mix)
    ffn_sums = lax.psum_scatter(ffn_grads, "z", scatter_dimension=0, tiled=False)
    local_back = backward_first(step_cut, mix_grad, maps, rate)
    state_back, mixer_grad = state_chain(
        planes, through, local_back, 5, False, gated, mixer_back
    )
    map_sum, step_back, select_part, extra = backward_all(
        step_cut,
        drive,
        mix_grad,
        maps,
        rate,
        states,
        state_out,
        state_back,
        slope,
        mixed_in,
        step_w,
    )
    mixer_grad, ffn_sums, select_part = lax.optimization_barrier(
        (mixer_grad, ffn_sums, select_part)
    )
    mixer_sum = lax.psum_scatter(mixer_grad, "z", scatter_dimension=0, tiled=True)
    select_grad = plane_sum(select_part, 7, BF16)
    one_part, inner_grad, slab_grad, first_grad, select_gain_grad = unwind(
        select_grad,
        proj,
        select_f,
        select_w,
        step,
        map_sum,
        mix_grad,
        rest,
        conv_input,
        masks,
        gate_back,
        normed_one,
        inner_w,
        mixed_in,
        step_low,
        step_back,
        first_f,
        extra,
    )
    results = closing(
        planes,
        one_part,
        block_input,
        first_f,
        resid_grad,
        inner_grad.reshape(planes, inner_block, width),
        slab_grad,
        (first_grad, second_grad, select_gain_grad),
        out_part,
        resid_mid,
        ffn_sums,
        mixer_sum,
    )
    (
        input_grad,
        inner_out,
        select_out,
        step_out,
        block_output,
        up_out,
        down_out,
        mixer_out,
        decay_out,
        conv_out,
        conv_b_out,
        step_b_out,
        skip_out,
        first_out,
        second_out,
        gain_out,
        gate_out,
    ) = hand_over((*results, gate_grad))
    return (
        block_output,
        input_grad,
        first_out[0],
        inner_out.T,
        conv_out,
        conv_b_out[0],
        select_out,
        gain_out[0],
        step_out,
        step_b_out[0],
        decay_out,
        skip_out[0],
        mixer_out,
        second_out[0],
        gate_out if gate_out.shape[0] == width else gate_out.T,
        up_out if up_out.shape[0] == width else up_out.T,
        down_out,
    )


def solution(mesh):
    planes = mesh.devices.size // PLANE
    grid = Mesh(mesh.devices.reshape(planes, PLANE), ("z", "p"))
    seq = ("z", "p")
    by_row, by_column, flat = P(seq, None), P(None, seq), P(seq)

    def program(*args):
        return on_device(planes, *args)

    return jax.shard_map(
        program,
        mesh=grid,
        in_specs=(
            by_row,
            P(),
            flat,
            by_column,
            by_column,
            flat,
            by_row,
            flat,
            by_column,
            flat,
            by_column,
            flat,
            by_row,
            flat,
            by_column,
            by_column,
            by_row,
            by_row,
        ),
        out_specs=(
            by_row,
            by_row,
            flat,
            by_column,
            by_column,
            flat,
            by_row,
            flat,
            by_column,
            flat,
            by_column,
            flat,
            by_row,
            flat,
            by_column,
            by_column,
            by_row,
        ),
        check_vma=False,
    )
```
